32 devices in a mesh: dp: 2 (over x), ctx: 8 (over z, y), fsdp: 2 (over core).
Axes of the slice: x: 2, y: 2, z: 4, core: 2. Of those that a mesh axis runs over, the one named last changes fastest.
Arguments:
- tokens: bfloat16 [8, 1024, 1024], P(('dp', 'fsdp'), 'ctx'), may hold values from -6 to 6
- query_key_value_weight: bfloat16 [1024, 3072], P('fsdp'), may hold values from -0.1875 to 0.1875
- bias_query: bfloat16 [1024], P('fsdp'), may hold values from -4 to 4
- bias_value: bfloat16 [1024], P('fsdp'), may hold values from -0.3125 to 0.3125
- attention_out_weight: bfloat16 [1024, 1024], P('fsdp'), may hold values from -3.5 to 3.5
- attention_out_bias: bfloat16 [1024], P('fsdp'), may hold values from -4 to 4
- gain_one: bfloat16 [1024], P('fsdp'), may hold values from 0.5 to 1.5
- shift_one: bfloat16 [1024], P('fsdp'), may hold values from -4 to 4
- feedforward_in_weight: bfloat16 [1024, 4096], P('fsdp'), may hold values from -0.1875 to 0.1875
- feedforward_in_bias: bfloat16 [4096], P('fsdp'), may hold values from -4 to 4
- feedforward_out_weight: bfloat16 [4096, 1024], P('fsdp'), may hold values from -0.09375 to 0.09375
- feedforward_out_bias: bfloat16 [1024], P('fsdp'), may hold values from -4 to 4
- gain_two: bfloat16 [1024], P('fsdp'), may hold values from 0.5 to 1.5
- shift_two: bfloat16 [1024], P('fsdp'), may hold values from -4 to 4
- d_out: bfloat16 [8, 1024, 1024], P(('dp', 'fsdp'), 'ctx'), may hold values from -6 to 6
Outputs:
- output: bfloat16 [8, 1024, 1024], P(('dp', 'fsdp'), 'ctx')
- grad_tokens: float32 [8, 1024, 1024], P(('dp', 'fsdp'), 'ctx')
- grad_qkv: float32 [1024, 3072], P('fsdp')
- grad_bias_query: float32 [1024], P('fsdp')
- grad_bias_value: float32 [1024], P('fsdp')
- grad_out: float32 [1024, 1024], P('fsdp')
- grad_bias_out: float32 [1024], P('fsdp')
- grad_gain_one: float32 [1024], P('fsdp')
- grad_shift_one: float32 [1024], P('fsdp')
- grad_in: float32 [1024, 4096], P('fsdp')
- grad_bias_in: float32 [4096], P('fsdp')
- grad_back: float32 [4096, 1024], P('fsdp')
- grad_bias_back: float32 [1024], P('fsdp')
- grad_gain_two: float32 [1024], P('fsdp')
- grad_shift_two: float32 [1024], P('fsdp')
The draws below stay inside these ranges and needn't reach their ends.
All inputs are finite; a program needn't handle non-finite values.
Results may differ from the reference program's by a relative error of at most 0.025.
Values may be sent and summed in bfloat16 or wider, within the bound.
No kernel may reach another device: no remote copies, remote signals or barrier semaphores. Data moves between devices by JAX's collectives and lax.ppermute only.
A program may use at most 192 MiB of HBM per device.

```python
import math
import jax
import jax.numpy as jnp
from jax import lax

D = 1024
HEADS = 16
HEAD_DIM = 64
FF = 4096
LENGTH = 1024
SEQS = 8


def steps_of(stream_key, dims, cuts, smallest, top_value):
    def one(dim, parts):
        steps = jax.random.uniform(jax.random.fold_in(jax.random.fold_in(stream_key, 6), dim), (parts,), jnp.float32, smallest / len(cuts), top_value / len(cuts))
        return jnp.repeat(jnp.exp(steps), dims[dim] // parts).reshape((-1,) + (1,) * (len(dims) - dim - 1))

    gain = one(*cuts[0])
    for cut in cuts[1:]:
        gain = gain * one(*cut)
    return gain


def normal_values(key, dims, scale, reach, shards=(), held_as=jnp.bfloat16):
    drawn = jax.random.normal(key, dims, jnp.float32) * scale
    if len(shards) > 0:
        drawn = steps_of(key, dims, shards, -0.22, 0.18) * drawn
    return jnp.clip(drawn, min=-reach, max=reach).astype(held_as)


def setup_inputs(seed: int = 0) -> dict:
    splits = jax.random.split(jax.random.key(seed), 16)
    return {
        "tokens": normal_values(splits[0], (SEQS, LENGTH, D), 1.0, 6.0, ((0, 4), (1, 8))),
        "query_key_value_weight": normal_values(splits[1], (D, 3 * D), D ** -0.5, 0.1875, ((0, 2),)),
        "bias_query": normal_values(splits[2], (D,), 0.3, 4.0, ((0, 2),)),
        "bias_value": normal_values(splits[3], (D,), 0.02, 0.3125, ((0, 2),)),
        "attention_out_weight": normal_values(splits[4], (D, D), (max(1, 3 * D // LENGTH)) ** -0.5, 3.5, ((0, 2),)),
        "attention_out_bias": normal_values(splits[5], (D,), 0.3, 4.0, ((0, 2),)),
        "gain_one": jnp.clip(1.0 + 0.1 * jax.random.normal(splits[6], (D,), jnp.float32), 0.5, 1.5).astype(jnp.bfloat16),
        "shift_one": normal_values(splits[7], (D,), 0.3, 4.0, ((0, 2),)),
        "feedforward_in_weight": normal_values(splits[8], (D, FF), D ** -0.5, 0.1875, ((0, 2),)),
        "feedforward_in_bias": normal_values(splits[9], (FF,), 0.3, 4.0, ((0, 2),)),
        "feedforward_out_weight": normal_values(splits[10], (FF, D), FF ** -0.5, 0.09375, ((0, 2),)),
        "feedforward_out_bias": normal_values(splits[11], (D,), 0.3, 4.0, ((0, 2),)),
        "gain_two": jnp.clip(1.0 + 0.1 * jax.random.normal(splits[12], (D,), jnp.float32), 0.5, 1.5).astype(jnp.bfloat16),
        "shift_two": normal_values(splits[13], (D,), 0.3, 4.0, ((0, 2),)),
        "d_out": normal_values(splits[14], (SEQS, LENGTH, D), 1.0, 6.0, ((0, 4), (1, 8))),
    }


@jax.custom_vjp
def reduced_width(v):
    return lax.optimization_barrier(v.astype(jnp.bfloat16)).astype(jnp.float32)

@jax.custom_vjp
def low_back(v):
    return v

def low_keep(v):
    return (reduced_width(v), None)

def low_pass(kept, grad):
    return (grad,)

def back_keep(v):
    return (v, None)

def back_low(kept, grad):
    return (reduced_width(grad),)
reduced_width.defvjp(low_keep, low_pass)
low_back.defvjp(back_keep, back_low)
EPSILON = 1e-06
MAXIMAL_PRECISION = lax.Precision.HIGHEST

def norm_apply(values, gain_vec, shift_vec):
    centre = lax.optimization_barrier(jnp.mean(values, axis=-1, keepdims=True))
    centred = values - centre
    variance = lax.optimization_barrier(jnp.mean(centred * centred, axis=-1, keepdims=True))
    return centred * lax.rsqrt(variance + EPSILON) * gain_vec + shift_vec

def attend_block(query_block, key_rows, value_rows):
    scores = jnp.einsum('qhd,khd->hqk', query_block, key_rows, precision=MAXIMAL_PRECISION) * HEAD_DIM ** (-0.5)
    scores = low_back(scores)
    row_max = lax.optimization_barrier(jnp.max(scores, axis=-1, keepdims=True))
    weights = jnp.exp(scores - row_max)
    probabilities = reduced_width(weights / lax.optimization_barrier(jnp.sum(weights, axis=-1, keepdims=True)))
    return jnp.einsum('hqk,khd->qhd', probabilities, value_rows, precision=MAXIMAL_PRECISION)
checked_block = jax.checkpoint(attend_block)

def attend_sequence(triple):
    query_rows, key_rows, value_rows = triple
    block_rows = math.gcd(LENGTH, 512)
    blocks = query_rows.reshape(LENGTH // block_rows, block_rows, HEADS, HEAD_DIM)
    results = lax.map(lambda query_block: checked_block(query_block, key_rows, value_rows), blocks)
    return results.reshape(LENGTH, HEADS * HEAD_DIM)

def forward(token_subset, query_key_value_weight, bias_query, bias_value, attention_out_weight, attention_out_bias, gain_one, shift_one, feedforward_in_weight, feedforward_in_bias, feedforward_out_weight, feedforward_out_bias, gain_two, shift_two):
    packed = token_subset.shape[0]
    projected_rows = jnp.einsum('ugj,jn->ugn', token_subset, query_key_value_weight, precision=MAXIMAL_PRECISION)
    projected_rows = projected_rows + jnp.concatenate([bias_query, jnp.zeros_like(bias_query), bias_value])
    projected_rows = reduced_width(low_back(projected_rows))
    query_all = projected_rows[..., :D].reshape(packed, LENGTH, HEADS, HEAD_DIM)
    key_all = projected_rows[..., D:2 * D].reshape(packed, LENGTH, HEADS, HEAD_DIM)
    value_all = projected_rows[..., 2 * D:].reshape(packed, LENGTH, HEADS, HEAD_DIM)
    attention_result = lax.map(attend_sequence, (query_all, key_all, value_all))
    attention_result = reduced_width(low_back(attention_result))
    attention_branch = jnp.einsum('ugj,jn->ugn', attention_result, attention_out_weight, precision=MAXIMAL_PRECISION) + attention_out_bias
    attention_branch = low_back(attention_branch)
    first_normalized = norm_apply(token_subset + attention_branch, gain_one, shift_one)
    hidden_before_gelu = jnp.einsum('ugj,jn->ugn', reduced_width(first_normalized), feedforward_in_weight, precision=MAXIMAL_PRECISION) + feedforward_in_bias
    hidden_before_gelu = low_back(hidden_before_gelu)
    activated_hidden = reduced_width(jax.nn.gelu(hidden_before_gelu, approximate=False))
    feedforward_branch = jnp.einsum('gfy,yq->gfq', activated_hidden, feedforward_out_weight, precision=MAXIMAL_PRECISION) + feedforward_out_bias
    feedforward_branch = low_back(feedforward_branch)
    return norm_apply(first_normalized + feedforward_branch, gain_two, shift_two)

def reference(tokens, query_key_value_weight, bias_query, bias_value, attention_out_weight, attention_out_bias, gain_one, shift_one, feedforward_in_weight, feedforward_in_bias, feedforward_out_weight, feedforward_out_bias, gain_two, shift_two, d_out):
    params = tuple((item.astype(jnp.float32) for item in (query_key_value_weight, bias_query, bias_value, attention_out_weight, attention_out_bias, gain_one, shift_one, feedforward_in_weight, feedforward_in_bias, feedforward_out_weight, feedforward_out_bias, gain_two, shift_two)))
    packed = math.gcd(SEQS, max(1, 4096 // LENGTH))
    token_groups = tokens.astype(jnp.float32).reshape(SEQS // packed, packed, LENGTH, D)
    grad_groups = d_out.astype(jnp.float32).reshape(SEQS // packed, packed, LENGTH, D)

    def one_group(totals, inputs):
        token_subset, grad_group = inputs
        result, pull_back = jax.vjp(forward, token_subset, *params)
        grads = pull_back(grad_group)
        totals = tuple((total_sum + grad_part for total_sum, grad_part in zip(totals, grads[1:])))
        return (totals, (result, grads[0]))
    initial = tuple((jnp.zeros_like(param_now) for param_now in params))
    totals, (results, token_grads) = lax.scan(one_group, initial, (token_groups, grad_groups))
    output = results.reshape(SEQS, LENGTH, D).astype(jnp.bfloat16)
    grad_tokens = token_grads.reshape(SEQS, LENGTH, D)
    return (output, grad_tokens, totals[0], totals[1], totals[2], totals[3], totals[4], totals[5], totals[6], totals[7], totals[8], totals[9], totals[10], totals[11], totals[12])
```

```python
from functools import partial

import jax
import jax.numpy as jnp
from jax import lax
from jax.experimental import pallas as pl
from jax.experimental.pallas import tpu as pltpu
from jax.sharding import PartitionSpec as P

HEADS = 16
HEAD_DIM = 64


EPSILON = 1e-06


def from_behind(block, axis, distance):
    devices = range(lax.axis_size(axis))
    route = [((i - distance) % len(devices), i) for i in devices]
    return lax.ppermute(block, axis, route)


def norm_apply(values, gain_vec, shift_vec):
    centre = jnp.mean(values, axis=-1, keepdims=True)
    centred = values - centre
    variance = jnp.mean(centred * centred, axis=-1, keepdims=True)
    return centred * lax.rsqrt(variance + EPSILON) * gain_vec + shift_vec


def lowered(values):
    return values.astype(jnp.bfloat16)


def widened(values):
    return values.astype(jnp.float32)


def project(left_operand_rows, right_operand_matrix):
    return jnp.einsum(
        "ugj,jn->ugn", left_operand_rows, right_operand_matrix, preferred_element_type=jnp.float32
    )


def weight_grad(left_operand_rows, gradient_row_block):
    return jnp.einsum(
        "xrb,xrw->bw", left_operand_rows, gradient_row_block, preferred_element_type=jnp.float32
    )


def back_project(gradient_row_block, right_operand_matrix):
    return jnp.einsum(
        "wkb,fb->wkf", gradient_row_block, right_operand_matrix, preferred_element_type=jnp.float32
    )


def column_sum(values):
    return jnp.sum(widened(values), axis=(0, 1))


def split_heads(values):
    return values.reshape(values.shape[0], values.shape[1], HEADS, HEAD_DIM)


def merge_heads(values):
    return values.reshape(values.shape[0], values.shape[1], HEADS * HEAD_DIM)


def split_blocks(values, block_rows):
    seq_count = values.shape[0]
    blocks = values.shape[1] // block_rows
    return jnp.moveaxis(values.reshape(seq_count, blocks, block_rows, values.shape[2]), 1, 0)


def block_scores(query_rows, key_rows):
    scores = jnp.einsum(
        "sqhd,skhd->shqk",
        split_heads(query_rows),
        split_heads(key_rows),
        preferred_element_type=jnp.float32,
    )
    return scores * HEAD_DIM ** (-0.5)


def fold_block(state_now, key_block, value_block, query_rows):
    running_max, running_sum, running_acc = state_now
    scores = block_scores(query_rows, key_block)
    new_max = jnp.maximum(running_max, jnp.max(scores, axis=-1))
    rescale = jnp.exp(running_max - new_max)
    weights = jnp.exp(scores - new_max[..., None])
    new_sum = running_sum * rescale + jnp.sum(weights, axis=-1)
    product = jnp.einsum(
        "shqk,skhd->shqd",
        lowered(weights),
        split_heads(value_block),
        preferred_element_type=jnp.float32,
    )
    return (new_max, new_sum, running_acc * rescale[..., None] + product)


def attend_forward(query_rows, key_rows, value_rows):
    seq_count = query_rows.shape[0]
    block_rows = query_rows.shape[1]
    initial = (
        jnp.full((seq_count, HEADS, block_rows), -1e30, jnp.float32),
        jnp.zeros((seq_count, HEADS, block_rows), jnp.float32),
        jnp.zeros((seq_count, HEADS, block_rows, HEAD_DIM), jnp.float32),
    )
    kept = None
    key_part = lax.all_gather(key_rows, "ctx", axis=1, tiled=True)
    value_part = lax.all_gather(value_rows, "ctx", axis=1, tiled=True)

    def one_block(state_in, block_pair):
        return (fold_block(state_in, block_pair[0], block_pair[1], query_rows), None)

    state_out, unused = lax.scan(
        one_block,
        initial,
        (split_blocks(key_part, block_rows), split_blocks(value_part, block_rows)),
    )
    running_max, running_sum, running_acc = state_out
    attention_result = running_acc / running_sum[..., None]
    attention_result = jnp.transpose(attention_result, (0, 2, 1, 3)).reshape(
        seq_count, block_rows, HEADS * HEAD_DIM
    )
    log_total = running_max + jnp.log(running_sum)
    return (attention_result, log_total, kept)


def attend_back(query_rows, gradient_row_block, log_total, row_inner, key_rows, value_rows):
    score_scale = HEAD_DIM ** (-0.5)
    scores = block_scores(query_rows, key_rows)
    probabilities = jnp.exp(scores - log_total[..., None])
    value_grad = jnp.einsum(
        "shqk,sqhd->skhd",
        lowered(probabilities),
        split_heads(gradient_row_block),
        preferred_element_type=jnp.float32,
    )
    prob_grad = jnp.einsum(
        "sqhd,skhd->shqk",
        split_heads(gradient_row_block),
        split_heads(value_rows),
        preferred_element_type=jnp.float32,
    )
    score_grad = lowered(probabilities * (prob_grad - row_inner[..., None]))
    query_grad = (
        jnp.einsum(
            "shqk,skhd->sqhd", score_grad, split_heads(key_rows), preferred_element_type=jnp.float32
        )
        * score_scale
    )
    key_grad = (
        jnp.einsum(
            "shqk,sqhd->skhd",
            score_grad,
            split_heads(query_rows),
            preferred_element_type=jnp.float32,
        )
        * score_scale
    )
    return (merge_heads(query_grad), merge_heads(key_grad), merge_heads(value_grad))


def attend_backward(query_rows, gradient_row_block, log_total, row_inner, key_rows, value_rows):
    zero_rows = jnp.zeros(query_rows.shape, jnp.float32)
    turn_count = lax.axis_size("ctx") // 2

    def turn_keys(turn_index, carried):
        moving_key, moving_value, key_acc, value_acc, query_acc = carried
        for half_step in range(2):
            pieces = attend_back(
                query_rows, gradient_row_block, log_total, row_inner, moving_key, moving_value
            )
            query_acc = query_acc + pieces[0]
            key_acc = key_acc + pieces[1]
            value_acc = value_acc + pieces[2]
            moving_key, moving_value = from_behind((moving_key, moving_value), "ctx", 1)
            key_acc, value_acc = (
                from_behind(key_acc.astype(jnp.bfloat16), "ctx", 1).astype(key_acc.dtype),
                from_behind(value_acc.astype(jnp.bfloat16), "ctx", 1).astype(value_acc.dtype),
            )
        return (moving_key, moving_value, key_acc, value_acc, query_acc)

    finished = lax.fori_loop(
        0, turn_count, turn_keys, (key_rows, value_rows, zero_rows, zero_rows, zero_rows)
    )
    return (finished[4], finished[2], finished[3])


def ring_on_device(
    tokens,
    query_key_value_weight,
    bias_query,
    bias_value,
    attention_out_weight,
    attention_out_bias,
    gain_one,
    shift_one,
    feedforward_in_weight,
    feedforward_in_bias,
    feedforward_out_weight,
    feedforward_out_bias,
    gain_two,
    shift_two,
    d_out,
):
    attn_full = (
        lax.all_gather(query_key_value_weight, "fsdp", axis=0, tiled=True),
        lax.all_gather(attention_out_weight, "fsdp", axis=0, tiled=True),
        lax.all_gather(bias_query, "fsdp", axis=0, tiled=True),
        lax.all_gather(bias_value, "fsdp", axis=0, tiled=True),
        lax.all_gather(attention_out_bias, "fsdp", axis=0, tiled=True),
        lax.all_gather(gain_one, "fsdp", axis=0, tiled=True),
        lax.all_gather(shift_one, "fsdp", axis=0, tiled=True),
    )
    qkv_full, out_full, query_bias, value_bias, out_bias, gain_first, shift_first = attn_full
    model_width = out_full.shape[0]
    projected_rows = project(tokens, qkv_full) + jnp.concatenate(
        [widened(query_bias), jnp.zeros((model_width,), jnp.float32), widened(value_bias)]
    )
    projected_low = lowered(projected_rows)
    query_rows = projected_low[..., :model_width]
    key_rows = projected_low[..., model_width : 2 * model_width]
    value_rows = projected_low[..., 2 * model_width :]
    attention_result, log_total, kept = attend_forward(query_rows, key_rows, value_rows)
    attended_low = lowered(attention_result)
    attention_branch = project(attended_low, out_full) + widened(out_bias)
    summed_one = widened(tokens) + attention_branch
    first_normalized, pull_one = jax.vjp(
        norm_apply, summed_one, widened(gain_first), widened(shift_first)
    )
    normed_low = lowered(first_normalized)
    ffn_full = (
        lax.all_gather(feedforward_in_weight, "fsdp", axis=0, tiled=True),
        lax.all_gather(feedforward_out_weight, "fsdp", axis=0, tiled=True),
        lax.all_gather(feedforward_in_bias, "fsdp", axis=0, tiled=True),
        lax.all_gather(feedforward_out_bias, "fsdp", axis=0, tiled=True),
        lax.all_gather(gain_two, "fsdp", axis=0, tiled=True),
        lax.all_gather(shift_two, "fsdp", axis=0, tiled=True),
    )
    in_full, back_full, inner_bias, back_bias, gain_second, shift_second = ffn_full
    hidden_before_gelu = project(normed_low, in_full) + widened(inner_bias)
    active_low = lowered(jax.nn.gelu(hidden_before_gelu, approximate=False))
    feedforward_branch = project(active_low, back_full) + widened(back_bias)

    def second_norm(residual_in, branch_in, gain_vec, shift_vec):
        return norm_apply(residual_in + branch_in, gain_vec, shift_vec)

    result, pull_two = jax.vjp(
        second_norm,
        first_normalized,
        feedforward_branch,
        widened(gain_second),
        widened(shift_second),
    )
    output = lowered(result)
    first_grad_res, second_grad, gain_two_grad, shift_two_grad = pull_two(widened(d_out))
    in_full, back_full = (
        lax.all_gather(feedforward_in_weight, "fsdp", axis=0, tiled=True),
        lax.all_gather(feedforward_out_weight, "fsdp", axis=0, tiled=True),
    )
    second_low = lowered(second_grad)
    back_grad = weight_grad(active_low, second_low)
    back_bias_grad = column_sum(second_low)
    active_grad = back_project(second_low, back_full)
    gelu_pull = jax.vjp(partial(jax.nn.gelu, approximate=False), hidden_before_gelu)[1]
    hidden_low = lowered(gelu_pull(active_grad)[0])
    in_grad = weight_grad(normed_low, hidden_low)
    in_bias_grad = column_sum(hidden_low)
    first_grad = first_grad_res + back_project(hidden_low, in_full)
    ffn_grads = (
        lax.psum_scatter(
            in_grad.astype(jnp.bfloat16), "fsdp", scatter_dimension=0, tiled=True
        ).astype(jnp.float32),
        lax.psum_scatter(
            in_bias_grad.astype(jnp.bfloat16), "fsdp", scatter_dimension=0, tiled=True
        ).astype(jnp.float32),
        lax.psum_scatter(
            back_grad.astype(jnp.bfloat16), "fsdp", scatter_dimension=0, tiled=True
        ).astype(jnp.float32),
        lax.psum_scatter(
            back_bias_grad.astype(jnp.bfloat16), "fsdp", scatter_dimension=0, tiled=True
        ).astype(jnp.float32),
        lax.psum_scatter(
            gain_two_grad.astype(jnp.bfloat16), "fsdp", scatter_dimension=0, tiled=True
        ).astype(jnp.float32),
        lax.psum_scatter(
            shift_two_grad.astype(jnp.bfloat16), "fsdp", scatter_dimension=0, tiled=True
        ).astype(jnp.float32),
    )
    ffn_grads = lax.psum(
        (ffn_grads[0], ffn_grads[1], ffn_grads[2], ffn_grads[3], ffn_grads[4], ffn_grads[5]),
        ("dp", "ctx"),
    )
    summed_grad, gain_one_grad, shift_one_grad = pull_one(first_grad)
    qkv_full, out_full = (
        lax.all_gather(query_key_value_weight, "fsdp", axis=0, tiled=True),
        lax.all_gather(attention_out_weight, "fsdp", axis=0, tiled=True),
    )
    branch_low = lowered(summed_grad)
    out_grad = weight_grad(attended_low, branch_low)
    out_bias_grad = column_sum(branch_low)
    attended_grad_low = lowered(back_project(branch_low, out_full))
    row_inner = jnp.sum(
        split_heads(widened(attended_grad_low)) * split_heads(attention_result), axis=-1
    )
    row_inner = jnp.transpose(row_inner, (0, 2, 1))
    query_grad, key_grad, value_grad = attend_backward(
        query_rows, attended_grad_low, log_total, row_inner, key_rows, value_rows
    )
    mixed_grad = lowered(jnp.concatenate([query_grad, key_grad, value_grad], axis=-1))
    qkv_grad = weight_grad(tokens, mixed_grad)
    bias_grads = column_sum(mixed_grad)
    query_bias_grad = bias_grads[:model_width]
    value_bias_grad = bias_grads[2 * model_width :]
    token_grad = summed_grad + back_project(mixed_grad, qkv_full)
    attn_grads = (
        lax.psum_scatter(
            qkv_grad.astype(jnp.bfloat16), "fsdp", scatter_dimension=0, tiled=True
        ).astype(jnp.float32),
        lax.psum_scatter(
            query_bias_grad.astype(jnp.bfloat16), "fsdp", scatter_dimension=0, tiled=True
        ).astype(jnp.float32),
        lax.psum_scatter(
            value_bias_grad.astype(jnp.bfloat16), "fsdp", scatter_dimension=0, tiled=True
        ).astype(jnp.float32),
        lax.psum_scatter(
            out_grad.astype(jnp.bfloat16), "fsdp", scatter_dimension=0, tiled=True
        ).astype(jnp.float32),
        lax.psum_scatter(
            out_bias_grad.astype(jnp.bfloat16), "fsdp", scatter_dimension=0, tiled=True
        ).astype(jnp.float32),
        lax.psum_scatter(
            gain_one_grad.astype(jnp.bfloat16), "fsdp", scatter_dimension=0, tiled=True
        ).astype(jnp.float32),
        lax.psum_scatter(
            shift_one_grad.astype(jnp.bfloat16), "fsdp", scatter_dimension=0, tiled=True
        ).astype(jnp.float32),
    )
    attn_grads = lax.psum(
        (
            attn_grads[0],
            attn_grads[1],
            attn_grads[2],
            attn_grads[3],
            attn_grads[4],
            attn_grads[5],
            attn_grads[6],
        ),
        ("dp", "ctx"),
    )
    return (
        output,
        token_grad,
        attn_grads[0],
        attn_grads[1],
        attn_grads[2],
        attn_grads[3],
        attn_grads[4],
        attn_grads[5],
        attn_grads[6],
        ffn_grads[0],
        ffn_grads[1],
        ffn_grads[2],
        ffn_grads[3],
        ffn_grads[4],
        ffn_grads[5],
    )


def exchange(values, axis, bit):
    count = lax.axis_size(axis)
    return lax.ppermute(values, axis, [(i, i ^ bit) for i in range(count)])


def bits_below(count):
    return [1 << k for k in range(count.bit_length() - 1)]


def reorder(pieces, index):
    for bit in bits_below(len(pieces)):
        taken = (index & bit) != 0
        pieces = [jnp.where(taken, pieces[k ^ bit], pieces[k]) for k in range(len(pieces))]
    return pieces


def pair_join(own, other, core, axis=0):
    first = jnp.where(core == 0, own, other)
    second = jnp.where(core == 0, other, own)
    return jnp.concatenate([first, second], axis=axis)


def half_of(values, which, axis):
    size = values.shape[axis] // 2
    low = lax.slice_in_dim(values, 0, size, axis=axis)
    high = lax.slice_in_dim(values, size, 2 * size, axis=axis)
    return jnp.where(which == 0, low, high)


def gather_blocks(block):
    count = lax.axis_size("ctx")
    pieces = {0: block}
    for bit in reversed(bits_below(count)):
        for k in list(pieces):
            pieces[k ^ bit] = exchange(pieces[k], "ctx", bit)
    return [pieces[k] for k in range(count)]


def swap_blocks(pieces):
    return [pieces[0]] + [exchange(pieces[k], "ctx", k) for k in range(1, len(pieces))]


def head_mask(value):
    lane = lax.broadcasted_iota(jnp.int32, (1, 2 * HEAD_DIM), 1)
    return [
        jnp.where(lane < HEAD_DIM, value, 0.0),
        jnp.where(lane < HEAD_DIM, 0.0, value),
    ]


def contract(left, right, left_dim, right_dim):
    return lax.dot_general(
        left, right, (((left_dim,), (right_dim,)), ((), ())), preferred_element_type=jnp.float32
    )


def forward_kernel(query_ref, key_ref, value_ref, result_ref, low_ref, log_ref):
    query = query_ref[0].astype(jnp.float32)
    keys = key_ref[0]
    values = value_ref[0]
    results = []
    logs = []
    for mask in head_mask(HEAD_DIM ** (-0.5)):
        scores = contract((query * mask).astype(jnp.bfloat16), keys, 1, 1)
        row_max = jnp.max(scores, axis=-1, keepdims=True)
        weights = jnp.exp(scores - row_max)
        total = jnp.sum(weights, axis=-1, keepdims=True)
        probabilities = (weights * (1.0 / total)).astype(jnp.bfloat16)
        results.append(contract(probabilities, values, 1, 0))
        logs.append(row_max + jnp.log(total))
    first = lax.broadcasted_iota(jnp.int32, results[0].shape, 1) < HEAD_DIM
    result = jnp.where(first, results[0], results[1])
    result_ref[0] = result
    low_ref[0] = result.astype(jnp.bfloat16)
    log_ref[0] = jnp.where(first, logs[0], logs[1])


def attention_forward(projected):
    seqs, length, width = projected.shape
    pair = width // 3
    rows = min(256, length)
    row_spec = pl.BlockSpec((1, rows, pair), lambda s, q: (s, q, 0))
    return pl.pallas_call(
        forward_kernel,
        grid=(seqs, length // rows),
        in_specs=[
            row_spec,
            pl.BlockSpec((1, length, pair), lambda s, q: (s, 0, 1)),
            pl.BlockSpec((1, length, pair), lambda s, q: (s, 0, 2)),
        ],
        out_specs=[row_spec, row_spec, row_spec],
        out_shape=[
            jax.ShapeDtypeStruct((seqs, length, pair), jnp.float32),
            jax.ShapeDtypeStruct((seqs, length, pair), jnp.bfloat16),
            jax.ShapeDtypeStruct((seqs, length, pair), jnp.float32),
        ],
        compiler_params=pltpu.CompilerParams(vmem_limit_bytes=48 << 20),
        name="attention_forward",
    )(projected, projected, projected)


def backward_kernel(
    query_ref, key_ref, value_ref, grad_ref, result_ref, log_ref,
    query_out, key_out, value_out, query_acc, log_rows, inner_rows,
):
    step = pl.program_id(1)

    @pl.when(step == 0)
    def first_step():
        query_acc[...] = jnp.zeros_like(query_acc)
        logs = jnp.transpose(log_ref[0])
        inner = jnp.transpose(grad_ref[0].astype(jnp.float32) * result_ref[0])
        for h in range(2):
            log_rows[h] = jnp.broadcast_to(
                logs[h * HEAD_DIM : h * HEAD_DIM + 1], log_rows.shape[1:]
            )
            inner_rows[h] = jnp.broadcast_to(
                jnp.sum(inner[h * HEAD_DIM : (h + 1) * HEAD_DIM], axis=0, keepdims=True),
                inner_rows.shape[1:],
            )

    queries = query_ref[0]
    grads = grad_ref[0]
    keys = key_ref[0]
    values = value_ref[0]
    scale = HEAD_DIM ** (-0.5)
    query_parts = []
    key_parts = []
    value_parts = []
    scaled_masks = head_mask(scale)
    masks = head_mask(1.0)
    for h in range(2):
        scores = contract(
            (keys.astype(jnp.float32) * scaled_masks[h]).astype(jnp.bfloat16), queries, 1, 1
        )
        probabilities = jnp.exp(scores - log_rows[h, :1])
        prob_grad = contract(
            (values.astype(jnp.float32) * masks[h]).astype(jnp.bfloat16), grads, 1, 1
        )
        score_grad = (probabilities * (prob_grad - inner_rows[h, :1])).astype(jnp.bfloat16)
        value_parts.append(contract(probabilities.astype(jnp.bfloat16), grads, 1, 0))
        key_parts.append(contract(score_grad, queries, 1, 0))
        query_parts.append(contract(score_grad, keys, 0, 0))
    first = lax.broadcasted_iota(jnp.int32, key_parts[0].shape, 1) < HEAD_DIM
    value_out[0] = jnp.where(first, value_parts[0], value_parts[1]).astype(jnp.bfloat16)
    key_out[0] = (jnp.where(first, key_parts[0], key_parts[1]) * scale).astype(jnp.bfloat16)
    first = lax.broadcasted_iota(jnp.int32, query_parts[0].shape, 1) < HEAD_DIM
    query_acc[...] += jnp.where(first, query_parts[0], query_parts[1])

    @pl.when(step == pl.num_programs(1) - 1)
    def last_step():
        query_out[0] = (query_acc[...] * scale).astype(jnp.bfloat16)


def attention_backward(projected, grads, result, logs):
    seqs, length, width = projected.shape
    pair = width // 3
    rows = min(256, length)
    whole = pl.BlockSpec((1, length, pair), lambda s, k: (s, 0, 0))
    block = pl.BlockSpec((1, rows, pair), lambda s, k: (s, k, 0))
    shape = jax.ShapeDtypeStruct((seqs, length, pair), jnp.bfloat16)
    return pl.pallas_call(
        backward_kernel,
        grid=(seqs, length // rows),
        in_specs=[
            whole,
            pl.BlockSpec((1, rows, pair), lambda s, k: (s, k, 1)),
            pl.BlockSpec((1, rows, pair), lambda s, k: (s, k, 2)),
            whole,
            whole,
            whole,
        ],
        out_specs=[whole, block, block],
        out_shape=[shape, shape, shape],
        scratch_shapes=[
            pltpu.VMEM((length, pair), jnp.float32),
            pltpu.VMEM((2, 8, length), jnp.float32),
            pltpu.VMEM((2, 8, length), jnp.float32),
        ],
        compiler_params=pltpu.CompilerParams(vmem_limit_bytes=48 << 20),
        name="attention_backward",
    )(projected, projected, projected, grads, result, logs)


def grad_kernel(place_ref, left_own, left_other, right_own, right_other, keep_ref, send_ref):
    step = pl.program_id(0)
    half = pl.num_programs(0) // 2
    total = contract(left_own[...], right_own[...], 0, 0)
    total = total + contract(left_other[...], right_other[...], 0, 0)
    total = total.astype(jnp.bfloat16)

    @pl.when(step < half)
    def outgoing():
        send_ref[0] = total

    @pl.when(step >= half)
    def kept():
        keep_ref[0] = total


def pair_grad(place, left_pair, right_pair, row_bits, col_bits, name):
    tokens, width = left_pair[0].shape
    columns = right_pair[0].shape[1]
    rows = width >> row_bits
    cols = columns >> col_bits
    count = 1 << (row_bits + col_bits)
    half = count // 2

    def chunk(step):
        return (step + half) % count

    left = pl.BlockSpec((tokens, rows), lambda s, p: (0, (chunk(s) ^ p[0]) >> col_bits))
    right = pl.BlockSpec(
        (tokens, cols), lambda s, p: (0, (chunk(s) ^ p[0]) & ((1 << col_bits) - 1))
    )
    shape = jax.ShapeDtypeStruct((half, rows, cols), jnp.bfloat16)
    return pl.pallas_call(
        grad_kernel,
        grid_spec=pltpu.PrefetchScalarGridSpec(
            num_scalar_prefetch=1,
            grid=(count,),
            in_specs=[left, left, right, right],
            out_specs=[
                pl.BlockSpec((1, rows, cols), lambda s, p: (jnp.maximum(s - half, 0), 0, 0)),
                pl.BlockSpec((1, rows, cols), lambda s, p: (jnp.minimum(s, half - 1), 0, 0)),
            ],
        ),
        out_shape=[shape, shape],
        compiler_params=pltpu.CompilerParams(vmem_limit_bytes=48 << 20),
        name=name,
    )(place, left_pair[0], left_pair[1], right_pair[0], right_pair[1])


def place_of(order):
    place = jnp.int32(0)
    for axis, bit in order:
        place = place * 2 + jnp.where((lax.axis_index(axis) & bit) != 0, 1, 0)
    return place.astype(jnp.int32).reshape(1)


def added(first, second):
    return lowered(widened(first) + widened(second))


def sum_to_owner(keep, send, order):
    for step, (axis, bit) in enumerate(order):
        arrived = exchange(send, axis, bit)
        half = keep.shape[0] // 2
        if step == len(order) - 1:
            return added(keep, arrived)
        send = added(keep[half:], arrived[half:])
        keep = added(keep[:half], arrived[:half])


def spread(owned, order):
    for axis, bit in reversed(order[1:]):
        owned = jnp.concatenate([owned, exchange(owned, axis, bit)], axis=0)
    return owned, exchange(owned, order[0][0], order[0][1])


def place_kernel(place_ref, near_ref, far_ref, out_ref):
    half = pl.num_programs(0) // 2

    @pl.when(pl.program_id(0) < half)
    def from_near():
        out_ref[...] = near_ref[0].astype(jnp.float32)

    @pl.when(pl.program_id(0) >= half)
    def from_far():
        out_ref[...] = far_ref[0].astype(jnp.float32)


def put_in_place(place, near, far, row_bits, col_bits, name):
    half, rows, cols = near.shape
    count = 2 * half
    return pl.pallas_call(
        place_kernel,
        grid_spec=pltpu.PrefetchScalarGridSpec(
            num_scalar_prefetch=1,
            grid=(count,),
            in_specs=[
                pl.BlockSpec((1, rows, cols), lambda s, p: (jnp.minimum(s, half - 1), 0, 0)),
                pl.BlockSpec((1, rows, cols), lambda s, p: (jnp.maximum(s - half, 0), 0, 0)),
            ],
            out_specs=pl.BlockSpec(
                (rows, cols),
                lambda s, p: ((s ^ p[0]) >> col_bits, (s ^ p[0]) & ((1 << col_bits) - 1)),
            ),
        ),
        out_shape=jax.ShapeDtypeStruct((rows << row_bits, cols << col_bits), jnp.float32),
        compiler_params=pltpu.CompilerParams(vmem_limit_bytes=48 << 20),
        name=name,
    )(place, near, far)


def place_three_kernel(place_ref, near_ref, far_ref, out_ref):
    half = pl.num_programs(0) // 2

    @pl.when(pl.program_id(0) < half)
    def from_near():
        out_ref[...] = near_ref[0, 0].astype(jnp.float32)

    @pl.when(pl.program_id(0) >= half)
    def from_far():
        out_ref[...] = far_ref[0, 0].astype(jnp.float32)


def put_three_in_place(place, near, far, row_bits, col_bits, name):
    half, three, rows, cols = near.shape
    count = 2 * half
    return pl.pallas_call(
        place_three_kernel,
        grid_spec=pltpu.PrefetchScalarGridSpec(
            num_scalar_prefetch=1,
            grid=(count, three),
            in_specs=[
                pl.BlockSpec(
                    (1, 1, rows, cols),
                    lambda s, t, p: (
                        jnp.minimum(s, half - 1), jnp.where(s < half, t, three - 1), 0, 0
                    ),
                ),
                pl.BlockSpec(
                    (1, 1, rows, cols),
                    lambda s, t, p: (jnp.maximum(s - half, 0), jnp.where(s < half, 0, t), 0, 0),
                ),
            ],
            out_specs=pl.BlockSpec(
                (rows, cols),
                lambda s, t, p: (
                    (s ^ p[0]) >> col_bits,
                    (t << col_bits) + ((s ^ p[0]) & ((1 << col_bits) - 1)),
                ),
            ),
        ),
        out_shape=jax.ShapeDtypeStruct((rows << row_bits, three * (cols << col_bits)), jnp.float32),
        compiler_params=pltpu.CompilerParams(vmem_limit_bytes=48 << 20),
        name=name,
    )(place, near, far)


def sum_everywhere(values, axes):
    for axis in axes:
        for bit in bits_below(lax.axis_size(axis)):
            values = values + exchange(values, axis, bit)
    return values


def on_device(
    tokens,
    query_key_value_weight,
    bias_query,
    bias_value,
    attention_out_weight,
    attention_out_bias,
    gain_one,
    shift_one,
    feedforward_in_weight,
    feedforward_in_bias,
    feedforward_out_weight,
    feedforward_out_bias,
    gain_two,
    shift_two,
    d_out,
):
    core = lax.axis_index("fsdp")
    ctx = lax.axis_index("ctx")
    ctx_count = lax.axis_size("ctx")
    seqs, block_rows, width = tokens.shape
    pair = width // ctx_count
    flat = seqs * block_rows

    token_pieces = gather_blocks(tokens)

    small = (
        bias_query, bias_value, attention_out_bias, gain_one, shift_one,
        feedforward_in_bias, feedforward_out_bias, gain_two, shift_two,
    )
    packed = jnp.concatenate(small)
    packed_other = exchange(packed, "fsdp", 1)
    vectors = []
    offset = 0
    for part in small:
        size = part.shape[0]
        vectors.append(widened(pair_join(part, packed_other[offset : offset + size], core)))
        offset += size
    (
        query_bias, value_bias, out_bias, gain_first, shift_first,
        inner_bias, back_bias, gain_second, shift_second,
    ) = vectors
    qkv_full = pair_join(
        query_key_value_weight, exchange(query_key_value_weight, "fsdp", 1), core
    )
    out_full = pair_join(attention_out_weight, exchange(attention_out_weight, "fsdp", 1), core)
    in_full = pair_join(feedforward_in_weight, exchange(feedforward_in_weight, "fsdp", 1), core)
    back_full = pair_join(feedforward_out_weight, exchange(feedforward_out_weight, "fsdp", 1), core)

    head_weight = jnp.concatenate(
        [lax.dynamic_slice_in_dim(qkv_full, t * width + ctx * pair, pair, axis=1) for t in range(3)],
        axis=1,
    )
    head_bias = jnp.concatenate(
        [
            lax.dynamic_slice_in_dim(query_bias, ctx * pair, pair),
            jnp.zeros((pair,), jnp.float32),
            lax.dynamic_slice_in_dim(value_bias, ctx * pair, pair),
        ]
    )
    token_rows = jnp.concatenate(token_pieces, axis=1)
    projected = lowered(project(token_rows, head_weight) + head_bias)
    head_result, head_low, head_logs = attention_forward(projected)

    def row_blocks(values):
        return [
            lax.slice_in_dim(values, k * block_rows, (k + 1) * block_rows, axis=1)
            for k in range(ctx_count)
        ]

    attended_pieces = reorder(swap_blocks(row_blocks(head_low)), ctx)
    attended_low = jnp.concatenate(attended_pieces, axis=-1)
    attention_branch = project(attended_low, out_full) + out_bias
    summed_one = widened(tokens) + attention_branch
    first_normalized, pull_one = jax.vjp(norm_apply, summed_one, gain_first, shift_first)
    normed_low = lowered(first_normalized)
    hidden_before_gelu = project(normed_low, in_full) + inner_bias
    active_low = lowered(jax.nn.gelu(hidden_before_gelu, approximate=False))
    feedforward_branch = project(active_low, back_full) + back_bias

    def second_norm(residual_in, branch_in, gain_vec, shift_vec):
        return norm_apply(residual_in + branch_in, gain_vec, shift_vec)

    result, pull_two = jax.vjp(
        second_norm, first_normalized, feedforward_branch, gain_second, shift_second
    )
    output = lowered(result)
    first_grad_res, second_grad, gain_two_grad, shift_two_grad = pull_two(widened(d_out))
    second_low = lowered(second_grad)

    def left_pair(values):
        rows = values.reshape(flat, values.shape[2])
        return (half_of(rows, core, 1), exchange(half_of(rows, 1 - core, 1), "fsdp", 1))

    def right_pair(values):
        rows = values.reshape(flat, values.shape[2])
        return (rows, exchange(rows, "fsdp", 1))

    ctx_bits = [("ctx", bit) for bit in bits_below(ctx_count)]
    dp_bits = [("dp", bit) for bit in bits_below(lax.axis_size("dp"))]
    order_x = dp_bits + ctx_bits
    order_y = ctx_bits[:1] + dp_bits + ctx_bits[1:]
    place_x = place_of(order_x)
    place_y = place_of(order_y)
    total_bits = len(order_x)

    back_bits = (total_bits - 1, 1)
    back_parts = pair_grad(
        place_x, left_pair(active_low), right_pair(second_low), *back_bits, "grad_back"
    )
    back_bias_grad = column_sum(second_low)
    active_grad = back_project(second_low, back_full)
    gelu_pull = jax.vjp(partial(jax.nn.gelu, approximate=False), hidden_before_gelu)[1]
    hidden_low = lowered(gelu_pull(active_grad)[0])
    in_bits = (0, total_bits)
    in_parts = pair_grad(
        place_y, left_pair(normed_low), right_pair(hidden_low), *in_bits, "grad_in"
    )
    in_bias_grad = column_sum(hidden_low)
    first_grad = first_grad_res + back_project(hidden_low, in_full)
    summed_grad, gain_one_grad, shift_one_grad = pull_one(first_grad)
    branch_low = lowered(summed_grad)
    out_bits = (1, total_bits - 1)
    out_parts = pair_grad(
        place_x, left_pair(attended_low), right_pair(branch_low), *out_bits, "grad_out"
    )
    out_bias_grad = column_sum(branch_low)
    attended_grad = lowered(back_project(branch_low, out_full))

    column_pieces = [attended_grad[..., k * pair : (k + 1) * pair] for k in range(ctx_count)]
    head_grad = jnp.concatenate(swap_blocks(reorder(column_pieces, ctx)), axis=1)
    query_grad, key_grad, value_grad = attention_backward(
        projected, head_grad, head_result, head_logs
    )
    head_grads = (query_grad, key_grad, value_grad)

    token_flat = token_rows.reshape(-1, width)
    qkv_part = jnp.stack(
        [contract(token_flat, g.reshape(-1, pair), 0, 0) for g in head_grads], axis=0
    )
    own_rows = half_of(qkv_part, core, 1)
    qkv_sum = own_rows + widened(exchange(lowered(half_of(qkv_part, 1 - core, 1)), "fsdp", 1))
    order_q = dp_bits + ctx_bits
    dp_index = lax.axis_index("dp")
    dp_count = lax.axis_size("dp")
    qkv_chunks = [
        qkv_sum[:, k * (qkv_sum.shape[1] // dp_count) : (k + 1) * (qkv_sum.shape[1] // dp_count)]
        for k in range(dp_count)
    ]
    qkv_chunks = reorder(qkv_chunks, dp_index)
    while len(qkv_chunks) > 1:
        half = len(qkv_chunks) // 2
        arrived = [exchange(lowered(c), "dp", half) for c in qkv_chunks[half:]]
        qkv_chunks = [c + widened(a) for c, a in zip(qkv_chunks[:half], arrived)]
    qkv_owned = lowered(qkv_chunks[0])[None]
    place_q = place_of(
        [("dp", bit) for bit in reversed(bits_below(dp_count))]
        + [("ctx", bit) for bit in reversed(bits_below(ctx_count))]
    )
    order_q = [("dp", bit) for bit in reversed(bits_below(dp_count))] + [
        ("ctx", bit) for bit in reversed(bits_below(ctx_count))
    ]
    qkv_near, qkv_far = spread(qkv_owned, order_q)
    qkv_grad = put_three_in_place(
        place_q, qkv_near, qkv_far, len(dp_bits), len(ctx_bits), "place_qkv"
    )

    back_grad = put_in_place(
        place_x, *spread(sum_to_owner(*back_parts, order_x), order_x), *back_bits, "place_back"
    )
    in_grad = put_in_place(
        place_y, *spread(sum_to_owner(*in_parts, order_y), order_y), *in_bits, "place_in"
    )
    out_grad = put_in_place(
        place_x, *spread(sum_to_owner(*out_parts, order_x), order_x), *out_bits, "place_out"
    )

    mixed_pieces = []
    for part in head_grads:
        mixed_pieces.append(row_blocks(part))
    mixed = [jnp.concatenate([m[k] for m in mixed_pieces], axis=-1) for k in range(ctx_count)]
    mixed = reorder(swap_blocks(mixed), ctx)
    mixed_grad = jnp.concatenate(
        [m[..., t * pair : (t + 1) * pair] for t in range(3) for m in mixed], axis=-1
    )
    token_grad = summed_grad + back_project(mixed_grad, qkv_full)

    layer_vectors = (
        in_bias_grad, back_bias_grad, gain_two_grad, shift_two_grad,
        out_bias_grad, gain_one_grad, shift_one_grad,
    )
    layer_sum = sum_everywhere(jnp.concatenate(layer_vectors), ("fsdp", "dp", "ctx"))
    reduced = []
    offset = 0
    for part in layer_vectors:
        size = part.shape[0]
        reduced.append(half_of(layer_sum[offset : offset + size], core, 0))
        offset += size
    bias_part = jnp.stack([column_sum(query_grad), column_sum(value_grad)])
    bias_part = sum_everywhere(bias_part, ("fsdp", "dp"))
    bias_pieces = reorder(gather_blocks(bias_part), ctx)
    bias_grads = half_of(jnp.concatenate(bias_pieces, axis=1), core, 1)
    return (
        output,
        token_grad,
        qkv_grad,
        bias_grads[0],
        bias_grads[1],
        out_grad,
        reduced[4],
        reduced[5],
        reduced[6],
        in_grad,
        reduced[0],
        back_grad,
        reduced[1],
        reduced[2],
        reduced[3],
    )


def head_parallel(mesh):
    sizes = [mesh.shape["dp"], mesh.shape["ctx"]]
    powers = all(size & (size - 1) == 0 for size in sizes)
    return powers and mesh.shape["fsdp"] == 2 and 2 * mesh.shape["ctx"] == HEADS


def solution(mesh):
    in_specs = (
        P(("dp", "fsdp"), "ctx", None),
        P("fsdp", None),
        P("fsdp"),
        P("fsdp"),
        P("fsdp", None),
        P("fsdp"),
        P("fsdp"),
        P("fsdp"),
        P("fsdp", None),
        P("fsdp"),
        P("fsdp", None),
        P("fsdp"),
        P("fsdp"),
        P("fsdp"),
        P(("dp", "fsdp"), "ctx", None),
    )
    out_specs = (
        P(("dp", "fsdp"), "ctx", None),
        P(("dp", "fsdp"), "ctx", None),
        P("fsdp", None),
        P("fsdp"),
        P("fsdp"),
        P("fsdp", None),
        P("fsdp"),
        P("fsdp"),
        P("fsdp"),
        P("fsdp", None),
        P("fsdp"),
        P("fsdp", None),
        P("fsdp"),
        P("fsdp"),
        P("fsdp"),
    )
    body = on_device if head_parallel(mesh) else ring_on_device
    return jax.shard_map(
        body, mesh=mesh, in_specs=in_specs, out_specs=out_specs, check_vma=False
    )
```

```python
from functools import partial

import jax
import jax.numpy as jnp
from jax import lax
from jax.experimental import pallas as pl
from jax.experimental.pallas import tpu as pltpu
from jax.sharding import PartitionSpec as P

HEADS = 16
HEAD_DIM = 64


EPSILON = 1e-06


def from_behind(block, axis, distance):
    devices = range(lax.axis_size(axis))
    route = [((i - distance) % len(devices), i) for i in devices]
    return lax.ppermute(block, axis, route)


def norm_apply(values, gain_vec, shift_vec):
    centre = jnp.mean(values, axis=-1, keepdims=True)
    centred = values - centre
    variance = jnp.mean(centred * centred, axis=-1, keepdims=True)
    return centred * lax.rsqrt(variance + EPSILON) * gain_vec + shift_vec


def lowered(values):
    return values.astype(jnp.bfloat16)


def widened(values):
    return values.astype(jnp.float32)


def project(left_operand_rows, right_operand_matrix):
    return jnp.einsum(
        "ugj,jn->ugn", left_operand_rows, right_operand_matrix, preferred_element_type=jnp.float32
    )


def weight_grad(left_operand_rows, gradient_row_block):
    return jnp.einsum(
        "xrb,xrw->bw", left_operand_rows, gradient_row_block, preferred_element_type=jnp.float32
    )


def back_project(gradient_row_block, right_operand_matrix):
    return jnp.einsum(
        "wkb,fb->wkf", gradient_row_block, right_operand_matrix, preferred_element_type=jnp.float32
    )


def column_sum(values):
    return jnp.sum(widened(values), axis=(0, 1))


def split_heads(values):
    return values.reshape(values.shape[0], values.shape[1], HEADS, HEAD_DIM)


def merge_heads(values):
    return values.reshape(values.shape[0], values.shape[1], HEADS * HEAD_DIM)


def split_blocks(values, block_rows):
    seq_count = values.shape[0]
    blocks = values.shape[1] // block_rows
    return jnp.moveaxis(values.reshape(seq_count, blocks, block_rows, values.shape[2]), 1, 0)


def block_scores(query_rows, key_rows):
    scores = jnp.einsum(
        "sqhd,skhd->shqk",
        split_heads(query_rows),
        split_heads(key_rows),
        preferred_element_type=jnp.float32,
    )
    return scores * HEAD_DIM ** (-0.5)


def fold_block(state_now, key_block, value_block, query_rows):
    running_max, running_sum, running_acc = state_now
    scores = block_scores(query_rows, key_block)
    new_max = jnp.maximum(running_max, jnp.max(scores, axis=-1))
    rescale = jnp.exp(running_max - new_max)
    weights = jnp.exp(scores - new_max[..., None])
    new_sum = running_sum * rescale + jnp.sum(weights, axis=-1)
    product = jnp.einsum(
        "shqk,skhd->shqd",
        lowered(weights),
        split_heads(value_block),
        preferred_element_type=jnp.float32,
    )
    return (new_max, new_sum, running_acc * rescale[..., None] + product)


def attend_forward(query_rows, key_rows, value_rows):
    seq_count = query_rows.shape[0]
    block_rows = query_rows.shape[1]
    initial = (
        jnp.full((seq_count, HEADS, block_rows), -1e30, jnp.float32),
        jnp.zeros((seq_count, HEADS, block_rows), jnp.float32),
        jnp.zeros((seq_count, HEADS, block_rows, HEAD_DIM), jnp.float32),
    )
    kept = None
    key_part = lax.all_gather(key_rows, "ctx", axis=1, tiled=True)
    value_part = lax.all_gather(value_rows, "ctx", axis=1, tiled=True)

    def one_block(state_in, block_pair):
        return (fold_block(state_in, block_pair[0], block_pair[1], query_rows), None)

    state_out, unused = lax.scan(
        one_block,
        initial,
        (split_blocks(key_part, block_rows), split_blocks(value_part, block_rows)),
    )
    running_max, running_sum, running_acc = state_out
    attention_result = running_acc / running_sum[..., None]
    attention_result = jnp.transpose(attention_result, (0, 2, 1, 3)).reshape(
        seq_count, block_rows, HEADS * HEAD_DIM
    )
    log_total = running_max + jnp.log(running_sum)
    return (attention_result, log_total, kept)


def attend_back(query_rows, gradient_row_block, log_total, row_inner, key_rows, value_rows):
    score_scale = HEAD_DIM ** (-0.5)
    scores = block_scores(query_rows, key_rows)
    probabilities = jnp.exp(scores - log_total[..., None])
    value_grad = jnp.einsum(
        "shqk,sqhd->skhd",
        lowered(probabilities),
        split_heads(gradient_row_block),
        preferred_element_type=jnp.float32,
    )
    prob_grad = jnp.einsum(
        "sqhd,skhd->shqk",
        split_heads(gradient_row_block),
        split_heads(value_rows),
        preferred_element_type=jnp.float32,
    )
    score_grad = lowered(probabilities * (prob_grad - row_inner[..., None]))
    query_grad = (
        jnp.einsum(
            "shqk,skhd->sqhd", score_grad, split_heads(key_rows), preferred_element_type=jnp.float32
        )
        * score_scale
    )
    key_grad = (
        jnp.einsum(
            "shqk,sqhd->skhd",
            score_grad,
            split_heads(query_rows),
            preferred_element_type=jnp.float32,
        )
        * score_scale
    )
    return (merge_heads(query_grad), merge_heads(key_grad), merge_heads(value_grad))


def attend_backward(query_rows, gradient_row_block, log_total, row_inner, key_rows, value_rows):
    zero_rows = jnp.zeros(query_rows.shape, jnp.float32)
    turn_count = lax.axis_size("ctx") // 2

    def turn_keys(turn_index, carried):
        moving_key, moving_value, key_acc, value_acc, query_acc = carried
        for half_step in range(2):
            pieces = attend_back(
                query_rows, gradient_row_block, log_total, row_inner, moving_key, moving_value
            )
            query_acc = query_acc + pieces[0]
            key_acc = key_acc + pieces[1]
            value_acc = value_acc + pieces[2]
            moving_key, moving_value = from_behind((moving_key, moving_value), "ctx", 1)
            key_acc, value_acc = (
                from_behind(key_acc.astype(jnp.bfloat16), "ctx", 1).astype(key_acc.dtype),
                from_behind(value_acc.astype(jnp.bfloat16), "ctx", 1).astype(value_acc.dtype),
            )
        return (moving_key, moving_value, key_acc, value_acc, query_acc)

    finished = lax.fori_loop(
        0, turn_count, turn_keys, (key_rows, value_rows, zero_rows, zero_rows, zero_rows)
    )
    return (finished[4], finished[2], finished[3])


def ring_on_device(
    tokens,
    query_key_value_weight,
    bias_query,
    bias_value,
    attention_out_weight,
    attention_out_bias,
    gain_one,
    shift_one,
    feedforward_in_weight,
    feedforward_in_bias,
    feedforward_out_weight,
    feedforward_out_bias,
    gain_two,
    shift_two,
    d_out,
):
    attn_full = (
        lax.all_gather(query_key_value_weight, "fsdp", axis=0, tiled=True),
        lax.all_gather(attention_out_weight, "fsdp", axis=0, tiled=True),
        lax.all_gather(bias_query, "fsdp", axis=0, tiled=True),
        lax.all_gather(bias_value, "fsdp", axis=0, tiled=True),
        lax.all_gather(attention_out_bias, "fsdp", axis=0, tiled=True),
        lax.all_gather(gain_one, "fsdp", axis=0, tiled=True),
        lax.all_gather(shift_one, "fsdp", axis=0, tiled=True),
    )
    qkv_full, out_full, query_bias, value_bias, out_bias, gain_first, shift_first = attn_full
    model_width = out_full.shape[0]
    projected_rows = project(tokens, qkv_full) + jnp.concatenate(
        [widened(query_bias), jnp.zeros((model_width,), jnp.float32), widened(value_bias)]
    )
    projected_low = lowered(projected_rows)
    query_rows = projected_low[..., :model_width]
    key_rows = projected_low[..., model_width : 2 * model_width]
    value_rows = projected_low[..., 2 * model_width :]
    attention_result, log_total, kept = attend_forward(query_rows, key_rows, value_rows)
    attended_low = lowered(attention_result)
    attention_branch = project(attended_low, out_full) + widened(out_bias)
    summed_one = widened(tokens) + attention_branch
    first_normalized, pull_one = jax.vjp(
        norm_apply, summed_one, widened(gain_first), widened(shift_first)
    )
    normed_low = lowered(first_normalized)
    ffn_full = (
        lax.all_gather(feedforward_in_weight, "fsdp", axis=0, tiled=True),
        lax.all_gather(feedforward_out_weight, "fsdp", axis=0, tiled=True),
        lax.all_gather(feedforward_in_bias, "fsdp", axis=0, tiled=True),
        lax.all_gather(feedforward_out_bias, "fsdp", axis=0, tiled=True),
        lax.all_gather(gain_two, "fsdp", axis=0, tiled=True),
        lax.all_gather(shift_two, "fsdp", axis=0, tiled=True),
    )
    in_full, back_full, inner_bias, back_bias, gain_second, shift_second = ffn_full
    hidden_before_gelu = project(normed_low, in_full) + widened(inner_bias)
    active_low = lowered(jax.nn.gelu(hidden_before_gelu, approximate=False))
    feedforward_branch = project(active_low, back_full) + widened(back_bias)

    def second_norm(residual_in, branch_in, gain_vec, shift_vec):
        return norm_apply(residual_in + branch_in, gain_vec, shift_vec)

    result, pull_two = jax.vjp(
        second_norm,
        first_normalized,
        feedforward_branch,
        widened(gain_second),
        widened(shift_second),
    )
    output = lowered(result)
    first_grad_res, second_grad, gain_two_grad, shift_two_grad = pull_two(widened(d_out))
    in_full, back_full = (
        lax.all_gather(feedforward_in_weight, "fsdp", axis=0, tiled=True),
        lax.all_gather(feedforward_out_weight, "fsdp", axis=0, tiled=True),
    )
    second_low = lowered(second_grad)
    back_grad = weight_grad(active_low, second_low)
    back_bias_grad = column_sum(second_low)
    active_grad = back_project(second_low, back_full)
    gelu_pull = jax.vjp(partial(jax.nn.gelu, approximate=False), hidden_before_gelu)[1]
    hidden_low = lowered(gelu_pull(active_grad)[0])
    in_grad = weight_grad(normed_low, hidden_low)
    in_bias_grad = column_sum(hidden_low)
    first_grad = first_grad_res + back_project(hidden_low, in_full)
    ffn_grads = (
        lax.psum_scatter(
            in_grad.astype(jnp.bfloat16), "fsdp", scatter_dimension=0, tiled=True
        ).astype(jnp.float32),
        lax.psum_scatter(
            in_bias_grad.astype(jnp.bfloat16), "fsdp", scatter_dimension=0, tiled=True
        ).astype(jnp.float32),
        lax.psum_scatter(
            back_grad.astype(jnp.bfloat16), "fsdp", scatter_dimension=0, tiled=True
        ).astype(jnp.float32),
        lax.psum_scatter(
            back_bias_grad.astype(jnp.bfloat16), "fsdp", scatter_dimension=0, tiled=True
        ).astype(jnp.float32),
        lax.psum_scatter(
            gain_two_grad.astype(jnp.bfloat16), "fsdp", scatter_dimension=0, tiled=True
        ).astype(jnp.float32),
        lax.psum_scatter(
            shift_two_grad.astype(jnp.bfloat16), "fsdp", scatter_dimension=0, tiled=True
        ).astype(jnp.float32),
    )
    ffn_grads = lax.psum(
        (ffn_grads[0], ffn_grads[1], ffn_grads[2], ffn_grads[3], ffn_grads[4], ffn_grads[5]),
        ("dp", "ctx"),
    )
    summed_grad, gain_one_grad, shift_one_grad = pull_one(first_grad)
    qkv_full, out_full = (
        lax.all_gather(query_key_value_weight, "fsdp", axis=0, tiled=True),
        lax.all_gather(attention_out_weight, "fsdp", axis=0, tiled=True),
    )
    branch_low = lowered(summed_grad)
    out_grad = weight_grad(attended_low, branch_low)
    out_bias_grad = column_sum(branch_low)
    attended_grad_low = lowered(back_project(branch_low, out_full))
    row_inner = jnp.sum(
        split_heads(widened(attended_grad_low)) * split_heads(attention_result), axis=-1
    )
    row_inner = jnp.transpose(row_inner, (0, 2, 1))
    query_grad, key_grad, value_grad = attend_backward(
        query_rows, attended_grad_low, log_total, row_inner, key_rows, value_rows
    )
    mixed_grad = lowered(jnp.concatenate([query_grad, key_grad, value_grad], axis=-1))
    qkv_grad = weight_grad(tokens, mixed_grad)
    bias_grads = column_sum(mixed_grad)
    query_bias_grad = bias_grads[:model_width]
    value_bias_grad = bias_grads[2 * model_width :]
    token_grad = summed_grad + back_project(mixed_grad, qkv_full)
    attn_grads = (
        lax.psum_scatter(
            qkv_grad.astype(jnp.bfloat16), "fsdp", scatter_dimension=0, tiled=True
        ).astype(jnp.float32),
        lax.psum_scatter(
            query_bias_grad.astype(jnp.bfloat16), "fsdp", scatter_dimension=0, tiled=True
        ).astype(jnp.float32),
        lax.psum_scatter(
            value_bias_grad.astype(jnp.bfloat16), "fsdp", scatter_dimension=0, tiled=True
        ).astype(jnp.float32),
        lax.psum_scatter(
            out_grad.astype(jnp.bfloat16), "fsdp", scatter_dimension=0, tiled=True
        ).astype(jnp.float32),
        lax.psum_scatter(
            out_bias_grad.astype(jnp.bfloat16), "fsdp", scatter_dimension=0, tiled=True
        ).astype(jnp.float32),
        lax.psum_scatter(
            gain_one_grad.astype(jnp.bfloat16), "fsdp", scatter_dimension=0, tiled=True
        ).astype(jnp.float32),
        lax.psum_scatter(
            shift_one_grad.astype(jnp.bfloat16), "fsdp", scatter_dimension=0, tiled=True
        ).astype(jnp.float32),
    )
    attn_grads = lax.psum(
        (
            attn_grads[0],
            attn_grads[1],
            attn_grads[2],
            attn_grads[3],
            attn_grads[4],
            attn_grads[5],
            attn_grads[6],
        ),
        ("dp", "ctx"),
    )
    return (
        output,
        token_grad,
        attn_grads[0],
        attn_grads[1],
        attn_grads[2],
        attn_grads[3],
        attn_grads[4],
        attn_grads[5],
        attn_grads[6],
        ffn_grads[0],
        ffn_grads[1],
        ffn_grads[2],
        ffn_grads[3],
        ffn_grads[4],
        ffn_grads[5],
    )


def exchange(values, axis, bit):
    count = lax.axis_size(axis)
    return lax.ppermute(values, axis, [(i, i ^ bit) for i in range(count)])


def bits_below(count):
    return [1 << k for k in range(count.bit_length() - 1)]


def reorder(pieces, index):
    for bit in bits_below(len(pieces)):
        taken = (index & bit) != 0
        pieces = [jnp.where(taken, pieces[k ^ bit], pieces[k]) for k in range(len(pieces))]
    return pieces


def pair_join(own, other, core, axis=0):
    first = jnp.where(core == 0, own, other)
    second = jnp.where(core == 0, other, own)
    return jnp.concatenate([first, second], axis=axis)


def half_of(values, which, axis):
    size = values.shape[axis] // 2
    low = lax.slice_in_dim(values, 0, size, axis=axis)
    high = lax.slice_in_dim(values, size, 2 * size, axis=axis)
    return jnp.where(which == 0, low, high)


def gather_blocks(block):
    count = lax.axis_size("ctx")
    pieces = {0: block}
    for bit in reversed(bits_below(count)):
        for k in list(pieces):
            pieces[k ^ bit] = exchange(pieces[k], "ctx", bit)
    return [pieces[k] for k in range(count)]


def swap_blocks(pieces):
    return [pieces[0]] + [exchange(pieces[k], "ctx", k) for k in range(1, len(pieces))]


def head_mask(value):
    lane = lax.broadcasted_iota(jnp.int32, (1, 2 * HEAD_DIM), 1)
    return [
        jnp.where(lane < HEAD_DIM, value, 0.0),
        jnp.where(lane < HEAD_DIM, 0.0, value),
    ]


def contract(left, right, left_dim, right_dim):
    return lax.dot_general(
        left, right, (((left_dim,), (right_dim,)), ((), ())), preferred_element_type=jnp.float32
    )


def forward_kernel(query_ref, key_ref, value_ref, result_ref, low_ref, log_ref):
    query = query_ref[0].astype(jnp.float32)
    keys = key_ref[0]
    values = value_ref[0]
    results = []
    logs = []
    for mask in head_mask(HEAD_DIM ** (-0.5)):
        scores = contract((query * mask).astype(jnp.bfloat16), keys, 1, 1)
        row_max = jnp.max(scores, axis=-1, keepdims=True)
        weights = jnp.exp(scores - row_max)
        total = jnp.sum(weights, axis=-1, keepdims=True)
        probabilities = (weights * (1.0 / total)).astype(jnp.bfloat16)
        results.append(contract(probabilities, values, 1, 0))
        logs.append(row_max + jnp.log(total))
    first = lax.broadcasted_iota(jnp.int32, results[0].shape, 1) < HEAD_DIM
    result = jnp.where(first, results[0], results[1])
    result_ref[0] = result
    low_ref[0] = result.astype(jnp.bfloat16)
    log_ref[0] = jnp.where(first, logs[0], logs[1])


def attention_forward(projected):
    seqs, length, width = projected.shape
    pair = width // 3
    rows = min(256, length)
    row_spec = pl.BlockSpec((1, rows, pair), lambda s, q: (s, q, 0))
    return pl.pallas_call(
        forward_kernel,
        grid=(seqs, length // rows),
        in_specs=[
            row_spec,
            pl.BlockSpec((1, length, pair), lambda s, q: (s, 0, 1)),
            pl.BlockSpec((1, length, pair), lambda s, q: (s, 0, 2)),
        ],
        out_specs=[row_spec, row_spec, row_spec],
        out_shape=[
            jax.ShapeDtypeStruct((seqs, length, pair), jnp.float32),
            jax.ShapeDtypeStruct((seqs, length, pair), jnp.bfloat16),
            jax.ShapeDtypeStruct((seqs, length, pair), jnp.float32),
        ],
        compiler_params=pltpu.CompilerParams(vmem_limit_bytes=48 << 20),
        name="attention_forward",
    )(projected, projected, projected)


def backward_kernel(
    query_ref, key_ref, value_ref, grad_ref, result_ref, log_ref,
    query_out, key_out, value_out, query_acc, log_rows, inner_rows,
):
    step = pl.program_id(1)

    @pl.when(step == 0)
    def first_step():
        query_acc[...] = jnp.zeros_like(query_acc)
        logs = jnp.transpose(log_ref[0])
        inner = jnp.transpose(grad_ref[0].astype(jnp.float32) * result_ref[0])
        for h in range(2):
            log_rows[h] = jnp.broadcast_to(
                logs[h * HEAD_DIM : h * HEAD_DIM + 1], log_rows.shape[1:]
            )
            inner_rows[h] = jnp.broadcast_to(
                jnp.sum(inner[h * HEAD_DIM : (h + 1) * HEAD_DIM], axis=0, keepdims=True),
                inner_rows.shape[1:],
            )

    queries = query_ref[0]
    grads = grad_ref[0]
    keys = key_ref[0]
    values = value_ref[0]
    scale = HEAD_DIM ** (-0.5)
    query_parts = []
    key_parts = []
    value_parts = []
    scaled_masks = head_mask(scale)
    masks = head_mask(1.0)
    for h in range(2):
        scores = contract(
            (keys.astype(jnp.float32) * scaled_masks[h]).astype(jnp.bfloat16), queries, 1, 1
        )
        probabilities = jnp.exp(scores - log_rows[h, :1])
        prob_grad = contract(
            (values.astype(jnp.float32) * masks[h]).astype(jnp.bfloat16), grads, 1, 1
        )
        score_grad = (probabilities * (prob_grad - inner_rows[h, :1])).astype(jnp.bfloat16)
        value_parts.append(contract(probabilities.astype(jnp.bfloat16), grads, 1, 0))
        key_parts.append(contract(score_grad, queries, 1, 0))
        query_parts.append(contract(score_grad, keys, 0, 0))
    first = lax.broadcasted_iota(jnp.int32, key_parts[0].shape, 1) < HEAD_DIM
    value_out[0] = jnp.where(first, value_parts[0], value_parts[1]).astype(jnp.bfloat16)
    key_out[0] = (jnp.where(first, key_parts[0], key_parts[1]) * scale).astype(jnp.bfloat16)
    first = lax.broadcasted_iota(jnp.int32, query_parts[0].shape, 1) < HEAD_DIM
    query_acc[...] += jnp.where(first, query_parts[0], query_parts[1])

    @pl.when(step == pl.num_programs(1) - 1)
    def last_step():
        query_out[0] = (query_acc[...] * scale).astype(jnp.bfloat16)


def attention_backward(projected, grads, result, logs):
    seqs, length, width = projected.shape
    pair = width // 3
    rows = min(256, length)
    whole = pl.BlockSpec((1, length, pair), lambda s, k: (s, 0, 0))
    block = pl.BlockSpec((1, rows, pair), lambda s, k: (s, k, 0))
    shape = jax.ShapeDtypeStruct((seqs, length, pair), jnp.bfloat16)
    return pl.pallas_call(
        backward_kernel,
        grid=(seqs, length // rows),
        in_specs=[
            whole,
            pl.BlockSpec((1, rows, pair), lambda s, k: (s, k, 1)),
            pl.BlockSpec((1, rows, pair), lambda s, k: (s, k, 2)),
            whole,
            whole,
            whole,
        ],
        out_specs=[whole, block, block],
        out_shape=[shape, shape, shape],
        scratch_shapes=[
            pltpu.VMEM((length, pair), jnp.float32),
            pltpu.VMEM((2, 8, length), jnp.float32),
            pltpu.VMEM((2, 8, length), jnp.float32),
        ],
        compiler_params=pltpu.CompilerParams(vmem_limit_bytes=48 << 20),
        name="attention_backward",
    )(projected, projected, projected, grads, result, logs)


LOW = 2


def grad_kernel(place_ref, left_own, left_other, right_own, right_other, keep_ref, send_ref, *, by_rows):
    step = pl.program_id(0)
    half = pl.num_programs(0) // 2
    total = contract(left_own[...], right_own[...], 0, 0)
    total = total + contract(left_other[...], right_other[...], 0, 0)
    total = total.astype(jnp.bfloat16)
    low = place_ref[0] & ((1 << LOW) - 1)
    _, rows, cols = keep_ref.shape

    def put(out_ref):
        for j in range(1 << LOW):
            if by_rows:
                out_ref[j ^ low] = total[j * rows : (j + 1) * rows]
            else:
                out_ref[j ^ low] = total[:, j * cols : (j + 1) * cols]

    @pl.when(step < half)
    def outgoing():
        put(send_ref)

    @pl.when(step >= half)
    def kept():
        put(keep_ref)


def pair_grad(place, left_pair, right_pair, count, part, parts, by_rows, name):
    tokens, width = left_pair[0].shape
    columns = right_pair[0].shape[1]
    steps = count >> LOW
    half = steps // 2

    def block(step, place_ref):
        return part * steps + (((step + half) % steps) ^ (place_ref[0] >> LOW))

    if by_rows:
        rows, cols = width // (parts * count), columns
        left = pl.BlockSpec((tokens, rows << LOW), lambda s, p: (0, block(s, p)))
        right = pl.BlockSpec((tokens, columns), lambda s, p: (0, 0))
    else:
        rows, cols = width, columns // (parts * count)
        left = pl.BlockSpec((tokens, width), lambda s, p: (0, 0))
        right = pl.BlockSpec((tokens, cols << LOW), lambda s, p: (0, block(s, p)))
    shape = jax.ShapeDtypeStruct((count // 2, rows, cols), jnp.bfloat16)
    out_block = (1 << LOW, rows, cols)
    return pl.pallas_call(
        partial(grad_kernel, by_rows=by_rows),
        grid_spec=pltpu.PrefetchScalarGridSpec(
            num_scalar_prefetch=1,
            grid=(steps,),
            in_specs=[left, left, right, right],
            out_specs=[
                pl.BlockSpec(out_block, lambda s, p: (jnp.maximum(s - half, 0), 0, 0)),
                pl.BlockSpec(out_block, lambda s, p: (jnp.minimum(s, half - 1), 0, 0)),
            ],
        ),
        out_shape=[shape, shape],
        compiler_params=pltpu.CompilerParams(vmem_limit_bytes=48 << 20),
        name=name,
    )(place, left_pair[0], left_pair[1], right_pair[0], right_pair[1])


def place_of(order):
    place = jnp.int32(0)
    for axis, bit in order:
        place = place * 2 + jnp.where((lax.axis_index(axis) & bit) != 0, 1, 0)
    return place.astype(jnp.int32).reshape(1)


def added(first, second):
    return lowered(widened(first) + widened(second))


def sum_to_owner(keep, send, order):
    for step, (axis, bit) in enumerate(order):
        arrived = exchange(send, axis, bit)
        half = keep.shape[0] // 2
        if step == len(order) - 1:
            return added(keep, arrived)
        send = added(keep[half:], arrived[half:])
        keep = added(keep[:half], arrived[:half])


def spread(owned, order):
    for axis, bit in reversed(order[1:]):
        owned = jnp.concatenate([owned, exchange(owned, axis, bit)], axis=0)
    return owned, exchange(owned, order[0][0], order[0][1])


def place_kernel(place_ref, chunks_ref, *rest, by_rows):
    out_ref = rest[-1]
    low = place_ref[0] & ((1 << LOW) - 1)
    _, rows, cols = chunks_ref.shape
    for j in range(1 << LOW):
        values = chunks_ref[j ^ low].astype(jnp.float32)
        if by_rows:
            out_ref[j * rows : (j + 1) * rows, :] = values
        else:
            out_ref[:, j * cols : (j + 1) * cols] = values


def put_in_place(place, chunks, far, into, part, parts, by_rows, name):
    half, rows, cols = chunks.shape
    steps = half >> LOW
    first = steps if far else 0

    def block(step, place_ref):
        return part * 2 * steps + ((step + first) ^ (place_ref[0] >> LOW))

    if by_rows:
        out_shape = (rows * 2 * half * parts, cols)
        out_spec = pl.BlockSpec((rows << LOW, cols), lambda s, p: (block(s, p), 0))
    else:
        out_shape = (rows, cols * 2 * half * parts)
        out_spec = pl.BlockSpec((rows, cols << LOW), lambda s, p: (0, block(s, p)))
    in_specs = [pl.BlockSpec((1 << LOW, rows, cols), lambda s, p: (s, 0, 0))]
    operands = [place, chunks]
    if into is not None:
        in_specs.append(pl.BlockSpec(memory_space=pl.ANY))
        operands.append(into)
    return pl.pallas_call(
        partial(place_kernel, by_rows=by_rows),
        grid_spec=pltpu.PrefetchScalarGridSpec(
            num_scalar_prefetch=1, grid=(steps,), in_specs=in_specs, out_specs=out_spec
        ),
        out_shape=jax.ShapeDtypeStruct(out_shape, jnp.float32),
        input_output_aliases={} if into is None else {2: 0},
        compiler_params=pltpu.CompilerParams(vmem_limit_bytes=48 << 20),
        name=name,
    )(*operands)


def place_three_kernel(place_ref, chunks_ref, *rest):
    out_ref = rest[-1]
    count, _, _, cols = chunks_ref.shape
    ctx = place_ref[0] & (count - 1)
    for j in range(count):
        out_ref[:, j * cols : (j + 1) * cols] = chunks_ref[j ^ ctx, 0].astype(jnp.float32)


def put_three_in_place(place, chunks, far, into, ctx_count, dp_count, name):
    total, three, rows, cols = chunks.shape
    steps = total // ctx_count
    first = steps if far else 0
    ctx_bits = ctx_count.bit_length() - 1
    in_specs = [
        pl.BlockSpec((ctx_count, 1, rows, cols), lambda s, t, p: (s, t, 0, 0))
    ]
    operands = [place, chunks]
    if into is not None:
        in_specs.append(pl.BlockSpec(memory_space=pl.ANY))
        operands.append(into)
    return pl.pallas_call(
        place_three_kernel,
        grid_spec=pltpu.PrefetchScalarGridSpec(
            num_scalar_prefetch=1,
            grid=(steps, three),
            in_specs=in_specs,
            out_specs=pl.BlockSpec(
                (rows, ctx_count * cols),
                lambda s, t, p: ((s + first) ^ (p[0] >> ctx_bits), t),
            ),
        ),
        out_shape=jax.ShapeDtypeStruct((rows * dp_count, three * ctx_count * cols), jnp.float32),
        input_output_aliases={} if into is None else {2: 0},
        compiler_params=pltpu.CompilerParams(vmem_limit_bytes=48 << 20),
        name=name,
    )(*operands)


def sum_everywhere(values, axes):
    for axis in axes:
        for bit in bits_below(lax.axis_size(axis)):
            values = values + exchange(values, axis, bit)
    return values


def on_device(
    tokens,
    query_key_value_weight,
    bias_query,
    bias_value,
    attention_out_weight,
    attention_out_bias,
    gain_one,
    shift_one,
    feedforward_in_weight,
    feedforward_in_bias,
    feedforward_out_weight,
    feedforward_out_bias,
    gain_two,
    shift_two,
    d_out,
):
    core = lax.axis_index("fsdp")
    ctx = lax.axis_index("ctx")
    ctx_count = lax.axis_size("ctx")
    seqs, block_rows, width = tokens.shape
    pair = width // ctx_count
    flat = seqs * block_rows

    token_pieces = gather_blocks(tokens)

    small = (
        bias_query, bias_value, attention_out_bias, gain_one, shift_one,
        feedforward_in_bias, feedforward_out_bias, gain_two, shift_two,
    )
    packed = jnp.concatenate(small)
    packed_other = exchange(packed, "fsdp", 1)
    vectors = []
    offset = 0
    for part in small:
        size = part.shape[0]
        vectors.append(widened(pair_join(part, packed_other[offset : offset + size], core)))
        offset += size
    (
        query_bias, value_bias, out_bias, gain_first, shift_first,
        inner_bias, back_bias, gain_second, shift_second,
    ) = vectors
    qkv_full = pair_join(
        query_key_value_weight, exchange(query_key_value_weight, "fsdp", 1), core
    )
    out_full = pair_join(attention_out_weight, exchange(attention_out_weight, "fsdp", 1), core)
    in_full = pair_join(feedforward_in_weight, exchange(feedforward_in_weight, "fsdp", 1), core)
    back_full = pair_join(feedforward_out_weight, exchange(feedforward_out_weight, "fsdp", 1), core)

    head_weight = jnp.concatenate(
        [lax.dynamic_slice_in_dim(qkv_full, t * width + ctx * pair, pair, axis=1) for t in range(3)],
        axis=1,
    )
    head_bias = jnp.concatenate(
        [
            lax.dynamic_slice_in_dim(query_bias, ctx * pair, pair),
            jnp.zeros((pair,), jnp.float32),
            lax.dynamic_slice_in_dim(value_bias, ctx * pair, pair),
        ]
    )
    token_rows = jnp.concatenate(token_pieces, axis=1)
    projected = lowered(project(token_rows, head_weight) + head_bias)
    head_result, head_low, head_logs = attention_forward(projected)

    def row_blocks(values):
        return [
            lax.slice_in_dim(values, k * block_rows, (k + 1) * block_rows, axis=1)
            for k in range(ctx_count)
        ]

    attended_pieces = reorder(swap_blocks(row_blocks(head_low)), ctx)
    attended_low = jnp.concatenate(attended_pieces, axis=-1)
    attention_branch = project(attended_low, out_full) + out_bias
    summed_one = widened(tokens) + attention_branch
    first_normalized, pull_one = jax.vjp(norm_apply, summed_one, gain_first, shift_first)
    normed_low = lowered(first_normalized)
    hidden_before_gelu = project(normed_low, in_full) + inner_bias
    active_low = lowered(jax.nn.gelu(hidden_before_gelu, approximate=False))
    feedforward_branch = project(active_low, back_full) + back_bias

    def second_norm(residual_in, branch_in, gain_vec, shift_vec):
        return norm_apply(residual_in + branch_in, gain_vec, shift_vec)

    result, pull_two = jax.vjp(
        second_norm, first_normalized, feedforward_branch, gain_second, shift_second
    )
    output = lowered(result)
    first_grad_res, second_grad, gain_two_grad, shift_two_grad = pull_two(widened(d_out))
    second_low = lowered(second_grad)

    def left_pair(values):
        rows = values.reshape(flat, values.shape[2])
        return (half_of(rows, core, 1), exchange(half_of(rows, 1 - core, 1), "fsdp", 1))

    def right_pair(values):
        rows = values.reshape(flat, values.shape[2])
        return (rows, exchange(rows, "fsdp", 1))

    ctx_bits = [("ctx", bit) for bit in bits_below(ctx_count)]
    dp_bits = [("dp", bit) for bit in bits_below(lax.axis_size("dp"))]
    order_x = dp_bits + ctx_bits
    order_y = ctx_bits[:1] + dp_bits + ctx_bits[1:]
    order_z = ctx_bits[1:] + ctx_bits[:1] + dp_bits
    place_x = place_of(order_x)
    place_y = place_of(order_y)
    place_z = place_of(order_z)
    count = 1 << len(order_x)

    active_pair = left_pair(active_low)
    normed_pair = left_pair(normed_low)
    attended_pair = left_pair(attended_low)
    second_pair = right_pair(second_low)
    back_parts = [
        pair_grad(place_x, active_pair, second_pair, count, part, 2, True, "grad_back")
        for part in range(2)
    ]
    back_bias_grad = column_sum(second_low)
    active_grad = back_project(second_low, back_full)
    gelu_pull = jax.vjp(partial(jax.nn.gelu, approximate=False), hidden_before_gelu)[1]
    hidden_low = lowered(gelu_pull(active_grad)[0])
    hidden_low, back_parts = lax.optimization_barrier((hidden_low, back_parts))
    hidden_pair = right_pair(hidden_low)
    in_parts = [
        pair_grad(place_y, normed_pair, hidden_pair, count, part, 2, False, "grad_in")
        for part in range(2)
    ]
    in_bias_grad = column_sum(hidden_low)
    first_grad = first_grad_res + back_project(hidden_low, in_full)
    summed_grad, gain_one_grad, shift_one_grad = pull_one(first_grad)
    branch_low = lowered(summed_grad)
    branch_low, in_parts = lax.optimization_barrier((branch_low, in_parts))
    out_parts = pair_grad(
        place_z, attended_pair, right_pair(branch_low), count, 0, 1, True, "grad_out"
    )
    out_bias_grad = column_sum(branch_low)
    attended_grad = lowered(back_project(branch_low, out_full))

    column_pieces = [attended_grad[..., k * pair : (k + 1) * pair] for k in range(ctx_count)]
    head_grad = jnp.concatenate(swap_blocks(reorder(column_pieces, ctx)), axis=1)
    query_grad, key_grad, value_grad = attention_backward(
        projected, head_grad, head_result, head_logs
    )
    head_grads = (query_grad, key_grad, value_grad)

    token_flat = token_rows.reshape(-1, width)
    qkv_part = jnp.stack(
        [contract(token_flat, g.reshape(-1, pair), 0, 0) for g in head_grads], axis=0
    )
    own_rows = half_of(qkv_part, core, 1)
    qkv_sum = own_rows + widened(exchange(lowered(half_of(qkv_part, 1 - core, 1)), "fsdp", 1))
    order_q = dp_bits + ctx_bits
    dp_index = lax.axis_index("dp")
    dp_count = lax.axis_size("dp")
    qkv_chunks = [
        qkv_sum[:, k * (qkv_sum.shape[1] // dp_count) : (k + 1) * (qkv_sum.shape[1] // dp_count)]
        for k in range(dp_count)
    ]
    qkv_chunks = reorder(qkv_chunks, dp_index)
    while len(qkv_chunks) > 1:
        half = len(qkv_chunks) // 2
        arrived = [exchange(lowered(c), "dp", half) for c in qkv_chunks[half:]]
        qkv_chunks = [c + widened(a) for c, a in zip(qkv_chunks[:half], arrived)]
    qkv_owned = lowered(qkv_chunks[0])[None]
    place_q = place_of(
        [("dp", bit) for bit in reversed(bits_below(dp_count))]
        + [("ctx", bit) for bit in reversed(bits_below(ctx_count))]
    )
    order_q = [("dp", bit) for bit in reversed(bits_below(dp_count))] + [
        ("ctx", bit) for bit in reversed(bits_below(ctx_count))
    ]
    qkv_near, qkv_far = spread(qkv_owned, order_q)
    qkv_grad = None
    for chunks, far in ((qkv_near, False), (qkv_far, True)):
        qkv_grad = put_three_in_place(
            place_q, chunks, far, qkv_grad, ctx_count, dp_count, "place_qkv"
        )

    def finish(parts, order, place, by_rows, name):
        whole = None
        for part, (keep, send) in enumerate(parts):
            near, far = spread(sum_to_owner(keep, send, order), order)
            whole = put_in_place(place, near, False, whole, part, len(parts), by_rows, name)
            whole = put_in_place(place, far, True, whole, part, len(parts), by_rows, name)
        return whole

    back_grad = finish(back_parts, order_x, place_x, True, "place_back")
    in_grad = finish(in_parts, order_y, place_y, False, "place_in")
    out_grad = finish([out_parts], order_z, place_z, True, "place_out")

    mixed_pieces = []
    for part in head_grads:
        mixed_pieces.append(row_blocks(part))
    mixed = [jnp.concatenate([m[k] for m in mixed_pieces], axis=-1) for k in range(ctx_count)]
    mixed = reorder(swap_blocks(mixed), ctx)
    mixed_grad = jnp.concatenate(
        [m[..., t * pair : (t + 1) * pair] for t in range(3) for m in mixed], axis=-1
    )
    token_grad = summed_grad + back_project(mixed_grad, qkv_full)

    layer_vectors = (
        in_bias_grad, back_bias_grad, gain_two_grad, shift_two_grad,
        out_bias_grad, gain_one_grad, shift_one_grad,
    )
    layer_sum = sum_everywhere(jnp.concatenate(layer_vectors), ("fsdp", "dp", "ctx"))
    reduced = []
    offset = 0
    for part in layer_vectors:
        size = part.shape[0]
        reduced.append(half_of(layer_sum[offset : offset + size], core, 0))
        offset += size
    bias_part = jnp.stack([column_sum(query_grad), column_sum(value_grad)])
    bias_part = sum_everywhere(bias_part, ("fsdp", "dp"))
    bias_pieces = reorder(gather_blocks(bias_part), ctx)
    bias_grads = half_of(jnp.concatenate(bias_pieces, axis=1), core, 1)
    return (
        output,
        token_grad,
        qkv_grad,
        bias_grads[0],
        bias_grads[1],
        out_grad,
        reduced[4],
        reduced[5],
        reduced[6],
        in_grad,
        reduced[0],
        back_grad,
        reduced[1],
        reduced[2],
        reduced[3],
    )


def head_parallel(mesh):
    sizes = [mesh.shape["dp"], mesh.shape["ctx"]]
    powers = all(size & (size - 1) == 0 for size in sizes)
    return powers and mesh.shape["fsdp"] == 2 and 2 * mesh.shape["ctx"] == HEADS


def solution(mesh):
    in_specs = (
        P(("dp", "fsdp"), "ctx", None),
        P("fsdp", None),
        P("fsdp"),
        P("fsdp"),
        P("fsdp", None),
        P("fsdp"),
        P("fsdp"),
        P("fsdp"),
        P("fsdp", None),
        P("fsdp"),
        P("fsdp", None),
        P("fsdp"),
        P("fsdp"),
        P("fsdp"),
        P(("dp", "fsdp"), "ctx", None),
    )
    out_specs = (
        P(("dp", "fsdp"), "ctx", None),
        P(("dp", "fsdp"), "ctx", None),
        P("fsdp", None),
        P("fsdp"),
        P("fsdp"),
        P("fsdp", None),
        P("fsdp"),
        P("fsdp"),
        P("fsdp"),
        P("fsdp", None),
        P("fsdp"),
        P("fsdp", None),
        P("fsdp"),
        P("fsdp"),
        P("fsdp"),
    )
    body = on_device if head_parallel(mesh) else ring_on_device
    return jax.shard_map(
        body, mesh=mesh, in_specs=in_specs, out_specs=out_specs, check_vma=False
    )
```

```python
from functools import partial

import jax
import jax.numpy as jnp
from jax import lax
from jax.experimental import pallas as pl
from jax.experimental.pallas import tpu as pltpu
from jax.sharding import PartitionSpec as P

HEADS = 16
HEAD_DIM = 64


EPSILON = 1e-06


def from_behind(block, axis, distance):
    devices = range(lax.axis_size(axis))
    route = [((i - distance) % len(devices), i) for i in devices]
    return lax.ppermute(block, axis, route)


def norm_apply(values, gain_vec, shift_vec):
    centre = jnp.mean(values, axis=-1, keepdims=True)
    centred = values - centre
    variance = jnp.mean(centred * centred, axis=-1, keepdims=True)
    return centred * lax.rsqrt(variance + EPSILON) * gain_vec + shift_vec


def lowered(values):
    return values.astype(jnp.bfloat16)


def widened(values):
    return values.astype(jnp.float32)


def project(left_operand_rows, right_operand_matrix):
    return jnp.einsum(
        "ugj,jn->ugn", left_operand_rows, right_operand_matrix, preferred_element_type=jnp.float32
    )


def weight_grad(left_operand_rows, gradient_row_block):
    return jnp.einsum(
        "xrb,xrw->bw", left_operand_rows, gradient_row_block, preferred_element_type=jnp.float32
    )


def back_project(gradient_row_block, right_operand_matrix):
    return jnp.einsum(
        "wkb,fb->wkf", gradient_row_block, right_operand_matrix, preferred_element_type=jnp.float32
    )


def column_sum(values):
    return jnp.sum(widened(values), axis=(0, 1))


def split_heads(values):
    return values.reshape(values.shape[0], values.shape[1], HEADS, HEAD_DIM)


def merge_heads(values):
    return values.reshape(values.shape[0], values.shape[1], HEADS * HEAD_DIM)


def split_blocks(values, block_rows):
    seq_count = values.shape[0]
    blocks = values.shape[1] // block_rows
    return jnp.moveaxis(values.reshape(seq_count, blocks, block_rows, values.shape[2]), 1, 0)


def block_scores(query_rows, key_rows):
    scores = jnp.einsum(
        "sqhd,skhd->shqk",
        split_heads(query_rows),
        split_heads(key_rows),
        preferred_element_type=jnp.float32,
    )
    return scores * HEAD_DIM ** (-0.5)


def fold_block(state_now, key_block, value_block, query_rows):
    running_max, running_sum, running_acc = state_now
    scores = block_scores(query_rows, key_block)
    new_max = jnp.maximum(running_max, jnp.max(scores, axis=-1))
    rescale = jnp.exp(running_max - new_max)
    weights = jnp.exp(scores - new_max[..., None])
    new_sum = running_sum * rescale + jnp.sum(weights, axis=-1)
    product = jnp.einsum(
        "shqk,skhd->shqd",
        lowered(weights),
        split_heads(value_block),
        preferred_element_type=jnp.float32,
    )
    return (new_max, new_sum, running_acc * rescale[..., None] + product)


def attend_forward(query_rows, key_rows, value_rows):
    seq_count = query_rows.shape[0]
    block_rows = query_rows.shape[1]
    initial = (
        jnp.full((seq_count, HEADS, block_rows), -1e30, jnp.float32),
        jnp.zeros((seq_count, HEADS, block_rows), jnp.float32),
        jnp.zeros((seq_count, HEADS, block_rows, HEAD_DIM), jnp.float32),
    )
    kept = None
    key_part = lax.all_gather(key_rows, "ctx", axis=1, tiled=True)
    value_part = lax.all_gather(value_rows, "ctx", axis=1, tiled=True)

    def one_block(state_in, block_pair):
        return (fold_block(state_in, block_pair[0], block_pair[1], query_rows), None)

    state_out, unused = lax.scan(
        one_block,
        initial,
        (split_blocks(key_part, block_rows), split_blocks(value_part, block_rows)),
    )
    running_max, running_sum, running_acc = state_out
    attention_result = running_acc / running_sum[..., None]
    attention_result = jnp.transpose(attention_result, (0, 2, 1, 3)).reshape(
        seq_count, block_rows, HEADS * HEAD_DIM
    )
    log_total = running_max + jnp.log(running_sum)
    return (attention_result, log_total, kept)


def attend_back(query_rows, gradient_row_block, log_total, row_inner, key_rows, value_rows):
    score_scale = HEAD_DIM ** (-0.5)
    scores = block_scores(query_rows, key_rows)
    probabilities = jnp.exp(scores - log_total[..., None])
    value_grad = jnp.einsum(
        "shqk,sqhd->skhd",
        lowered(probabilities),
        split_heads(gradient_row_block),
        preferred_element_type=jnp.float32,
    )
    prob_grad = jnp.einsum(
        "sqhd,skhd->shqk",
        split_heads(gradient_row_block),
        split_heads(value_rows),
        preferred_element_type=jnp.float32,
    )
    score_grad = lowered(probabilities * (prob_grad - row_inner[..., None]))
    query_grad = (
        jnp.einsum(
            "shqk,skhd->sqhd", score_grad, split_heads(key_rows), preferred_element_type=jnp.float32
        )
        * score_scale
    )
    key_grad = (
        jnp.einsum(
            "shqk,sqhd->skhd",
            score_grad,
            split_heads(query_rows),
            preferred_element_type=jnp.float32,
        )
        * score_scale
    )
    return (merge_heads(query_grad), merge_heads(key_grad), merge_heads(value_grad))


def attend_backward(query_rows, gradient_row_block, log_total, row_inner, key_rows, value_rows):
    zero_rows = jnp.zeros(query_rows.shape, jnp.float32)
    turn_count = lax.axis_size("ctx") // 2

    def turn_keys(turn_index, carried):
        moving_key, moving_value, key_acc, value_acc, query_acc = carried
        for half_step in range(2):
            pieces = attend_back(
                query_rows, gradient_row_block, log_total, row_inner, moving_key, moving_value
            )
            query_acc = query_acc + pieces[0]
            key_acc = key_acc + pieces[1]
            value_acc = value_acc + pieces[2]
            moving_key, moving_value = from_behind((moving_key, moving_value), "ctx", 1)
            key_acc, value_acc = (
                from_behind(key_acc.astype(jnp.bfloat16), "ctx", 1).astype(key_acc.dtype),
                from_behind(value_acc.astype(jnp.bfloat16), "ctx", 1).astype(value_acc.dtype),
            )
        return (moving_key, moving_value, key_acc, value_acc, query_acc)

    finished = lax.fori_loop(
        0, turn_count, turn_keys, (key_rows, value_rows, zero_rows, zero_rows, zero_rows)
    )
    return (finished[4], finished[2], finished[3])


def ring_on_device(
    tokens,
    query_key_value_weight,
    bias_query,
    bias_value,
    attention_out_weight,
    attention_out_bias,
    gain_one,
    shift_one,
    feedforward_in_weight,
    feedforward_in_bias,
    feedforward_out_weight,
    feedforward_out_bias,
    gain_two,
    shift_two,
    d_out,
):
    attn_full = (
        lax.all_gather(query_key_value_weight, "fsdp", axis=0, tiled=True),
        lax.all_gather(attention_out_weight, "fsdp", axis=0, tiled=True),
        lax.all_gather(bias_query, "fsdp", axis=0, tiled=True),
        lax.all_gather(bias_value, "fsdp", axis=0, tiled=True),
        lax.all_gather(attention_out_bias, "fsdp", axis=0, tiled=True),
        lax.all_gather(gain_one, "fsdp", axis=0, tiled=True),
        lax.all_gather(shift_one, "fsdp", axis=0, tiled=True),
    )
    qkv_full, out_full, query_bias, value_bias, out_bias, gain_first, shift_first = attn_full
    model_width = out_full.shape[0]
    projected_rows = project(tokens, qkv_full) + jnp.concatenate(
        [widened(query_bias), jnp.zeros((model_width,), jnp.float32), widened(value_bias)]
    )
    projected_low = lowered(projected_rows)
    query_rows = projected_low[..., :model_width]
    key_rows = projected_low[..., model_width : 2 * model_width]
    value_rows = projected_low[..., 2 * model_width :]
    attention_result, log_total, kept = attend_forward(query_rows, key_rows, value_rows)
    attended_low = lowered(attention_result)
    attention_branch = project(attended_low, out_full) + widened(out_bias)
    summed_one = widened(tokens) + attention_branch
    first_normalized, pull_one = jax.vjp(
        norm_apply, summed_one, widened(gain_first), widened(shift_first)
    )
    normed_low = lowered(first_normalized)
    ffn_full = (
        lax.all_gather(feedforward_in_weight, "fsdp", axis=0, tiled=True),
        lax.all_gather(feedforward_out_weight, "fsdp", axis=0, tiled=True),
        lax.all_gather(feedforward_in_bias, "fsdp", axis=0, tiled=True),
        lax.all_gather(feedforward_out_bias, "fsdp", axis=0, tiled=True),
        lax.all_gather(gain_two, "fsdp", axis=0, tiled=True),
        lax.all_gather(shift_two, "fsdp", axis=0, tiled=True),
    )
    in_full, back_full, inner_bias, back_bias, gain_second, shift_second = ffn_full
    hidden_before_gelu = project(normed_low, in_full) + widened(inner_bias)
    active_low = lowered(jax.nn.gelu(hidden_before_gelu, approximate=False))
    feedforward_branch = project(active_low, back_full) + widened(back_bias)

    def second_norm(residual_in, branch_in, gain_vec, shift_vec):
        return norm_apply(residual_in + branch_in, gain_vec, shift_vec)

    result, pull_two = jax.vjp(
        second_norm,
        first_normalized,
        feedforward_branch,
        widened(gain_second),
        widened(shift_second),
    )
    output = lowered(result)
    first_grad_res, second_grad, gain_two_grad, shift_two_grad = pull_two(widened(d_out))
    in_full, back_full = (
        lax.all_gather(feedforward_in_weight, "fsdp", axis=0, tiled=True),
        lax.all_gather(feedforward_out_weight, "fsdp", axis=0, tiled=True),
    )
    second_low = lowered(second_grad)
    back_grad = weight_grad(active_low, second_low)
    back_bias_grad = column_sum(second_low)
    active_grad = back_project(second_low, back_full)
    gelu_pull = jax.vjp(partial(jax.nn.gelu, approximate=False), hidden_before_gelu)[1]
    hidden_low = lowered(gelu_pull(active_grad)[0])
    in_grad = weight_grad(normed_low, hidden_low)
    in_bias_grad = column_sum(hidden_low)
    first_grad = first_grad_res + back_project(hidden_low, in_full)
    ffn_grads = (
        lax.psum_scatter(
            in_grad.astype(jnp.bfloat16), "fsdp", scatter_dimension=0, tiled=True
        ).astype(jnp.float32),
        lax.psum_scatter(
            in_bias_grad.astype(jnp.bfloat16), "fsdp", scatter_dimension=0, tiled=True
        ).astype(jnp.float32),
        lax.psum_scatter(
            back_grad.astype(jnp.bfloat16), "fsdp", scatter_dimension=0, tiled=True
        ).astype(jnp.float32),
        lax.psum_scatter(
            back_bias_grad.astype(jnp.bfloat16), "fsdp", scatter_dimension=0, tiled=True
        ).astype(jnp.float32),
        lax.psum_scatter(
            gain_two_grad.astype(jnp.bfloat16), "fsdp", scatter_dimension=0, tiled=True
        ).astype(jnp.float32),
        lax.psum_scatter(
            shift_two_grad.astype(jnp.bfloat16), "fsdp", scatter_dimension=0, tiled=True
        ).astype(jnp.float32),
    )
    ffn_grads = lax.psum(
        (ffn_grads[0], ffn_grads[1], ffn_grads[2], ffn_grads[3], ffn_grads[4], ffn_grads[5]),
        ("dp", "ctx"),
    )
    summed_grad, gain_one_grad, shift_one_grad = pull_one(first_grad)
    qkv_full, out_full = (
        lax.all_gather(query_key_value_weight, "fsdp", axis=0, tiled=True),
        lax.all_gather(attention_out_weight, "fsdp", axis=0, tiled=True),
    )
    branch_low = lowered(summed_grad)
    out_grad = weight_grad(attended_low, branch_low)
    out_bias_grad = column_sum(branch_low)
    attended_grad_low = lowered(back_project(branch_low, out_full))
    row_inner = jnp.sum(
        split_heads(widened(attended_grad_low)) * split_heads(attention_result), axis=-1
    )
    row_inner = jnp.transpose(row_inner, (0, 2, 1))
    query_grad, key_grad, value_grad = attend_backward(
        query_rows, attended_grad_low, log_total, row_inner, key_rows, value_rows
    )
    mixed_grad = lowered(jnp.concatenate([query_grad, key_grad, value_grad], axis=-1))
    qkv_grad = weight_grad(tokens, mixed_grad)
    bias_grads = column_sum(mixed_grad)
    query_bias_grad = bias_grads[:model_width]
    value_bias_grad = bias_grads[2 * model_width :]
    token_grad = summed_grad + back_project(mixed_grad, qkv_full)
    attn_grads = (
        lax.psum_scatter(
            qkv_grad.astype(jnp.bfloat16), "fsdp", scatter_dimension=0, tiled=True
        ).astype(jnp.float32),
        lax.psum_scatter(
            query_bias_grad.astype(jnp.bfloat16), "fsdp", scatter_dimension=0, tiled=True
        ).astype(jnp.float32),
        lax.psum_scatter(
            value_bias_grad.astype(jnp.bfloat16), "fsdp", scatter_dimension=0, tiled=True
        ).astype(jnp.float32),
        lax.psum_scatter(
            out_grad.astype(jnp.bfloat16), "fsdp", scatter_dimension=0, tiled=True
        ).astype(jnp.float32),
        lax.psum_scatter(
            out_bias_grad.astype(jnp.bfloat16), "fsdp", scatter_dimension=0, tiled=True
        ).astype(jnp.float32),
        lax.psum_scatter(
            gain_one_grad.astype(jnp.bfloat16), "fsdp", scatter_dimension=0, tiled=True
        ).astype(jnp.float32),
        lax.psum_scatter(
            shift_one_grad.astype(jnp.bfloat16), "fsdp", scatter_dimension=0, tiled=True
        ).astype(jnp.float32),
    )
    attn_grads = lax.psum(
        (
            attn_grads[0],
            attn_grads[1],
            attn_grads[2],
            attn_grads[3],
            attn_grads[4],
            attn_grads[5],
            attn_grads[6],
        ),
        ("dp", "ctx"),
    )
    return (
        output,
        token_grad,
        attn_grads[0],
        attn_grads[1],
        attn_grads[2],
        attn_grads[3],
        attn_grads[4],
        attn_grads[5],
        attn_grads[6],
        ffn_grads[0],
        ffn_grads[1],
        ffn_grads[2],
        ffn_grads[3],
        ffn_grads[4],
        ffn_grads[5],
    )


def exchange(values, axis, bit):
    count = lax.axis_size(axis)
    return lax.ppermute(values, axis, [(i, i ^ bit) for i in range(count)])


def bits_below(count):
    return [1 << k for k in range(count.bit_length() - 1)]


def reorder(pieces, index):
    for bit in bits_below(len(pieces)):
        taken = (index & bit) != 0
        pieces = [jnp.where(taken, pieces[k ^ bit], pieces[k]) for k in range(len(pieces))]
    return pieces


def pair_join(own, other, core, axis=0):
    first = jnp.where(core == 0, own, other)
    second = jnp.where(core == 0, other, own)
    return jnp.concatenate([first, second], axis=axis)


def half_of(values, which, axis):
    size = values.shape[axis] // 2
    low = lax.slice_in_dim(values, 0, size, axis=axis)
    high = lax.slice_in_dim(values, size, 2 * size, axis=axis)
    return jnp.where(which == 0, low, high)


def gather_blocks(block):
    count = lax.axis_size("ctx")
    pieces = {0: block}
    for bit in reversed(bits_below(count)):
        for k in list(pieces):
            pieces[k ^ bit] = exchange(pieces[k], "ctx", bit)
    return [pieces[k] for k in range(count)]


def swap_blocks(pieces):
    return [pieces[0]] + [exchange(pieces[k], "ctx", k) for k in range(1, len(pieces))]


def head_mask(value):
    lane = lax.broadcasted_iota(jnp.int32, (1, 2 * HEAD_DIM), 1)
    return [
        jnp.where(lane < HEAD_DIM, value, 0.0),
        jnp.where(lane < HEAD_DIM, 0.0, value),
    ]


def contract(left, right, left_dim, right_dim):
    return lax.dot_general(
        left, right, (((left_dim,), (right_dim,)), ((), ())), preferred_element_type=jnp.float32
    )


def forward_kernel(query_ref, key_ref, value_ref, result_ref, low_ref, log_ref):
    query = query_ref[0].astype(jnp.float32)
    keys = key_ref[0]
    values = value_ref[0]
    results = []
    logs = []
    for mask in head_mask(HEAD_DIM ** (-0.5)):
        scores = contract((query * mask).astype(jnp.bfloat16), keys, 1, 1)
        row_max = jnp.max(scores, axis=-1, keepdims=True)
        weights = jnp.exp(scores - row_max)
        total = jnp.sum(weights, axis=-1, keepdims=True)
        probabilities = (weights * (1.0 / total)).astype(jnp.bfloat16)
        results.append(contract(probabilities, values, 1, 0))
        logs.append(row_max + jnp.log(total))
    first = lax.broadcasted_iota(jnp.int32, results[0].shape, 1) < HEAD_DIM
    result = jnp.where(first, results[0], results[1])
    result_ref[0] = result
    low_ref[0] = result.astype(jnp.bfloat16)
    log_ref[0] = jnp.where(first, logs[0], logs[1])


def attention_forward(projected):
    seqs, length, width = projected.shape
    pair = width // 3
    rows = min(256, length)
    row_spec = pl.BlockSpec((1, rows, pair), lambda s, q: (s, q, 0))
    return pl.pallas_call(
        forward_kernel,
        grid=(seqs, length // rows),
        in_specs=[
            row_spec,
            pl.BlockSpec((1, length, pair), lambda s, q: (s, 0, 1)),
            pl.BlockSpec((1, length, pair), lambda s, q: (s, 0, 2)),
        ],
        out_specs=[row_spec, row_spec, row_spec],
        out_shape=[
            jax.ShapeDtypeStruct((seqs, length, pair), jnp.float32),
            jax.ShapeDtypeStruct((seqs, length, pair), jnp.bfloat16),
            jax.ShapeDtypeStruct((seqs, length, pair), jnp.float32),
        ],
        compiler_params=pltpu.CompilerParams(vmem_limit_bytes=48 << 20),
        name="attention_forward",
    )(projected, projected, projected)


def backward_kernel(
    query_ref, key_ref, value_ref, grad_ref, result_ref, log_ref,
    query_out, key_out, value_out, query_acc, log_rows, inner_rows,
):
    step = pl.program_id(1)

    @pl.when(step == 0)
    def first_step():
        query_acc[...] = jnp.zeros_like(query_acc)
        logs = jnp.transpose(log_ref[0])
        inner = jnp.transpose(grad_ref[0].astype(jnp.float32) * result_ref[0])
        for h in range(2):
            log_rows[h] = jnp.broadcast_to(
                logs[h * HEAD_DIM : h * HEAD_DIM + 1], log_rows.shape[1:]
            )
            inner_rows[h] = jnp.broadcast_to(
                jnp.sum(inner[h * HEAD_DIM : (h + 1) * HEAD_DIM], axis=0, keepdims=True),
                inner_rows.shape[1:],
            )

    queries = query_ref[0]
    grads = grad_ref[0]
    keys = key_ref[0]
    values = value_ref[0]
    scale = HEAD_DIM ** (-0.5)
    query_parts = []
    key_parts = []
    value_parts = []
    scaled_masks = head_mask(scale)
    masks = head_mask(1.0)
    for h in range(2):
        scores = contract(
            (keys.astype(jnp.float32) * scaled_masks[h]).astype(jnp.bfloat16), queries, 1, 1
        )
        probabilities = jnp.exp(scores - log_rows[h, :1])
        prob_grad = contract(
            (values.astype(jnp.float32) * masks[h]).astype(jnp.bfloat16), grads, 1, 1
        )
        score_grad = (probabilities * (prob_grad - inner_rows[h, :1])).astype(jnp.bfloat16)
        value_parts.append(contract(probabilities.astype(jnp.bfloat16), grads, 1, 0))
        key_parts.append(contract(score_grad, queries, 1, 0))
        query_parts.append(contract(score_grad, keys, 0, 0))
    first = lax.broadcasted_iota(jnp.int32, key_parts[0].shape, 1) < HEAD_DIM
    value_out[0] = jnp.where(first, value_parts[0], value_parts[1]).astype(jnp.bfloat16)
    key_out[0] = (jnp.where(first, key_parts[0], key_parts[1]) * scale).astype(jnp.bfloat16)
    first = lax.broadcasted_iota(jnp.int32, query_parts[0].shape, 1) < HEAD_DIM
    query_acc[...] += jnp.where(first, query_parts[0], query_parts[1])

    @pl.when(step == pl.num_programs(1) - 1)
    def last_step():
        query_out[0] = (query_acc[...] * scale).astype(jnp.bfloat16)


def attention_backward(projected, grads, result, logs):
    seqs, length, width = projected.shape
    pair = width // 3
    rows = min(256, length)
    whole = pl.BlockSpec((1, length, pair), lambda s, k: (s, 0, 0))
    block = pl.BlockSpec((1, rows, pair), lambda s, k: (s, k, 0))
    shape = jax.ShapeDtypeStruct((seqs, length, pair), jnp.bfloat16)
    return pl.pallas_call(
        backward_kernel,
        grid=(seqs, length // rows),
        in_specs=[
            whole,
            pl.BlockSpec((1, rows, pair), lambda s, k: (s, k, 1)),
            pl.BlockSpec((1, rows, pair), lambda s, k: (s, k, 2)),
            whole,
            whole,
            whole,
        ],
        out_specs=[whole, block, block],
        out_shape=[shape, shape, shape],
        scratch_shapes=[
            pltpu.VMEM((length, pair), jnp.float32),
            pltpu.VMEM((2, 8, length), jnp.float32),
            pltpu.VMEM((2, 8, length), jnp.float32),
        ],
        compiler_params=pltpu.CompilerParams(vmem_limit_bytes=48 << 20),
        name="attention_backward",
    )(projected, projected, projected, grads, result, logs)


LOW = 2


def grad_kernel(place_ref, left_own, left_other, right_own, right_other, keep_ref, send_ref, *, by_rows):
    step = pl.program_id(0)
    half = pl.num_programs(0) // 2
    total = contract(left_own[...], right_own[...], 0, 0)
    total = total + contract(left_other[...], right_other[...], 0, 0)
    total = total.astype(jnp.bfloat16)
    low = place_ref[0] & ((1 << LOW) - 1)
    _, rows, cols = keep_ref.shape

    def put(out_ref):
        for j in range(1 << LOW):
            if by_rows:
                out_ref[j ^ low] = total[j * rows : (j + 1) * rows]
            else:
                out_ref[j ^ low] = total[:, j * cols : (j + 1) * cols]

    @pl.when(step < half)
    def outgoing():
        put(send_ref)

    @pl.when(step >= half)
    def kept():
        put(keep_ref)


def pair_grad(place, left_pair, right_pair, count, part, parts, by_rows, name):
    tokens, width = left_pair[0].shape
    columns = right_pair[0].shape[1]
    steps = count >> LOW
    half = steps // 2

    def block(step, place_ref):
        return part * steps + (((step + half) % steps) ^ (place_ref[0] >> LOW))

    if by_rows:
        rows, cols = width // (parts * count), columns
        left = pl.BlockSpec((tokens, rows << LOW), lambda s, p: (0, block(s, p)))
        right = pl.BlockSpec((tokens, columns), lambda s, p: (0, 0))
    else:
        rows, cols = width, columns // (parts * count)
        left = pl.BlockSpec((tokens, width), lambda s, p: (0, 0))
        right = pl.BlockSpec((tokens, cols << LOW), lambda s, p: (0, block(s, p)))
    shape = jax.ShapeDtypeStruct((count // 2, rows, cols), jnp.bfloat16)
    out_block = (1 << LOW, rows, cols)
    return pl.pallas_call(
        partial(grad_kernel, by_rows=by_rows),
        grid_spec=pltpu.PrefetchScalarGridSpec(
            num_scalar_prefetch=1,
            grid=(steps,),
            in_specs=[left, left, right, right],
            out_specs=[
                pl.BlockSpec(out_block, lambda s, p: (jnp.maximum(s - half, 0), 0, 0)),
                pl.BlockSpec(out_block, lambda s, p: (jnp.minimum(s, half - 1), 0, 0)),
            ],
        ),
        out_shape=[shape, shape],
        compiler_params=pltpu.CompilerParams(vmem_limit_bytes=48 << 20),
        name=name,
    )(place, left_pair[0], left_pair[1], right_pair[0], right_pair[1])


def place_of(order):
    place = jnp.int32(0)
    for axis, bit in order:
        place = place * 2 + jnp.where((lax.axis_index(axis) & bit) != 0, 1, 0)
    return place.astype(jnp.int32).reshape(1)


def added(first, second):
    return lowered(widened(first) + widened(second))


LINKS = {"x": ("dp", 1), "y": ("ctx", 1), "p": ("ctx", 2), "r": ("ctx", 4)}
ORDERS = {"b0": "xpyr", "b1": "ryxp", "i0": "yxrp", "i1": "pyxr", "o": "yxpr", "q": "xypr", "v": "rpyx"}
EVENTS = (
    "b0", "A", "q", "i0", "b1", "i1", "v", "o", "q", "b0", "v", "i0", "b1", "v",
    "o", "q", "i1", "b1", "o", "b0", "i0", "v", "i1", "q", "b1", "o", "v", "b0",
    "i0", "i1", "b1", "T", "o", "b0", "i0", "q", "i1", "b1", "K", "b0", "o", "q",
    "i1", "b1", "i0", "o", "b0", "i1", "i0", "o", "b0", "i0", "b1", "i1",
)


def hops(name):
    return [LINKS[letter] for letter in ORDERS[name]]


class Line:
    def __init__(self):
        self.last = None

    def after(self, values):
        if self.last is None:
            return values
        values, self.last.value = lax.optimization_barrier((values, self.last.value))
        return values

    def done(self, holder):
        self.last = holder


class Reduction:
    def __init__(self, line, name, keep, send, put):
        self.line, self.order, self.put = line, hops(name), put
        self.value, self.step = keep, 0
        self.arrived = exchange(send, *self.order[0])

    def advance(self):
        last = len(self.order) - 1
        step = self.step
        self.step += 1
        arrived, value = self.line.after((self.arrived, self.value))
        if step < last:
            half = value.shape[0] // 2
            send = added(value[half:], arrived[half:])
            self.value = added(value[:half], arrived[:half])
            self.arrived = exchange(send, *self.order[step + 1])
        elif step == last:
            self.value = added(value, arrived)
            self.arrived = exchange(self.value, *self.order[last])
        elif step <= 2 * last:
            self.value = jnp.concatenate([value, arrived], axis=0)
            self.arrived = exchange(self.value, *self.order[2 * last - step])
            if step == 2 * last:
                self.put(self.value, False)
        else:
            self.value = self.put(arrived, True)
        self.line.done(self)


def place_kernel(place_ref, chunks_ref, *rest, by_rows):
    out_ref = rest[-1]
    low = place_ref[0] & ((1 << LOW) - 1)
    _, rows, cols = chunks_ref.shape
    for j in range(1 << LOW):
        values = chunks_ref[j ^ low].astype(jnp.float32)
        if by_rows:
            out_ref[j * rows : (j + 1) * rows, :] = values
        else:
            out_ref[:, j * cols : (j + 1) * cols] = values


def put_in_place(place, chunks, far, into, part, parts, by_rows, name):
    half, rows, cols = chunks.shape
    steps = half >> LOW
    first = steps if far else 0

    def block(step, place_ref):
        return part * 2 * steps + ((step + first) ^ (place_ref[0] >> LOW))

    if by_rows:
        out_shape = (rows * 2 * half * parts, cols)
        out_spec = pl.BlockSpec((rows << LOW, cols), lambda s, p: (block(s, p), 0))
    else:
        out_shape = (rows, cols * 2 * half * parts)
        out_spec = pl.BlockSpec((rows, cols << LOW), lambda s, p: (0, block(s, p)))
    in_specs = [pl.BlockSpec((1 << LOW, rows, cols), lambda s, p: (s, 0, 0))]
    operands = [place, chunks]
    if into is not None:
        in_specs.append(pl.BlockSpec(memory_space=pl.ANY))
        operands.append(into)
    return pl.pallas_call(
        partial(place_kernel, by_rows=by_rows),
        grid_spec=pltpu.PrefetchScalarGridSpec(
            num_scalar_prefetch=1, grid=(steps,), in_specs=in_specs, out_specs=out_spec
        ),
        out_shape=jax.ShapeDtypeStruct(out_shape, jnp.float32),
        input_output_aliases={} if into is None else {2: 0},
        compiler_params=pltpu.CompilerParams(vmem_limit_bytes=48 << 20),
        name=name,
    )(*operands)


def place_three_kernel(place_ref, chunks_ref, *rest, bits):
    out_ref = rest[-1]
    count, _, _, cols = chunks_ref.shape
    low = place_ref[0] & (count - 1)
    for j in range(count):
        spot = sum(((j // bit) & 1) << (len(bits) - 1 - k) for k, bit in enumerate(bits))
        out_ref[:, j * cols : (j + 1) * cols] = chunks_ref[spot ^ low, 0].astype(jnp.float32)


def put_three_in_place(place, chunks, far, into, bits, dp_count, name):
    total, three, rows, cols = chunks.shape
    ctx_count = 1 << len(bits)
    steps = total // ctx_count
    first = steps if far else 0
    in_specs = [pl.BlockSpec((ctx_count, 1, rows, cols), lambda s, t, p: (s, t, 0, 0))]
    operands = [place, chunks]
    if into is not None:
        in_specs.append(pl.BlockSpec(memory_space=pl.ANY))
        operands.append(into)
    return pl.pallas_call(
        partial(place_three_kernel, bits=bits),
        grid_spec=pltpu.PrefetchScalarGridSpec(
            num_scalar_prefetch=1,
            grid=(steps, three),
            in_specs=in_specs,
            out_specs=pl.BlockSpec(
                (rows, ctx_count * cols),
                lambda s, t, p: ((s + first) ^ (p[0] >> len(bits)), t),
            ),
        ),
        out_shape=jax.ShapeDtypeStruct((rows * dp_count, three * ctx_count * cols), jnp.float32),
        input_output_aliases={} if into is None else {2: 0},
        compiler_params=pltpu.CompilerParams(vmem_limit_bytes=48 << 20),
        name=name,
    )(*operands)


def on_device(
    tokens,
    query_key_value_weight,
    bias_query,
    bias_value,
    attention_out_weight,
    attention_out_bias,
    gain_one,
    shift_one,
    feedforward_in_weight,
    feedforward_in_bias,
    feedforward_out_weight,
    feedforward_out_bias,
    gain_two,
    shift_two,
    d_out,
):
    core = lax.axis_index("fsdp")
    ctx = lax.axis_index("ctx")
    ctx_count = lax.axis_size("ctx")
    seqs, block_rows, width = tokens.shape
    pair = width // ctx_count
    flat = seqs * block_rows

    token_pieces = gather_blocks(tokens)

    small = (
        bias_query, bias_value, attention_out_bias, gain_one, shift_one,
        feedforward_in_bias, feedforward_out_bias, gain_two, shift_two,
    )
    packed = jnp.concatenate(small)
    packed_other = exchange(packed, "fsdp", 1)
    vectors = []
    offset = 0
    for part in small:
        size = part.shape[0]
        vectors.append(widened(pair_join(part, packed_other[offset : offset + size], core)))
        offset += size
    (
        query_bias, value_bias, out_bias, gain_first, shift_first,
        inner_bias, back_bias, gain_second, shift_second,
    ) = vectors
    qkv_full = pair_join(
        query_key_value_weight, exchange(query_key_value_weight, "fsdp", 1), core
    )
    out_full = pair_join(attention_out_weight, exchange(attention_out_weight, "fsdp", 1), core)
    in_full = pair_join(feedforward_in_weight, exchange(feedforward_in_weight, "fsdp", 1), core)
    back_full = pair_join(feedforward_out_weight, exchange(feedforward_out_weight, "fsdp", 1), core)

    head_weight = jnp.concatenate(
        [lax.dynamic_slice_in_dim(qkv_full, t * width + ctx * pair, pair, axis=1) for t in range(3)],
        axis=1,
    )
    head_bias = jnp.concatenate(
        [
            lax.dynamic_slice_in_dim(query_bias, ctx * pair, pair),
            jnp.zeros((pair,), jnp.float32),
            lax.dynamic_slice_in_dim(value_bias, ctx * pair, pair),
        ]
    )
    token_rows = jnp.concatenate(token_pieces, axis=1)
    projected = lowered(project(token_rows, head_weight) + head_bias)
    head_result, head_low, head_logs = attention_forward(projected)

    def row_blocks(values):
        return [
            lax.slice_in_dim(values, k * block_rows, (k + 1) * block_rows, axis=1)
            for k in range(ctx_count)
        ]

    attended_pieces = reorder(swap_blocks(row_blocks(head_low)), ctx)
    attended_low = jnp.concatenate(attended_pieces, axis=-1)
    attention_branch = project(attended_low, out_full) + out_bias
    summed_one = widened(tokens) + attention_branch
    first_normalized, pull_one = jax.vjp(norm_apply, summed_one, gain_first, shift_first)
    normed_low = lowered(first_normalized)
    hidden_before_gelu = project(normed_low, in_full) + inner_bias
    active_low = lowered(jax.nn.gelu(hidden_before_gelu, approximate=False))
    feedforward_branch = project(active_low, back_full) + back_bias

    def second_norm(residual_in, branch_in, gain_vec, shift_vec):
        return norm_apply(residual_in + branch_in, gain_vec, shift_vec)

    result, pull_two = jax.vjp(
        second_norm, first_normalized, feedforward_branch, gain_second, shift_second
    )
    output = lowered(result)
    first_grad_res, second_grad, gain_two_grad, shift_two_grad = pull_two(widened(d_out))
    second_low = lowered(second_grad)

    def left_pair(values):
        rows = values.reshape(flat, values.shape[2])
        return (half_of(rows, core, 1), exchange(half_of(rows, 1 - core, 1), "fsdp", 1))

    def right_pair(values):
        rows = values.reshape(flat, values.shape[2])
        return (rows, exchange(rows, "fsdp", 1))

    places = {name: place_of(hops(name)) for name in ORDERS}
    count = 1 << len(hops("b0"))

    active_pair = left_pair(active_low)
    normed_pair = left_pair(normed_low)
    attended_pair = left_pair(attended_low)
    second_pair = right_pair(second_low)
    back_parts = [
        pair_grad(places[n], active_pair, second_pair, count, part, 2, True, "grad_back")
        for part, n in enumerate(("b0", "b1"))
    ]
    back_bias_grad = column_sum(second_low)
    active_grad = back_project(second_low, back_full)
    gelu_pull = jax.vjp(partial(jax.nn.gelu, approximate=False), hidden_before_gelu)[1]
    hidden_low = lowered(gelu_pull(active_grad)[0])
    hidden_low, back_parts = lax.optimization_barrier((hidden_low, back_parts))
    hidden_pair = right_pair(hidden_low)
    in_bias_grad = column_sum(hidden_low)
    first_grad = first_grad_res + back_project(hidden_low, in_full)
    summed_grad, gain_one_grad, shift_one_grad = pull_one(first_grad)
    branch_low = lowered(summed_grad)
    branch_pair = right_pair(branch_low)
    out_bias_grad = column_sum(branch_low)
    attended_grad = lowered(back_project(branch_low, out_full))
    column_pieces = reorder(
        [attended_grad[..., k * pair : (k + 1) * pair] for k in range(ctx_count)], ctx
    )
    column_pieces, hidden_pair = lax.optimization_barrier((column_pieces, hidden_pair))
    head_grad_pieces = swap_blocks(column_pieces)
    in_parts = [
        pair_grad(places[n], normed_pair, hidden_pair, count, part, 2, False, "grad_in")
        for part, n in enumerate(("i0", "i1"))
    ]
    branch_pair, in_parts = lax.optimization_barrier((branch_pair, in_parts))
    out_parts = pair_grad(
        places["o"], attended_pair, branch_pair, count, 0, 1, True, "grad_out"
    )

    whole = {"back": None, "in": None, "out": None, "qkv": None}

    def placer(target, name, part, parts, by_rows):
        def put(chunks, far):
            whole[target] = put_in_place(
                places[name], chunks, far, whole[target], part, parts, by_rows, "place_" + target
            )
            return whole[target]

        return put

    class Placed:
        def __init__(self, target):
            self.target = target

        @property
        def value(self):
            return whole[self.target]

        @value.setter
        def value(self, new):
            whole[self.target] = new

    line = Line()
    chains = {
        "b0": Reduction(line, "b0", *back_parts[0], placer("back", "b0", 0, 2, True)),
        "b1": Reduction(line, "b1", *back_parts[1], placer("back", "b1", 1, 2, True)),
        "i0": Reduction(line, "i0", *in_parts[0], placer("in", "i0", 0, 2, False)),
        "i1": Reduction(line, "i1", *in_parts[1], placer("in", "i1", 1, 2, False)),
        "o": Reduction(line, "o", *out_parts, placer("out", "o", 0, 1, True)),
    }
    targets = {"b0": "back", "b1": "back", "i0": "in", "i1": "in", "o": "out"}
    line.done(chains["o"])
    token_flat = token_rows.reshape(-1, width)

    class Attention:
        def advance(self):
            head_grad = jnp.concatenate(line.after(head_grad_pieces), axis=1)
            self.head_grads = attention_backward(projected, head_grad, head_result, head_logs)
            qkv_part = jnp.stack(
                [contract(token_flat, g.reshape(-1, pair), 0, 0) for g in self.head_grads], axis=0
            )
            self.value = half_of(qkv_part, core, 1)
            self.other = exchange(lowered(half_of(qkv_part, 1 - core, 1)), "fsdp", 1)
            chains["v"].begin(self.head_grads)
            line.done(self)

    layer_vectors = (
        in_bias_grad, back_bias_grad, gain_two_grad, shift_two_grad,
        out_bias_grad, gain_one_grad, shift_one_grad,
    )

    class Vectors:
        def begin(self, head_grads):
            spread_out = []
            for part in (head_grads[0], head_grads[2]):
                spread_out.append(
                    lax.dynamic_update_slice_in_dim(
                        jnp.zeros((width,), jnp.float32), column_sum(part), ctx * pair, 0
                    )
                )
            self.value = jnp.concatenate(layer_vectors + tuple(spread_out))
            self.routes = [("fsdp", 1)] + hops("v")
            self.step = 0
            self.arrived = exchange(self.value, *self.routes[0])

        def advance(self):
            arrived, value = line.after((self.arrived, self.value))
            self.value = value + arrived
            self.step += 1
            if self.step < len(self.routes):
                self.arrived = exchange(self.value, *self.routes[self.step])
            line.done(self)

    class QueryKeyValue:
        def __init__(self):
            self.step = 0

        def advance(self):
            step = self.step
            self.step += 1
            order = hops("q")
            if step == 0:
                other, own = line.after((chains["A"].other, chains["A"].value))
                total = own + widened(other)
                half = total.shape[1] // 2
                low, high = total[:, :half], total[:, half:]
                first = lax.axis_index("dp") == 0
                self.value = jnp.where(first, low, high)
                self.arrived = exchange(lowered(jnp.where(first, high, low)), *order[0])
            elif step == 1:
                arrived, value = line.after((self.arrived, self.value))
                self.value = lowered(value + widened(arrived))[None]
                self.arrived = exchange(self.value, *order[-1])
            elif step <= len(order):
                arrived, value = line.after((self.arrived, self.value))
                self.value = jnp.concatenate([value, arrived], axis=0)
                self.arrived = exchange(self.value, *order[len(order) - step])
                if step == len(order):
                    self.put(self.value, False)
            else:
                arrived, value = line.after((self.arrived, self.value))
                self.value = self.put(arrived, True)
                line.done(Placed("qkv"))
                return
            line.done(self)

        def put(self, chunks, far):
            bits = [bit for axis, bit in hops("q")[1:]]
            whole["qkv"] = put_three_in_place(
                places["q"], chunks, far, whole["qkv"], bits, 2, "place_qkv"
            )
            return whole["qkv"]

    class TokenStart:
        def advance(self):
            blocks = [row_blocks(part) for part in chains["A"].head_grads]
            pieces = [jnp.concatenate([m[k] for m in blocks], axis=-1) for k in range(ctx_count)]
            pieces = line.after(pieces)
            self.value = pieces[0]
            self.arrived = swap_blocks(pieces)[1:]
            line.done(self)

    class TokenEnd:
        def advance(self):
            start = chains["T"]
            arrived, own = line.after((start.arrived, start.value))
            mixed = reorder([own] + arrived, ctx)
            mixed_grad = jnp.concatenate(
                [m[..., t * pair : (t + 1) * pair] for t in range(3) for m in mixed], axis=-1
            )
            self.value = summed_grad + back_project(mixed_grad, qkv_full)
            line.done(self)

    chains.update(A=Attention(), v=Vectors(), q=QueryKeyValue(), T=TokenStart(), K=TokenEnd())
    for name in EVENTS:
        chain = chains[name]
        chain.advance()
        if name in targets and chain.step == 8:
            line.done(Placed(targets[name]))

    reduced = []
    offset = 0
    sizes = [part.shape[0] for part in layer_vectors] + [width, width]
    for size in sizes:
        reduced.append(half_of(chains["v"].value[offset : offset + size], core, 0))
        offset += size
    token_grad = chains["K"].value
    qkv_grad, in_grad, back_grad, out_grad = (
        whole["qkv"], whole["in"], whole["back"], whole["out"]
    )
    bias_grads = reduced[7:]
    return (
        output,
        token_grad,
        qkv_grad,
        bias_grads[0],
        bias_grads[1],
        out_grad,
        reduced[4],
        reduced[5],
        reduced[6],
        in_grad,
        reduced[0],
        back_grad,
        reduced[1],
        reduced[2],
        reduced[3],
    )


def head_parallel(mesh):
    sizes = [mesh.shape["dp"], mesh.shape["ctx"]]
    return sizes == [2, 8] and mesh.shape["fsdp"] == 2 and 2 * sizes[1] == HEADS


def solution(mesh):
    in_specs = (
        P(("dp", "fsdp"), "ctx", None),
        P("fsdp", None),
        P("fsdp"),
        P("fsdp"),
        P("fsdp", None),
        P("fsdp"),
        P("fsdp"),
        P("fsdp"),
        P("fsdp", None),
        P("fsdp"),
        P("fsdp", None),
        P("fsdp"),
        P("fsdp"),
        P("fsdp"),
        P(("dp", "fsdp"), "ctx", None),
    )
    out_specs = (
        P(("dp", "fsdp"), "ctx", None),
        P(("dp", "fsdp"), "ctx", None),
        P("fsdp", None),
        P("fsdp"),
        P("fsdp"),
        P("fsdp", None),
        P("fsdp"),
        P("fsdp"),
        P("fsdp"),
        P("fsdp", None),
        P("fsdp"),
        P("fsdp", None),
        P("fsdp"),
        P("fsdp"),
        P("fsdp"),
    )
    body = on_device if head_parallel(mesh) else ring_on_device
    return jax.shard_map(
        body, mesh=mesh, in_specs=in_specs, out_specs=out_specs, check_vma=False
    )
```

```python
from functools import partial

import jax
import jax.numpy as jnp
from jax import lax
from jax.experimental import pallas as pl
from jax.experimental.pallas import tpu as pltpu
from jax.sharding import PartitionSpec as P

HEADS = 16
HEAD_DIM = 64


EPSILON = 1e-06


def from_behind(block, axis, distance):
    devices = range(lax.axis_size(axis))
    route = [((i - distance) % len(devices), i) for i in devices]
    return lax.ppermute(block, axis, route)


def norm_apply(values, gain_vec, shift_vec):
    centre = jnp.mean(values, axis=-1, keepdims=True)
    centred = values - centre
    variance = jnp.mean(centred * centred, axis=-1, keepdims=True)
    return centred * lax.rsqrt(variance + EPSILON) * gain_vec + shift_vec


def lowered(values):
    return values.astype(jnp.bfloat16)


def widened(values):
    return values.astype(jnp.float32)


def project(left_operand_rows, right_operand_matrix):
    return jnp.einsum(
        "ugj,jn->ugn", left_operand_rows, right_operand_matrix, preferred_element_type=jnp.float32
    )


def weight_grad(left_operand_rows, gradient_row_block):
    return jnp.einsum(
        "xrb,xrw->bw", left_operand_rows, gradient_row_block, preferred_element_type=jnp.float32
    )


def back_project(gradient_row_block, right_operand_matrix):
    return jnp.einsum(
        "wkb,fb->wkf", gradient_row_block, right_operand_matrix, preferred_element_type=jnp.float32
    )


def column_sum(values):
    return jnp.sum(widened(values), axis=(0, 1))


def split_heads(values):
    return values.reshape(values.shape[0], values.shape[1], HEADS, HEAD_DIM)


def merge_heads(values):
    return values.reshape(values.shape[0], values.shape[1], HEADS * HEAD_DIM)


def split_blocks(values, block_rows):
    seq_count = values.shape[0]
    blocks = values.shape[1] // block_rows
    return jnp.moveaxis(values.reshape(seq_count, blocks, block_rows, values.shape[2]), 1, 0)


def block_scores(query_rows, key_rows):
    scores = jnp.einsum(
        "sqhd,skhd->shqk",
        split_heads(query_rows),
        split_heads(key_rows),
        preferred_element_type=jnp.float32,
    )
    return scores * HEAD_DIM ** (-0.5)


def fold_block(state_now, key_block, value_block, query_rows):
    running_max, running_sum, running_acc = state_now
    scores = block_scores(query_rows, key_block)
    new_max = jnp.maximum(running_max, jnp.max(scores, axis=-1))
    rescale = jnp.exp(running_max - new_max)
    weights = jnp.exp(scores - new_max[..., None])
    new_sum = running_sum * rescale + jnp.sum(weights, axis=-1)
    product = jnp.einsum(
        "shqk,skhd->shqd",
        lowered(weights),
        split_heads(value_block),
        preferred_element_type=jnp.float32,
    )
    return (new_max, new_sum, running_acc * rescale[..., None] + product)


def attend_forward(query_rows, key_rows, value_rows):
    seq_count = query_rows.shape[0]
    block_rows = query_rows.shape[1]
    initial = (
        jnp.full((seq_count, HEADS, block_rows), -1e30, jnp.float32),
        jnp.zeros((seq_count, HEADS, block_rows), jnp.float32),
        jnp.zeros((seq_count, HEADS, block_rows, HEAD_DIM), jnp.float32),
    )
    kept = None
    key_part = lax.all_gather(key_rows, "ctx", axis=1, tiled=True)
    value_part = lax.all_gather(value_rows, "ctx", axis=1, tiled=True)

    def one_block(state_in, block_pair):
        return (fold_block(state_in, block_pair[0], block_pair[1], query_rows), None)

    state_out, unused = lax.scan(
        one_block,
        initial,
        (split_blocks(key_part, block_rows), split_blocks(value_part, block_rows)),
    )
    running_max, running_sum, running_acc = state_out
    attention_result = running_acc / running_sum[..., None]
    attention_result = jnp.transpose(attention_result, (0, 2, 1, 3)).reshape(
        seq_count, block_rows, HEADS * HEAD_DIM
    )
    log_total = running_max + jnp.log(running_sum)
    return (attention_result, log_total, kept)


def attend_back(query_rows, gradient_row_block, log_total, row_inner, key_rows, value_rows):
    score_scale = HEAD_DIM ** (-0.5)
    scores = block_scores(query_rows, key_rows)
    probabilities = jnp.exp(scores - log_total[..., None])
    value_grad = jnp.einsum(
        "shqk,sqhd->skhd",
        lowered(probabilities),
        split_heads(gradient_row_block),
        preferred_element_type=jnp.float32,
    )
    prob_grad = jnp.einsum(
        "sqhd,skhd->shqk",
        split_heads(gradient_row_block),
        split_heads(value_rows),
        preferred_element_type=jnp.float32,
    )
    score_grad = lowered(probabilities * (prob_grad - row_inner[..., None]))
    query_grad = (
        jnp.einsum(
            "shqk,skhd->sqhd", score_grad, split_heads(key_rows), preferred_element_type=jnp.float32
        )
        * score_scale
    )
    key_grad = (
        jnp.einsum(
            "shqk,sqhd->skhd",
            score_grad,
            split_heads(query_rows),
            preferred_element_type=jnp.float32,
        )
        * score_scale
    )
    return (merge_heads(query_grad), merge_heads(key_grad), merge_heads(value_grad))


def attend_backward(query_rows, gradient_row_block, log_total, row_inner, key_rows, value_rows):
    zero_rows = jnp.zeros(query_rows.shape, jnp.float32)
    turn_count = lax.axis_size("ctx") // 2

    def turn_keys(turn_index, carried):
        moving_key, moving_value, key_acc, value_acc, query_acc = carried
        for half_step in range(2):
            pieces = attend_back(
                query_rows, gradient_row_block, log_total, row_inner, moving_key, moving_value
            )
            query_acc = query_acc + pieces[0]
            key_acc = key_acc + pieces[1]
            value_acc = value_acc + pieces[2]
            moving_key, moving_value = from_behind((moving_key, moving_value), "ctx", 1)
            key_acc, value_acc = (
                from_behind(key_acc.astype(jnp.bfloat16), "ctx", 1).astype(key_acc.dtype),
                from_behind(value_acc.astype(jnp.bfloat16), "ctx", 1).astype(value_acc.dtype),
            )
        return (moving_key, moving_value, key_acc, value_acc, query_acc)

    finished = lax.fori_loop(
        0, turn_count, turn_keys, (key_rows, value_rows, zero_rows, zero_rows, zero_rows)
    )
    return (finished[4], finished[2], finished[3])


def ring_on_device(
    tokens,
    query_key_value_weight,
    bias_query,
    bias_value,
    attention_out_weight,
    attention_out_bias,
    gain_one,
    shift_one,
    feedforward_in_weight,
    feedforward_in_bias,
    feedforward_out_weight,
    feedforward_out_bias,
    gain_two,
    shift_two,
    d_out,
):
    attn_full = (
        lax.all_gather(query_key_value_weight, "fsdp", axis=0, tiled=True),
        lax.all_gather(attention_out_weight, "fsdp", axis=0, tiled=True),
        lax.all_gather(bias_query, "fsdp", axis=0, tiled=True),
        lax.all_gather(bias_value, "fsdp", axis=0, tiled=True),
        lax.all_gather(attention_out_bias, "fsdp", axis=0, tiled=True),
        lax.all_gather(gain_one, "fsdp", axis=0, tiled=True),
        lax.all_gather(shift_one, "fsdp", axis=0, tiled=True),
    )
    qkv_full, out_full, query_bias, value_bias, out_bias, gain_first, shift_first = attn_full
    model_width = out_full.shape[0]
    projected_rows = project(tokens, qkv_full) + jnp.concatenate(
        [widened(query_bias), jnp.zeros((model_width,), jnp.float32), widened(value_bias)]
    )
    projected_low = lowered(projected_rows)
    query_rows = projected_low[..., :model_width]
    key_rows = projected_low[..., model_width : 2 * model_width]
    value_rows = projected_low[..., 2 * model_width :]
    attention_result, log_total, kept = attend_forward(query_rows, key_rows, value_rows)
    attended_low = lowered(attention_result)
    attention_branch = project(attended_low, out_full) + widened(out_bias)
    summed_one = widened(tokens) + attention_branch
    first_normalized, pull_one = jax.vjp(
        norm_apply, summed_one, widened(gain_first), widened(shift_first)
    )
    normed_low = lowered(first_normalized)
    ffn_full = (
        lax.all_gather(feedforward_in_weight, "fsdp", axis=0, tiled=True),
        lax.all_gather(feedforward_out_weight, "fsdp", axis=0, tiled=True),
        lax.all_gather(feedforward_in_bias, "fsdp", axis=0, tiled=True),
        lax.all_gather(feedforward_out_bias, "fsdp", axis=0, tiled=True),
        lax.all_gather(gain_two, "fsdp", axis=0, tiled=True),
        lax.all_gather(shift_two, "fsdp", axis=0, tiled=True),
    )
    in_full, back_full, inner_bias, back_bias, gain_second, shift_second = ffn_full
    hidden_before_gelu = project(normed_low, in_full) + widened(inner_bias)
    active_low = lowered(jax.nn.gelu(hidden_before_gelu, approximate=False))
    feedforward_branch = project(active_low, back_full) + widened(back_bias)

    def second_norm(residual_in, branch_in, gain_vec, shift_vec):
        return norm_apply(residual_in + branch_in, gain_vec, shift_vec)

    result, pull_two = jax.vjp(
        second_norm,
        first_normalized,
        feedforward_branch,
        widened(gain_second),
        widened(shift_second),
    )
    output = lowered(result)
    first_grad_res, second_grad, gain_two_grad, shift_two_grad = pull_two(widened(d_out))
    in_full, back_full = (
        lax.all_gather(feedforward_in_weight, "fsdp", axis=0, tiled=True),
        lax.all_gather(feedforward_out_weight, "fsdp", axis=0, tiled=True),
    )
    second_low = lowered(second_grad)
    back_grad = weight_grad(active_low, second_low)
    back_bias_grad = column_sum(second_low)
    active_grad = back_project(second_low, back_full)
    gelu_pull = jax.vjp(partial(jax.nn.gelu, approximate=False), hidden_before_gelu)[1]
    hidden_low = lowered(gelu_pull(active_grad)[0])
    in_grad = weight_grad(normed_low, hidden_low)
    in_bias_grad = column_sum(hidden_low)
    first_grad = first_grad_res + back_project(hidden_low, in_full)
    ffn_grads = (
        lax.psum_scatter(
            in_grad.astype(jnp.bfloat16), "fsdp", scatter_dimension=0, tiled=True
        ).astype(jnp.float32),
        lax.psum_scatter(
            in_bias_grad.astype(jnp.bfloat16), "fsdp", scatter_dimension=0, tiled=True
        ).astype(jnp.float32),
        lax.psum_scatter(
            back_grad.astype(jnp.bfloat16), "fsdp", scatter_dimension=0, tiled=True
        ).astype(jnp.float32),
        lax.psum_scatter(
            back_bias_grad.astype(jnp.bfloat16), "fsdp", scatter_dimension=0, tiled=True
        ).astype(jnp.float32),
        lax.psum_scatter(
            gain_two_grad.astype(jnp.bfloat16), "fsdp", scatter_dimension=0, tiled=True
        ).astype(jnp.float32),
        lax.psum_scatter(
            shift_two_grad.astype(jnp.bfloat16), "fsdp", scatter_dimension=0, tiled=True
        ).astype(jnp.float32),
    )
    ffn_grads = lax.psum(
        (ffn_grads[0], ffn_grads[1], ffn_grads[2], ffn_grads[3], ffn_grads[4], ffn_grads[5]),
        ("dp", "ctx"),
    )
    summed_grad, gain_one_grad, shift_one_grad = pull_one(first_grad)
    qkv_full, out_full = (
        lax.all_gather(query_key_value_weight, "fsdp", axis=0, tiled=True),
        lax.all_gather(attention_out_weight, "fsdp", axis=0, tiled=True),
    )
    branch_low = lowered(summed_grad)
    out_grad = weight_grad(attended_low, branch_low)
    out_bias_grad = column_sum(branch_low)
    attended_grad_low = lowered(back_project(branch_low, out_full))
    row_inner = jnp.sum(
        split_heads(widened(attended_grad_low)) * split_heads(attention_result), axis=-1
    )
    row_inner = jnp.transpose(row_inner, (0, 2, 1))
    query_grad, key_grad, value_grad = attend_backward(
        query_rows, attended_grad_low, log_total, row_inner, key_rows, value_rows
    )
    mixed_grad = lowered(jnp.concatenate([query_grad, key_grad, value_grad], axis=-1))
    qkv_grad = weight_grad(tokens, mixed_grad)
    bias_grads = column_sum(mixed_grad)
    query_bias_grad = bias_grads[:model_width]
    value_bias_grad = bias_grads[2 * model_width :]
    token_grad = summed_grad + back_project(mixed_grad, qkv_full)
    attn_grads = (
        lax.psum_scatter(
            qkv_grad.astype(jnp.bfloat16), "fsdp", scatter_dimension=0, tiled=True
        ).astype(jnp.float32),
        lax.psum_scatter(
            query_bias_grad.astype(jnp.bfloat16), "fsdp", scatter_dimension=0, tiled=True
        ).astype(jnp.float32),
        lax.psum_scatter(
            value_bias_grad.astype(jnp.bfloat16), "fsdp", scatter_dimension=0, tiled=True
        ).astype(jnp.float32),
        lax.psum_scatter(
            out_grad.astype(jnp.bfloat16), "fsdp", scatter_dimension=0, tiled=True
        ).astype(jnp.float32),
        lax.psum_scatter(
            out_bias_grad.astype(jnp.bfloat16), "fsdp", scatter_dimension=0, tiled=True
        ).astype(jnp.float32),
        lax.psum_scatter(
            gain_one_grad.astype(jnp.bfloat16), "fsdp", scatter_dimension=0, tiled=True
        ).astype(jnp.float32),
        lax.psum_scatter(
            shift_one_grad.astype(jnp.bfloat16), "fsdp", scatter_dimension=0, tiled=True
        ).astype(jnp.float32),
    )
    attn_grads = lax.psum(
        (
            attn_grads[0],
            attn_grads[1],
            attn_grads[2],
            attn_grads[3],
            attn_grads[4],
            attn_grads[5],
            attn_grads[6],
        ),
        ("dp", "ctx"),
    )
    return (
        output,
        token_grad,
        attn_grads[0],
        attn_grads[1],
        attn_grads[2],
        attn_grads[3],
        attn_grads[4],
        attn_grads[5],
        attn_grads[6],
        ffn_grads[0],
        ffn_grads[1],
        ffn_grads[2],
        ffn_grads[3],
        ffn_grads[4],
        ffn_grads[5],
    )


def exchange(values, axis, bit):
    count = lax.axis_size(axis)
    return lax.ppermute(values, axis, [(i, i ^ bit) for i in range(count)])


def bits_below(count):
    return [1 << k for k in range(count.bit_length() - 1)]


def reorder(pieces, index):
    for bit in bits_below(len(pieces)):
        taken = (index & bit) != 0
        pieces = [jnp.where(taken, pieces[k ^ bit], pieces[k]) for k in range(len(pieces))]
    return pieces


def pair_join(own, other, core, axis=0):
    first = jnp.where(core == 0, own, other)
    second = jnp.where(core == 0, other, own)
    return jnp.concatenate([first, second], axis=axis)


def half_of(values, which, axis):
    size = values.shape[axis] // 2
    low = lax.slice_in_dim(values, 0, size, axis=axis)
    high = lax.slice_in_dim(values, size, 2 * size, axis=axis)
    return jnp.where(which == 0, low, high)


def gather_blocks(block, order):
    pieces = {0: block}
    for bit in order:
        for k in list(pieces):
            pieces[k ^ bit] = exchange(pieces[k], "ctx", bit)
    return [pieces[k] for k in range(len(pieces))]


def swap_blocks(pieces):
    return [pieces[0]] + [exchange(pieces[k], "ctx", k) for k in range(1, len(pieces))]


def head_mask(value):
    lane = lax.broadcasted_iota(jnp.int32, (1, 2 * HEAD_DIM), 1)
    return [
        jnp.where(lane < HEAD_DIM, value, 0.0),
        jnp.where(lane < HEAD_DIM, 0.0, value),
    ]


def contract(left, right, left_dim, right_dim):
    return lax.dot_general(
        left, right, (((left_dim,), (right_dim,)), ((), ())), preferred_element_type=jnp.float32
    )


def forward_kernel(query_ref, key_ref, value_ref, result_ref, low_ref, log_ref):
    query = query_ref[0].astype(jnp.float32)
    keys = key_ref[0]
    values = value_ref[0]
    results = []
    logs = []
    for mask in head_mask(HEAD_DIM ** (-0.5)):
        scores = contract((query * mask).astype(jnp.bfloat16), keys, 1, 1)
        row_max = jnp.max(scores, axis=-1, keepdims=True)
        weights = jnp.exp(scores - row_max)
        total = jnp.sum(weights, axis=-1, keepdims=True)
        probabilities = (weights * (1.0 / total)).astype(jnp.bfloat16)
        results.append(contract(probabilities, values, 1, 0))
        logs.append(row_max + jnp.log(total))
    first = lax.broadcasted_iota(jnp.int32, results[0].shape, 1) < HEAD_DIM
    result = jnp.where(first, results[0], results[1])
    result_ref[0] = result
    low_ref[0] = result.astype(jnp.bfloat16)
    log_ref[0] = jnp.where(first, logs[0], logs[1])


def attention_forward(projected):
    seqs, length, width = projected.shape
    pair = width // 3
    rows = min(256, length)
    row_spec = pl.BlockSpec((1, rows, pair), lambda s, q: (s, q, 0))
    return pl.pallas_call(
        forward_kernel,
        grid=(seqs, length // rows),
        in_specs=[
            row_spec,
            pl.BlockSpec((1, length, pair), lambda s, q: (s, 0, 1)),
            pl.BlockSpec((1, length, pair), lambda s, q: (s, 0, 2)),
        ],
        out_specs=[row_spec, row_spec, row_spec],
        out_shape=[
            jax.ShapeDtypeStruct((seqs, length, pair), jnp.float32),
            jax.ShapeDtypeStruct((seqs, length, pair), jnp.bfloat16),
            jax.ShapeDtypeStruct((seqs, length, pair), jnp.float32),
        ],
        compiler_params=pltpu.CompilerParams(vmem_limit_bytes=48 << 20),
        name="attention_forward",
    )(projected, projected, projected)


def backward_kernel(
    query_ref, key_ref, value_ref, grad_ref, result_ref, log_ref,
    query_out, key_out, value_out, query_acc, log_rows, inner_rows,
):
    step = pl.program_id(1)

    @pl.when(step == 0)
    def first_step():
        query_acc[...] = jnp.zeros_like(query_acc)
        logs = jnp.transpose(log_ref[0])
        inner = jnp.transpose(grad_ref[0].astype(jnp.float32) * result_ref[0])
        for h in range(2):
            log_rows[h] = jnp.broadcast_to(
                logs[h * HEAD_DIM : h * HEAD_DIM + 1], log_rows.shape[1:]
            )
            inner_rows[h] = jnp.broadcast_to(
                jnp.sum(inner[h * HEAD_DIM : (h + 1) * HEAD_DIM], axis=0, keepdims=True),
                inner_rows.shape[1:],
            )

    queries = query_ref[0]
    grads = grad_ref[0]
    keys = key_ref[0]
    values = value_ref[0]
    scale = HEAD_DIM ** (-0.5)
    query_parts = []
    key_parts = []
    value_parts = []
    scaled_masks = head_mask(scale)
    masks = head_mask(1.0)
    for h in range(2):
        scores = contract(
            (keys.astype(jnp.float32) * scaled_masks[h]).astype(jnp.bfloat16), queries, 1, 1
        )
        probabilities = jnp.exp(scores - log_rows[h, :1])
        prob_grad = contract(
            (values.astype(jnp.float32) * masks[h]).astype(jnp.bfloat16), grads, 1, 1
        )
        score_grad = (probabilities * (prob_grad - inner_rows[h, :1])).astype(jnp.bfloat16)
        value_parts.append(contract(probabilities.astype(jnp.bfloat16), grads, 1, 0))
        key_parts.append(contract(score_grad, queries, 1, 0))
        query_parts.append(contract(score_grad, keys, 0, 0))
    first = lax.broadcasted_iota(jnp.int32, key_parts[0].shape, 1) < HEAD_DIM
    value_out[0] = jnp.where(first, value_parts[0], value_parts[1]).astype(jnp.bfloat16)
    key_out[0] = (jnp.where(first, key_parts[0], key_parts[1]) * scale).astype(jnp.bfloat16)
    first = lax.broadcasted_iota(jnp.int32, query_parts[0].shape, 1) < HEAD_DIM
    query_acc[...] += jnp.where(first, query_parts[0], query_parts[1])

    @pl.when(step == pl.num_programs(1) - 1)
    def last_step():
        query_out[0] = (query_acc[...] * scale).astype(jnp.bfloat16)


def attention_backward(projected, grads, result, logs):
    seqs, length, width = projected.shape
    pair = width // 3
    rows = min(256, length)
    whole = pl.BlockSpec((1, length, pair), lambda s, k: (s, 0, 0))
    block = pl.BlockSpec((1, rows, pair), lambda s, k: (s, k, 0))
    shape = jax.ShapeDtypeStruct((seqs, length, pair), jnp.bfloat16)
    return pl.pallas_call(
        backward_kernel,
        grid=(seqs, length // rows),
        in_specs=[
            whole,
            pl.BlockSpec((1, rows, pair), lambda s, k: (s, k, 1)),
            pl.BlockSpec((1, rows, pair), lambda s, k: (s, k, 2)),
            whole,
            whole,
            whole,
        ],
        out_specs=[whole, block, block],
        out_shape=[shape, shape, shape],
        scratch_shapes=[
            pltpu.VMEM((length, pair), jnp.float32),
            pltpu.VMEM((2, 8, length), jnp.float32),
            pltpu.VMEM((2, 8, length), jnp.float32),
        ],
        compiler_params=pltpu.CompilerParams(vmem_limit_bytes=48 << 20),
        name="attention_backward",
    )(projected, projected, projected, grads, result, logs)


LOW = 2


def grad_kernel(place_ref, left_own, left_other, right_own, right_other, keep_ref, send_ref, *, by_rows):
    step = pl.program_id(0)
    half = pl.num_programs(0) // 2
    total = contract(left_own[...], right_own[...], 0, 0)
    total = total + contract(left_other[...], right_other[...], 0, 0)
    total = total.astype(jnp.bfloat16)
    low = place_ref[0] & ((1 << LOW) - 1)
    _, rows, cols = keep_ref.shape

    def put(out_ref):
        for j in range(1 << LOW):
            if by_rows:
                out_ref[j ^ low] = total[j * rows : (j + 1) * rows]
            else:
                out_ref[j ^ low] = total[:, j * cols : (j + 1) * cols]

    @pl.when(step < half)
    def outgoing():
        put(send_ref)

    @pl.when(step >= half)
    def kept():
        put(keep_ref)


def pair_grad(place, left_pair, right_pair, count, part, parts, by_rows, name):
    tokens, width = left_pair[0].shape
    columns = right_pair[0].shape[1]
    steps = count >> LOW
    half = steps // 2

    def block(step, place_ref):
        return part * steps + (((step + half) % steps) ^ (place_ref[0] >> LOW))

    if by_rows:
        rows, cols = width // (parts * count), columns
        left = pl.BlockSpec((tokens, rows << LOW), lambda s, p: (0, block(s, p)))
        right = pl.BlockSpec((tokens, columns), lambda s, p: (0, 0))
    else:
        rows, cols = width, columns // (parts * count)
        left = pl.BlockSpec((tokens, width), lambda s, p: (0, 0))
        right = pl.BlockSpec((tokens, cols << LOW), lambda s, p: (0, block(s, p)))
    shape = jax.ShapeDtypeStruct((count // 2, rows, cols), jnp.bfloat16)
    out_block = (1 << LOW, rows, cols)
    return pl.pallas_call(
        partial(grad_kernel, by_rows=by_rows),
        grid_spec=pltpu.PrefetchScalarGridSpec(
            num_scalar_prefetch=1,
            grid=(steps,),
            in_specs=[left, left, right, right],
            out_specs=[
                pl.BlockSpec(out_block, lambda s, p: (jnp.maximum(s - half, 0), 0, 0)),
                pl.BlockSpec(out_block, lambda s, p: (jnp.minimum(s, half - 1), 0, 0)),
            ],
        ),
        out_shape=[shape, shape],
        compiler_params=pltpu.CompilerParams(vmem_limit_bytes=48 << 20),
        name=name,
    )(place, left_pair[0], left_pair[1], right_pair[0], right_pair[1])


def place_of(order):
    place = jnp.int32(0)
    for axis, bit in order:
        place = place * 2 + jnp.where((lax.axis_index(axis) & bit) != 0, 1, 0)
    return place.astype(jnp.int32).reshape(1)


def added(first, second):
    return lowered(widened(first) + widened(second))


LINKS = {"x": ("dp", 1), "y": ("ctx", 1), "p": ("ctx", 2), "r": ("ctx", 4)}
ORDERS = {"b0": "pyrx", "b1": "yprx", "i0": "xypr", "i1": "yxpr", "o": "rxpy", "q": "xypr", "v": "xypr", "T": "ypr"}
EVENTS = (
    "b", "A", "i", "q", "o", "b", "i", "q", "v", "o", "v", "b", "i", "v", "o", "q",
    "b", "o", "v", "i", "T", "o", "q", "b", "v", "o", "i", "T", "o", "b", "i", "q",
    "T", "i", "o", "b", "q", "T", "i", "b",
)


def hops(name):
    return [LINKS[letter] for letter in ORDERS[name]]


class Line:
    def __init__(self):
        self.last = None

    def after(self, values):
        if self.last is None:
            return values
        values, self.last.value = lax.optimization_barrier((values, self.last.value))
        return values

    def done(self, holder):
        self.last = holder


class Reduction:
    def __init__(self, line, name, keep, send, put):
        self.line, self.order, self.put = line, hops(name), put
        self.value, self.step = keep, 0
        self.arrived = exchange(send, *self.order[0])

    def advance(self):
        last = len(self.order) - 1
        step = self.step
        self.step += 1
        arrived, value = self.line.after((self.arrived, self.value))
        if step < last:
            half = value.shape[0] // 2
            send = added(value[half:], arrived[half:])
            self.value = added(value[:half], arrived[:half])
            self.arrived = exchange(send, *self.order[step + 1])
        elif step == last:
            self.value = added(value, arrived)
            self.arrived = exchange(self.value, *self.order[last])
        elif step <= 2 * last:
            self.value = jnp.concatenate([value, arrived], axis=0)
            self.arrived = exchange(self.value, *self.order[2 * last - step])
            if step == 2 * last:
                self.put(self.value, False)
        else:
            self.value = self.put(arrived, True)
        self.line.done(self)


class Group:
    def __init__(self, line, names, parts, put):
        self.line, self.put, self.step = line, put, 1
        self.orders = [hops(name) for name in names]
        self.value = [keep for keep, send in parts]
        self.arrived = [exchange(send, *o[0]) for (keep, send), o in zip(parts, self.orders)]

    def advance(self):
        arrived, value = self.line.after((self.arrived, self.value))
        tail = self.orders[0][2:]
        step = self.step
        self.step += 1
        if step == 1:
            self.arrived = [
                exchange(added(v[v.shape[0] // 2 :], a[v.shape[0] // 2 :]), *o[1])
                for v, a, o in zip(value, arrived, self.orders)
            ]
            self.value = [
                added(v[: v.shape[0] // 2], a[: v.shape[0] // 2]) for v, a in zip(value, arrived)
            ]
        elif step == 2:
            total = jnp.stack([added(v, a) for v, a in zip(value, arrived)], axis=1)
            self.value = total[:2]
            self.arrived = exchange(total[2:], *tail[0])
        elif step == 3:
            self.value = added(value[:1], arrived[:1])
            self.arrived = exchange(added(value[1:], arrived[1:]), *tail[1])
        elif step == 4:
            self.value = added(value, arrived)
            self.arrived = exchange(self.value, *tail[1])
        elif step == 5:
            self.value = jnp.concatenate([value, arrived], axis=0)
            self.arrived = exchange(self.value, *tail[0])
        elif step == 6:
            total = jnp.concatenate([value, arrived], axis=0)
            self.value = [total[:, 0], total[:, 1]]
            self.arrived = [exchange(v, *o[1]) for v, o in zip(self.value, self.orders)]
        elif step == 7:
            self.value = [jnp.concatenate([v, a], axis=0) for v, a in zip(value, arrived)]
            self.arrived = [exchange(v, *o[0]) for v, o in zip(self.value, self.orders)]
            for part, chunks in enumerate(self.value):
                self.put(chunks, part, False)
        else:
            for part, chunks in enumerate(arrived):
                self.value = self.put(chunks, part, True)
        self.line.done(self)


def place_kernel(place_ref, chunks_ref, *rest, by_rows):
    out_ref = rest[-1]
    low = place_ref[0] & ((1 << LOW) - 1)
    _, rows, cols = chunks_ref.shape
    for j in range(1 << LOW):
        values = chunks_ref[j ^ low].astype(jnp.float32)
        if by_rows:
            out_ref[j * rows : (j + 1) * rows, :] = values
        else:
            out_ref[:, j * cols : (j + 1) * cols] = values


def put_in_place(place, chunks, far, into, part, parts, by_rows, name):
    half, rows, cols = chunks.shape
    steps = half >> LOW
    first = steps if far else 0

    def block(step, place_ref):
        return part * 2 * steps + ((step + first) ^ (place_ref[0] >> LOW))

    if by_rows:
        out_shape = (rows * 2 * half * parts, cols)
        out_spec = pl.BlockSpec((rows << LOW, cols), lambda s, p: (block(s, p), 0))
    else:
        out_shape = (rows, cols * 2 * half * parts)
        out_spec = pl.BlockSpec((rows, cols << LOW), lambda s, p: (0, block(s, p)))
    in_specs = [pl.BlockSpec((1 << LOW, rows, cols), lambda s, p: (s, 0, 0))]
    operands = [place, chunks]
    if into is not None:
        in_specs.append(pl.BlockSpec(memory_space=pl.ANY))
        operands.append(into)
    return pl.pallas_call(
        partial(place_kernel, by_rows=by_rows),
        grid_spec=pltpu.PrefetchScalarGridSpec(
            num_scalar_prefetch=1, grid=(steps,), in_specs=in_specs, out_specs=out_spec
        ),
        out_shape=jax.ShapeDtypeStruct(out_shape, jnp.float32),
        input_output_aliases={} if into is None else {2: 0},
        compiler_params=pltpu.CompilerParams(vmem_limit_bytes=48 << 20),
        name=name,
    )(*operands)


def place_three_kernel(place_ref, chunks_ref, *rest, bits):
    out_ref = rest[-1]
    count, _, _, cols = chunks_ref.shape
    low = place_ref[0] & (count - 1)
    for j in range(count):
        spot = sum(((j // bit) & 1) << (len(bits) - 1 - k) for k, bit in enumerate(bits))
        out_ref[:, j * cols : (j + 1) * cols] = chunks_ref[spot ^ low, 0].astype(jnp.float32)


def put_three_in_place(place, chunks, far, into, bits, dp_count, name):
    total, three, rows, cols = chunks.shape
    ctx_count = 1 << len(bits)
    steps = total // ctx_count
    first = steps if far else 0
    in_specs = [pl.BlockSpec((ctx_count, 1, rows, cols), lambda s, t, p: (s, t, 0, 0))]
    operands = [place, chunks]
    if into is not None:
        in_specs.append(pl.BlockSpec(memory_space=pl.ANY))
        operands.append(into)
    return pl.pallas_call(
        partial(place_three_kernel, bits=bits),
        grid_spec=pltpu.PrefetchScalarGridSpec(
            num_scalar_prefetch=1,
            grid=(steps, three),
            in_specs=in_specs,
            out_specs=pl.BlockSpec(
                (rows, ctx_count * cols),
                lambda s, t, p: ((s + first) ^ (p[0] >> len(bits)), t),
            ),
        ),
        out_shape=jax.ShapeDtypeStruct((rows * dp_count, three * ctx_count * cols), jnp.float32),
        input_output_aliases={} if into is None else {2: 0},
        compiler_params=pltpu.CompilerParams(vmem_limit_bytes=48 << 20),
        name=name,
    )(*operands)


def on_device(
    tokens,
    query_key_value_weight,
    bias_query,
    bias_value,
    attention_out_weight,
    attention_out_bias,
    gain_one,
    shift_one,
    feedforward_in_weight,
    feedforward_in_bias,
    feedforward_out_weight,
    feedforward_out_bias,
    gain_two,
    shift_two,
    d_out,
):
    core = lax.axis_index("fsdp")
    ctx = lax.axis_index("ctx")
    ctx_count = lax.axis_size("ctx")
    seqs, block_rows, width = tokens.shape
    pair = width // ctx_count
    flat = seqs * block_rows

    cut = block_rows // 4
    token_pieces = [
        jnp.concatenate(pair_of, axis=1)
        for pair_of in zip(
            gather_blocks(tokens[:, :cut], (1, 4, 2)), gather_blocks(tokens[:, cut:], (4, 2, 1))
        )
    ]

    small = (
        bias_query, bias_value, attention_out_bias, gain_one, shift_one,
        feedforward_in_bias, feedforward_out_bias, gain_two, shift_two,
    )
    packed = jnp.concatenate(small)
    packed_other = exchange(packed, "fsdp", 1)
    vectors = []
    offset = 0
    for part in small:
        size = part.shape[0]
        vectors.append(widened(pair_join(part, packed_other[offset : offset + size], core)))
        offset += size
    (
        query_bias, value_bias, out_bias, gain_first, shift_first,
        inner_bias, back_bias, gain_second, shift_second,
    ) = vectors
    qkv_full = pair_join(
        query_key_value_weight, exchange(query_key_value_weight, "fsdp", 1), core
    )
    out_full = pair_join(attention_out_weight, exchange(attention_out_weight, "fsdp", 1), core)
    in_full = pair_join(feedforward_in_weight, exchange(feedforward_in_weight, "fsdp", 1), core)
    back_full = pair_join(feedforward_out_weight, exchange(feedforward_out_weight, "fsdp", 1), core)

    head_weight = jnp.concatenate(
        [lax.dynamic_slice_in_dim(qkv_full, t * width + ctx * pair, pair, axis=1) for t in range(3)],
        axis=1,
    )
    head_bias = jnp.concatenate(
        [
            lax.dynamic_slice_in_dim(query_bias, ctx * pair, pair),
            jnp.zeros((pair,), jnp.float32),
            lax.dynamic_slice_in_dim(value_bias, ctx * pair, pair),
        ]
    )
    token_rows = jnp.concatenate(token_pieces, axis=1)
    projected = jnp.concatenate(
        [lowered(project(piece, head_weight) + head_bias) for piece in token_pieces], axis=1
    )
    head_result, head_low, head_logs = attention_forward(projected)

    def row_blocks(values):
        return [
            lax.slice_in_dim(values, k * block_rows, (k + 1) * block_rows, axis=1)
            for k in range(ctx_count)
        ]

    attended_pieces = reorder(swap_blocks(row_blocks(head_low)), ctx)
    attended_low = jnp.concatenate(attended_pieces, axis=-1)
    attention_branch = project(attended_low, out_full) + out_bias
    summed_one = widened(tokens) + attention_branch
    first_normalized, pull_one = jax.vjp(norm_apply, summed_one, gain_first, shift_first)
    normed_low = lowered(first_normalized)
    hidden_before_gelu = project(normed_low, in_full) + inner_bias
    active_low = lowered(jax.nn.gelu(hidden_before_gelu, approximate=False))
    feedforward_branch = project(active_low, back_full) + back_bias

    def second_norm(residual_in, branch_in, gain_vec, shift_vec):
        return norm_apply(residual_in + branch_in, gain_vec, shift_vec)

    result, pull_two = jax.vjp(
        second_norm, first_normalized, feedforward_branch, gain_second, shift_second
    )
    output = lowered(result)
    first_grad_res, second_grad, gain_two_grad, shift_two_grad = pull_two(widened(d_out))
    second_low = lowered(second_grad)

    def left_pair(values):
        rows = values.reshape(flat, values.shape[2])
        return (half_of(rows, core, 1), exchange(half_of(rows, 1 - core, 1), "fsdp", 1))

    def right_pair(values):
        rows = values.reshape(flat, values.shape[2])
        return (rows, exchange(rows, "fsdp", 1))

    places = {name: place_of(hops(name)) for name in ORDERS}
    count = 1 << len(hops("q"))

    active_pair = left_pair(active_low)
    normed_pair = left_pair(normed_low)
    attended_pair = left_pair(attended_low)
    second_pair = right_pair(second_low)
    back_parts = [
        pair_grad(places[n], active_pair, second_pair, count, part, 2, True, "grad_back")
        for part, n in enumerate(("b0", "b1"))
    ]
    back_bias_grad = column_sum(second_low)
    active_grad = back_project(second_low, back_full)
    gelu_pull = jax.vjp(partial(jax.nn.gelu, approximate=False), hidden_before_gelu)[1]
    hidden_low = lowered(gelu_pull(active_grad)[0])
    hidden_low, back_parts = lax.optimization_barrier((hidden_low, back_parts))
    hidden_pair = right_pair(hidden_low)
    in_bias_grad = column_sum(hidden_low)
    first_grad = first_grad_res + back_project(hidden_low, in_full)
    summed_grad, gain_one_grad, shift_one_grad = pull_one(first_grad)
    branch_low = lowered(summed_grad)
    branch_pair = right_pair(branch_low)
    out_bias_grad = column_sum(branch_low)
    attended_grad = lowered(back_project(branch_low, out_full))
    column_pieces = reorder(
        [attended_grad[..., k * pair : (k + 1) * pair] for k in range(ctx_count)], ctx
    )
    column_pieces, hidden_pair = lax.optimization_barrier((column_pieces, hidden_pair))
    head_grad_pieces = swap_blocks(column_pieces)
    in_parts = [
        pair_grad(places[n], normed_pair, hidden_pair, count, part, 2, False, "grad_in")
        for part, n in enumerate(("i0", "i1"))
    ]
    branch_pair, in_parts = lax.optimization_barrier((branch_pair, in_parts))
    out_parts = pair_grad(
        places["o"], attended_pair, branch_pair, count, 0, 1, True, "grad_out"
    )

    whole = {"back": None, "in": None, "out": None, "qkv": None}

    def placer(target, names, by_rows):
        def put(chunks, part, far):
            whole[target] = put_in_place(
                places[names[part]], chunks, far, whole[target], part, len(names), by_rows,
                "place_" + target,
            )
            return whole[target]

        return put

    put_out = placer("out", ("o",), True)

    class Placed:
        def __init__(self, target):
            self.target = target

        @property
        def value(self):
            return whole[self.target]

        @value.setter
        def value(self, new):
            whole[self.target] = new

    line = Line()
    chains = {
        "b": Group(line, ("b0", "b1"), back_parts, placer("back", ("b0", "b1"), True)),
        "i": Group(line, ("i0", "i1"), in_parts, placer("in", ("i0", "i1"), False)),
        "o": Reduction(line, "o", *out_parts, lambda chunks, far: put_out(chunks, 0, far)),
    }
    targets = {"b": ("back", 9), "i": ("in", 9), "o": ("out", 8)}
    line.done(chains["o"])
    token_flat = token_rows.reshape(-1, width)

    class Attention:
        def advance(self):
            head_grad = jnp.concatenate(line.after(head_grad_pieces), axis=1)
            self.head_grads = attention_backward(projected, head_grad, head_result, head_logs)
            qkv_part = jnp.stack(
                [contract(token_flat, g.reshape(-1, pair), 0, 0) for g in self.head_grads], axis=0
            )
            self.value = half_of(qkv_part, core, 1)
            self.other = exchange(lowered(half_of(qkv_part, 1 - core, 1)), "fsdp", 1)
            chains["v"].begin(self.head_grads)
            line.done(self)

    layer_vectors = (
        in_bias_grad, back_bias_grad, gain_two_grad, shift_two_grad,
        out_bias_grad, gain_one_grad, shift_one_grad,
    )

    class Vectors:
        def begin(self, head_grads):
            spread_out = []
            for part in (head_grads[0], head_grads[2]):
                spread_out.append(
                    lax.dynamic_update_slice_in_dim(
                        jnp.zeros((width,), jnp.float32), column_sum(part), ctx * pair, 0
                    )
                )
            self.value = jnp.concatenate(layer_vectors + tuple(spread_out))
            self.routes = [("fsdp", 1)] + hops("v")
            self.step = 0
            self.arrived = exchange(self.value, *self.routes[0])

        def advance(self):
            arrived, value = line.after((self.arrived, self.value))
            self.value = value + arrived
            self.step += 1
            if self.step < len(self.routes):
                self.arrived = exchange(self.value, *self.routes[self.step])
            line.done(self)

    class QueryKeyValue:
        def __init__(self):
            self.step = 0

        def advance(self):
            step = self.step
            self.step += 1
            order = hops("q")
            if step == 0:
                other, own = line.after((chains["A"].other, chains["A"].value))
                total = own + widened(other)
                half = total.shape[1] // 2
                low, high = total[:, :half], total[:, half:]
                first = lax.axis_index("dp") == 0
                self.value = jnp.where(first, low, high)
                self.arrived = exchange(lowered(jnp.where(first, high, low)), *order[0])
            elif step == 1:
                arrived, value = line.after((self.arrived, self.value))
                self.value = lowered(value + widened(arrived))[None]
                self.arrived = exchange(self.value, *order[-1])
            elif step <= len(order):
                arrived, value = line.after((self.arrived, self.value))
                self.value = jnp.concatenate([value, arrived], axis=0)
                self.arrived = exchange(self.value, *order[len(order) - step])
                if step == len(order):
                    self.put(self.value, False)
            else:
                arrived, value = line.after((self.arrived, self.value))
                self.value = self.put(arrived, True)
                line.done(Placed("qkv"))
                return
            line.done(self)

        def put(self, chunks, far):
            bits = [bit for axis, bit in hops("q")[1:]]
            whole["qkv"] = put_three_in_place(
                places["q"], chunks, far, whole["qkv"], bits, 2, "place_qkv"
            )
            return whole["qkv"]

    class Tokens:
        def __init__(self):
            self.step = 0

        def advance(self):
            order = hops("T")
            if self.step == 0:
                blocks = [row_blocks(part) for part in chains["A"].head_grads]
                pieces = line.after(
                    [jnp.concatenate([m[k] for m in blocks], axis=-1) for k in range(ctx_count)]
                )
                held = {(0, k): piece for k, piece in enumerate(pieces)}
            else:
                bit = order[self.step - 1][1]
                arrived, kept = line.after((self.arrived, self.value))
                held = dict(zip(self.kept, kept))
                for n, (source, target) in enumerate(self.sent):
                    held[source ^ bit, target ^ bit] = arrived[n]
            if self.step < len(order):
                bit = order[self.step][1]
                self.sent = [key for key in sorted(held) if key[1] & bit]
                self.kept = [key for key in sorted(held) if not key[1] & bit]
                self.arrived = exchange(jnp.stack([held[key] for key in self.sent]), *order[self.step])
                self.value = [held[key] for key in self.kept]
            else:
                mixed = reorder([held[k, 0] for k in range(ctx_count)], ctx)
                mixed_grad = jnp.concatenate(
                    [m[..., t * pair : (t + 1) * pair] for t in range(3) for m in mixed], axis=-1
                )
                self.value = summed_grad + back_project(mixed_grad, qkv_full)
            self.step += 1
            line.done(self)

    chains.update(A=Attention(), v=Vectors(), q=QueryKeyValue(), T=Tokens())
    for name in EVENTS:
        chain = chains[name]
        chain.advance()
        if name in targets and chain.step == targets[name][1]:
            line.done(Placed(targets[name][0]))

    reduced = []
    offset = 0
    sizes = [part.shape[0] for part in layer_vectors] + [width, width]
    for size in sizes:
        reduced.append(half_of(chains["v"].value[offset : offset + size], core, 0))
        offset += size
    token_grad = chains["T"].value
    qkv_grad, in_grad, back_grad, out_grad = (
        whole["qkv"], whole["in"], whole["back"], whole["out"]
    )
    bias_grads = reduced[7:]
    return (
        output,
        token_grad,
        qkv_grad,
        bias_grads[0],
        bias_grads[1],
        out_grad,
        reduced[4],
        reduced[5],
        reduced[6],
        in_grad,
        reduced[0],
        back_grad,
        reduced[1],
        reduced[2],
        reduced[3],
    )


def head_parallel(mesh):
    sizes = [mesh.shape["dp"], mesh.shape["ctx"]]
    return sizes == [2, 8] and mesh.shape["fsdp"] == 2 and 2 * sizes[1] == HEADS


def solution(mesh):
    in_specs = (
        P(("dp", "fsdp"), "ctx", None),
        P("fsdp", None),
        P("fsdp"),
        P("fsdp"),
        P("fsdp", None),
        P("fsdp"),
        P("fsdp"),
        P("fsdp"),
        P("fsdp", None),
        P("fsdp"),
        P("fsdp", None),
        P("fsdp"),
        P("fsdp"),
        P("fsdp"),
        P(("dp", "fsdp"), "ctx", None),
    )
    out_specs = (
        P(("dp", "fsdp"), "ctx", None),
        P(("dp", "fsdp"), "ctx", None),
        P("fsdp", None),
        P("fsdp"),
        P("fsdp"),
        P("fsdp", None),
        P("fsdp"),
        P("fsdp"),
        P("fsdp"),
        P("fsdp", None),
        P("fsdp"),
        P("fsdp", None),
        P("fsdp"),
        P("fsdp"),
        P("fsdp"),
    )
    body = on_device if head_parallel(mesh) else ring_on_device
    return jax.shard_map(
        body, mesh=mesh, in_specs=in_specs, out_specs=out_specs, check_vma=False
    )
```

```python
from functools import partial

import jax
import jax.numpy as jnp
from jax import lax
from jax.experimental import pallas as pl
from jax.experimental.pallas import tpu as pltpu
from jax.sharding import PartitionSpec as P

HEADS = 16
HEAD_DIM = 64


EPSILON = 1e-06


def from_behind(block, axis, distance):
    devices = range(lax.axis_size(axis))
    route = [((i - distance) % len(devices), i) for i in devices]
    return lax.ppermute(block, axis, route)


def norm_apply(values, gain_vec, shift_vec):
    centre = jnp.mean(values, axis=-1, keepdims=True)
    centred = values - centre
    variance = jnp.mean(centred * centred, axis=-1, keepdims=True)
    return centred * lax.rsqrt(variance + EPSILON) * gain_vec + shift_vec


def lowered(values):
    return values.astype(jnp.bfloat16)


def widened(values):
    return values.astype(jnp.float32)


def project(left_operand_rows, right_operand_matrix):
    return jnp.einsum(
        "ugj,jn->ugn", left_operand_rows, right_operand_matrix, preferred_element_type=jnp.float32
    )


def weight_grad(left_operand_rows, gradient_row_block):
    return jnp.einsum(
        "xrb,xrw->bw", left_operand_rows, gradient_row_block, preferred_element_type=jnp.float32
    )


def back_project(gradient_row_block, right_operand_matrix):
    return jnp.einsum(
        "wkb,fb->wkf", gradient_row_block, right_operand_matrix, preferred_element_type=jnp.float32
    )


def column_sum(values):
    return jnp.sum(widened(values), axis=(0, 1))


def split_heads(values):
    return values.reshape(values.shape[0], values.shape[1], HEADS, HEAD_DIM)


def merge_heads(values):
    return values.reshape(values.shape[0], values.shape[1], HEADS * HEAD_DIM)


def split_blocks(values, block_rows):
    seq_count = values.shape[0]
    blocks = values.shape[1] // block_rows
    return jnp.moveaxis(values.reshape(seq_count, blocks, block_rows, values.shape[2]), 1, 0)


def block_scores(query_rows, key_rows):
    scores = jnp.einsum(
        "sqhd,skhd->shqk",
        split_heads(query_rows),
        split_heads(key_rows),
        preferred_element_type=jnp.float32,
    )
    return scores * HEAD_DIM ** (-0.5)


def fold_block(state_now, key_block, value_block, query_rows):
    running_max, running_sum, running_acc = state_now
    scores = block_scores(query_rows, key_block)
    new_max = jnp.maximum(running_max, jnp.max(scores, axis=-1))
    rescale = jnp.exp(running_max - new_max)
    weights = jnp.exp(scores - new_max[..., None])
    new_sum = running_sum * rescale + jnp.sum(weights, axis=-1)
    product = jnp.einsum(
        "shqk,skhd->shqd",
        lowered(weights),
        split_heads(value_block),
        preferred_element_type=jnp.float32,
    )
    return (new_max, new_sum, running_acc * rescale[..., None] + product)


def attend_forward(query_rows, key_rows, value_rows):
    seq_count = query_rows.shape[0]
    block_rows = query_rows.shape[1]
    initial = (
        jnp.full((seq_count, HEADS, block_rows), -1e30, jnp.float32),
        jnp.zeros((seq_count, HEADS, block_rows), jnp.float32),
        jnp.zeros((seq_count, HEADS, block_rows, HEAD_DIM), jnp.float32),
    )
    kept = None
    key_part = lax.all_gather(key_rows, "ctx", axis=1, tiled=True)
    value_part = lax.all_gather(value_rows, "ctx", axis=1, tiled=True)

    def one_block(state_in, block_pair):
        return (fold_block(state_in, block_pair[0], block_pair[1], query_rows), None)

    state_out, unused = lax.scan(
        one_block,
        initial,
        (split_blocks(key_part, block_rows), split_blocks(value_part, block_rows)),
    )
    running_max, running_sum, running_acc = state_out
    attention_result = running_acc / running_sum[..., None]
    attention_result = jnp.transpose(attention_result, (0, 2, 1, 3)).reshape(
        seq_count, block_rows, HEADS * HEAD_DIM
    )
    log_total = running_max + jnp.log(running_sum)
    return (attention_result, log_total, kept)


def attend_back(query_rows, gradient_row_block, log_total, row_inner, key_rows, value_rows):
    score_scale = HEAD_DIM ** (-0.5)
    scores = block_scores(query_rows, key_rows)
    probabilities = jnp.exp(scores - log_total[..., None])
    value_grad = jnp.einsum(
        "shqk,sqhd->skhd",
        lowered(probabilities),
        split_heads(gradient_row_block),
        preferred_element_type=jnp.float32,
    )
    prob_grad = jnp.einsum(
        "sqhd,skhd->shqk",
        split_heads(gradient_row_block),
        split_heads(value_rows),
        preferred_element_type=jnp.float32,
    )
    score_grad = lowered(probabilities * (prob_grad - row_inner[..., None]))
    query_grad = (
        jnp.einsum(
            "shqk,skhd->sqhd", score_grad, split_heads(key_rows), preferred_element_type=jnp.float32
        )
        * score_scale
    )
    key_grad = (
        jnp.einsum(
            "shqk,sqhd->skhd",
            score_grad,
            split_heads(query_rows),
            preferred_element_type=jnp.float32,
        )
        * score_scale
    )
    return (merge_heads(query_grad), merge_heads(key_grad), merge_heads(value_grad))


def attend_backward(query_rows, gradient_row_block, log_total, row_inner, key_rows, value_rows):
    zero_rows = jnp.zeros(query_rows.shape, jnp.float32)
    turn_count = lax.axis_size("ctx") // 2

    def turn_keys(turn_index, carried):
        moving_key, moving_value, key_acc, value_acc, query_acc = carried
        for half_step in range(2):
            pieces = attend_back(
                query_rows, gradient_row_block, log_total, row_inner, moving_key, moving_value
            )
            query_acc = query_acc + pieces[0]
            key_acc = key_acc + pieces[1]
            value_acc = value_acc + pieces[2]
            moving_key, moving_value = from_behind((moving_key, moving_value), "ctx", 1)
            key_acc, value_acc = (
                from_behind(key_acc.astype(jnp.bfloat16), "ctx", 1).astype(key_acc.dtype),
                from_behind(value_acc.astype(jnp.bfloat16), "ctx", 1).astype(value_acc.dtype),
            )
        return (moving_key, moving_value, key_acc, value_acc, query_acc)

    finished = lax.fori_loop(
        0, turn_count, turn_keys, (key_rows, value_rows, zero_rows, zero_rows, zero_rows)
    )
    return (finished[4], finished[2], finished[3])


def ring_on_device(
    tokens,
    query_key_value_weight,
    bias_query,
    bias_value,
    attention_out_weight,
    attention_out_bias,
    gain_one,
    shift_one,
    feedforward_in_weight,
    feedforward_in_bias,
    feedforward_out_weight,
    feedforward_out_bias,
    gain_two,
    shift_two,
    d_out,
):
    attn_full = (
        lax.all_gather(query_key_value_weight, "fsdp", axis=0, tiled=True),
        lax.all_gather(attention_out_weight, "fsdp", axis=0, tiled=True),
        lax.all_gather(bias_query, "fsdp", axis=0, tiled=True),
        lax.all_gather(bias_value, "fsdp", axis=0, tiled=True),
        lax.all_gather(attention_out_bias, "fsdp", axis=0, tiled=True),
        lax.all_gather(gain_one, "fsdp", axis=0, tiled=True),
        lax.all_gather(shift_one, "fsdp", axis=0, tiled=True),
    )
    qkv_full, out_full, query_bias, value_bias, out_bias, gain_first, shift_first = attn_full
    model_width = out_full.shape[0]
    projected_rows = project(tokens, qkv_full) + jnp.concatenate(
        [widened(query_bias), jnp.zeros((model_width,), jnp.float32), widened(value_bias)]
    )
    projected_low = lowered(projected_rows)
    query_rows = projected_low[..., :model_width]
    key_rows = projected_low[..., model_width : 2 * model_width]
    value_rows = projected_low[..., 2 * model_width :]
    attention_result, log_total, kept = attend_forward(query_rows, key_rows, value_rows)
    attended_low = lowered(attention_result)
    attention_branch = project(attended_low, out_full) + widened(out_bias)
    summed_one = widened(tokens) + attention_branch
    first_normalized, pull_one = jax.vjp(
        norm_apply, summed_one, widened(gain_first), widened(shift_first)
    )
    normed_low = lowered(first_normalized)
    ffn_full = (
        lax.all_gather(feedforward_in_weight, "fsdp", axis=0, tiled=True),
        lax.all_gather(feedforward_out_weight, "fsdp", axis=0, tiled=True),
        lax.all_gather(feedforward_in_bias, "fsdp", axis=0, tiled=True),
        lax.all_gather(feedforward_out_bias, "fsdp", axis=0, tiled=True),
        lax.all_gather(gain_two, "fsdp", axis=0, tiled=True),
        lax.all_gather(shift_two, "fsdp", axis=0, tiled=True),
    )
    in_full, back_full, inner_bias, back_bias, gain_second, shift_second = ffn_full
    hidden_before_gelu = project(normed_low, in_full) + widened(inner_bias)
    active_low = lowered(jax.nn.gelu(hidden_before_gelu, approximate=False))
    feedforward_branch = project(active_low, back_full) + widened(back_bias)

    def second_norm(residual_in, branch_in, gain_vec, shift_vec):
        return norm_apply(residual_in + branch_in, gain_vec, shift_vec)

    result, pull_two = jax.vjp(
        second_norm,
        first_normalized,
        feedforward_branch,
        widened(gain_second),
        widened(shift_second),
    )
    output = lowered(result)
    first_grad_res, second_grad, gain_two_grad, shift_two_grad = pull_two(widened(d_out))
    in_full, back_full = (
        lax.all_gather(feedforward_in_weight, "fsdp", axis=0, tiled=True),
        lax.all_gather(feedforward_out_weight, "fsdp", axis=0, tiled=True),
    )
    second_low = lowered(second_grad)
    back_grad = weight_grad(active_low, second_low)
    back_bias_grad = column_sum(second_low)
    active_grad = back_project(second_low, back_full)
    gelu_pull = jax.vjp(partial(jax.nn.gelu, approximate=False), hidden_before_gelu)[1]
    hidden_low = lowered(gelu_pull(active_grad)[0])
    in_grad = weight_grad(normed_low, hidden_low)
    in_bias_grad = column_sum(hidden_low)
    first_grad = first_grad_res + back_project(hidden_low, in_full)
    ffn_grads = (
        lax.psum_scatter(
            in_grad.astype(jnp.bfloat16), "fsdp", scatter_dimension=0, tiled=True
        ).astype(jnp.float32),
        lax.psum_scatter(
            in_bias_grad.astype(jnp.bfloat16), "fsdp", scatter_dimension=0, tiled=True
        ).astype(jnp.float32),
        lax.psum_scatter(
            back_grad.astype(jnp.bfloat16), "fsdp", scatter_dimension=0, tiled=True
        ).astype(jnp.float32),
        lax.psum_scatter(
            back_bias_grad.astype(jnp.bfloat16), "fsdp", scatter_dimension=0, tiled=True
        ).astype(jnp.float32),
        lax.psum_scatter(
            gain_two_grad.astype(jnp.bfloat16), "fsdp", scatter_dimension=0, tiled=True
        ).astype(jnp.float32),
        lax.psum_scatter(
            shift_two_grad.astype(jnp.bfloat16), "fsdp", scatter_dimension=0, tiled=True
        ).astype(jnp.float32),
    )
    ffn_grads = lax.psum(
        (ffn_grads[0], ffn_grads[1], ffn_grads[2], ffn_grads[3], ffn_grads[4], ffn_grads[5]),
        ("dp", "ctx"),
    )
    summed_grad, gain_one_grad, shift_one_grad = pull_one(first_grad)
    qkv_full, out_full = (
        lax.all_gather(query_key_value_weight, "fsdp", axis=0, tiled=True),
        lax.all_gather(attention_out_weight, "fsdp", axis=0, tiled=True),
    )
    branch_low = lowered(summed_grad)
    out_grad = weight_grad(attended_low, branch_low)
    out_bias_grad = column_sum(branch_low)
    attended_grad_low = lowered(back_project(branch_low, out_full))
    row_inner = jnp.sum(
        split_heads(widened(attended_grad_low)) * split_heads(attention_result), axis=-1
    )
    row_inner = jnp.transpose(row_inner, (0, 2, 1))
    query_grad, key_grad, value_grad = attend_backward(
        query_rows, attended_grad_low, log_total, row_inner, key_rows, value_rows
    )
    mixed_grad = lowered(jnp.concatenate([query_grad, key_grad, value_grad], axis=-1))
    qkv_grad = weight_grad(tokens, mixed_grad)
    bias_grads = column_sum(mixed_grad)
    query_bias_grad = bias_grads[:model_width]
    value_bias_grad = bias_grads[2 * model_width :]
    token_grad = summed_grad + back_project(mixed_grad, qkv_full)
    attn_grads = (
        lax.psum_scatter(
            qkv_grad.astype(jnp.bfloat16), "fsdp", scatter_dimension=0, tiled=True
        ).astype(jnp.float32),
        lax.psum_scatter(
            query_bias_grad.astype(jnp.bfloat16), "fsdp", scatter_dimension=0, tiled=True
        ).astype(jnp.float32),
        lax.psum_scatter(
            value_bias_grad.astype(jnp.bfloat16), "fsdp", scatter_dimension=0, tiled=True
        ).astype(jnp.float32),
        lax.psum_scatter(
            out_grad.astype(jnp.bfloat16), "fsdp", scatter_dimension=0, tiled=True
        ).astype(jnp.float32),
        lax.psum_scatter(
            out_bias_grad.astype(jnp.bfloat16), "fsdp", scatter_dimension=0, tiled=True
        ).astype(jnp.float32),
        lax.psum_scatter(
            gain_one_grad.astype(jnp.bfloat16), "fsdp", scatter_dimension=0, tiled=True
        ).astype(jnp.float32),
        lax.psum_scatter(
            shift_one_grad.astype(jnp.bfloat16), "fsdp", scatter_dimension=0, tiled=True
        ).astype(jnp.float32),
    )
    attn_grads = lax.psum(
        (
            attn_grads[0],
            attn_grads[1],
            attn_grads[2],
            attn_grads[3],
            attn_grads[4],
            attn_grads[5],
            attn_grads[6],
        ),
        ("dp", "ctx"),
    )
    return (
        output,
        token_grad,
        attn_grads[0],
        attn_grads[1],
        attn_grads[2],
        attn_grads[3],
        attn_grads[4],
        attn_grads[5],
        attn_grads[6],
        ffn_grads[0],
        ffn_grads[1],
        ffn_grads[2],
        ffn_grads[3],
        ffn_grads[4],
        ffn_grads[5],
    )


def exchange(values, axis, bit):
    count = lax.axis_size(axis)
    return lax.ppermute(values, axis, [(i, i ^ bit) for i in range(count)])


def bits_below(count):
    return [1 << k for k in range(count.bit_length() - 1)]


def reorder(pieces, index):
    for bit in bits_below(len(pieces)):
        taken = (index & bit) != 0
        pieces = [jnp.where(taken, pieces[k ^ bit], pieces[k]) for k in range(len(pieces))]
    return pieces


def pair_join(own, other, core, axis=0):
    first = jnp.where(core == 0, own, other)
    second = jnp.where(core == 0, other, own)
    return jnp.concatenate([first, second], axis=axis)


def half_of(values, which, axis):
    size = values.shape[axis] // 2
    low = lax.slice_in_dim(values, 0, size, axis=axis)
    high = lax.slice_in_dim(values, size, 2 * size, axis=axis)
    return jnp.where(which == 0, low, high)


def gather_blocks(block):
    line = Line()
    pieces = {k: exchange(block, "ctx", k) for k in (4, 2, 1)}
    held = Held(pieces[2])
    line.done(held)
    pieces[3] = exchange(held.value, "ctx", 1)
    far = Held(line.after(pieces[4]))
    line.done(far)
    pieces[6] = exchange(far.value, "ctx", 2)
    pieces[5] = exchange(far.value, "ctx", 1)
    last = line.after(pieces[6])
    pieces[7] = exchange(last, "ctx", 1)
    return [block, pieces[1], held.value, pieces[3], far.value, pieces[5], last, pieces[7]]


def swap_blocks(pieces):
    return [pieces[0]] + [exchange(pieces[k], "ctx", k) for k in range(1, len(pieces))]


def head_mask(value):
    lane = lax.broadcasted_iota(jnp.int32, (1, 2 * HEAD_DIM), 1)
    return [
        jnp.where(lane < HEAD_DIM, value, 0.0),
        jnp.where(lane < HEAD_DIM, 0.0, value),
    ]


def contract(left, right, left_dim, right_dim):
    return lax.dot_general(
        left, right, (((left_dim,), (right_dim,)), ((), ())), preferred_element_type=jnp.float32
    )


def forward_kernel(query_ref, key_ref, value_ref, result_ref, low_ref, log_ref):
    query = query_ref[0].astype(jnp.float32)
    keys = key_ref[0]
    values = value_ref[0]
    results = []
    logs = []
    for mask in head_mask(HEAD_DIM ** (-0.5)):
        scores = contract((query * mask).astype(jnp.bfloat16), keys, 1, 1)
        row_max = jnp.max(scores, axis=-1, keepdims=True)
        weights = jnp.exp(scores - row_max)
        total = jnp.sum(weights, axis=-1, keepdims=True)
        probabilities = (weights * (1.0 / total)).astype(jnp.bfloat16)
        results.append(contract(probabilities, values, 1, 0))
        logs.append(row_max + jnp.log(total))
    first = lax.broadcasted_iota(jnp.int32, results[0].shape, 1) < HEAD_DIM
    result = jnp.where(first, results[0], results[1])
    result_ref[0] = result
    low_ref[0] = result.astype(jnp.bfloat16)
    log_ref[0] = jnp.where(first, logs[0], logs[1])


def attention_forward(projected):
    seqs, length, width = projected.shape
    pair = width // 3
    rows = min(256, length)
    row_spec = pl.BlockSpec((1, rows, pair), lambda s, q: (s, q, 0))
    return pl.pallas_call(
        forward_kernel,
        grid=(seqs, length // rows),
        in_specs=[
            row_spec,
            pl.BlockSpec((1, length, pair), lambda s, q: (s, 0, 1)),
            pl.BlockSpec((1, length, pair), lambda s, q: (s, 0, 2)),
        ],
        out_specs=[row_spec, row_spec, row_spec],
        out_shape=[
            jax.ShapeDtypeStruct((seqs, length, pair), jnp.float32),
            jax.ShapeDtypeStruct((seqs, length, pair), jnp.bfloat16),
            jax.ShapeDtypeStruct((seqs, length, pair), jnp.float32),
        ],
        compiler_params=pltpu.CompilerParams(vmem_limit_bytes=48 << 20),
        name="attention_forward",
    )(projected, projected, projected)


def backward_kernel(
    query_ref, key_ref, value_ref, grad_ref, result_ref, log_ref,
    query_out, key_out, value_out, query_acc, log_rows, inner_rows,
):
    step = pl.program_id(1)

    @pl.when(step == 0)
    def first_step():
        query_acc[...] = jnp.zeros_like(query_acc)
        logs = jnp.transpose(log_ref[0])
        inner = jnp.transpose(grad_ref[0].astype(jnp.float32) * result_ref[0])
        for h in range(2):
            log_rows[h] = jnp.broadcast_to(
                logs[h * HEAD_DIM : h * HEAD_DIM + 1], log_rows.shape[1:]
            )
            inner_rows[h] = jnp.broadcast_to(
                jnp.sum(inner[h * HEAD_DIM : (h + 1) * HEAD_DIM], axis=0, keepdims=True),
                inner_rows.shape[1:],
            )

    queries = query_ref[0]
    grads = grad_ref[0]
    keys = key_ref[0]
    values = value_ref[0]
    scale = HEAD_DIM ** (-0.5)
    query_parts = []
    key_parts = []
    value_parts = []
    scaled_masks = head_mask(scale)
    masks = head_mask(1.0)
    for h in range(2):
        scores = contract(
            (keys.astype(jnp.float32) * scaled_masks[h]).astype(jnp.bfloat16), queries, 1, 1
        )
        probabilities = jnp.exp(scores - log_rows[h, :1])
        prob_grad = contract(
            (values.astype(jnp.float32) * masks[h]).astype(jnp.bfloat16), grads, 1, 1
        )
        score_grad = (probabilities * (prob_grad - inner_rows[h, :1])).astype(jnp.bfloat16)
        value_parts.append(contract(probabilities.astype(jnp.bfloat16), grads, 1, 0))
        key_parts.append(contract(score_grad, queries, 1, 0))
        query_parts.append(contract(score_grad, keys, 0, 0))
    first = lax.broadcasted_iota(jnp.int32, key_parts[0].shape, 1) < HEAD_DIM
    value_out[0] = jnp.where(first, value_parts[0], value_parts[1]).astype(jnp.bfloat16)
    key_out[0] = (jnp.where(first, key_parts[0], key_parts[1]) * scale).astype(jnp.bfloat16)
    first = lax.broadcasted_iota(jnp.int32, query_parts[0].shape, 1) < HEAD_DIM
    query_acc[...] += jnp.where(first, query_parts[0], query_parts[1])

    @pl.when(step == pl.num_programs(1) - 1)
    def last_step():
        query_out[0] = (query_acc[...] * scale).astype(jnp.bfloat16)


def attention_backward(projected, grads, result, logs):
    seqs, length, width = projected.shape
    pair = width // 3
    rows = min(256, length)
    whole = pl.BlockSpec((1, length, pair), lambda s, k: (s, 0, 0))
    block = pl.BlockSpec((1, rows, pair), lambda s, k: (s, k, 0))
    shape = jax.ShapeDtypeStruct((seqs, length, pair), jnp.bfloat16)
    return pl.pallas_call(
        backward_kernel,
        grid=(seqs, length // rows),
        in_specs=[
            whole,
            pl.BlockSpec((1, rows, pair), lambda s, k: (s, k, 1)),
            pl.BlockSpec((1, rows, pair), lambda s, k: (s, k, 2)),
            whole,
            whole,
            whole,
        ],
        out_specs=[whole, block, block],
        out_shape=[shape, shape, shape],
        scratch_shapes=[
            pltpu.VMEM((length, pair), jnp.float32),
            pltpu.VMEM((2, 8, length), jnp.float32),
            pltpu.VMEM((2, 8, length), jnp.float32),
        ],
        compiler_params=pltpu.CompilerParams(vmem_limit_bytes=48 << 20),
        name="attention_backward",
    )(projected, projected, projected, grads, result, logs)


def ffn_forward_kernel(
    core_ref, left_own, left_other, in_own, in_other, bias_ref, back_own, back_other,
    active_ref, slope_ref, second_ref,
):
    step = pl.program_id(0)
    hidden = contract(left_own[...], in_own[...], 1, 0)
    hidden = hidden + contract(left_other[...], in_other[...], 1, 0) + bias_ref[...]
    below = 0.5 * (1.0 + lax.erf(hidden * 0.7071067811865476))
    slope = below + hidden * (jnp.exp(-0.5 * hidden * hidden) * 0.3989422804014327)
    active = (hidden * below).astype(jnp.bfloat16)
    active_ref[...] = active
    slope_ref[...] = slope.astype(jnp.bfloat16)

    @pl.when(step == 0)
    def first():
        second_ref[...] = contract(active, back_own[...], 1, 0)

    @pl.when((step > 0) & (step < pl.num_programs(0) // 2))
    def own():
        second_ref[...] += contract(active, back_own[...], 1, 0)

    @pl.when(step >= pl.num_programs(0) // 2)
    def other():
        second_ref[...] += contract(active, back_other[...], 1, 0)


def ffn_specs(half, block, width, hidden):
    near = hidden // (2 * block)

    def spot(s, p):
        return jnp.where(s < near, s + p[0] * near, s - p[0] * near)

    weights = [
        pl.BlockSpec((half, block), lambda s, p: (0, spot(s, p))),
        pl.BlockSpec((half, block), lambda s, p: (0, spot(s, p))),
        pl.BlockSpec((block, width), lambda s, p: (jnp.minimum(s, near - 1), 0)),
        pl.BlockSpec((block, width), lambda s, p: (jnp.maximum(s - near, 0), 0)),
    ]
    return spot, weights


def ffn_forward(core, left, in_pair, back_pair, bias):
    tokens, width = left.shape
    half, hidden = in_pair[0].shape
    block = 512
    spot, weights = ffn_specs(half, block, width, hidden)
    wide = pl.BlockSpec((tokens, block), lambda s, p: (0, spot(s, p)))
    return pl.pallas_call(
        ffn_forward_kernel,
        grid_spec=pltpu.PrefetchScalarGridSpec(
            num_scalar_prefetch=1,
            grid=(hidden // block,),
            in_specs=[
                pl.BlockSpec((tokens, half), lambda s, p: (0, p[0])),
                pl.BlockSpec((tokens, half), lambda s, p: (0, 1 - p[0])),
                weights[0],
                weights[1],
                pl.BlockSpec((1, block), lambda s, p: (0, spot(s, p))),
                weights[2],
                weights[3],
            ],
            out_specs=[wide, wide, pl.BlockSpec((tokens, width), lambda s, p: (0, 0))],
        ),
        out_shape=[
            jax.ShapeDtypeStruct((tokens, hidden), jnp.bfloat16),
            jax.ShapeDtypeStruct((tokens, hidden), jnp.bfloat16),
            jax.ShapeDtypeStruct((tokens, width), jnp.float32),
        ],
        compiler_params=pltpu.CompilerParams(vmem_limit_bytes=40 << 20),
        name="ffn_forward",
    )(core, left, left, *in_pair, bias, *back_pair)


def ffn_backward_kernel(
    core_ref, grad_ref, slope_ref, in_own, in_other, back_own, back_other,
    hidden_ref, total_ref, own_acc, other_acc,
):
    step = pl.program_id(0)
    half = own_acc.shape[1]

    def rest(back_ref):
        active_grad = contract(grad_ref[...], back_ref[...], 1, 1)
        hidden = (active_grad * slope_ref[...].astype(jnp.float32)).astype(jnp.bfloat16)
        hidden_ref[...] = hidden
        own = contract(hidden, in_own[...], 1, 1)
        other = contract(hidden, in_other[...], 1, 1)

        @pl.when(step == 0)
        def first():
            own_acc[...] = own
            other_acc[...] = other

        @pl.when(step > 0)
        def later():
            own_acc[...] += own
            other_acc[...] += other

    @pl.when(step < pl.num_programs(0) // 2)
    def with_own():
        rest(back_own)

    @pl.when(step >= pl.num_programs(0) // 2)
    def with_other():
        rest(back_other)

    @pl.when(step == pl.num_programs(0) - 1)
    def last():
        @pl.when(core_ref[0] == 0)
        def straight():
            total_ref[:, :half] = own_acc[...]
            total_ref[:, half:] = other_acc[...]

        @pl.when(core_ref[0] != 0)
        def crossed():
            total_ref[:, :half] = other_acc[...]
            total_ref[:, half:] = own_acc[...]


def ffn_backward(core, grad, slope, in_pair, back_pair):
    tokens, width = grad.shape
    half, hidden = in_pair[0].shape
    block = 512
    spot, weights = ffn_specs(half, block, width, hidden)
    wide = pl.BlockSpec((tokens, block), lambda s, p: (0, spot(s, p)))
    whole = pl.BlockSpec((tokens, width), lambda s, p: (0, 0))
    return pl.pallas_call(
        ffn_backward_kernel,
        grid_spec=pltpu.PrefetchScalarGridSpec(
            num_scalar_prefetch=1,
            grid=(hidden // block,),
            in_specs=[whole, wide, *weights],
            out_specs=[wide, whole],
            scratch_shapes=[
                pltpu.VMEM((tokens, half), jnp.float32),
                pltpu.VMEM((tokens, half), jnp.float32),
            ],
        ),
        out_shape=[
            jax.ShapeDtypeStruct((tokens, hidden), jnp.bfloat16),
            jax.ShapeDtypeStruct((tokens, width), jnp.float32),
        ],
        compiler_params=pltpu.CompilerParams(vmem_limit_bytes=40 << 20),
        name="ffn_backward",
    )(core, grad, slope, *in_pair, *back_pair)


def qkv_grad_kernel(core_ref, *refs, pieces):
    token_refs, grad_refs = refs[:pieces], refs[pieces : pieces + 3]
    own_ref, other_ref = refs[pieces + 3 :]
    seqs = token_refs[0].shape[0]
    rows = jnp.concatenate([ref[s] for s in range(seqs) for ref in token_refs], axis=0)
    parts = []
    for ref in grad_refs:
        grads = jnp.concatenate([ref[s] for s in range(seqs)], axis=0)
        parts.append(contract(rows, grads, 0, 0))
    half = pl.num_programs(0) // 2

    @pl.when(pl.program_id(0) < half)
    def outgoing():
        for t in range(3):
            other_ref[t] = parts[t].astype(jnp.bfloat16)

    @pl.when(pl.program_id(0) >= half)
    def kept():
        for t in range(3):
            own_ref[t] = parts[t]


def qkv_grad_parts(core, token_pieces, head_grads):
    seqs, rows, width = token_pieces[0].shape
    pair = head_grads[0].shape[2]
    cols = 256
    steps = width // cols
    half = steps // 2

    def spot(s, p):
        return jnp.where(s < half, s + (1 - p[0]) * half, s - half + p[0] * half)

    grads = pl.BlockSpec(head_grads[0].shape, lambda s, p: (0, 0, 0))
    return pl.pallas_call(
        partial(qkv_grad_kernel, pieces=len(token_pieces)),
        grid_spec=pltpu.PrefetchScalarGridSpec(
            num_scalar_prefetch=1,
            grid=(steps,),
            in_specs=[pl.BlockSpec((seqs, rows, cols), lambda s, p: (0, 0, spot(s, p)))]
            * len(token_pieces)
            + [grads] * 3,
            out_specs=[
                pl.BlockSpec((3, cols, pair), lambda s, p: (0, jnp.maximum(s - half, 0), 0)),
                pl.BlockSpec((3, cols, pair), lambda s, p: (0, jnp.minimum(s, half - 1), 0)),
            ],
        ),
        out_shape=[
            jax.ShapeDtypeStruct((3, width // 2, pair), jnp.float32),
            jax.ShapeDtypeStruct((3, width // 2, pair), jnp.bfloat16),
        ],
        compiler_params=pltpu.CompilerParams(vmem_limit_bytes=40 << 20),
        name="grad_qkv",
    )(core, *token_pieces, *head_grads)


LOW = 2


def grad_kernel(place_ref, left_own, left_other, right_own, right_other, keep_ref, send_ref, *, by_rows):
    step = pl.program_id(0)
    half = pl.num_programs(0) // 2
    total = contract(left_own[...], right_own[...], 0, 0)
    total = total + contract(left_other[...], right_other[...], 0, 0)
    total = total.astype(jnp.bfloat16)
    low = place_ref[0] & ((1 << LOW) - 1)
    _, rows, cols = keep_ref.shape

    def put(out_ref):
        for j in range(1 << LOW):
            if by_rows:
                out_ref[j ^ low] = total[j * rows : (j + 1) * rows]
            else:
                out_ref[j ^ low] = total[:, j * cols : (j + 1) * cols]

    @pl.when(step < half)
    def outgoing():
        put(send_ref)

    @pl.when(step >= half)
    def kept():
        put(keep_ref)


def pair_grad(place, left_pair, right_pair, count, part, parts, by_rows, name):
    tokens, width = left_pair[0].shape
    columns = right_pair[0].shape[1]
    steps = count >> LOW
    half = steps // 2

    def block(step, place_ref):
        return part * steps + (((step + half) % steps) ^ (place_ref[0] >> LOW))

    if by_rows:
        rows, cols = width // (parts * count), columns
        left = pl.BlockSpec((tokens, rows << LOW), lambda s, p: (0, block(s, p)))
        right = pl.BlockSpec((tokens, columns), lambda s, p: (0, 0))
    else:
        rows, cols = width, columns // (parts * count)
        left = pl.BlockSpec((tokens, width), lambda s, p: (0, 0))
        right = pl.BlockSpec((tokens, cols << LOW), lambda s, p: (0, block(s, p)))
    shape = jax.ShapeDtypeStruct((count // 2, rows, cols), jnp.bfloat16)
    out_block = (1 << LOW, rows, cols)
    return pl.pallas_call(
        partial(grad_kernel, by_rows=by_rows),
        grid_spec=pltpu.PrefetchScalarGridSpec(
            num_scalar_prefetch=1,
            grid=(steps,),
            in_specs=[left, left, right, right],
            out_specs=[
                pl.BlockSpec(out_block, lambda s, p: (jnp.maximum(s - half, 0), 0, 0)),
                pl.BlockSpec(out_block, lambda s, p: (jnp.minimum(s, half - 1), 0, 0)),
            ],
        ),
        out_shape=[shape, shape],
        compiler_params=pltpu.CompilerParams(vmem_limit_bytes=48 << 20),
        name=name,
    )(place, left_pair[0], left_pair[1], right_pair[0], right_pair[1])


def place_of(order):
    place = jnp.int32(0)
    for axis, bit in order:
        place = place * 2 + jnp.where((lax.axis_index(axis) & bit) != 0, 1, 0)
    return place.astype(jnp.int32).reshape(1)


def added(first, second):
    return lowered(widened(first) + widened(second))


LINKS = {"x": ("dp", 1), "y": ("ctx", 1), "p": ("ctx", 2), "r": ("ctx", 4)}
ORDERS = {"b0": "pyrx", "b1": "yprx", "i0": "xypr", "i1": "yxpr", "o": "rxpy", "q": "xypr", "v": "xypr", "T": "ypr"}
EVENTS = (
    "b", "A", "i", "q", "o", "b", "i", "q", "v", "o", "v", "b", "i", "v", "o", "q",
    "b", "o", "v", "i", "T", "o", "q", "b", "v", "o", "i", "T", "o", "b", "i", "q",
    "T", "i", "o", "b", "q", "T", "i", "b",
)


def hops(name):
    return [LINKS[letter] for letter in ORDERS[name]]


class Line:
    def __init__(self):
        self.last = None

    def after(self, values):
        if self.last is None:
            return values
        values, self.last.value = lax.optimization_barrier((values, self.last.value))
        return values

    def done(self, holder):
        self.last = holder


class Held:
    def __init__(self, value):
        self.value = value


class Reduction:
    def __init__(self, line, name, keep, send, put):
        self.line, self.order, self.put = line, hops(name), put
        self.value, self.step = keep, 0
        self.arrived = exchange(send, *self.order[0])

    def advance(self):
        last = len(self.order) - 1
        step = self.step
        self.step += 1
        arrived, value = self.line.after((self.arrived, self.value))
        if step < last:
            half = value.shape[0] // 2
            send = added(value[half:], arrived[half:])
            self.value = added(value[:half], arrived[:half])
            self.arrived = exchange(send, *self.order[step + 1])
        elif step == last:
            self.value = added(value, arrived)
            self.arrived = exchange(self.value, *self.order[last])
        elif step <= 2 * last:
            self.value = jnp.concatenate([value, arrived], axis=0)
            self.arrived = exchange(self.value, *self.order[2 * last - step])
            if step == 2 * last:
                self.put(self.value, False)
        else:
            self.value = self.put(arrived, True)
        self.line.done(self)


class Group:
    def __init__(self, line, names, parts, put):
        self.line, self.put, self.step = line, put, 1
        self.orders = [hops(name) for name in names]
        self.value = [keep for keep, send in parts]
        self.arrived = [exchange(send, *o[0]) for (keep, send), o in zip(parts, self.orders)]

    def advance(self):
        arrived, value = self.line.after((self.arrived, self.value))
        tail = self.orders[0][2:]
        step = self.step
        self.step += 1
        if step == 1:
            self.arrived = [
                exchange(added(v[v.shape[0] // 2 :], a[v.shape[0] // 2 :]), *o[1])
                for v, a, o in zip(value, arrived, self.orders)
            ]
            self.value = [
                added(v[: v.shape[0] // 2], a[: v.shape[0] // 2]) for v, a in zip(value, arrived)
            ]
        elif step == 2:
            total = jnp.stack([added(v, a) for v, a in zip(value, arrived)], axis=1)
            self.value = total[:2]
            self.arrived = exchange(total[2:], *tail[0])
        elif step == 3:
            self.value = added(value[:1], arrived[:1])
            self.arrived = exchange(added(value[1:], arrived[1:]), *tail[1])
        elif step == 4:
            self.value = added(value, arrived)
            self.arrived = exchange(self.value, *tail[1])
        elif step == 5:
            self.value = jnp.concatenate([value, arrived], axis=0)
            self.arrived = exchange(self.value, *tail[0])
        elif step == 6:
            total = jnp.concatenate([value, arrived], axis=0)
            self.value = [total[:, 0], total[:, 1]]
            self.arrived = [exchange(v, *o[1]) for v, o in zip(self.value, self.orders)]
        elif step == 7:
            self.value = [jnp.concatenate([v, a], axis=0) for v, a in zip(value, arrived)]
            self.arrived = [exchange(v, *o[0]) for v, o in zip(self.value, self.orders)]
            for part, chunks in enumerate(self.value):
                self.put(chunks, part, False)
        else:
            for part, chunks in enumerate(arrived):
                self.value = self.put(chunks, part, True)
        self.line.done(self)


def place_kernel(place_ref, chunks_ref, *rest, by_rows):
    out_ref = rest[-1]
    low = place_ref[0] & ((1 << LOW) - 1)
    _, rows, cols = chunks_ref.shape
    for j in range(1 << LOW):
        values = chunks_ref[j ^ low].astype(jnp.float32)
        if by_rows:
            out_ref[j * rows : (j + 1) * rows, :] = values
        else:
            out_ref[:, j * cols : (j + 1) * cols] = values


def put_in_place(place, chunks, far, into, part, parts, by_rows, name):
    half, rows, cols = chunks.shape
    steps = half >> LOW
    first = steps if far else 0

    def block(step, place_ref):
        return part * 2 * steps + ((step + first) ^ (place_ref[0] >> LOW))

    if by_rows:
        out_shape = (rows * 2 * half * parts, cols)
        out_spec = pl.BlockSpec((rows << LOW, cols), lambda s, p: (block(s, p), 0))
    else:
        out_shape = (rows, cols * 2 * half * parts)
        out_spec = pl.BlockSpec((rows, cols << LOW), lambda s, p: (0, block(s, p)))
    in_specs = [pl.BlockSpec((1 << LOW, rows, cols), lambda s, p: (s, 0, 0))]
    operands = [place, chunks]
    if into is not None:
        in_specs.append(pl.BlockSpec(memory_space=pl.ANY))
        operands.append(into)
    return pl.pallas_call(
        partial(place_kernel, by_rows=by_rows),
        grid_spec=pltpu.PrefetchScalarGridSpec(
            num_scalar_prefetch=1, grid=(steps,), in_specs=in_specs, out_specs=out_spec
        ),
        out_shape=jax.ShapeDtypeStruct(out_shape, jnp.float32),
        input_output_aliases={} if into is None else {2: 0},
        compiler_params=pltpu.CompilerParams(vmem_limit_bytes=48 << 20),
        name=name,
    )(*operands)


def place_three_kernel(place_ref, chunks_ref, *rest, bits):
    out_ref = rest[-1]
    count, _, _, cols = chunks_ref.shape
    low = place_ref[0] & (count - 1)
    for j in range(count):
        spot = sum(((j // bit) & 1) << (len(bits) - 1 - k) for k, bit in enumerate(bits))
        out_ref[:, j * cols : (j + 1) * cols] = chunks_ref[spot ^ low, 0].astype(jnp.float32)


def put_three_in_place(place, chunks, far, into, bits, dp_count, name):
    total, three, rows, cols = chunks.shape
    ctx_count = 1 << len(bits)
    steps = total // ctx_count
    first = steps if far else 0
    in_specs = [pl.BlockSpec((ctx_count, 1, rows, cols), lambda s, t, p: (s, t, 0, 0))]
    operands = [place, chunks]
    if into is not None:
        in_specs.append(pl.BlockSpec(memory_space=pl.ANY))
        operands.append(into)
    return pl.pallas_call(
        partial(place_three_kernel, bits=bits),
        grid_spec=pltpu.PrefetchScalarGridSpec(
            num_scalar_prefetch=1,
            grid=(steps, three),
            in_specs=in_specs,
            out_specs=pl.BlockSpec(
                (rows, ctx_count * cols),
                lambda s, t, p: ((s + first) ^ (p[0] >> len(bits)), t),
            ),
        ),
        out_shape=jax.ShapeDtypeStruct((rows * dp_count, three * ctx_count * cols), jnp.float32),
        input_output_aliases={} if into is None else {2: 0},
        compiler_params=pltpu.CompilerParams(vmem_limit_bytes=48 << 20),
        name=name,
    )(*operands)


def on_device(
    tokens,
    query_key_value_weight,
    bias_query,
    bias_value,
    attention_out_weight,
    attention_out_bias,
    gain_one,
    shift_one,
    feedforward_in_weight,
    feedforward_in_bias,
    feedforward_out_weight,
    feedforward_out_bias,
    gain_two,
    shift_two,
    d_out,
):
    core = lax.axis_index("fsdp")
    ctx = lax.axis_index("ctx")
    ctx_count = lax.axis_size("ctx")
    seqs, block_rows, width = tokens.shape
    pair = width // ctx_count
    flat = seqs * block_rows

    token_pieces = gather_blocks(tokens)

    small = (
        bias_query, bias_value, attention_out_bias, gain_one, shift_one,
        feedforward_in_bias, feedforward_out_bias, gain_two, shift_two,
    )
    small, token_pieces[1] = lax.optimization_barrier((small, token_pieces[1]))
    packed = jnp.concatenate(small)
    packed_other = exchange(packed, "fsdp", 1)
    vectors = []
    offset = 0
    for part in small:
        size = part.shape[0]
        vectors.append(widened(pair_join(part, packed_other[offset : offset + size], core)))
        offset += size
    (
        query_bias, value_bias, out_bias, gain_first, shift_first,
        inner_bias, back_bias, gain_second, shift_second,
    ) = vectors
    qkv_full = pair_join(
        query_key_value_weight, exchange(query_key_value_weight, "fsdp", 1), core
    )
    out_full = pair_join(attention_out_weight, exchange(attention_out_weight, "fsdp", 1), core)
    in_pair = (feedforward_in_weight, exchange(feedforward_in_weight, "fsdp", 1))
    back_pair = (feedforward_out_weight, exchange(feedforward_out_weight, "fsdp", 1))
    core_index = core.astype(jnp.int32).reshape(1)

    head_weight = jnp.concatenate(
        [lax.dynamic_slice_in_dim(qkv_full, t * width + ctx * pair, pair, axis=1) for t in range(3)],
        axis=1,
    )
    head_bias = jnp.concatenate(
        [
            lax.dynamic_slice_in_dim(query_bias, ctx * pair, pair),
            jnp.zeros((pair,), jnp.float32),
            lax.dynamic_slice_in_dim(value_bias, ctx * pair, pair),
        ]
    )
    projected = jnp.concatenate(
        [lowered(project(piece, head_weight) + head_bias) for piece in token_pieces], axis=1
    )
    head_result, head_low, head_logs = attention_forward(projected)

    def row_blocks(values):
        return [
            lax.slice_in_dim(values, k * block_rows, (k + 1) * block_rows, axis=1)
            for k in range(ctx_count)
        ]

    attended_pieces = reorder(swap_blocks(row_blocks(head_low)), ctx)
    attended_low = jnp.concatenate(attended_pieces, axis=-1)
    attention_branch = project(attended_low, out_full) + out_bias
    summed_one = widened(tokens) + attention_branch
    first_normalized, pull_one = jax.vjp(norm_apply, summed_one, gain_first, shift_first)
    normed_low = lowered(first_normalized)
    active_flat, slope, second = ffn_forward(
        core_index, normed_low.reshape(flat, width), in_pair, back_pair, inner_bias[None]
    )
    active_low = active_flat.reshape(seqs, block_rows, -1)
    feedforward_branch = second.reshape(tokens.shape) + back_bias

    def second_norm(residual_in, branch_in, gain_vec, shift_vec):
        return norm_apply(residual_in + branch_in, gain_vec, shift_vec)

    result, pull_two = jax.vjp(
        second_norm, first_normalized, feedforward_branch, gain_second, shift_second
    )
    output = lowered(result)
    first_grad_res, second_grad, gain_two_grad, shift_two_grad = pull_two(widened(d_out))
    second_low = lowered(second_grad)

    def left_pair(values):
        rows = values.reshape(flat, values.shape[2])
        return (half_of(rows, core, 1), exchange(half_of(rows, 1 - core, 1), "fsdp", 1))

    def right_pair(values):
        rows = values.reshape(flat, values.shape[2])
        return (rows, exchange(rows, "fsdp", 1))

    places = {name: place_of(hops(name)) for name in ORDERS}
    count = 1 << len(hops("q"))

    active_pair = left_pair(active_low)
    normed_pair = left_pair(normed_low)
    attended_pair = left_pair(attended_low)
    second_pair = right_pair(second_low)
    back_parts = [
        pair_grad(places[n], active_pair, second_pair, count, part, 2, True, "grad_back")
        for part, n in enumerate(("b0", "b1"))
    ]
    back_bias_grad = column_sum(second_low)
    hidden_flat, first_part = ffn_backward(
        core_index, second_low.reshape(flat, width), slope, in_pair, back_pair
    )
    hidden_low = hidden_flat.reshape(seqs, block_rows, -1)
    hidden_low, back_parts = lax.optimization_barrier((hidden_low, back_parts))
    hidden_pair = right_pair(hidden_low)
    in_bias_grad = column_sum(hidden_low)
    first_grad = first_grad_res + first_part.reshape(tokens.shape)
    summed_grad, gain_one_grad, shift_one_grad = pull_one(first_grad)
    branch_low = lowered(summed_grad)
    branch_pair = right_pair(branch_low)
    out_bias_grad = column_sum(branch_low)
    attended_grad = lowered(back_project(branch_low, out_full))
    column_pieces = reorder(
        [attended_grad[..., k * pair : (k + 1) * pair] for k in range(ctx_count)], ctx
    )
    column_pieces, hidden_pair = lax.optimization_barrier((column_pieces, hidden_pair))
    head_grad_pieces = swap_blocks(column_pieces)
    in_parts = [
        pair_grad(places[n], normed_pair, hidden_pair, count, part, 2, False, "grad_in")
        for part, n in enumerate(("i0", "i1"))
    ]
    branch_pair, in_parts = lax.optimization_barrier((branch_pair, in_parts))
    out_parts = pair_grad(
        places["o"], attended_pair, branch_pair, count, 0, 1, True, "grad_out"
    )

    whole = {"back": None, "in": None, "out": None, "qkv": None}

    def placer(target, names, by_rows):
        def put(chunks, part, far):
            whole[target] = put_in_place(
                places[names[part]], chunks, far, whole[target], part, len(names), by_rows,
                "place_" + target,
            )
            return whole[target]

        return put

    put_out = placer("out", ("o",), True)

    class Placed:
        def __init__(self, target):
            self.target = target

        @property
        def value(self):
            return whole[self.target]

        @value.setter
        def value(self, new):
            whole[self.target] = new

    line = Line()
    chains = {
        "b": Group(line, ("b0", "b1"), back_parts, placer("back", ("b0", "b1"), True)),
        "i": Group(line, ("i0", "i1"), in_parts, placer("in", ("i0", "i1"), False)),
        "o": Reduction(line, "o", *out_parts, lambda chunks, far: put_out(chunks, 0, far)),
    }
    targets = {"b": ("back", 9), "i": ("in", 9), "o": ("out", 8)}
    line.done(chains["o"])

    class Attention:
        def advance(self):
            head_grad = jnp.concatenate(line.after(head_grad_pieces), axis=1)
            self.head_grads = attention_backward(projected, head_grad, head_result, head_logs)
            self.value, other = qkv_grad_parts(core_index, token_pieces, self.head_grads)
            self.other = exchange(other, "fsdp", 1)
            chains["v"].begin(self.head_grads)
            line.done(self)

    layer_vectors = (
        in_bias_grad, back_bias_grad, gain_two_grad, shift_two_grad,
        out_bias_grad, gain_one_grad, shift_one_grad,
    )

    class Vectors:
        def begin(self, head_grads):
            spread_out = []
            for part in (head_grads[0], head_grads[2]):
                spread_out.append(
                    lax.dynamic_update_slice_in_dim(
                        jnp.zeros((width,), jnp.float32), column_sum(part), ctx * pair, 0
                    )
                )
            self.value = jnp.concatenate(layer_vectors + tuple(spread_out))
            self.routes = [("fsdp", 1)] + hops("v")
            self.step = 0
            self.arrived = exchange(self.value, *self.routes[0])

        def advance(self):
            arrived, value = line.after((self.arrived, self.value))
            self.value = value + arrived
            self.step += 1
            if self.step < len(self.routes):
                self.arrived = exchange(self.value, *self.routes[self.step])
            line.done(self)

    class QueryKeyValue:
        def __init__(self):
            self.step = 0

        def advance(self):
            step = self.step
            self.step += 1
            order = hops("q")
            if step == 0:
                other, own = line.after((chains["A"].other, chains["A"].value))
                total = own + widened(other)
                half = total.shape[1] // 2
                low, high = total[:, :half], total[:, half:]
                first = lax.axis_index("dp") == 0
                self.value = jnp.where(first, low, high)
                self.arrived = exchange(lowered(jnp.where(first, high, low)), *order[0])
            elif step == 1:
                arrived, value = line.after((self.arrived, self.value))
                self.value = lowered(value + widened(arrived))[None]
                self.arrived = exchange(self.value, *order[-1])
            elif step <= len(order):
                arrived, value = line.after((self.arrived, self.value))
                self.value = jnp.concatenate([value, arrived], axis=0)
                self.arrived = exchange(self.value, *order[len(order) - step])
                if step == len(order):
                    self.put(self.value, False)
            else:
                arrived, value = line.after((self.arrived, self.value))
                self.value = self.put(arrived, True)
                line.done(Placed("qkv"))
                return
            line.done(self)

        def put(self, chunks, far):
            bits = [bit for axis, bit in hops("q")[1:]]
            whole["qkv"] = put_three_in_place(
                places["q"], chunks, far, whole["qkv"], bits, 2, "place_qkv"
            )
            return whole["qkv"]

    class Tokens:
        def __init__(self):
            self.step = 0

        def advance(self):
            order = hops("T")
            if self.step == 0:
                blocks = [row_blocks(part) for part in chains["A"].head_grads]
                pieces = line.after(
                    [jnp.concatenate([m[k] for m in blocks], axis=-1) for k in range(ctx_count)]
                )
                held = {(0, k): piece for k, piece in enumerate(pieces)}
            else:
                bit = order[self.step - 1][1]
                arrived, kept = line.after((self.arrived, self.value))
                held = dict(zip(self.kept, kept))
                for n, (source, target) in enumerate(self.sent):
                    held[source ^ bit, target ^ bit] = arrived[n]
            if self.step < len(order):
                bit = order[self.step][1]
                self.sent = [key for key in sorted(held) if key[1] & bit]
                self.kept = [key for key in sorted(held) if not key[1] & bit]
                self.arrived = exchange(jnp.stack([held[key] for key in self.sent]), *order[self.step])
                self.value = [held[key] for key in self.kept]
            else:
                mixed = reorder([held[k, 0] for k in range(ctx_count)], ctx)
                mixed_grad = jnp.concatenate(
                    [m[..., t * pair : (t + 1) * pair] for t in range(3) for m in mixed], axis=-1
                )
                self.value = summed_grad + back_project(mixed_grad, qkv_full)
            self.step += 1
            line.done(self)

    chains.update(A=Attention(), v=Vectors(), q=QueryKeyValue(), T=Tokens())
    for name in EVENTS:
        chain = chains[name]
        chain.advance()
        if name in targets and chain.step == targets[name][1]:
            line.done(Placed(targets[name][0]))

    reduced = []
    offset = 0
    sizes = [part.shape[0] for part in layer_vectors] + [width, width]
    for size in sizes:
        reduced.append(half_of(chains["v"].value[offset : offset + size], core, 0))
        offset += size
    token_grad = chains["T"].value
    qkv_grad, in_grad, back_grad, out_grad = (
        whole["qkv"], whole["in"], whole["back"], whole["out"]
    )
    bias_grads = reduced[7:]
    return (
        output,
        token_grad,
        qkv_grad,
        bias_grads[0],
        bias_grads[1],
        out_grad,
        reduced[4],
        reduced[5],
        reduced[6],
        in_grad,
        reduced[0],
        back_grad,
        reduced[1],
        reduced[2],
        reduced[3],
    )


def head_parallel(mesh):
    sizes = [mesh.shape["dp"], mesh.shape["ctx"]]
    return sizes == [2, 8] and mesh.shape["fsdp"] == 2 and 2 * sizes[1] == HEADS


def solution(mesh):
    in_specs = (
        P(("dp", "fsdp"), "ctx", None),
        P("fsdp", None),
        P("fsdp"),
        P("fsdp"),
        P("fsdp", None),
        P("fsdp"),
        P("fsdp"),
        P("fsdp"),
        P("fsdp", None),
        P("fsdp"),
        P("fsdp", None),
        P("fsdp"),
        P("fsdp"),
        P("fsdp"),
        P(("dp", "fsdp"), "ctx", None),
    )
    out_specs = (
        P(("dp", "fsdp"), "ctx", None),
        P(("dp", "fsdp"), "ctx", None),
        P("fsdp", None),
        P("fsdp"),
        P("fsdp"),
        P("fsdp", None),
        P("fsdp"),
        P("fsdp"),
        P("fsdp"),
        P("fsdp", None),
        P("fsdp"),
        P("fsdp", None),
        P("fsdp"),
        P("fsdp"),
        P("fsdp"),
    )
    body = on_device if head_parallel(mesh) else ring_on_device
    return jax.shard_map(
        body, mesh=mesh, in_specs=in_specs, out_specs=out_specs, check_vma=False
    )
```

```python
from functools import partial

import jax
import jax.numpy as jnp
from jax import lax
from jax.experimental import pallas as pl
from jax.experimental.pallas import tpu as pltpu
from jax.sharding import PartitionSpec as P

HEADS = 16
HEAD_DIM = 64


EPSILON = 1e-06


def from_behind(block, axis, distance):
    devices = range(lax.axis_size(axis))
    route = [((i - distance) % len(devices), i) for i in devices]
    return lax.ppermute(block, axis, route)


def norm_apply(values, gain_vec, shift_vec):
    centre = jnp.mean(values, axis=-1, keepdims=True)
    centred = values - centre
    variance = jnp.mean(centred * centred, axis=-1, keepdims=True)
    return centred * lax.rsqrt(variance + EPSILON) * gain_vec + shift_vec


def lowered(values):
    return values.astype(jnp.bfloat16)


def widened(values):
    return values.astype(jnp.float32)


def project(left_operand_rows, right_operand_matrix):
    return jnp.einsum(
        "ugj,jn->ugn", left_operand_rows, right_operand_matrix, preferred_element_type=jnp.float32
    )


def weight_grad(left_operand_rows, gradient_row_block):
    return jnp.einsum(
        "xrb,xrw->bw", left_operand_rows, gradient_row_block, preferred_element_type=jnp.float32
    )


def back_project(gradient_row_block, right_operand_matrix):
    return jnp.einsum(
        "wkb,fb->wkf", gradient_row_block, right_operand_matrix, preferred_element_type=jnp.float32
    )


def column_sum(values):
    return jnp.sum(widened(values), axis=(0, 1))


def split_heads(values):
    return values.reshape(values.shape[0], values.shape[1], HEADS, HEAD_DIM)


def merge_heads(values):
    return values.reshape(values.shape[0], values.shape[1], HEADS * HEAD_DIM)


def split_blocks(values, block_rows):
    seq_count = values.shape[0]
    blocks = values.shape[1] // block_rows
    return jnp.moveaxis(values.reshape(seq_count, blocks, block_rows, values.shape[2]), 1, 0)


def block_scores(query_rows, key_rows):
    scores = jnp.einsum(
        "sqhd,skhd->shqk",
        split_heads(query_rows),
        split_heads(key_rows),
        preferred_element_type=jnp.float32,
    )
    return scores * HEAD_DIM ** (-0.5)


def fold_block(state_now, key_block, value_block, query_rows):
    running_max, running_sum, running_acc = state_now
    scores = block_scores(query_rows, key_block)
    new_max = jnp.maximum(running_max, jnp.max(scores, axis=-1))
    rescale = jnp.exp(running_max - new_max)
    weights = jnp.exp(scores - new_max[..., None])
    new_sum = running_sum * rescale + jnp.sum(weights, axis=-1)
    product = jnp.einsum(
        "shqk,skhd->shqd",
        lowered(weights),
        split_heads(value_block),
        preferred_element_type=jnp.float32,
    )
    return (new_max, new_sum, running_acc * rescale[..., None] + product)


def attend_forward(query_rows, key_rows, value_rows):
    seq_count = query_rows.shape[0]
    block_rows = query_rows.shape[1]
    initial = (
        jnp.full((seq_count, HEADS, block_rows), -1e30, jnp.float32),
        jnp.zeros((seq_count, HEADS, block_rows), jnp.float32),
        jnp.zeros((seq_count, HEADS, block_rows, HEAD_DIM), jnp.float32),
    )
    kept = None
    key_part = lax.all_gather(key_rows, "ctx", axis=1, tiled=True)
    value_part = lax.all_gather(value_rows, "ctx", axis=1, tiled=True)

    def one_block(state_in, block_pair):
        return (fold_block(state_in, block_pair[0], block_pair[1], query_rows), None)

    state_out, unused = lax.scan(
        one_block,
        initial,
        (split_blocks(key_part, block_rows), split_blocks(value_part, block_rows)),
    )
    running_max, running_sum, running_acc = state_out
    attention_result = running_acc / running_sum[..., None]
    attention_result = jnp.transpose(attention_result, (0, 2, 1, 3)).reshape(
        seq_count, block_rows, HEADS * HEAD_DIM
    )
    log_total = running_max + jnp.log(running_sum)
    return (attention_result, log_total, kept)


def attend_back(query_rows, gradient_row_block, log_total, row_inner, key_rows, value_rows):
    score_scale = HEAD_DIM ** (-0.5)
    scores = block_scores(query_rows, key_rows)
    probabilities = jnp.exp(scores - log_total[..., None])
    value_grad = jnp.einsum(
        "shqk,sqhd->skhd",
        lowered(probabilities),
        split_heads(gradient_row_block),
        preferred_element_type=jnp.float32,
    )
    prob_grad = jnp.einsum(
        "sqhd,skhd->shqk",
        split_heads(gradient_row_block),
        split_heads(value_rows),
        preferred_element_type=jnp.float32,
    )
    score_grad = lowered(probabilities * (prob_grad - row_inner[..., None]))
    query_grad = (
        jnp.einsum(
            "shqk,skhd->sqhd", score_grad, split_heads(key_rows), preferred_element_type=jnp.float32
        )
        * score_scale
    )
    key_grad = (
        jnp.einsum(
            "shqk,sqhd->skhd",
            score_grad,
            split_heads(query_rows),
            preferred_element_type=jnp.float32,
        )
        * score_scale
    )
    return (merge_heads(query_grad), merge_heads(key_grad), merge_heads(value_grad))


def attend_backward(query_rows, gradient_row_block, log_total, row_inner, key_rows, value_rows):
    zero_rows = jnp.zeros(query_rows.shape, jnp.float32)
    turn_count = lax.axis_size("ctx") // 2

    def turn_keys(turn_index, carried):
        moving_key, moving_value, key_acc, value_acc, query_acc = carried
        for half_step in range(2):
            pieces = attend_back(
                query_rows, gradient_row_block, log_total, row_inner, moving_key, moving_value
            )
            query_acc = query_acc + pieces[0]
            key_acc = key_acc + pieces[1]
            value_acc = value_acc + pieces[2]
            moving_key, moving_value = from_behind((moving_key, moving_value), "ctx", 1)
            key_acc, value_acc = (
                from_behind(key_acc.astype(jnp.bfloat16), "ctx", 1).astype(key_acc.dtype),
                from_behind(value_acc.astype(jnp.bfloat16), "ctx", 1).astype(value_acc.dtype),
            )
        return (moving_key, moving_value, key_acc, value_acc, query_acc)

    finished = lax.fori_loop(
        0, turn_count, turn_keys, (key_rows, value_rows, zero_rows, zero_rows, zero_rows)
    )
    return (finished[4], finished[2], finished[3])


def ring_on_device(
    tokens,
    query_key_value_weight,
    bias_query,
    bias_value,
    attention_out_weight,
    attention_out_bias,
    gain_one,
    shift_one,
    feedforward_in_weight,
    feedforward_in_bias,
    feedforward_out_weight,
    feedforward_out_bias,
    gain_two,
    shift_two,
    d_out,
):
    attn_full = (
        lax.all_gather(query_key_value_weight, "fsdp", axis=0, tiled=True),
        lax.all_gather(attention_out_weight, "fsdp", axis=0, tiled=True),
        lax.all_gather(bias_query, "fsdp", axis=0, tiled=True),
        lax.all_gather(bias_value, "fsdp", axis=0, tiled=True),
        lax.all_gather(attention_out_bias, "fsdp", axis=0, tiled=True),
        lax.all_gather(gain_one, "fsdp", axis=0, tiled=True),
        lax.all_gather(shift_one, "fsdp", axis=0, tiled=True),
    )
    qkv_full, out_full, query_bias, value_bias, out_bias, gain_first, shift_first = attn_full
    model_width = out_full.shape[0]
    projected_rows = project(tokens, qkv_full) + jnp.concatenate(
        [widened(query_bias), jnp.zeros((model_width,), jnp.float32), widened(value_bias)]
    )
    projected_low = lowered(projected_rows)
    query_rows = projected_low[..., :model_width]
    key_rows = projected_low[..., model_width : 2 * model_width]
    value_rows = projected_low[..., 2 * model_width :]
    attention_result, log_total, kept = attend_forward(query_rows, key_rows, value_rows)
    attended_low = lowered(attention_result)
    attention_branch = project(attended_low, out_full) + widened(out_bias)
    summed_one = widened(tokens) + attention_branch
    first_normalized, pull_one = jax.vjp(
        norm_apply, summed_one, widened(gain_first), widened(shift_first)
    )
    normed_low = lowered(first_normalized)
    ffn_full = (
        lax.all_gather(feedforward_in_weight, "fsdp", axis=0, tiled=True),
        lax.all_gather(feedforward_out_weight, "fsdp", axis=0, tiled=True),
        lax.all_gather(feedforward_in_bias, "fsdp", axis=0, tiled=True),
        lax.all_gather(feedforward_out_bias, "fsdp", axis=0, tiled=True),
        lax.all_gather(gain_two, "fsdp", axis=0, tiled=True),
        lax.all_gather(shift_two, "fsdp", axis=0, tiled=True),
    )
    in_full, back_full, inner_bias, back_bias, gain_second, shift_second = ffn_full
    hidden_before_gelu = project(normed_low, in_full) + widened(inner_bias)
    active_low = lowered(jax.nn.gelu(hidden_before_gelu, approximate=False))
    feedforward_branch = project(active_low, back_full) + widened(back_bias)

    def second_norm(residual_in, branch_in, gain_vec, shift_vec):
        return norm_apply(residual_in + branch_in, gain_vec, shift_vec)

    result, pull_two = jax.vjp(
        second_norm,
        first_normalized,
        feedforward_branch,
        widened(gain_second),
        widened(shift_second),
    )
    output = lowered(result)
    first_grad_res, second_grad, gain_two_grad, shift_two_grad = pull_two(widened(d_out))
    in_full, back_full = (
        lax.all_gather(feedforward_in_weight, "fsdp", axis=0, tiled=True),
        lax.all_gather(feedforward_out_weight, "fsdp", axis=0, tiled=True),
    )
    second_low = lowered(second_grad)
    back_grad = weight_grad(active_low, second_low)
    back_bias_grad = column_sum(second_low)
    active_grad = back_project(second_low, back_full)
    gelu_pull = jax.vjp(partial(jax.nn.gelu, approximate=False), hidden_before_gelu)[1]
    hidden_low = lowered(gelu_pull(active_grad)[0])
    in_grad = weight_grad(normed_low, hidden_low)
    in_bias_grad = column_sum(hidden_low)
    first_grad = first_grad_res + back_project(hidden_low, in_full)
    ffn_grads = (
        lax.psum_scatter(
            in_grad.astype(jnp.bfloat16), "fsdp", scatter_dimension=0, tiled=True
        ).astype(jnp.float32),
        lax.psum_scatter(
            in_bias_grad.astype(jnp.bfloat16), "fsdp", scatter_dimension=0, tiled=True
        ).astype(jnp.float32),
        lax.psum_scatter(
            back_grad.astype(jnp.bfloat16), "fsdp", scatter_dimension=0, tiled=True
        ).astype(jnp.float32),
        lax.psum_scatter(
            back_bias_grad.astype(jnp.bfloat16), "fsdp", scatter_dimension=0, tiled=True
        ).astype(jnp.float32),
        lax.psum_scatter(
            gain_two_grad.astype(jnp.bfloat16), "fsdp", scatter_dimension=0, tiled=True
        ).astype(jnp.float32),
        lax.psum_scatter(
            shift_two_grad.astype(jnp.bfloat16), "fsdp", scatter_dimension=0, tiled=True
        ).astype(jnp.float32),
    )
    ffn_grads = lax.psum(
        (ffn_grads[0], ffn_grads[1], ffn_grads[2], ffn_grads[3], ffn_grads[4], ffn_grads[5]),
        ("dp", "ctx"),
    )
    summed_grad, gain_one_grad, shift_one_grad = pull_one(first_grad)
    qkv_full, out_full = (
        lax.all_gather(query_key_value_weight, "fsdp", axis=0, tiled=True),
        lax.all_gather(attention_out_weight, "fsdp", axis=0, tiled=True),
    )
    branch_low = lowered(summed_grad)
    out_grad = weight_grad(attended_low, branch_low)
    out_bias_grad = column_sum(branch_low)
    attended_grad_low = lowered(back_project(branch_low, out_full))
    row_inner = jnp.sum(
        split_heads(widened(attended_grad_low)) * split_heads(attention_result), axis=-1
    )
    row_inner = jnp.transpose(row_inner, (0, 2, 1))
    query_grad, key_grad, value_grad = attend_backward(
        query_rows, attended_grad_low, log_total, row_inner, key_rows, value_rows
    )
    mixed_grad = lowered(jnp.concatenate([query_grad, key_grad, value_grad], axis=-1))
    qkv_grad = weight_grad(tokens, mixed_grad)
    bias_grads = column_sum(mixed_grad)
    query_bias_grad = bias_grads[:model_width]
    value_bias_grad = bias_grads[2 * model_width :]
    token_grad = summed_grad + back_project(mixed_grad, qkv_full)
    attn_grads = (
        lax.psum_scatter(
            qkv_grad.astype(jnp.bfloat16), "fsdp", scatter_dimension=0, tiled=True
        ).astype(jnp.float32),
        lax.psum_scatter(
            query_bias_grad.astype(jnp.bfloat16), "fsdp", scatter_dimension=0, tiled=True
        ).astype(jnp.float32),
        lax.psum_scatter(
            value_bias_grad.astype(jnp.bfloat16), "fsdp", scatter_dimension=0, tiled=True
        ).astype(jnp.float32),
        lax.psum_scatter(
            out_grad.astype(jnp.bfloat16), "fsdp", scatter_dimension=0, tiled=True
        ).astype(jnp.float32),
        lax.psum_scatter(
            out_bias_grad.astype(jnp.bfloat16), "fsdp", scatter_dimension=0, tiled=True
        ).astype(jnp.float32),
        lax.psum_scatter(
            gain_one_grad.astype(jnp.bfloat16), "fsdp", scatter_dimension=0, tiled=True
        ).astype(jnp.float32),
        lax.psum_scatter(
            shift_one_grad.astype(jnp.bfloat16), "fsdp", scatter_dimension=0, tiled=True
        ).astype(jnp.float32),
    )
    attn_grads = lax.psum(
        (
            attn_grads[0],
            attn_grads[1],
            attn_grads[2],
            attn_grads[3],
            attn_grads[4],
            attn_grads[5],
            attn_grads[6],
        ),
        ("dp", "ctx"),
    )
    return (
        output,
        token_grad,
        attn_grads[0],
        attn_grads[1],
        attn_grads[2],
        attn_grads[3],
        attn_grads[4],
        attn_grads[5],
        attn_grads[6],
        ffn_grads[0],
        ffn_grads[1],
        ffn_grads[2],
        ffn_grads[3],
        ffn_grads[4],
        ffn_grads[5],
    )


def exchange(values, axis, bit):
    count = lax.axis_size(axis)
    return lax.ppermute(values, axis, [(i, i ^ bit) for i in range(count)])


def bits_below(count):
    return [1 << k for k in range(count.bit_length() - 1)]


def reorder(pieces, index):
    for bit in bits_below(len(pieces)):
        taken = (index & bit) != 0
        pieces = [jnp.where(taken, pieces[k ^ bit], pieces[k]) for k in range(len(pieces))]
    return pieces


def pair_join(own, other, core, axis=0):
    first = jnp.where(core == 0, own, other)
    second = jnp.where(core == 0, other, own)
    return jnp.concatenate([first, second], axis=axis)


def half_of(values, which, axis):
    size = values.shape[axis] // 2
    low = lax.slice_in_dim(values, 0, size, axis=axis)
    high = lax.slice_in_dim(values, size, 2 * size, axis=axis)
    return jnp.where(which == 0, low, high)


def gather_blocks(block):
    line = Line()

    def arrived(values):
        holder = Held(line.after(values))
        line.done(holder)
        return holder

    near, middle, far = (exchange(block, "ctx", bit) for bit in (1, 2, 4))
    second = arrived(lax.optimization_barrier((middle, far)))
    third = exchange(second.value[0], "ctx", 1)
    sixth = exchange(second.value[1], "ctx", 2)
    fifth = exchange(second.value[1], "ctx", 1)
    middle, far = second.value
    third, fifth, sixth = lax.optimization_barrier((third, fifth, sixth))
    seventh = exchange(sixth, "ctx", 1)
    return [block, near, middle, third, far, fifth, sixth, seventh]


def swap_blocks(pieces):
    return [pieces[0]] + [exchange(pieces[k], "ctx", k) for k in range(1, len(pieces))]


def head_mask(value):
    lane = lax.broadcasted_iota(jnp.int32, (1, 2 * HEAD_DIM), 1)
    return [
        jnp.where(lane < HEAD_DIM, value, 0.0),
        jnp.where(lane < HEAD_DIM, 0.0, value),
    ]


def contract(left, right, left_dim, right_dim):
    return lax.dot_general(
        left, right, (((left_dim,), (right_dim,)), ((), ())), preferred_element_type=jnp.float32
    )


def forward_kernel(query_ref, key_ref, value_ref, result_ref, low_ref, log_ref):
    query = query_ref[0].astype(jnp.float32)
    keys = key_ref[0]
    values = value_ref[0]
    results = []
    logs = []
    for mask in head_mask(HEAD_DIM ** (-0.5)):
        scores = contract((query * mask).astype(jnp.bfloat16), keys, 1, 1)
        row_max = jnp.max(scores, axis=-1, keepdims=True)
        weights = jnp.exp(scores - row_max)
        total = jnp.sum(weights, axis=-1, keepdims=True)
        probabilities = (weights * (1.0 / total)).astype(jnp.bfloat16)
        results.append(contract(probabilities, values, 1, 0))
        logs.append(row_max + jnp.log(total))
    first = lax.broadcasted_iota(jnp.int32, results[0].shape, 1) < HEAD_DIM
    result = jnp.where(first, results[0], results[1])
    result_ref[0] = result
    low_ref[0] = result.astype(jnp.bfloat16)
    log_ref[0] = jnp.where(first, logs[0], logs[1])


def attention_forward(projected):
    seqs, length, width = projected.shape
    pair = width // 3
    rows = min(256, length)
    row_spec = pl.BlockSpec((1, rows, pair), lambda s, q: (s, q, 0))
    return pl.pallas_call(
        forward_kernel,
        grid=(seqs, length // rows),
        in_specs=[
            row_spec,
            pl.BlockSpec((1, length, pair), lambda s, q: (s, 0, 1)),
            pl.BlockSpec((1, length, pair), lambda s, q: (s, 0, 2)),
        ],
        out_specs=[row_spec, row_spec, row_spec],
        out_shape=[
            jax.ShapeDtypeStruct((seqs, length, pair), jnp.float32),
            jax.ShapeDtypeStruct((seqs, length, pair), jnp.bfloat16),
            jax.ShapeDtypeStruct((seqs, length, pair), jnp.float32),
        ],
        compiler_params=pltpu.CompilerParams(vmem_limit_bytes=48 << 20),
        name="attention_forward",
    )(projected, projected, projected)


def backward_kernel(
    query_ref, key_ref, value_ref, grad_ref, result_ref, log_ref,
    query_out, key_out, value_out, query_acc, log_rows, inner_rows,
):
    step = pl.program_id(1)

    @pl.when(step == 0)
    def first_step():
        query_acc[...] = jnp.zeros_like(query_acc)
        logs = jnp.transpose(log_ref[0])
        inner = jnp.transpose(grad_ref[0].astype(jnp.float32) * result_ref[0])
        for h in range(2):
            log_rows[h] = jnp.broadcast_to(
                logs[h * HEAD_DIM : h * HEAD_DIM + 1], log_rows.shape[1:]
            )
            inner_rows[h] = jnp.broadcast_to(
                jnp.sum(inner[h * HEAD_DIM : (h + 1) * HEAD_DIM], axis=0, keepdims=True),
                inner_rows.shape[1:],
            )

    queries = query_ref[0]
    grads = grad_ref[0]
    keys = key_ref[0]
    values = value_ref[0]
    scale = HEAD_DIM ** (-0.5)
    query_parts = []
    key_parts = []
    value_parts = []
    scaled_masks = head_mask(scale)
    masks = head_mask(1.0)
    for h in range(2):
        scores = contract(
            (keys.astype(jnp.float32) * scaled_masks[h]).astype(jnp.bfloat16), queries, 1, 1
        )
        probabilities = jnp.exp(scores - log_rows[h, :1])
        prob_grad = contract(
            (values.astype(jnp.float32) * masks[h]).astype(jnp.bfloat16), grads, 1, 1
        )
        score_grad = (probabilities * (prob_grad - inner_rows[h, :1])).astype(jnp.bfloat16)
        value_parts.append(contract(probabilities.astype(jnp.bfloat16), grads, 1, 0))
        key_parts.append(contract(score_grad, queries, 1, 0))
        query_parts.append(contract(score_grad, keys, 0, 0))
    first = lax.broadcasted_iota(jnp.int32, key_parts[0].shape, 1) < HEAD_DIM
    value_out[0] = jnp.where(first, value_parts[0], value_parts[1]).astype(jnp.bfloat16)
    key_out[0] = (jnp.where(first, key_parts[0], key_parts[1]) * scale).astype(jnp.bfloat16)
    first = lax.broadcasted_iota(jnp.int32, query_parts[0].shape, 1) < HEAD_DIM
    query_acc[...] += jnp.where(first, query_parts[0], query_parts[1])

    @pl.when(step == pl.num_programs(1) - 1)
    def last_step():
        query_out[0] = (query_acc[...] * scale).astype(jnp.bfloat16)


def attention_backward(projected, grads, result, logs):
    seqs, length, width = projected.shape
    pair = width // 3
    rows = min(256, length)
    whole = pl.BlockSpec((1, length, pair), lambda s, k: (s, 0, 0))
    block = pl.BlockSpec((1, rows, pair), lambda s, k: (s, k, 0))
    shape = jax.ShapeDtypeStruct((seqs, length, pair), jnp.bfloat16)
    return pl.pallas_call(
        backward_kernel,
        grid=(seqs, length // rows),
        in_specs=[
            whole,
            pl.BlockSpec((1, rows, pair), lambda s, k: (s, k, 1)),
            pl.BlockSpec((1, rows, pair), lambda s, k: (s, k, 2)),
            whole,
            whole,
            whole,
        ],
        out_specs=[whole, block, block],
        out_shape=[shape, shape, shape],
        scratch_shapes=[
            pltpu.VMEM((length, pair), jnp.float32),
            pltpu.VMEM((2, 8, length), jnp.float32),
            pltpu.VMEM((2, 8, length), jnp.float32),
        ],
        compiler_params=pltpu.CompilerParams(vmem_limit_bytes=48 << 20),
        name="attention_backward",
    )(projected, projected, projected, grads, result, logs)


def ffn_forward_kernel(
    core_ref, left_own, left_other, in_own, in_other, bias_ref, back_own, back_other,
    active_ref, slope_ref, second_ref,
):
    step = pl.program_id(0)
    hidden = contract(left_own[...], in_own[...], 1, 0)
    hidden = hidden + contract(left_other[...], in_other[...], 1, 0) + bias_ref[...]
    below = 0.5 * (1.0 + lax.erf(hidden * 0.7071067811865476))
    slope = below + hidden * (jnp.exp(-0.5 * hidden * hidden) * 0.3989422804014327)
    active = (hidden * below).astype(jnp.bfloat16)
    active_ref[...] = active
    slope_ref[...] = slope.astype(jnp.bfloat16)

    @pl.when(step == 0)
    def first():
        second_ref[...] = contract(active, back_own[...], 1, 0)

    @pl.when((step > 0) & (step < pl.num_programs(0) // 2))
    def own():
        second_ref[...] += contract(active, back_own[...], 1, 0)

    @pl.when(step >= pl.num_programs(0) // 2)
    def other():
        second_ref[...] += contract(active, back_other[...], 1, 0)


def ffn_specs(half, block, width, hidden):
    near = hidden // (2 * block)

    def spot(s, p):
        return jnp.where(s < near, s + p[0] * near, s - p[0] * near)

    weights = [
        pl.BlockSpec((half, block), lambda s, p: (0, spot(s, p))),
        pl.BlockSpec((half, block), lambda s, p: (0, spot(s, p))),
        pl.BlockSpec((block, width), lambda s, p: (jnp.minimum(s, near - 1), 0)),
        pl.BlockSpec((block, width), lambda s, p: (jnp.maximum(s - near, 0), 0)),
    ]
    return spot, weights


def ffn_forward(core, left, in_pair, back_pair, bias):
    tokens, width = left.shape
    half, hidden = in_pair[0].shape
    block = 1024
    spot, weights = ffn_specs(half, block, width, hidden)
    wide = pl.BlockSpec((tokens, block), lambda s, p: (0, spot(s, p)))
    return pl.pallas_call(
        ffn_forward_kernel,
        grid_spec=pltpu.PrefetchScalarGridSpec(
            num_scalar_prefetch=1,
            grid=(hidden // block,),
            in_specs=[
                pl.BlockSpec((tokens, half), lambda s, p: (0, p[0])),
                pl.BlockSpec((tokens, half), lambda s, p: (0, 1 - p[0])),
                weights[0],
                weights[1],
                pl.BlockSpec((1, block), lambda s, p: (0, spot(s, p))),
                weights[2],
                weights[3],
            ],
            out_specs=[wide, wide, pl.BlockSpec((tokens, width), lambda s, p: (0, 0))],
        ),
        out_shape=[
            jax.ShapeDtypeStruct((tokens, hidden), jnp.bfloat16),
            jax.ShapeDtypeStruct((tokens, hidden), jnp.bfloat16),
            jax.ShapeDtypeStruct((tokens, width), jnp.float32),
        ],
        compiler_params=pltpu.CompilerParams(vmem_limit_bytes=40 << 20),
        name="ffn_forward",
    )(core, left, left, *in_pair, bias, *back_pair)


def ffn_backward_kernel(
    core_ref, grad_ref, slope_ref, in_own, in_other, back_own, back_other,
    hidden_ref, total_ref, own_acc, other_acc,
):
    step = pl.program_id(0)
    half = own_acc.shape[1]

    def rest(back_ref):
        active_grad = contract(grad_ref[...], back_ref[...], 1, 1)
        hidden = (active_grad * slope_ref[...].astype(jnp.float32)).astype(jnp.bfloat16)
        hidden_ref[...] = hidden
        own = contract(hidden, in_own[...], 1, 1)
        other = contract(hidden, in_other[...], 1, 1)

        @pl.when(step == 0)
        def first():
            own_acc[...] = own
            other_acc[...] = other

        @pl.when(step > 0)
        def later():
            own_acc[...] += own
            other_acc[...] += other

    @pl.when(step < pl.num_programs(0) // 2)
    def with_own():
        rest(back_own)

    @pl.when(step >= pl.num_programs(0) // 2)
    def with_other():
        rest(back_other)

    @pl.when(step == pl.num_programs(0) - 1)
    def last():
        @pl.when(core_ref[0] == 0)
        def straight():
            total_ref[:, :half] = own_acc[...]
            total_ref[:, half:] = other_acc[...]

        @pl.when(core_ref[0] != 0)
        def crossed():
            total_ref[:, :half] = other_acc[...]
            total_ref[:, half:] = own_acc[...]


def ffn_backward(core, grad, slope, in_pair, back_pair):
    tokens, width = grad.shape
    half, hidden = in_pair[0].shape
    block = 1024
    spot, weights = ffn_specs(half, block, width, hidden)
    wide = pl.BlockSpec((tokens, block), lambda s, p: (0, spot(s, p)))
    whole = pl.BlockSpec((tokens, width), lambda s, p: (0, 0))
    return pl.pallas_call(
        ffn_backward_kernel,
        grid_spec=pltpu.PrefetchScalarGridSpec(
            num_scalar_prefetch=1,
            grid=(hidden // block,),
            in_specs=[whole, wide, *weights],
            out_specs=[wide, whole],
            scratch_shapes=[
                pltpu.VMEM((tokens, half), jnp.float32),
                pltpu.VMEM((tokens, half), jnp.float32),
            ],
        ),
        out_shape=[
            jax.ShapeDtypeStruct((tokens, hidden), jnp.bfloat16),
            jax.ShapeDtypeStruct((tokens, width), jnp.float32),
        ],
        compiler_params=pltpu.CompilerParams(vmem_limit_bytes=40 << 20),
        name="ffn_backward",
    )(core, grad, slope, *in_pair, *back_pair)


def qkv_grad_kernel(core_ref, *refs, pieces):
    token_refs, grad_refs = refs[:pieces], refs[pieces : pieces + 3]
    own_ref, other_ref = refs[pieces + 3 :]
    seqs = token_refs[0].shape[0]
    rows = jnp.concatenate([ref[s] for s in range(seqs) for ref in token_refs], axis=0)
    parts = []
    for ref in grad_refs:
        grads = jnp.concatenate([ref[s] for s in range(seqs)], axis=0)
        parts.append(contract(rows, grads, 0, 0))
    half = pl.num_programs(0) // 2

    @pl.when(pl.program_id(0) < half)
    def outgoing():
        for t in range(3):
            other_ref[t] = parts[t].astype(jnp.bfloat16)

    @pl.when(pl.program_id(0) >= half)
    def kept():
        for t in range(3):
            own_ref[t] = parts[t]


def qkv_grad_parts(core, token_pieces, head_grads):
    seqs, rows, width = token_pieces[0].shape
    pair = head_grads[0].shape[2]
    cols = 256
    steps = width // cols
    half = steps // 2

    def spot(s, p):
        return jnp.where(s < half, s + (1 - p[0]) * half, s - half + p[0] * half)

    grads = pl.BlockSpec(head_grads[0].shape, lambda s, p: (0, 0, 0))
    return pl.pallas_call(
        partial(qkv_grad_kernel, pieces=len(token_pieces)),
        grid_spec=pltpu.PrefetchScalarGridSpec(
            num_scalar_prefetch=1,
            grid=(steps,),
            in_specs=[pl.BlockSpec((seqs, rows, cols), lambda s, p: (0, 0, spot(s, p)))]
            * len(token_pieces)
            + [grads] * 3,
            out_specs=[
                pl.BlockSpec((3, cols, pair), lambda s, p: (0, jnp.maximum(s - half, 0), 0)),
                pl.BlockSpec((3, cols, pair), lambda s, p: (0, jnp.minimum(s, half - 1), 0)),
            ],
        ),
        out_shape=[
            jax.ShapeDtypeStruct((3, width // 2, pair), jnp.float32),
            jax.ShapeDtypeStruct((3, width // 2, pair), jnp.bfloat16),
        ],
        compiler_params=pltpu.CompilerParams(vmem_limit_bytes=40 << 20),
        name="grad_qkv",
    )(core, *token_pieces, *head_grads)


LOW = 2


def grad_kernel(place_ref, left_own, left_other, right_own, right_other, keep_ref, send_ref, *, by_rows):
    step = pl.program_id(0)
    half = pl.num_programs(0) // 2
    total = contract(left_own[...], right_own[...], 0, 0)
    total = total + contract(left_other[...], right_other[...], 0, 0)
    total = total.astype(jnp.bfloat16)
    low = place_ref[0] & ((1 << LOW) - 1)
    _, rows, cols = keep_ref.shape

    def put(out_ref):
        for j in range(1 << LOW):
            if by_rows:
                out_ref[j ^ low] = total[j * rows : (j + 1) * rows]
            else:
                out_ref[j ^ low] = total[:, j * cols : (j + 1) * cols]

    @pl.when(step < half)
    def outgoing():
        put(send_ref)

    @pl.when(step >= half)
    def kept():
        put(keep_ref)


def pair_grad(place, left_pair, right_pair, count, part, parts, by_rows, name):
    tokens, width = left_pair[0].shape
    columns = right_pair[0].shape[1]
    steps = count >> LOW
    half = steps // 2

    def block(step, place_ref):
        return part * steps + (((step + half) % steps) ^ (place_ref[0] >> LOW))

    if by_rows:
        rows, cols = width // (parts * count), columns
        left = pl.BlockSpec((tokens, rows << LOW), lambda s, p: (0, block(s, p)))
        right = pl.BlockSpec((tokens, columns), lambda s, p: (0, 0))
    else:
        rows, cols = width, columns // (parts * count)
        left = pl.BlockSpec((tokens, width), lambda s, p: (0, 0))
        right = pl.BlockSpec((tokens, cols << LOW), lambda s, p: (0, block(s, p)))
    shape = jax.ShapeDtypeStruct((count // 2, rows, cols), jnp.bfloat16)
    out_block = (1 << LOW, rows, cols)
    return pl.pallas_call(
        partial(grad_kernel, by_rows=by_rows),
        grid_spec=pltpu.PrefetchScalarGridSpec(
            num_scalar_prefetch=1,
            grid=(steps,),
            in_specs=[left, left, right, right],
            out_specs=[
                pl.BlockSpec(out_block, lambda s, p: (jnp.maximum(s - half, 0), 0, 0)),
                pl.BlockSpec(out_block, lambda s, p: (jnp.minimum(s, half - 1), 0, 0)),
            ],
        ),
        out_shape=[shape, shape],
        compiler_params=pltpu.CompilerParams(vmem_limit_bytes=48 << 20),
        name=name,
    )(place, left_pair[0], left_pair[1], right_pair[0], right_pair[1])


def place_of(order):
    place = jnp.int32(0)
    for axis, bit in order:
        place = place * 2 + jnp.where((lax.axis_index(axis) & bit) != 0, 1, 0)
    return place.astype(jnp.int32).reshape(1)


def added(first, second):
    return lowered(widened(first) + widened(second))


LINKS = {"x": ("dp", 1), "y": ("ctx", 1), "p": ("ctx", 2), "r": ("ctx", 4)}
ORDERS = {"b0": "pyrx", "b1": "yprx", "i0": "xypr", "i1": "yxpr", "o": "rxpy", "q": "xypr", "v": "xypr", "T": "ypr"}
EVENTS = (
    "b", "A", "i", "q", "o", "b", "i", "q", "v", "o", "v", "b", "i", "v", "o", "q",
    "b", "o", "v", "i", "T", "o", "q", "b", "v", "o", "i", "T", "o", "b", "i", "q",
    "T", "i", "o", "b", "q", "T", "i", "b",
)


def hops(name):
    return [LINKS[letter] for letter in ORDERS[name]]


class Line:
    def __init__(self):
        self.last = None

    def after(self, values):
        if self.last is None:
            return values
        values, self.last.value = lax.optimization_barrier((values, self.last.value))
        return values

    def done(self, holder):
        self.last = holder


class Held:
    def __init__(self, value):
        self.value = value


class Reduction:
    def __init__(self, line, name, keep, send, put):
        self.line, self.order, self.put = line, hops(name), put
        self.value, self.step = keep, 0
        self.arrived = exchange(send, *self.order[0])

    def advance(self):
        last = len(self.order) - 1
        step = self.step
        self.step += 1
        arrived, value = self.line.after((self.arrived, self.value))
        if step < last:
            half = value.shape[0] // 2
            send = added(value[half:], arrived[half:])
            self.value = added(value[:half], arrived[:half])
            self.arrived = exchange(send, *self.order[step + 1])
        elif step == last:
            self.value = added(value, arrived)
            self.arrived = exchange(self.value, *self.order[last])
        elif step <= 2 * last:
            self.value = jnp.concatenate([value, arrived], axis=0)
            self.arrived = exchange(self.value, *self.order[2 * last - step])
            if step == 2 * last:
                self.put(self.value, False)
        else:
            self.value = self.put(arrived, True)
        self.line.done(self)


class Group:
    def __init__(self, line, names, parts, put):
        self.line, self.put, self.step = line, put, 1
        self.orders = [hops(name) for name in names]
        self.value = [keep for keep, send in parts]
        self.arrived = [exchange(send, *o[0]) for (keep, send), o in zip(parts, self.orders)]

    def advance(self):
        arrived, value = self.line.after((self.arrived, self.value))
        tail = self.orders[0][2:]
        step = self.step
        self.step += 1
        if step == 1:
            self.arrived = [
                exchange(added(v[v.shape[0] // 2 :], a[v.shape[0] // 2 :]), *o[1])
                for v, a, o in zip(value, arrived, self.orders)
            ]
            self.value = [
                added(v[: v.shape[0] // 2], a[: v.shape[0] // 2]) for v, a in zip(value, arrived)
            ]
        elif step == 2:
            total = jnp.stack([added(v, a) for v, a in zip(value, arrived)], axis=1)
            self.value = total[:2]
            self.arrived = exchange(total[2:], *tail[0])
        elif step == 3:
            self.value = added(value[:1], arrived[:1])
            self.arrived = exchange(added(value[1:], arrived[1:]), *tail[1])
        elif step == 4:
            self.value = added(value, arrived)
            self.arrived = exchange(self.value, *tail[1])
        elif step == 5:
            self.value = jnp.concatenate([value, arrived], axis=0)
            self.arrived = exchange(self.value, *tail[0])
        elif step == 6:
            total = jnp.concatenate([value, arrived], axis=0)
            self.value = [total[:, 0], total[:, 1]]
            self.arrived = [exchange(v, *o[1]) for v, o in zip(self.value, self.orders)]
        elif step == 7:
            self.value = [jnp.concatenate([v, a], axis=0) for v, a in zip(value, arrived)]
            self.arrived = [exchange(v, *o[0]) for v, o in zip(self.value, self.orders)]
            for part, chunks in enumerate(self.value):
                self.put(chunks, part, False)
        else:
            for part, chunks in enumerate(arrived):
                self.value = self.put(chunks, part, True)
        self.line.done(self)


def place_kernel(place_ref, chunks_ref, *rest, by_rows):
    out_ref = rest[-1]
    low = place_ref[0] & ((1 << LOW) - 1)
    _, rows, cols = chunks_ref.shape
    for j in range(1 << LOW):
        values = chunks_ref[j ^ low].astype(jnp.float32)
        if by_rows:
            out_ref[j * rows : (j + 1) * rows, :] = values
        else:
            out_ref[:, j * cols : (j + 1) * cols] = values


def put_in_place(place, chunks, far, into, part, parts, by_rows, name):
    half, rows, cols = chunks.shape
    steps = half >> LOW
    first = steps if far else 0

    def block(step, place_ref):
        return part * 2 * steps + ((step + first) ^ (place_ref[0] >> LOW))

    if by_rows:
        out_shape = (rows * 2 * half * parts, cols)
        out_spec = pl.BlockSpec((rows << LOW, cols), lambda s, p: (block(s, p), 0))
    else:
        out_shape = (rows, cols * 2 * half * parts)
        out_spec = pl.BlockSpec((rows, cols << LOW), lambda s, p: (0, block(s, p)))
    in_specs = [pl.BlockSpec((1 << LOW, rows, cols), lambda s, p: (s, 0, 0))]
    operands = [place, chunks]
    if into is not None:
        in_specs.append(pl.BlockSpec(memory_space=pl.ANY))
        operands.append(into)
    return pl.pallas_call(
        partial(place_kernel, by_rows=by_rows),
        grid_spec=pltpu.PrefetchScalarGridSpec(
            num_scalar_prefetch=1, grid=(steps,), in_specs=in_specs, out_specs=out_spec
        ),
        out_shape=jax.ShapeDtypeStruct(out_shape, jnp.float32),
        input_output_aliases={} if into is None else {2: 0},
        compiler_params=pltpu.CompilerParams(vmem_limit_bytes=48 << 20),
        name=name,
    )(*operands)


def place_three_kernel(place_ref, chunks_ref, *rest, bits):
    out_ref = rest[-1]
    count, _, _, cols = chunks_ref.shape
    low = place_ref[0] & (count - 1)
    for j in range(count):
        spot = sum(((j // bit) & 1) << (len(bits) - 1 - k) for k, bit in enumerate(bits))
        out_ref[:, j * cols : (j + 1) * cols] = chunks_ref[spot ^ low, 0].astype(jnp.float32)


def put_three_in_place(place, chunks, far, into, bits, dp_count, name):
    total, three, rows, cols = chunks.shape
    ctx_count = 1 << len(bits)
    steps = total // ctx_count
    first = steps if far else 0
    in_specs = [pl.BlockSpec((ctx_count, 1, rows, cols), lambda s, t, p: (s, t, 0, 0))]
    operands = [place, chunks]
    if into is not None:
        in_specs.append(pl.BlockSpec(memory_space=pl.ANY))
        operands.append(into)
    return pl.pallas_call(
        partial(place_three_kernel, bits=bits),
        grid_spec=pltpu.PrefetchScalarGridSpec(
            num_scalar_prefetch=1,
            grid=(steps, three),
            in_specs=in_specs,
            out_specs=pl.BlockSpec(
                (rows, ctx_count * cols),
                lambda s, t, p: ((s + first) ^ (p[0] >> len(bits)), t),
            ),
        ),
        out_shape=jax.ShapeDtypeStruct((rows * dp_count, three * ctx_count * cols), jnp.float32),
        input_output_aliases={} if into is None else {2: 0},
        compiler_params=pltpu.CompilerParams(vmem_limit_bytes=48 << 20),
        name=name,
    )(*operands)


def on_device(
    tokens,
    query_key_value_weight,
    bias_query,
    bias_value,
    attention_out_weight,
    attention_out_bias,
    gain_one,
    shift_one,
    feedforward_in_weight,
    feedforward_in_bias,
    feedforward_out_weight,
    feedforward_out_bias,
    gain_two,
    shift_two,
    d_out,
):
    core = lax.axis_index("fsdp")
    ctx = lax.axis_index("ctx")
    ctx_count = lax.axis_size("ctx")
    seqs, block_rows, width = tokens.shape
    pair = width // ctx_count
    flat = seqs * block_rows

    token_pieces = gather_blocks(tokens)

    small = (
        bias_query, bias_value, attention_out_bias, gain_one, shift_one,
        feedforward_in_bias, feedforward_out_bias, gain_two, shift_two,
    )
    small, token_pieces[1] = lax.optimization_barrier((small, token_pieces[1]))
    packed = jnp.concatenate(small)
    packed_other = exchange(packed, "fsdp", 1)
    vectors = []
    offset = 0
    for part in small:
        size = part.shape[0]
        vectors.append(widened(pair_join(part, packed_other[offset : offset + size], core)))
        offset += size
    (
        query_bias, value_bias, out_bias, gain_first, shift_first,
        inner_bias, back_bias, gain_second, shift_second,
    ) = vectors
    qkv_full = pair_join(
        query_key_value_weight, exchange(query_key_value_weight, "fsdp", 1), core
    )
    out_full = pair_join(attention_out_weight, exchange(attention_out_weight, "fsdp", 1), core)
    in_pair = (feedforward_in_weight, exchange(feedforward_in_weight, "fsdp", 1))
    back_pair = (feedforward_out_weight, exchange(feedforward_out_weight, "fsdp", 1))
    core_index = core.astype(jnp.int32).reshape(1)

    head_weight = jnp.concatenate(
        [lax.dynamic_slice_in_dim(qkv_full, t * width + ctx * pair, pair, axis=1) for t in range(3)],
        axis=1,
    )
    head_bias = jnp.concatenate(
        [
            lax.dynamic_slice_in_dim(query_bias, ctx * pair, pair),
            jnp.zeros((pair,), jnp.float32),
            lax.dynamic_slice_in_dim(value_bias, ctx * pair, pair),
        ]
    )
    projected = jnp.concatenate(
        [lowered(project(piece, head_weight) + head_bias) for piece in token_pieces], axis=1
    )
    head_result, head_low, head_logs = attention_forward(projected)

    def row_blocks(values):
        return [
            lax.slice_in_dim(values, k * block_rows, (k + 1) * block_rows, axis=1)
            for k in range(ctx_count)
        ]

    attended_pieces = reorder(swap_blocks(row_blocks(head_low)), ctx)
    attended_low = jnp.concatenate(attended_pieces, axis=-1)
    attention_branch = project(attended_low, out_full) + out_bias
    summed_one = widened(tokens) + attention_branch
    first_normalized, pull_one = jax.vjp(norm_apply, summed_one, gain_first, shift_first)
    normed_low = lowered(first_normalized)
    active_flat, slope, second = ffn_forward(
        core_index, normed_low.reshape(flat, width), in_pair, back_pair, inner_bias[None]
    )
    active_low = active_flat.reshape(seqs, block_rows, -1)
    feedforward_branch = second.reshape(tokens.shape) + back_bias

    def second_norm(residual_in, branch_in, gain_vec, shift_vec):
        return norm_apply(residual_in + branch_in, gain_vec, shift_vec)

    result, pull_two = jax.vjp(
        second_norm, first_normalized, feedforward_branch, gain_second, shift_second
    )
    output = lowered(result)
    first_grad_res, second_grad, gain_two_grad, shift_two_grad = pull_two(widened(d_out))
    second_low = lowered(second_grad)

    def left_pair(values):
        rows = values.reshape(flat, values.shape[2])
        return (half_of(rows, core, 1), exchange(half_of(rows, 1 - core, 1), "fsdp", 1))

    def right_pair(values):
        rows = values.reshape(flat, values.shape[2])
        return (rows, exchange(rows, "fsdp", 1))

    places = {name: place_of(hops(name)) for name in ORDERS}
    count = 1 << len(hops("q"))

    active_pair = left_pair(active_low)
    normed_pair = left_pair(normed_low)
    attended_pair = left_pair(attended_low)
    second_pair = right_pair(second_low)
    back_parts = [
        pair_grad(places[n], active_pair, second_pair, count, part, 2, True, "grad_back")
        for part, n in enumerate(("b0", "b1"))
    ]
    back_bias_grad = column_sum(second_low)
    hidden_flat, first_part = ffn_backward(
        core_index, second_low.reshape(flat, width), slope, in_pair, back_pair
    )
    hidden_low = hidden_flat.reshape(seqs, block_rows, -1)
    hidden_low, back_parts = lax.optimization_barrier((hidden_low, back_parts))
    hidden_pair = right_pair(hidden_low)
    in_bias_grad = column_sum(hidden_low)
    first_grad = first_grad_res + first_part.reshape(tokens.shape)
    summed_grad, gain_one_grad, shift_one_grad = pull_one(first_grad)
    branch_low = lowered(summed_grad)
    branch_pair = right_pair(branch_low)
    out_bias_grad = column_sum(branch_low)
    attended_grad = lowered(back_project(branch_low, out_full))
    column_pieces = reorder(
        [attended_grad[..., k * pair : (k + 1) * pair] for k in range(ctx_count)], ctx
    )
    column_pieces, hidden_pair = lax.optimization_barrier((column_pieces, hidden_pair))
    head_grad_pieces = swap_blocks(column_pieces)
    in_parts = [
        pair_grad(places[n], normed_pair, hidden_pair, count, part, 2, False, "grad_in")
        for part, n in enumerate(("i0", "i1"))
    ]
    branch_pair, in_parts = lax.optimization_barrier((branch_pair, in_parts))
    out_parts = pair_grad(
        places["o"], attended_pair, branch_pair, count, 0, 1, True, "grad_out"
    )

    whole = {"back": None, "in": None, "out": None, "qkv": None}

    def placer(target, names, by_rows):
        def put(chunks, part, far):
            whole[target] = put_in_place(
                places[names[part]], chunks, far, whole[target], part, len(names), by_rows,
                "place_" + target,
            )
            return whole[target]

        return put

    put_out = placer("out", ("o",), True)

    class Placed:
        def __init__(self, target):
            self.target = target

        @property
        def value(self):
            return whole[self.target]

        @value.setter
        def value(self, new):
            whole[self.target] = new

    line = Line()
    chains = {
        "b": Group(line, ("b0", "b1"), back_parts, placer("back", ("b0", "b1"), True)),
        "i": Group(line, ("i0", "i1"), in_parts, placer("in", ("i0", "i1"), False)),
        "o": Reduction(line, "o", *out_parts, lambda chunks, far: put_out(chunks, 0, far)),
    }
    targets = {"b": ("back", 9), "i": ("in", 9), "o": ("out", 8)}
    line.done(chains["o"])

    class Attention:
        def advance(self):
            head_grad = jnp.concatenate(line.after(head_grad_pieces), axis=1)
            self.head_grads = attention_backward(projected, head_grad, head_result, head_logs)
            self.value, other = qkv_grad_parts(core_index, token_pieces, self.head_grads)
            self.other = exchange(other, "fsdp", 1)
            chains["v"].begin(self.head_grads)
            line.done(self)

    layer_vectors = (
        in_bias_grad, back_bias_grad, gain_two_grad, shift_two_grad,
        out_bias_grad, gain_one_grad, shift_one_grad,
    )

    class Vectors:
        def begin(self, head_grads):
            spread_out = []
            for part in (head_grads[0], head_grads[2]):
                spread_out.append(
                    lax.dynamic_update_slice_in_dim(
                        jnp.zeros((width,), jnp.float32), column_sum(part), ctx * pair, 0
                    )
                )
            self.value = jnp.concatenate(layer_vectors + tuple(spread_out))
            self.routes = [("fsdp", 1)] + hops("v")
            self.step = 0
            self.arrived = exchange(self.value, *self.routes[0])

        def advance(self):
            arrived, value = line.after((self.arrived, self.value))
            self.value = value + arrived
            self.step += 1
            if self.step < len(self.routes):
                self.arrived = exchange(self.value, *self.routes[self.step])
            line.done(self)

    class QueryKeyValue:
        def __init__(self):
            self.step = 0

        def advance(self):
            step = self.step
            self.step += 1
            order = hops("q")
            if step == 0:
                other, own = line.after((chains["A"].other, chains["A"].value))
                total = own + widened(other)
                half = total.shape[1] // 2
                low, high = total[:, :half], total[:, half:]
                first = lax.axis_index("dp") == 0
                self.value = jnp.where(first, low, high)
                self.arrived = exchange(lowered(jnp.where(first, high, low)), *order[0])
            elif step == 1:
                arrived, value = line.after((self.arrived, self.value))
                self.value = lowered(value + widened(arrived))[None]
                self.arrived = exchange(self.value, *order[-1])
            elif step <= len(order):
                arrived, value = line.after((self.arrived, self.value))
                self.value = jnp.concatenate([value, arrived], axis=0)
                self.arrived = exchange(self.value, *order[len(order) - step])
                if step == len(order):
                    self.put(self.value, False)
            else:
                arrived, value = line.after((self.arrived, self.value))
                self.value = self.put(arrived, True)
                line.done(Placed("qkv"))
                return
            line.done(self)

        def put(self, chunks, far):
            bits = [bit for axis, bit in hops("q")[1:]]
            whole["qkv"] = put_three_in_place(
                places["q"], chunks, far, whole["qkv"], bits, 2, "place_qkv"
            )
            return whole["qkv"]

    class Tokens:
        def __init__(self):
            self.step = 0

        def advance(self):
            order = hops("T")
            if self.step == 0:
                blocks = [row_blocks(part) for part in chains["A"].head_grads]
                pieces = line.after(
                    [jnp.concatenate([m[k] for m in blocks], axis=-1) for k in range(ctx_count)]
                )
                held = {(0, k): piece for k, piece in enumerate(pieces)}
            else:
                bit = order[self.step - 1][1]
                arrived, kept = line.after((self.arrived, self.value))
                held = dict(zip(self.kept, kept))
                for n, (source, target) in enumerate(self.sent):
                    held[source ^ bit, target ^ bit] = arrived[n]
            if self.step < len(order):
                bit = order[self.step][1]
                self.sent = [key for key in sorted(held) if key[1] & bit]
                self.kept = [key for key in sorted(held) if not key[1] & bit]
                self.arrived = exchange(jnp.stack([held[key] for key in self.sent]), *order[self.step])
                self.value = [held[key] for key in self.kept]
            else:
                mixed = reorder([held[k, 0] for k in range(ctx_count)], ctx)
                mixed_grad = jnp.concatenate(
                    [m[..., t * pair : (t + 1) * pair] for t in range(3) for m in mixed], axis=-1
                )
                self.value = summed_grad + back_project(mixed_grad, qkv_full)
            self.step += 1
            line.done(self)

    chains.update(A=Attention(), v=Vectors(), q=QueryKeyValue(), T=Tokens())
    for name in EVENTS:
        chain = chains[name]
        chain.advance()
        if name in targets and chain.step == targets[name][1]:
            line.done(Placed(targets[name][0]))

    reduced = []
    offset = 0
    sizes = [part.shape[0] for part in layer_vectors] + [width, width]
    for size in sizes:
        reduced.append(half_of(chains["v"].value[offset : offset + size], core, 0))
        offset += size
    token_grad = chains["T"].value
    qkv_grad, in_grad, back_grad, out_grad = (
        whole["qkv"], whole["in"], whole["back"], whole["out"]
    )
    bias_grads = reduced[7:]
    return (
        output,
        token_grad,
        qkv_grad,
        bias_grads[0],
        bias_grads[1],
        out_grad,
        reduced[4],
        reduced[5],
        reduced[6],
        in_grad,
        reduced[0],
        back_grad,
        reduced[1],
        reduced[2],
        reduced[3],
    )


def head_parallel(mesh):
    sizes = [mesh.shape["dp"], mesh.shape["ctx"]]
    return sizes == [2, 8] and mesh.shape["fsdp"] == 2 and 2 * sizes[1] == HEADS


def solution(mesh):
    in_specs = (
        P(("dp", "fsdp"), "ctx", None),
        P("fsdp", None),
        P("fsdp"),
        P("fsdp"),
        P("fsdp", None),
        P("fsdp"),
        P("fsdp"),
        P("fsdp"),
        P("fsdp", None),
        P("fsdp"),
        P("fsdp", None),
        P("fsdp"),
        P("fsdp"),
        P("fsdp"),
        P(("dp", "fsdp"), "ctx", None),
    )
    out_specs = (
        P(("dp", "fsdp"), "ctx", None),
        P(("dp", "fsdp"), "ctx", None),
        P("fsdp", None),
        P("fsdp"),
        P("fsdp"),
        P("fsdp", None),
        P("fsdp"),
        P("fsdp"),
        P("fsdp"),
        P("fsdp", None),
        P("fsdp"),
        P("fsdp", None),
        P("fsdp"),
        P("fsdp"),
        P("fsdp"),
    )
    body = on_device if head_parallel(mesh) else ring_on_device
    return jax.shard_map(
        body, mesh=mesh, in_specs=in_specs, out_specs=out_specs, check_vma=False
    )
```

```python
from functools import partial

import jax
import jax.numpy as jnp
from jax import lax
from jax.experimental import pallas as pl
from jax.experimental.pallas import tpu as pltpu
from jax.sharding import PartitionSpec as P

HEADS = 16
HEAD_DIM = 64


EPSILON = 1e-06


def from_behind(block, axis, distance):
    devices = range(lax.axis_size(axis))
    route = [((i - distance) % len(devices), i) for i in devices]
    return lax.ppermute(block, axis, route)


def norm_apply(values, gain_vec, shift_vec):
    centre = jnp.mean(values, axis=-1, keepdims=True)
    centred = values - centre
    variance = jnp.mean(centred * centred, axis=-1, keepdims=True)
    return centred * lax.rsqrt(variance + EPSILON) * gain_vec + shift_vec


def lowered(values):
    return values.astype(jnp.bfloat16)


def widened(values):
    return values.astype(jnp.float32)


def project(left_operand_rows, right_operand_matrix):
    return jnp.einsum(
        "ugj,jn->ugn", left_operand_rows, right_operand_matrix, preferred_element_type=jnp.float32
    )


def weight_grad(left_operand_rows, gradient_row_block):
    return jnp.einsum(
        "xrb,xrw->bw", left_operand_rows, gradient_row_block, preferred_element_type=jnp.float32
    )


def back_project(gradient_row_block, right_operand_matrix):
    return jnp.einsum(
        "wkb,fb->wkf", gradient_row_block, right_operand_matrix, preferred_element_type=jnp.float32
    )


def column_sum(values):
    return jnp.sum(widened(values), axis=(0, 1))


def split_heads(values):
    return values.reshape(values.shape[0], values.shape[1], HEADS, HEAD_DIM)


def merge_heads(values):
    return values.reshape(values.shape[0], values.shape[1], HEADS * HEAD_DIM)


def split_blocks(values, block_rows):
    seq_count = values.shape[0]
    blocks = values.shape[1] // block_rows
    return jnp.moveaxis(values.reshape(seq_count, blocks, block_rows, values.shape[2]), 1, 0)


def block_scores(query_rows, key_rows):
    scores = jnp.einsum(
        "sqhd,skhd->shqk",
        split_heads(query_rows),
        split_heads(key_rows),
        preferred_element_type=jnp.float32,
    )
    return scores * HEAD_DIM ** (-0.5)


def fold_block(state_now, key_block, value_block, query_rows):
    running_max, running_sum, running_acc = state_now
    scores = block_scores(query_rows, key_block)
    new_max = jnp.maximum(running_max, jnp.max(scores, axis=-1))
    rescale = jnp.exp(running_max - new_max)
    weights = jnp.exp(scores - new_max[..., None])
    new_sum = running_sum * rescale + jnp.sum(weights, axis=-1)
    product = jnp.einsum(
        "shqk,skhd->shqd",
        lowered(weights),
        split_heads(value_block),
        preferred_element_type=jnp.float32,
    )
    return (new_max, new_sum, running_acc * rescale[..., None] + product)


def attend_forward(query_rows, key_rows, value_rows):
    seq_count = query_rows.shape[0]
    block_rows = query_rows.shape[1]
    initial = (
        jnp.full((seq_count, HEADS, block_rows), -1e30, jnp.float32),
        jnp.zeros((seq_count, HEADS, block_rows), jnp.float32),
        jnp.zeros((seq_count, HEADS, block_rows, HEAD_DIM), jnp.float32),
    )
    kept = None
    key_part = lax.all_gather(key_rows, "ctx", axis=1, tiled=True)
    value_part = lax.all_gather(value_rows, "ctx", axis=1, tiled=True)

    def one_block(state_in, block_pair):
        return (fold_block(state_in, block_pair[0], block_pair[1], query_rows), None)

    state_out, unused = lax.scan(
        one_block,
        initial,
        (split_blocks(key_part, block_rows), split_blocks(value_part, block_rows)),
    )
    running_max, running_sum, running_acc = state_out
    attention_result = running_acc / running_sum[..., None]
    attention_result = jnp.transpose(attention_result, (0, 2, 1, 3)).reshape(
        seq_count, block_rows, HEADS * HEAD_DIM
    )
    log_total = running_max + jnp.log(running_sum)
    return (attention_result, log_total, kept)


def attend_back(query_rows, gradient_row_block, log_total, row_inner, key_rows, value_rows):
    score_scale = HEAD_DIM ** (-0.5)
    scores = block_scores(query_rows, key_rows)
    probabilities = jnp.exp(scores - log_total[..., None])
    value_grad = jnp.einsum(
        "shqk,sqhd->skhd",
        lowered(probabilities),
        split_heads(gradient_row_block),
        preferred_element_type=jnp.float32,
    )
    prob_grad = jnp.einsum(
        "sqhd,skhd->shqk",
        split_heads(gradient_row_block),
        split_heads(value_rows),
        preferred_element_type=jnp.float32,
    )
    score_grad = lowered(probabilities * (prob_grad - row_inner[..., None]))
    query_grad = (
        jnp.einsum(
            "shqk,skhd->sqhd", score_grad, split_heads(key_rows), preferred_element_type=jnp.float32
        )
        * score_scale
    )
    key_grad = (
        jnp.einsum(
            "shqk,sqhd->skhd",
            score_grad,
            split_heads(query_rows),
            preferred_element_type=jnp.float32,
        )
        * score_scale
    )
    return (merge_heads(query_grad), merge_heads(key_grad), merge_heads(value_grad))


def attend_backward(query_rows, gradient_row_block, log_total, row_inner, key_rows, value_rows):
    zero_rows = jnp.zeros(query_rows.shape, jnp.float32)
    turn_count = lax.axis_size("ctx") // 2

    def turn_keys(turn_index, carried):
        moving_key, moving_value, key_acc, value_acc, query_acc = carried
        for half_step in range(2):
            pieces = attend_back(
                query_rows, gradient_row_block, log_total, row_inner, moving_key, moving_value
            )
            query_acc = query_acc + pieces[0]
            key_acc = key_acc + pieces[1]
            value_acc = value_acc + pieces[2]
            moving_key, moving_value = from_behind((moving_key, moving_value), "ctx", 1)
            key_acc, value_acc = (
                from_behind(key_acc.astype(jnp.bfloat16), "ctx", 1).astype(key_acc.dtype),
                from_behind(value_acc.astype(jnp.bfloat16), "ctx", 1).astype(value_acc.dtype),
            )
        return (moving_key, moving_value, key_acc, value_acc, query_acc)

    finished = lax.fori_loop(
        0, turn_count, turn_keys, (key_rows, value_rows, zero_rows, zero_rows, zero_rows)
    )
    return (finished[4], finished[2], finished[3])


def ring_on_device(
    tokens,
    query_key_value_weight,
    bias_query,
    bias_value,
    attention_out_weight,
    attention_out_bias,
    gain_one,
    shift_one,
    feedforward_in_weight,
    feedforward_in_bias,
    feedforward_out_weight,
    feedforward_out_bias,
    gain_two,
    shift_two,
    d_out,
):
    attn_full = (
        lax.all_gather(query_key_value_weight, "fsdp", axis=0, tiled=True),
        lax.all_gather(attention_out_weight, "fsdp", axis=0, tiled=True),
        lax.all_gather(bias_query, "fsdp", axis=0, tiled=True),
        lax.all_gather(bias_value, "fsdp", axis=0, tiled=True),
        lax.all_gather(attention_out_bias, "fsdp", axis=0, tiled=True),
        lax.all_gather(gain_one, "fsdp", axis=0, tiled=True),
        lax.all_gather(shift_one, "fsdp", axis=0, tiled=True),
    )
    qkv_full, out_full, query_bias, value_bias, out_bias, gain_first, shift_first = attn_full
    model_width = out_full.shape[0]
    projected_rows = project(tokens, qkv_full) + jnp.concatenate(
        [widened(query_bias), jnp.zeros((model_width,), jnp.float32), widened(value_bias)]
    )
    projected_low = lowered(projected_rows)
    query_rows = projected_low[..., :model_width]
    key_rows = projected_low[..., model_width : 2 * model_width]
    value_rows = projected_low[..., 2 * model_width :]
    attention_result, log_total, kept = attend_forward(query_rows, key_rows, value_rows)
    attended_low = lowered(attention_result)
    attention_branch = project(attended_low, out_full) + widened(out_bias)
    summed_one = widened(tokens) + attention_branch
    first_normalized, pull_one = jax.vjp(
        norm_apply, summed_one, widened(gain_first), widened(shift_first)
    )
    normed_low = lowered(first_normalized)
    ffn_full = (
        lax.all_gather(feedforward_in_weight, "fsdp", axis=0, tiled=True),
        lax.all_gather(feedforward_out_weight, "fsdp", axis=0, tiled=True),
        lax.all_gather(feedforward_in_bias, "fsdp", axis=0, tiled=True),
        lax.all_gather(feedforward_out_bias, "fsdp", axis=0, tiled=True),
        lax.all_gather(gain_two, "fsdp", axis=0, tiled=True),
        lax.all_gather(shift_two, "fsdp", axis=0, tiled=True),
    )
    in_full, back_full, inner_bias, back_bias, gain_second, shift_second = ffn_full
    hidden_before_gelu = project(normed_low, in_full) + widened(inner_bias)
    active_low = lowered(jax.nn.gelu(hidden_before_gelu, approximate=False))
    feedforward_branch = project(active_low, back_full) + widened(back_bias)

    def second_norm(residual_in, branch_in, gain_vec, shift_vec):
        return norm_apply(residual_in + branch_in, gain_vec, shift_vec)

    result, pull_two = jax.vjp(
        second_norm,
        first_normalized,
        feedforward_branch,
        widened(gain_second),
        widened(shift_second),
    )
    output = lowered(result)
    first_grad_res, second_grad, gain_two_grad, shift_two_grad = pull_two(widened(d_out))
    in_full, back_full = (
        lax.all_gather(feedforward_in_weight, "fsdp", axis=0, tiled=True),
        lax.all_gather(feedforward_out_weight, "fsdp", axis=0, tiled=True),
    )
    second_low = lowered(second_grad)
    back_grad = weight_grad(active_low, second_low)
    back_bias_grad = column_sum(second_low)
    active_grad = back_project(second_low, back_full)
    gelu_pull = jax.vjp(partial(jax.nn.gelu, approximate=False), hidden_before_gelu)[1]
    hidden_low = lowered(gelu_pull(active_grad)[0])
    in_grad = weight_grad(normed_low, hidden_low)
    in_bias_grad = column_sum(hidden_low)
    first_grad = first_grad_res + back_project(hidden_low, in_full)
    ffn_grads = (
        lax.psum_scatter(
            in_grad.astype(jnp.bfloat16), "fsdp", scatter_dimension=0, tiled=True
        ).astype(jnp.float32),
        lax.psum_scatter(
            in_bias_grad.astype(jnp.bfloat16), "fsdp", scatter_dimension=0, tiled=True
        ).astype(jnp.float32),
        lax.psum_scatter(
            back_grad.astype(jnp.bfloat16), "fsdp", scatter_dimension=0, tiled=True
        ).astype(jnp.float32),
        lax.psum_scatter(
            back_bias_grad.astype(jnp.bfloat16), "fsdp", scatter_dimension=0, tiled=True
        ).astype(jnp.float32),
        lax.psum_scatter(
            gain_two_grad.astype(jnp.bfloat16), "fsdp", scatter_dimension=0, tiled=True
        ).astype(jnp.float32),
        lax.psum_scatter(
            shift_two_grad.astype(jnp.bfloat16), "fsdp", scatter_dimension=0, tiled=True
        ).astype(jnp.float32),
    )
    ffn_grads = lax.psum(
        (ffn_grads[0], ffn_grads[1], ffn_grads[2], ffn_grads[3], ffn_grads[4], ffn_grads[5]),
        ("dp", "ctx"),
    )
    summed_grad, gain_one_grad, shift_one_grad = pull_one(first_grad)
    qkv_full, out_full = (
        lax.all_gather(query_key_value_weight, "fsdp", axis=0, tiled=True),
        lax.all_gather(attention_out_weight, "fsdp", axis=0, tiled=True),
    )
    branch_low = lowered(summed_grad)
    out_grad = weight_grad(attended_low, branch_low)
    out_bias_grad = column_sum(branch_low)
    attended_grad_low = lowered(back_project(branch_low, out_full))
    row_inner = jnp.sum(
        split_heads(widened(attended_grad_low)) * split_heads(attention_result), axis=-1
    )
    row_inner = jnp.transpose(row_inner, (0, 2, 1))
    query_grad, key_grad, value_grad = attend_backward(
        query_rows, attended_grad_low, log_total, row_inner, key_rows, value_rows
    )
    mixed_grad = lowered(jnp.concatenate([query_grad, key_grad, value_grad], axis=-1))
    qkv_grad = weight_grad(tokens, mixed_grad)
    bias_grads = column_sum(mixed_grad)
    query_bias_grad = bias_grads[:model_width]
    value_bias_grad = bias_grads[2 * model_width :]
    token_grad = summed_grad + back_project(mixed_grad, qkv_full)
    attn_grads = (
        lax.psum_scatter(
            qkv_grad.astype(jnp.bfloat16), "fsdp", scatter_dimension=0, tiled=True
        ).astype(jnp.float32),
        lax.psum_scatter(
            query_bias_grad.astype(jnp.bfloat16), "fsdp", scatter_dimension=0, tiled=True
        ).astype(jnp.float32),
        lax.psum_scatter(
            value_bias_grad.astype(jnp.bfloat16), "fsdp", scatter_dimension=0, tiled=True
        ).astype(jnp.float32),
        lax.psum_scatter(
            out_grad.astype(jnp.bfloat16), "fsdp", scatter_dimension=0, tiled=True
        ).astype(jnp.float32),
        lax.psum_scatter(
            out_bias_grad.astype(jnp.bfloat16), "fsdp", scatter_dimension=0, tiled=True
        ).astype(jnp.float32),
        lax.psum_scatter(
            gain_one_grad.astype(jnp.bfloat16), "fsdp", scatter_dimension=0, tiled=True
        ).astype(jnp.float32),
        lax.psum_scatter(
            shift_one_grad.astype(jnp.bfloat16), "fsdp", scatter_dimension=0, tiled=True
        ).astype(jnp.float32),
    )
    attn_grads = lax.psum(
        (
            attn_grads[0],
            attn_grads[1],
            attn_grads[2],
            attn_grads[3],
            attn_grads[4],
            attn_grads[5],
            attn_grads[6],
        ),
        ("dp", "ctx"),
    )
    return (
        output,
        token_grad,
        attn_grads[0],
        attn_grads[1],
        attn_grads[2],
        attn_grads[3],
        attn_grads[4],
        attn_grads[5],
        attn_grads[6],
        ffn_grads[0],
        ffn_grads[1],
        ffn_grads[2],
        ffn_grads[3],
        ffn_grads[4],
        ffn_grads[5],
    )


def exchange(values, axis, bit):
    count = lax.axis_size(axis)
    return lax.ppermute(values, axis, [(i, i ^ bit) for i in range(count)])


def bits_below(count):
    return [1 << k for k in range(count.bit_length() - 1)]


def reorder(pieces, index):
    for bit in bits_below(len(pieces)):
        taken = (index & bit) != 0
        pieces = [jnp.where(taken, pieces[k ^ bit], pieces[k]) for k in range(len(pieces))]
    return pieces


def pair_join(own, other, core, axis=0):
    first = jnp.where(core == 0, own, other)
    second = jnp.where(core == 0, other, own)
    return jnp.concatenate([first, second], axis=axis)


def half_of(values, which, axis):
    size = values.shape[axis] // 2
    low = lax.slice_in_dim(values, 0, size, axis=axis)
    high = lax.slice_in_dim(values, size, 2 * size, axis=axis)
    return jnp.where(which == 0, low, high)


def gather_first(block):
    near, middle, far = (exchange(block, "ctx", bit) for bit in (1, 2, 4))
    return near, middle, far


def gather_rest(block, first, use):
    near, (middle, far) = first[0], lax.optimization_barrier(first[1:])
    third = exchange(middle, "ctx", 1)
    sixth = exchange(far, "ctx", 2)
    fifth = exchange(far, "ctx", 1)
    used = [use(piece) for piece in (block, near, middle, far)]
    third, fifth, sixth, used = lax.optimization_barrier((third, fifth, sixth, used))
    seventh = exchange(sixth, "ctx", 1)
    pieces = [block, near, middle, third, far, fifth, sixth, seventh]
    used = {0: used[0], 1: used[1], 2: used[2], 4: used[3]}
    for k in (3, 5, 6, 7):
        used[k] = use(pieces[k])
    return pieces, [used[k] for k in range(8)]


def swap_blocks(pieces):
    return [pieces[0]] + [exchange(pieces[k], "ctx", k) for k in range(1, len(pieces))]


def head_mask(value):
    lane = lax.broadcasted_iota(jnp.int32, (1, 2 * HEAD_DIM), 1)
    return [
        jnp.where(lane < HEAD_DIM, value, 0.0),
        jnp.where(lane < HEAD_DIM, 0.0, value),
    ]


def contract(left, right, left_dim, right_dim):
    return lax.dot_general(
        left, right, (((left_dim,), (right_dim,)), ((), ())), preferred_element_type=jnp.float32
    )


def project_kernel(block_ref, weight_ref, bias_ref, out_ref):
    for s in range(block_ref.shape[0]):
        out_ref[s] = (contract(block_ref[s], weight_ref[...], 1, 0) + bias_ref[...]).astype(
            jnp.bfloat16
        )


def project_block(block, weight, bias):
    shape = block.shape[:2] + (weight.shape[1],)
    return pl.pallas_call(
        project_kernel,
        out_shape=jax.ShapeDtypeStruct(shape, jnp.bfloat16),
        compiler_params=pltpu.CompilerParams(vmem_limit_bytes=40 << 20),
        name="project_block",
    )(block, weight, bias)


def forward_kernel(query_ref, key_ref, value_ref, result_ref, low_ref, log_ref):
    query = query_ref[0].astype(jnp.float32)
    keys = key_ref[0]
    values = value_ref[0]
    results = []
    logs = []
    for mask in head_mask(HEAD_DIM ** (-0.5)):
        scores = contract((query * mask).astype(jnp.bfloat16), keys, 1, 1)
        row_max = jnp.max(scores, axis=-1, keepdims=True)
        weights = jnp.exp(scores - row_max)
        total = jnp.sum(weights, axis=-1, keepdims=True)
        probabilities = (weights * (1.0 / total)).astype(jnp.bfloat16)
        results.append(contract(probabilities, values, 1, 0))
        logs.append(row_max + jnp.log(total))
    first = lax.broadcasted_iota(jnp.int32, results[0].shape, 1) < HEAD_DIM
    result = jnp.where(first, results[0], results[1])
    result_ref[0] = result
    low_ref[0] = result.astype(jnp.bfloat16)
    log_ref[0] = jnp.where(first, logs[0], logs[1])


def attention_forward(projected):
    seqs, length, width = projected.shape
    pair = width // 3
    rows = min(256, length)
    row_spec = pl.BlockSpec((1, rows, pair), lambda s, q: (s, q, 0))
    return pl.pallas_call(
        forward_kernel,
        grid=(seqs, length // rows),
        in_specs=[
            row_spec,
            pl.BlockSpec((1, length, pair), lambda s, q: (s, 0, 1)),
            pl.BlockSpec((1, length, pair), lambda s, q: (s, 0, 2)),
        ],
        out_specs=[row_spec, row_spec, row_spec],
        out_shape=[
            jax.ShapeDtypeStruct((seqs, length, pair), jnp.float32),
            jax.ShapeDtypeStruct((seqs, length, pair), jnp.bfloat16),
            jax.ShapeDtypeStruct((seqs, length, pair), jnp.float32),
        ],
        compiler_params=pltpu.CompilerParams(vmem_limit_bytes=48 << 20),
        name="attention_forward",
    )(projected, projected, projected)


def backward_kernel(
    query_ref, key_ref, value_ref, grad_ref, result_ref, log_ref,
    query_out, key_out, value_out, query_acc, log_rows, inner_rows,
):
    step = pl.program_id(1)

    @pl.when(step == 0)
    def first_step():
        query_acc[...] = jnp.zeros_like(query_acc)
        logs = jnp.transpose(log_ref[0])
        inner = jnp.transpose(grad_ref[0].astype(jnp.float32) * result_ref[0])
        for h in range(2):
            log_rows[h] = jnp.broadcast_to(
                logs[h * HEAD_DIM : h * HEAD_DIM + 1], log_rows.shape[1:]
            )
            inner_rows[h] = jnp.broadcast_to(
                jnp.sum(inner[h * HEAD_DIM : (h + 1) * HEAD_DIM], axis=0, keepdims=True),
                inner_rows.shape[1:],
            )

    queries = query_ref[0]
    grads = grad_ref[0]
    keys = key_ref[0]
    values = value_ref[0]
    scale = HEAD_DIM ** (-0.5)
    query_parts = []
    key_parts = []
    value_parts = []
    scaled_masks = head_mask(scale)
    masks = head_mask(1.0)
    for h in range(2):
        scores = contract(
            (keys.astype(jnp.float32) * scaled_masks[h]).astype(jnp.bfloat16), queries, 1, 1
        )
        probabilities = jnp.exp(scores - log_rows[h, :1])
        prob_grad = contract(
            (values.astype(jnp.float32) * masks[h]).astype(jnp.bfloat16), grads, 1, 1
        )
        score_grad = (probabilities * (prob_grad - inner_rows[h, :1])).astype(jnp.bfloat16)
        value_parts.append(contract(probabilities.astype(jnp.bfloat16), grads, 1, 0))
        key_parts.append(contract(score_grad, queries, 1, 0))
        query_parts.append(contract(score_grad, keys, 0, 0))
    first = lax.broadcasted_iota(jnp.int32, key_parts[0].shape, 1) < HEAD_DIM
    value_out[0] = jnp.where(first, value_parts[0], value_parts[1]).astype(jnp.bfloat16)
    key_out[0] = (jnp.where(first, key_parts[0], key_parts[1]) * scale).astype(jnp.bfloat16)
    first = lax.broadcasted_iota(jnp.int32, query_parts[0].shape, 1) < HEAD_DIM
    query_acc[...] += jnp.where(first, query_parts[0], query_parts[1])

    @pl.when(step == pl.num_programs(1) - 1)
    def last_step():
        query_out[0] = (query_acc[...] * scale).astype(jnp.bfloat16)


def attention_backward(projected, grads, result, logs):
    seqs, length, width = projected.shape
    pair = width // 3
    rows = min(256, length)
    whole = pl.BlockSpec((1, length, pair), lambda s, k: (s, 0, 0))
    block = pl.BlockSpec((1, rows, pair), lambda s, k: (s, k, 0))
    shape = jax.ShapeDtypeStruct((seqs, length, pair), jnp.bfloat16)
    return pl.pallas_call(
        backward_kernel,
        grid=(seqs, length // rows),
        in_specs=[
            whole,
            pl.BlockSpec((1, rows, pair), lambda s, k: (s, k, 1)),
            pl.BlockSpec((1, rows, pair), lambda s, k: (s, k, 2)),
            whole,
            whole,
            whole,
        ],
        out_specs=[whole, block, block],
        out_shape=[shape, shape, shape],
        scratch_shapes=[
            pltpu.VMEM((length, pair), jnp.float32),
            pltpu.VMEM((2, 8, length), jnp.float32),
            pltpu.VMEM((2, 8, length), jnp.float32),
        ],
        compiler_params=pltpu.CompilerParams(vmem_limit_bytes=48 << 20),
        name="attention_backward",
    )(projected, projected, projected, grads, result, logs)


def ffn_forward_kernel(
    core_ref, left_own, left_other, in_own, in_other, bias_ref, back_own, back_other,
    active_ref, slope_ref, second_ref,
):
    step = pl.program_id(0)
    hidden = contract(left_own[...], in_own[...], 1, 0)
    hidden = hidden + contract(left_other[...], in_other[...], 1, 0) + bias_ref[...]
    below = 0.5 * (1.0 + lax.erf(hidden * 0.7071067811865476))
    slope = below + hidden * (jnp.exp(-0.5 * hidden * hidden) * 0.3989422804014327)
    active = (hidden * below).astype(jnp.bfloat16)
    active_ref[...] = active
    slope_ref[...] = slope.astype(jnp.bfloat16)

    @pl.when(step == 0)
    def first():
        second_ref[...] = contract(active, back_own[...], 1, 0)

    @pl.when((step > 0) & (step < pl.num_programs(0) // 2))
    def own():
        second_ref[...] += contract(active, back_own[...], 1, 0)

    @pl.when(step >= pl.num_programs(0) // 2)
    def other():
        second_ref[...] += contract(active, back_other[...], 1, 0)


def ffn_specs(half, block, width, hidden):
    near = hidden // (2 * block)

    def spot(s, p):
        return jnp.where(s < near, s + p[0] * near, s - p[0] * near)

    weights = [
        pl.BlockSpec((half, block), lambda s, p: (0, spot(s, p))),
        pl.BlockSpec((half, block), lambda s, p: (0, spot(s, p))),
        pl.BlockSpec((block, width), lambda s, p: (jnp.minimum(s, near - 1), 0)),
        pl.BlockSpec((block, width), lambda s, p: (jnp.maximum(s - near, 0), 0)),
    ]
    return spot, weights


def ffn_forward(core, left, in_pair, back_pair, bias):
    tokens, width = left.shape
    half, hidden = in_pair[0].shape
    block = 1024
    spot, weights = ffn_specs(half, block, width, hidden)
    wide = pl.BlockSpec((tokens, block), lambda s, p: (0, spot(s, p)))
    return pl.pallas_call(
        ffn_forward_kernel,
        grid_spec=pltpu.PrefetchScalarGridSpec(
            num_scalar_prefetch=1,
            grid=(hidden // block,),
            in_specs=[
                pl.BlockSpec((tokens, half), lambda s, p: (0, p[0])),
                pl.BlockSpec((tokens, half), lambda s, p: (0, 1 - p[0])),
                weights[0],
                weights[1],
                pl.BlockSpec((1, block), lambda s, p: (0, spot(s, p))),
                weights[2],
                weights[3],
            ],
            out_specs=[wide, wide, pl.BlockSpec((tokens, width), lambda s, p: (0, 0))],
        ),
        out_shape=[
            jax.ShapeDtypeStruct((tokens, hidden), jnp.bfloat16),
            jax.ShapeDtypeStruct((tokens, hidden), jnp.bfloat16),
            jax.ShapeDtypeStruct((tokens, width), jnp.float32),
        ],
        compiler_params=pltpu.CompilerParams(vmem_limit_bytes=40 << 20),
        name="ffn_forward",
    )(core, left, left, *in_pair, bias, *back_pair)


def ffn_backward_kernel(
    core_ref, grad_ref, slope_ref, in_own, in_other, back_own, back_other,
    hidden_ref, total_ref, own_acc, other_acc,
):
    step = pl.program_id(0)
    half = own_acc.shape[1]

    def rest(back_ref):
        active_grad = contract(grad_ref[...], back_ref[...], 1, 1)
        hidden = (active_grad * slope_ref[...].astype(jnp.float32)).astype(jnp.bfloat16)
        hidden_ref[...] = hidden
        own = contract(hidden, in_own[...], 1, 1)
        other = contract(hidden, in_other[...], 1, 1)

        @pl.when(step == 0)
        def first():
            own_acc[...] = own
            other_acc[...] = other

        @pl.when(step > 0)
        def later():
            own_acc[...] += own
            other_acc[...] += other

    @pl.when(step < pl.num_programs(0) // 2)
    def with_own():
        rest(back_own)

    @pl.when(step >= pl.num_programs(0) // 2)
    def with_other():
        rest(back_other)

    @pl.when(step == pl.num_programs(0) - 1)
    def last():
        @pl.when(core_ref[0] == 0)
        def straight():
            total_ref[:, :half] = own_acc[...]
            total_ref[:, half:] = other_acc[...]

        @pl.when(core_ref[0] != 0)
        def crossed():
            total_ref[:, :half] = other_acc[...]
            total_ref[:, half:] = own_acc[...]


def ffn_backward(core, grad, slope, in_pair, back_pair):
    tokens, width = grad.shape
    half, hidden = in_pair[0].shape
    block = 1024
    spot, weights = ffn_specs(half, block, width, hidden)
    wide = pl.BlockSpec((tokens, block), lambda s, p: (0, spot(s, p)))
    whole = pl.BlockSpec((tokens, width), lambda s, p: (0, 0))
    return pl.pallas_call(
        ffn_backward_kernel,
        grid_spec=pltpu.PrefetchScalarGridSpec(
            num_scalar_prefetch=1,
            grid=(hidden // block,),
            in_specs=[whole, wide, *weights],
            out_specs=[wide, whole],
            scratch_shapes=[
                pltpu.VMEM((tokens, half), jnp.float32),
                pltpu.VMEM((tokens, half), jnp.float32),
            ],
        ),
        out_shape=[
            jax.ShapeDtypeStruct((tokens, hidden), jnp.bfloat16),
            jax.ShapeDtypeStruct((tokens, width), jnp.float32),
        ],
        compiler_params=pltpu.CompilerParams(vmem_limit_bytes=40 << 20),
        name="ffn_backward",
    )(core, grad, slope, *in_pair, *back_pair)


def qkv_grad_kernel(core_ref, *refs, pieces):
    token_refs, grad_refs = refs[:pieces], refs[pieces : pieces + 3]
    own_ref, other_ref = refs[pieces + 3 :]
    seqs = token_refs[0].shape[0]
    rows = jnp.concatenate([ref[s] for s in range(seqs) for ref in token_refs], axis=0)
    parts = []
    for ref in grad_refs:
        grads = jnp.concatenate([ref[s] for s in range(seqs)], axis=0)
        parts.append(contract(rows, grads, 0, 0))
    half = pl.num_programs(0) // 2

    @pl.when(pl.program_id(0) < half)
    def outgoing():
        for t in range(3):
            other_ref[t] = parts[t].astype(jnp.bfloat16)

    @pl.when(pl.program_id(0) >= half)
    def kept():
        for t in range(3):
            own_ref[t] = parts[t]


def qkv_grad_parts(core, token_pieces, head_grads):
    seqs, rows, width = token_pieces[0].shape
    pair = head_grads[0].shape[2]
    cols = 256
    steps = width // cols
    half = steps // 2

    def spot(s, p):
        return jnp.where(s < half, s + (1 - p[0]) * half, s - half + p[0] * half)

    grads = pl.BlockSpec(head_grads[0].shape, lambda s, p: (0, 0, 0))
    return pl.pallas_call(
        partial(qkv_grad_kernel, pieces=len(token_pieces)),
        grid_spec=pltpu.PrefetchScalarGridSpec(
            num_scalar_prefetch=1,
            grid=(steps,),
            in_specs=[pl.BlockSpec((seqs, rows, cols), lambda s, p: (0, 0, spot(s, p)))]
            * len(token_pieces)
            + [grads] * 3,
            out_specs=[
                pl.BlockSpec((3, cols, pair), lambda s, p: (0, jnp.maximum(s - half, 0), 0)),
                pl.BlockSpec((3, cols, pair), lambda s, p: (0, jnp.minimum(s, half - 1), 0)),
            ],
        ),
        out_shape=[
            jax.ShapeDtypeStruct((3, width // 2, pair), jnp.float32),
            jax.ShapeDtypeStruct((3, width // 2, pair), jnp.bfloat16),
        ],
        compiler_params=pltpu.CompilerParams(vmem_limit_bytes=40 << 20),
        name="grad_qkv",
    )(core, *token_pieces, *head_grads)


LOW = 2


def grad_kernel(place_ref, left_own, left_other, right_own, right_other, keep_ref, send_ref, *, by_rows):
    step = pl.program_id(0)
    half = pl.num_programs(0) // 2
    total = contract(left_own[...], right_own[...], 0, 0)
    total = total + contract(left_other[...], right_other[...], 0, 0)
    total = total.astype(jnp.bfloat16)
    low = place_ref[0] & ((1 << LOW) - 1)
    _, rows, cols = keep_ref.shape

    def put(out_ref):
        for j in range(1 << LOW):
            if by_rows:
                out_ref[j ^ low] = total[j * rows : (j + 1) * rows]
            else:
                out_ref[j ^ low] = total[:, j * cols : (j + 1) * cols]

    @pl.when(step < half)
    def outgoing():
        put(send_ref)

    @pl.when(step >= half)
    def kept():
        put(keep_ref)


def pair_grad(place, left_pair, right_pair, count, part, parts, by_rows, name):
    tokens, width = left_pair[0].shape
    columns = right_pair[0].shape[1]
    steps = count >> LOW
    half = steps // 2

    def block(step, place_ref):
        return part * steps + (((step + half) % steps) ^ (place_ref[0] >> LOW))

    if by_rows:
        rows, cols = width // (parts * count), columns
        left = pl.BlockSpec((tokens, rows << LOW), lambda s, p: (0, block(s, p)))
        right = pl.BlockSpec((tokens, columns), lambda s, p: (0, 0))
    else:
        rows, cols = width, columns // (parts * count)
        left = pl.BlockSpec((tokens, width), lambda s, p: (0, 0))
        right = pl.BlockSpec((tokens, cols << LOW), lambda s, p: (0, block(s, p)))
    shape = jax.ShapeDtypeStruct((count // 2, rows, cols), jnp.bfloat16)
    out_block = (1 << LOW, rows, cols)
    return pl.pallas_call(
        partial(grad_kernel, by_rows=by_rows),
        grid_spec=pltpu.PrefetchScalarGridSpec(
            num_scalar_prefetch=1,
            grid=(steps,),
            in_specs=[left, left, right, right],
            out_specs=[
                pl.BlockSpec(out_block, lambda s, p: (jnp.maximum(s - half, 0), 0, 0)),
                pl.BlockSpec(out_block, lambda s, p: (jnp.minimum(s, half - 1), 0, 0)),
            ],
        ),
        out_shape=[shape, shape],
        compiler_params=pltpu.CompilerParams(vmem_limit_bytes=48 << 20),
        name=name,
    )(place, left_pair[0], left_pair[1], right_pair[0], right_pair[1])


def place_of(order):
    place = jnp.int32(0)
    for axis, bit in order:
        place = place * 2 + jnp.where((lax.axis_index(axis) & bit) != 0, 1, 0)
    return place.astype(jnp.int32).reshape(1)


def added(first, second):
    return lowered(widened(first) + widened(second))


LINKS = {"x": ("dp", 1), "y": ("ctx", 1), "p": ("ctx", 2), "r": ("ctx", 4)}
ORDERS = {"b0": "pyrx", "b1": "yprx", "i0": "xypr", "i1": "yxpr", "o": "rxpy", "q": "xypr", "v": "xypr", "T": "ypr"}
EVENTS = (
    "b", "A", "i", "q", "o", "b", "i", "q", "v", "o", "v", "b", "i", "v", "o", "q",
    "b", "o", "v", "i", "T", "o", "q", "b", "v", "o", "i", "T", "o", "b", "i", "q",
    "T", "i", "o", "b", "q", "T", "i", "b",
)


def hops(name):
    return [LINKS[letter] for letter in ORDERS[name]]


class Line:
    def __init__(self):
        self.last = None

    def after(self, values):
        if self.last is None:
            return values
        values, self.last.value = lax.optimization_barrier((values, self.last.value))
        return values

    def done(self, holder):
        self.last = holder


class Held:
    def __init__(self, value):
        self.value = value


class Reduction:
    def __init__(self, line, name, keep, send, put):
        self.line, self.order, self.put = line, hops(name), put
        self.value, self.step = keep, 0
        self.arrived = exchange(send, *self.order[0])

    def advance(self):
        last = len(self.order) - 1
        step = self.step
        self.step += 1
        arrived, value = self.line.after((self.arrived, self.value))
        if step < last:
            half = value.shape[0] // 2
            send = added(value[half:], arrived[half:])
            self.value = added(value[:half], arrived[:half])
            self.arrived = exchange(send, *self.order[step + 1])
        elif step == last:
            self.value = added(value, arrived)
            self.arrived = exchange(self.value, *self.order[last])
        elif step <= 2 * last:
            self.value = jnp.concatenate([value, arrived], axis=0)
            self.arrived = exchange(self.value, *self.order[2 * last - step])
            if step == 2 * last:
                self.put(self.value, False)
        else:
            self.value = self.put(arrived, True)
        self.line.done(self)


class Group:
    def __init__(self, line, names, parts, put):
        self.line, self.put, self.step = line, put, 1
        self.orders = [hops(name) for name in names]
        self.value = [keep for keep, send in parts]
        self.arrived = [exchange(send, *o[0]) for (keep, send), o in zip(parts, self.orders)]

    def advance(self):
        arrived, value = self.line.after((self.arrived, self.value))
        tail = self.orders[0][2:]
        step = self.step
        self.step += 1
        if step == 1:
            self.arrived = [
                exchange(added(v[v.shape[0] // 2 :], a[v.shape[0] // 2 :]), *o[1])
                for v, a, o in zip(value, arrived, self.orders)
            ]
            self.value = [
                added(v[: v.shape[0] // 2], a[: v.shape[0] // 2]) for v, a in zip(value, arrived)
            ]
        elif step == 2:
            total = jnp.stack([added(v, a) for v, a in zip(value, arrived)], axis=1)
            self.value = total[:2]
            self.arrived = exchange(total[2:], *tail[0])
        elif step == 3:
            self.value = added(value[:1], arrived[:1])
            self.arrived = exchange(added(value[1:], arrived[1:]), *tail[1])
        elif step == 4:
            self.value = added(value, arrived)
            self.arrived = exchange(self.value, *tail[1])
        elif step == 5:
            self.value = jnp.concatenate([value, arrived], axis=0)
            self.arrived = exchange(self.value, *tail[0])
        elif step == 6:
            total = jnp.concatenate([value, arrived], axis=0)
            self.value = [total[:, 0], total[:, 1]]
            self.arrived = [exchange(v, *o[1]) for v, o in zip(self.value, self.orders)]
        elif step == 7:
            self.value = [jnp.concatenate([v, a], axis=0) for v, a in zip(value, arrived)]
            self.arrived = [exchange(v, *o[0]) for v, o in zip(self.value, self.orders)]
            for part, chunks in enumerate(self.value):
                self.put(chunks, part, False)
        else:
            for part, chunks in enumerate(arrived):
                self.value = self.put(chunks, part, True)
        self.line.done(self)


def place_kernel(place_ref, chunks_ref, *rest, by_rows):
    out_ref = rest[-1]
    low = place_ref[0] & ((1 << LOW) - 1)
    _, rows, cols = chunks_ref.shape
    for j in range(1 << LOW):
        values = chunks_ref[j ^ low].astype(jnp.float32)
        if by_rows:
            out_ref[j * rows : (j + 1) * rows, :] = values
        else:
            out_ref[:, j * cols : (j + 1) * cols] = values


def put_in_place(place, chunks, far, into, part, parts, by_rows, name):
    half, rows, cols = chunks.shape
    steps = half >> LOW
    first = steps if far else 0

    def block(step, place_ref):
        return part * 2 * steps + ((step + first) ^ (place_ref[0] >> LOW))

    if by_rows:
        out_shape = (rows * 2 * half * parts, cols)
        out_spec = pl.BlockSpec((rows << LOW, cols), lambda s, p: (block(s, p), 0))
    else:
        out_shape = (rows, cols * 2 * half * parts)
        out_spec = pl.BlockSpec((rows, cols << LOW), lambda s, p: (0, block(s, p)))
    in_specs = [pl.BlockSpec((1 << LOW, rows, cols), lambda s, p: (s, 0, 0))]
    operands = [place, chunks]
    if into is not None:
        in_specs.append(pl.BlockSpec(memory_space=pl.ANY))
        operands.append(into)
    return pl.pallas_call(
        partial(place_kernel, by_rows=by_rows),
        grid_spec=pltpu.PrefetchScalarGridSpec(
            num_scalar_prefetch=1, grid=(steps,), in_specs=in_specs, out_specs=out_spec
        ),
        out_shape=jax.ShapeDtypeStruct(out_shape, jnp.float32),
        input_output_aliases={} if into is None else {2: 0},
        compiler_params=pltpu.CompilerParams(vmem_limit_bytes=48 << 20),
        name=name,
    )(*operands)


def place_three_kernel(place_ref, chunks_ref, *rest, bits):
    out_ref = rest[-1]
    count, _, _, cols = chunks_ref.shape
    low = place_ref[0] & (count - 1)
    for j in range(count):
        spot = sum(((j // bit) & 1) << (len(bits) - 1 - k) for k, bit in enumerate(bits))
        out_ref[:, j * cols : (j + 1) * cols] = chunks_ref[spot ^ low, 0].astype(jnp.float32)


def put_three_in_place(place, chunks, far, into, bits, dp_count, name):
    total, three, rows, cols = chunks.shape
    ctx_count = 1 << len(bits)
    steps = total // ctx_count
    first = steps if far else 0
    in_specs = [pl.BlockSpec((ctx_count, 1, rows, cols), lambda s, t, p: (s, t, 0, 0))]
    operands = [place, chunks]
    if into is not None:
        in_specs.append(pl.BlockSpec(memory_space=pl.ANY))
        operands.append(into)
    return pl.pallas_call(
        partial(place_three_kernel, bits=bits),
        grid_spec=pltpu.PrefetchScalarGridSpec(
            num_scalar_prefetch=1,
            grid=(steps, three),
            in_specs=in_specs,
            out_specs=pl.BlockSpec(
                (rows, ctx_count * cols),
                lambda s, t, p: ((s + first) ^ (p[0] >> len(bits)), t),
            ),
        ),
        out_shape=jax.ShapeDtypeStruct((rows * dp_count, three * ctx_count * cols), jnp.float32),
        input_output_aliases={} if into is None else {2: 0},
        compiler_params=pltpu.CompilerParams(vmem_limit_bytes=48 << 20),
        name=name,
    )(*operands)


def on_device(
    tokens,
    query_key_value_weight,
    bias_query,
    bias_value,
    attention_out_weight,
    attention_out_bias,
    gain_one,
    shift_one,
    feedforward_in_weight,
    feedforward_in_bias,
    feedforward_out_weight,
    feedforward_out_bias,
    gain_two,
    shift_two,
    d_out,
):
    core = lax.axis_index("fsdp")
    ctx = lax.axis_index("ctx")
    ctx_count = lax.axis_size("ctx")
    seqs, block_rows, width = tokens.shape
    pair = width // ctx_count
    flat = seqs * block_rows

    first_pieces = gather_first(tokens)

    small = (
        bias_query, bias_value, attention_out_bias, gain_one, shift_one,
        feedforward_in_bias, feedforward_out_bias, gain_two, shift_two,
    )
    small, near_piece = lax.optimization_barrier((small, first_pieces[0]))
    first_pieces = (near_piece,) + first_pieces[1:]
    packed = jnp.concatenate(small)
    packed_other = exchange(packed, "fsdp", 1)
    vectors = []
    offset = 0
    for part in small:
        size = part.shape[0]
        vectors.append(widened(pair_join(part, packed_other[offset : offset + size], core)))
        offset += size
    (
        query_bias, value_bias, out_bias, gain_first, shift_first,
        inner_bias, back_bias, gain_second, shift_second,
    ) = vectors
    qkv_full = pair_join(
        query_key_value_weight, exchange(query_key_value_weight, "fsdp", 1), core
    )
    out_full = pair_join(attention_out_weight, exchange(attention_out_weight, "fsdp", 1), core)
    in_pair = (feedforward_in_weight, exchange(feedforward_in_weight, "fsdp", 1))
    back_pair = (feedforward_out_weight, exchange(feedforward_out_weight, "fsdp", 1))
    core_index = core.astype(jnp.int32).reshape(1)

    head_weight = jnp.concatenate(
        [lax.dynamic_slice_in_dim(qkv_full, t * width + ctx * pair, pair, axis=1) for t in range(3)],
        axis=1,
    )
    head_bias = jnp.concatenate(
        [
            lax.dynamic_slice_in_dim(query_bias, ctx * pair, pair),
            jnp.zeros((pair,), jnp.float32),
            lax.dynamic_slice_in_dim(value_bias, ctx * pair, pair),
        ]
    )
    token_pieces, projected_pieces = gather_rest(
        tokens, first_pieces, lambda piece: project_block(piece, head_weight, head_bias[None])
    )
    projected = jnp.concatenate(projected_pieces, axis=1)
    head_result, head_low, head_logs = attention_forward(projected)

    def row_blocks(values):
        return [
            lax.slice_in_dim(values, k * block_rows, (k + 1) * block_rows, axis=1)
            for k in range(ctx_count)
        ]

    attended_pieces = reorder(swap_blocks(row_blocks(head_low)), ctx)
    attended_low = jnp.concatenate(attended_pieces, axis=-1)
    attention_branch = project(attended_low, out_full) + out_bias
    summed_one = widened(tokens) + attention_branch
    first_normalized, pull_one = jax.vjp(norm_apply, summed_one, gain_first, shift_first)
    normed_low = lowered(first_normalized)
    active_flat, slope, second = ffn_forward(
        core_index, normed_low.reshape(flat, width), in_pair, back_pair, inner_bias[None]
    )
    active_low = active_flat.reshape(seqs, block_rows, -1)
    feedforward_branch = second.reshape(tokens.shape) + back_bias

    def second_norm(residual_in, branch_in, gain_vec, shift_vec):
        return norm_apply(residual_in + branch_in, gain_vec, shift_vec)

    result, pull_two = jax.vjp(
        second_norm, first_normalized, feedforward_branch, gain_second, shift_second
    )
    output = lowered(result)
    first_grad_res, second_grad, gain_two_grad, shift_two_grad = pull_two(widened(d_out))
    second_low = lowered(second_grad)

    def left_pair(values):
        rows = values.reshape(flat, values.shape[2])
        return (half_of(rows, core, 1), exchange(half_of(rows, 1 - core, 1), "fsdp", 1))

    def right_pair(values):
        rows = values.reshape(flat, values.shape[2])
        return (rows, exchange(rows, "fsdp", 1))

    places = {name: place_of(hops(name)) for name in ORDERS}
    count = 1 << len(hops("q"))

    active_pair = left_pair(active_low)
    normed_pair = left_pair(normed_low)
    attended_pair = left_pair(attended_low)
    second_pair = right_pair(second_low)
    back_parts = [
        pair_grad(places[n], active_pair, second_pair, count, part, 2, True, "grad_back")
        for part, n in enumerate(("b0", "b1"))
    ]
    back_bias_grad = column_sum(second_low)
    hidden_flat, first_part = ffn_backward(
        core_index, second_low.reshape(flat, width), slope, in_pair, back_pair
    )
    hidden_low = hidden_flat.reshape(seqs, block_rows, -1)
    hidden_low, back_parts = lax.optimization_barrier((hidden_low, back_parts))
    hidden_pair = right_pair(hidden_low)
    in_bias_grad = column_sum(hidden_low)
    first_grad = first_grad_res + first_part.reshape(tokens.shape)
    summed_grad, gain_one_grad, shift_one_grad = pull_one(first_grad)
    branch_low = lowered(summed_grad)
    branch_pair = right_pair(branch_low)
    out_bias_grad = column_sum(branch_low)
    attended_grad = lowered(back_project(branch_low, out_full))
    column_pieces = reorder(
        [attended_grad[..., k * pair : (k + 1) * pair] for k in range(ctx_count)], ctx
    )
    column_pieces, hidden_pair = lax.optimization_barrier((column_pieces, hidden_pair))
    head_grad_pieces = swap_blocks(column_pieces)
    in_parts = [
        pair_grad(places[n], normed_pair, hidden_pair, count, part, 2, False, "grad_in")
        for part, n in enumerate(("i0", "i1"))
    ]
    branch_pair, in_parts = lax.optimization_barrier((branch_pair, in_parts))
    out_parts = pair_grad(
        places["o"], attended_pair, branch_pair, count, 0, 1, True, "grad_out"
    )

    whole = {"back": None, "in": None, "out": None, "qkv": None}

    def placer(target, names, by_rows):
        def put(chunks, part, far):
            whole[target] = put_in_place(
                places[names[part]], chunks, far, whole[target], part, len(names), by_rows,
                "place_" + target,
            )
            return whole[target]

        return put

    put_out = placer("out", ("o",), True)

    class Placed:
        def __init__(self, target):
            self.target = target

        @property
        def value(self):
            return whole[self.target]

        @value.setter
        def value(self, new):
            whole[self.target] = new

    line = Line()
    chains = {
        "b": Group(line, ("b0", "b1"), back_parts, placer("back", ("b0", "b1"), True)),
        "i": Group(line, ("i0", "i1"), in_parts, placer("in", ("i0", "i1"), False)),
        "o": Reduction(line, "o", *out_parts, lambda chunks, far: put_out(chunks, 0, far)),
    }
    targets = {"b": ("back", 9), "i": ("in", 9), "o": ("out", 8)}
    line.done(chains["o"])

    class Attention:
        def advance(self):
            head_grad = jnp.concatenate(line.after(head_grad_pieces), axis=1)
            self.head_grads = attention_backward(projected, head_grad, head_result, head_logs)
            self.value, other = qkv_grad_parts(core_index, token_pieces, self.head_grads)
            self.other = exchange(other, "fsdp", 1)
            chains["v"].begin(self.head_grads)
            line.done(self)

    layer_vectors = (
        in_bias_grad, back_bias_grad, gain_two_grad, shift_two_grad,
        out_bias_grad, gain_one_grad, shift_one_grad,
    )

    class Vectors:
        def begin(self, head_grads):
            spread_out = []
            for part in (head_grads[0], head_grads[2]):
                spread_out.append(
                    lax.dynamic_update_slice_in_dim(
                        jnp.zeros((width,), jnp.float32), column_sum(part), ctx * pair, 0
                    )
                )
            self.value = jnp.concatenate(layer_vectors + tuple(spread_out))
            self.routes = [("fsdp", 1)] + hops("v")
            self.step = 0
            self.arrived = exchange(self.value, *self.routes[0])

        def advance(self):
            arrived, value = line.after((self.arrived, self.value))
            self.value = value + arrived
            self.step += 1
            if self.step < len(self.routes):
                self.arrived = exchange(self.value, *self.routes[self.step])
            line.done(self)

    class QueryKeyValue:
        def __init__(self):
            self.step = 0

        def advance(self):
            step = self.step
            self.step += 1
            order = hops("q")
            if step == 0:
                other, own = line.after((chains["A"].other, chains["A"].value))
                total = own + widened(other)
                half = total.shape[1] // 2
                low, high = total[:, :half], total[:, half:]
                first = lax.axis_index("dp") == 0
                self.value = jnp.where(first, low, high)
                self.arrived = exchange(lowered(jnp.where(first, high, low)), *order[0])
            elif step == 1:
                arrived, value = line.after((self.arrived, self.value))
                self.value = lowered(value + widened(arrived))[None]
                self.arrived = exchange(self.value, *order[-1])
            elif step <= len(order):
                arrived, value = line.after((self.arrived, self.value))
                self.value = jnp.concatenate([value, arrived], axis=0)
                self.arrived = exchange(self.value, *order[len(order) - step])
                if step == len(order):
                    self.put(self.value, False)
            else:
                arrived, value = line.after((self.arrived, self.value))
                self.value = self.put(arrived, True)
                line.done(Placed("qkv"))
                return
            line.done(self)

        def put(self, chunks, far):
            bits = [bit for axis, bit in hops("q")[1:]]
            whole["qkv"] = put_three_in_place(
                places["q"], chunks, far, whole["qkv"], bits, 2, "place_qkv"
            )
            return whole["qkv"]

    class Tokens:
        def __init__(self):
            self.step = 0

        def advance(self):
            order = hops("T")
            if self.step == 0:
                blocks = [row_blocks(part) for part in chains["A"].head_grads]
                pieces = line.after(
                    [jnp.concatenate([m[k] for m in blocks], axis=-1) for k in range(ctx_count)]
                )
                held = {(0, k): piece for k, piece in enumerate(pieces)}
            else:
                bit = order[self.step - 1][1]
                arrived, kept = line.after((self.arrived, self.value))
                held = dict(zip(self.kept, kept))
                for n, (source, target) in enumerate(self.sent):
                    held[source ^ bit, target ^ bit] = arrived[n]
            if self.step < len(order):
                bit = order[self.step][1]
                self.sent = [key for key in sorted(held) if key[1] & bit]
                self.kept = [key for key in sorted(held) if not key[1] & bit]
                self.arrived = exchange(jnp.stack([held[key] for key in self.sent]), *order[self.step])
                self.value = [held[key] for key in self.kept]
            else:
                mixed = reorder([held[k, 0] for k in range(ctx_count)], ctx)
                mixed_grad = jnp.concatenate(
                    [m[..., t * pair : (t + 1) * pair] for t in range(3) for m in mixed], axis=-1
                )
                self.value = summed_grad + back_project(mixed_grad, qkv_full)
            self.step += 1
            line.done(self)

    chains.update(A=Attention(), v=Vectors(), q=QueryKeyValue(), T=Tokens())
    for name in EVENTS:
        chain = chains[name]
        chain.advance()
        if name in targets and chain.step == targets[name][1]:
            line.done(Placed(targets[name][0]))

    reduced = []
    offset = 0
    sizes = [part.shape[0] for part in layer_vectors] + [width, width]
    for size in sizes:
        reduced.append(half_of(chains["v"].value[offset : offset + size], core, 0))
        offset += size
    token_grad = chains["T"].value
    qkv_grad, in_grad, back_grad, out_grad = (
        whole["qkv"], whole["in"], whole["back"], whole["out"]
    )
    bias_grads = reduced[7:]
    return (
        output,
        token_grad,
        qkv_grad,
        bias_grads[0],
        bias_grads[1],
        out_grad,
        reduced[4],
        reduced[5],
        reduced[6],
        in_grad,
        reduced[0],
        back_grad,
        reduced[1],
        reduced[2],
        reduced[3],
    )


def head_parallel(mesh):
    sizes = [mesh.shape["dp"], mesh.shape["ctx"]]
    return sizes == [2, 8] and mesh.shape["fsdp"] == 2 and 2 * sizes[1] == HEADS


def solution(mesh):
    in_specs = (
        P(("dp", "fsdp"), "ctx", None),
        P("fsdp", None),
        P("fsdp"),
        P("fsdp"),
        P("fsdp", None),
        P("fsdp"),
        P("fsdp"),
        P("fsdp"),
        P("fsdp", None),
        P("fsdp"),
        P("fsdp", None),
        P("fsdp"),
        P("fsdp"),
        P("fsdp"),
        P(("dp", "fsdp"), "ctx", None),
    )
    out_specs = (
        P(("dp", "fsdp"), "ctx", None),
        P(("dp", "fsdp"), "ctx", None),
        P("fsdp", None),
        P("fsdp"),
        P("fsdp"),
        P("fsdp", None),
        P("fsdp"),
        P("fsdp"),
        P("fsdp"),
        P("fsdp", None),
        P("fsdp"),
        P("fsdp", None),
        P("fsdp"),
        P("fsdp"),
        P("fsdp"),
    )
    body = on_device if head_parallel(mesh) else ring_on_device
    return jax.shard_map(
        body, mesh=mesh, in_specs=in_specs, out_specs=out_specs, check_vma=False
    )
```

```python
from functools import partial

import jax
import jax.numpy as jnp
from jax import lax
from jax.experimental import pallas as pl
from jax.experimental.pallas import tpu as pltpu
from jax.sharding import PartitionSpec as P

HEADS = 16
HEAD_DIM = 64


EPSILON = 1e-06


def from_behind(block, axis, distance):
    devices = range(lax.axis_size(axis))
    route = [((i - distance) % len(devices), i) for i in devices]
    return lax.ppermute(block, axis, route)


def norm_apply(values, gain_vec, shift_vec):
    centre = jnp.mean(values, axis=-1, keepdims=True)
    centred = values - centre
    variance = jnp.mean(centred * centred, axis=-1, keepdims=True)
    return centred * lax.rsqrt(variance + EPSILON) * gain_vec + shift_vec


def lowered(values):
    return values.astype(jnp.bfloat16)


def widened(values):
    return values.astype(jnp.float32)


def project(left_operand_rows, right_operand_matrix):
    return jnp.einsum(
        "ugj,jn->ugn", left_operand_rows, right_operand_matrix, preferred_element_type=jnp.float32
    )


def weight_grad(left_operand_rows, gradient_row_block):
    return jnp.einsum(
        "xrb,xrw->bw", left_operand_rows, gradient_row_block, preferred_element_type=jnp.float32
    )


def back_project(gradient_row_block, right_operand_matrix):
    return jnp.einsum(
        "wkb,fb->wkf", gradient_row_block, right_operand_matrix, preferred_element_type=jnp.float32
    )


def column_sum(values):
    return jnp.sum(widened(values), axis=(0, 1))


def split_heads(values):
    return values.reshape(values.shape[0], values.shape[1], HEADS, HEAD_DIM)


def merge_heads(values):
    return values.reshape(values.shape[0], values.shape[1], HEADS * HEAD_DIM)


def split_blocks(values, block_rows):
    seq_count = values.shape[0]
    blocks = values.shape[1] // block_rows
    return jnp.moveaxis(values.reshape(seq_count, blocks, block_rows, values.shape[2]), 1, 0)


def block_scores(query_rows, key_rows):
    scores = jnp.einsum(
        "sqhd,skhd->shqk",
        split_heads(query_rows),
        split_heads(key_rows),
        preferred_element_type=jnp.float32,
    )
    return scores * HEAD_DIM ** (-0.5)


def fold_block(state_now, key_block, value_block, query_rows):
    running_max, running_sum, running_acc = state_now
    scores = block_scores(query_rows, key_block)
    new_max = jnp.maximum(running_max, jnp.max(scores, axis=-1))
    rescale = jnp.exp(running_max - new_max)
    weights = jnp.exp(scores - new_max[..., None])
    new_sum = running_sum * rescale + jnp.sum(weights, axis=-1)
    product = jnp.einsum(
        "shqk,skhd->shqd",
        lowered(weights),
        split_heads(value_block),
        preferred_element_type=jnp.float32,
    )
    return (new_max, new_sum, running_acc * rescale[..., None] + product)


def attend_forward(query_rows, key_rows, value_rows):
    seq_count = query_rows.shape[0]
    block_rows = query_rows.shape[1]
    initial = (
        jnp.full((seq_count, HEADS, block_rows), -1e30, jnp.float32),
        jnp.zeros((seq_count, HEADS, block_rows), jnp.float32),
        jnp.zeros((seq_count, HEADS, block_rows, HEAD_DIM), jnp.float32),
    )
    kept = None
    key_part = lax.all_gather(key_rows, "ctx", axis=1, tiled=True)
    value_part = lax.all_gather(value_rows, "ctx", axis=1, tiled=True)

    def one_block(state_in, block_pair):
        return (fold_block(state_in, block_pair[0], block_pair[1], query_rows), None)

    state_out, unused = lax.scan(
        one_block,
        initial,
        (split_blocks(key_part, block_rows), split_blocks(value_part, block_rows)),
    )
    running_max, running_sum, running_acc = state_out
    attention_result = running_acc / running_sum[..., None]
    attention_result = jnp.transpose(attention_result, (0, 2, 1, 3)).reshape(
        seq_count, block_rows, HEADS * HEAD_DIM
    )
    log_total = running_max + jnp.log(running_sum)
    return (attention_result, log_total, kept)


def attend_back(query_rows, gradient_row_block, log_total, row_inner, key_rows, value_rows):
    score_scale = HEAD_DIM ** (-0.5)
    scores = block_scores(query_rows, key_rows)
    probabilities = jnp.exp(scores - log_total[..., None])
    value_grad = jnp.einsum(
        "shqk,sqhd->skhd",
        lowered(probabilities),
        split_heads(gradient_row_block),
        preferred_element_type=jnp.float32,
    )
    prob_grad = jnp.einsum(
        "sqhd,skhd->shqk",
        split_heads(gradient_row_block),
        split_heads(value_rows),
        preferred_element_type=jnp.float32,
    )
    score_grad = lowered(probabilities * (prob_grad - row_inner[..., None]))
    query_grad = (
        jnp.einsum(
            "shqk,skhd->sqhd", score_grad, split_heads(key_rows), preferred_element_type=jnp.float32
        )
        * score_scale
    )
    key_grad = (
        jnp.einsum(
            "shqk,sqhd->skhd",
            score_grad,
            split_heads(query_rows),
            preferred_element_type=jnp.float32,
        )
        * score_scale
    )
    return (merge_heads(query_grad), merge_heads(key_grad), merge_heads(value_grad))


def attend_backward(query_rows, gradient_row_block, log_total, row_inner, key_rows, value_rows):
    zero_rows = jnp.zeros(query_rows.shape, jnp.float32)
    turn_count = lax.axis_size("ctx") // 2

    def turn_keys(turn_index, carried):
        moving_key, moving_value, key_acc, value_acc, query_acc = carried
        for half_step in range(2):
            pieces = attend_back(
                query_rows, gradient_row_block, log_total, row_inner, moving_key, moving_value
            )
            query_acc = query_acc + pieces[0]
            key_acc = key_acc + pieces[1]
            value_acc = value_acc + pieces[2]
            moving_key, moving_value = from_behind((moving_key, moving_value), "ctx", 1)
            key_acc, value_acc = (
                from_behind(key_acc.astype(jnp.bfloat16), "ctx", 1).astype(key_acc.dtype),
                from_behind(value_acc.astype(jnp.bfloat16), "ctx", 1).astype(value_acc.dtype),
            )
        return (moving_key, moving_value, key_acc, value_acc, query_acc)

    finished = lax.fori_loop(
        0, turn_count, turn_keys, (key_rows, value_rows, zero_rows, zero_rows, zero_rows)
    )
    return (finished[4], finished[2], finished[3])


def ring_on_device(
    tokens,
    query_key_value_weight,
    bias_query,
    bias_value,
    attention_out_weight,
    attention_out_bias,
    gain_one,
    shift_one,
    feedforward_in_weight,
    feedforward_in_bias,
    feedforward_out_weight,
    feedforward_out_bias,
    gain_two,
    shift_two,
    d_out,
):
    attn_full = (
        lax.all_gather(query_key_value_weight, "fsdp", axis=0, tiled=True),
        lax.all_gather(attention_out_weight, "fsdp", axis=0, tiled=True),
        lax.all_gather(bias_query, "fsdp", axis=0, tiled=True),
        lax.all_gather(bias_value, "fsdp", axis=0, tiled=True),
        lax.all_gather(attention_out_bias, "fsdp", axis=0, tiled=True),
        lax.all_gather(gain_one, "fsdp", axis=0, tiled=True),
        lax.all_gather(shift_one, "fsdp", axis=0, tiled=True),
    )
    qkv_full, out_full, query_bias, value_bias, out_bias, gain_first, shift_first = attn_full
    model_width = out_full.shape[0]
    projected_rows = project(tokens, qkv_full) + jnp.concatenate(
        [widened(query_bias), jnp.zeros((model_width,), jnp.float32), widened(value_bias)]
    )
    projected_low = lowered(projected_rows)
    query_rows = projected_low[..., :model_width]
    key_rows = projected_low[..., model_width : 2 * model_width]
    value_rows = projected_low[..., 2 * model_width :]
    attention_result, log_total, kept = attend_forward(query_rows, key_rows, value_rows)
    attended_low = lowered(attention_result)
    attention_branch = project(attended_low, out_full) + widened(out_bias)
    summed_one = widened(tokens) + attention_branch
    first_normalized, pull_one = jax.vjp(
        norm_apply, summed_one, widened(gain_first), widened(shift_first)
    )
    normed_low = lowered(first_normalized)
    ffn_full = (
        lax.all_gather(feedforward_in_weight, "fsdp", axis=0, tiled=True),
        lax.all_gather(feedforward_out_weight, "fsdp", axis=0, tiled=True),
        lax.all_gather(feedforward_in_bias, "fsdp", axis=0, tiled=True),
        lax.all_gather(feedforward_out_bias, "fsdp", axis=0, tiled=True),
        lax.all_gather(gain_two, "fsdp", axis=0, tiled=True),
        lax.all_gather(shift_two, "fsdp", axis=0, tiled=True),
    )
    in_full, back_full, inner_bias, back_bias, gain_second, shift_second = ffn_full
    hidden_before_gelu = project(normed_low, in_full) + widened(inner_bias)
    active_low = lowered(jax.nn.gelu(hidden_before_gelu, approximate=False))
    feedforward_branch = project(active_low, back_full) + widened(back_bias)

    def second_norm(residual_in, branch_in, gain_vec, shift_vec):
        return norm_apply(residual_in + branch_in, gain_vec, shift_vec)

    result, pull_two = jax.vjp(
        second_norm,
        first_normalized,
        feedforward_branch,
        widened(gain_second),
        widened(shift_second),
    )
    output = lowered(result)
    first_grad_res, second_grad, gain_two_grad, shift_two_grad = pull_two(widened(d_out))
    in_full, back_full = (
        lax.all_gather(feedforward_in_weight, "fsdp", axis=0, tiled=True),
        lax.all_gather(feedforward_out_weight, "fsdp", axis=0, tiled=True),
    )
    second_low = lowered(second_grad)
    back_grad = weight_grad(active_low, second_low)
    back_bias_grad = column_sum(second_low)
    active_grad = back_project(second_low, back_full)
    gelu_pull = jax.vjp(partial(jax.nn.gelu, approximate=False), hidden_before_gelu)[1]
    hidden_low = lowered(gelu_pull(active_grad)[0])
    in_grad = weight_grad(normed_low, hidden_low)
    in_bias_grad = column_sum(hidden_low)
    first_grad = first_grad_res + back_project(hidden_low, in_full)
    ffn_grads = (
        lax.psum_scatter(
            in_grad.astype(jnp.bfloat16), "fsdp", scatter_dimension=0, tiled=True
        ).astype(jnp.float32),
        lax.psum_scatter(
            in_bias_grad.astype(jnp.bfloat16), "fsdp", scatter_dimension=0, tiled=True
        ).astype(jnp.float32),
        lax.psum_scatter(
            back_grad.astype(jnp.bfloat16), "fsdp", scatter_dimension=0, tiled=True
        ).astype(jnp.float32),
        lax.psum_scatter(
            back_bias_grad.astype(jnp.bfloat16), "fsdp", scatter_dimension=0, tiled=True
        ).astype(jnp.float32),
        lax.psum_scatter(
            gain_two_grad.astype(jnp.bfloat16), "fsdp", scatter_dimension=0, tiled=True
        ).astype(jnp.float32),
        lax.psum_scatter(
            shift_two_grad.astype(jnp.bfloat16), "fsdp", scatter_dimension=0, tiled=True
        ).astype(jnp.float32),
    )
    ffn_grads = lax.psum(
        (ffn_grads[0], ffn_grads[1], ffn_grads[2], ffn_grads[3], ffn_grads[4], ffn_grads[5]),
        ("dp", "ctx"),
    )
    summed_grad, gain_one_grad, shift_one_grad = pull_one(first_grad)
    qkv_full, out_full = (
        lax.all_gather(query_key_value_weight, "fsdp", axis=0, tiled=True),
        lax.all_gather(attention_out_weight, "fsdp", axis=0, tiled=True),
    )
    branch_low = lowered(summed_grad)
    out_grad = weight_grad(attended_low, branch_low)
    out_bias_grad = column_sum(branch_low)
    attended_grad_low = lowered(back_project(branch_low, out_full))
    row_inner = jnp.sum(
        split_heads(widened(attended_grad_low)) * split_heads(attention_result), axis=-1
    )
    row_inner = jnp.transpose(row_inner, (0, 2, 1))
    query_grad, key_grad, value_grad = attend_backward(
        query_rows, attended_grad_low, log_total, row_inner, key_rows, value_rows
    )
    mixed_grad = lowered(jnp.concatenate([query_grad, key_grad, value_grad], axis=-1))
    qkv_grad = weight_grad(tokens, mixed_grad)
    bias_grads = column_sum(mixed_grad)
    query_bias_grad = bias_grads[:model_width]
    value_bias_grad = bias_grads[2 * model_width :]
    token_grad = summed_grad + back_project(mixed_grad, qkv_full)
    attn_grads = (
        lax.psum_scatter(
            qkv_grad.astype(jnp.bfloat16), "fsdp", scatter_dimension=0, tiled=True
        ).astype(jnp.float32),
        lax.psum_scatter(
            query_bias_grad.astype(jnp.bfloat16), "fsdp", scatter_dimension=0, tiled=True
        ).astype(jnp.float32),
        lax.psum_scatter(
            value_bias_grad.astype(jnp.bfloat16), "fsdp", scatter_dimension=0, tiled=True
        ).astype(jnp.float32),
        lax.psum_scatter(
            out_grad.astype(jnp.bfloat16), "fsdp", scatter_dimension=0, tiled=True
        ).astype(jnp.float32),
        lax.psum_scatter(
            out_bias_grad.astype(jnp.bfloat16), "fsdp", scatter_dimension=0, tiled=True
        ).astype(jnp.float32),
        lax.psum_scatter(
            gain_one_grad.astype(jnp.bfloat16), "fsdp", scatter_dimension=0, tiled=True
        ).astype(jnp.float32),
        lax.psum_scatter(
            shift_one_grad.astype(jnp.bfloat16), "fsdp", scatter_dimension=0, tiled=True
        ).astype(jnp.float32),
    )
    attn_grads = lax.psum(
        (
            attn_grads[0],
            attn_grads[1],
            attn_grads[2],
            attn_grads[3],
            attn_grads[4],
            attn_grads[5],
            attn_grads[6],
        ),
        ("dp", "ctx"),
    )
    return (
        output,
        token_grad,
        attn_grads[0],
        attn_grads[1],
        attn_grads[2],
        attn_grads[3],
        attn_grads[4],
        attn_grads[5],
        attn_grads[6],
        ffn_grads[0],
        ffn_grads[1],
        ffn_grads[2],
        ffn_grads[3],
        ffn_grads[4],
        ffn_grads[5],
    )


def exchange(values, axis, bit):
    count = lax.axis_size(axis)
    return lax.ppermute(values, axis, [(i, i ^ bit) for i in range(count)])


def bits_below(count):
    return [1 << k for k in range(count.bit_length() - 1)]


def reorder(pieces, index):
    for bit in bits_below(len(pieces)):
        taken = (index & bit) != 0
        pieces = [jnp.where(taken, pieces[k ^ bit], pieces[k]) for k in range(len(pieces))]
    return pieces


def pair_join(own, other, core, axis=0):
    first = jnp.where(core == 0, own, other)
    second = jnp.where(core == 0, other, own)
    return jnp.concatenate([first, second], axis=axis)


def half_of(values, which, axis):
    size = values.shape[axis] // 2
    low = lax.slice_in_dim(values, 0, size, axis=axis)
    high = lax.slice_in_dim(values, size, 2 * size, axis=axis)
    return jnp.where(which == 0, low, high)


def gather_first(block):
    near, middle, far = (exchange(block, "ctx", bit) for bit in (1, 2, 4))
    return near, middle, far


def gather_rest(block, first, use, early):
    near, (middle, far) = first[0], lax.optimization_barrier(first[1:])
    third = exchange(middle, "ctx", 1)
    sixth = exchange(far, "ctx", 2)
    fifth = exchange(far, "ctx", 1)
    used = [use(piece) for piece in (block, near, middle, far)]
    third, fifth, sixth, used, early = lax.optimization_barrier(
        (third, fifth, sixth, used, early)
    )
    seventh = exchange(sixth, "ctx", 1)
    pieces = [block, near, middle, third, far, fifth, sixth, seventh]
    used = {0: used[0], 1: used[1], 2: used[2], 4: used[3]}
    for k in (3, 5, 6, 7):
        used[k] = use(pieces[k])
    return pieces, [used[k] for k in range(8)], early


def swap_blocks(pieces):
    return [pieces[0]] + [exchange(pieces[k], "ctx", k) for k in range(1, len(pieces))]


def head_mask(value):
    lane = lax.broadcasted_iota(jnp.int32, (1, 2 * HEAD_DIM), 1)
    return [
        jnp.where(lane < HEAD_DIM, value, 0.0),
        jnp.where(lane < HEAD_DIM, 0.0, value),
    ]


def contract(left, right, left_dim, right_dim):
    return lax.dot_general(
        left, right, (((left_dim,), (right_dim,)), ((), ())), preferred_element_type=jnp.float32
    )


def project_kernel(block_ref, weight_ref, bias_ref, out_ref):
    for s in range(block_ref.shape[0]):
        out_ref[s] = (contract(block_ref[s], weight_ref[...], 1, 0) + bias_ref[...]).astype(
            jnp.bfloat16
        )


def project_block(block, weight, bias):
    shape = block.shape[:2] + (weight.shape[1],)
    return pl.pallas_call(
        project_kernel,
        out_shape=jax.ShapeDtypeStruct(shape, jnp.bfloat16),
        compiler_params=pltpu.CompilerParams(vmem_limit_bytes=40 << 20),
        name="project_block",
    )(block, weight, bias)


def forward_kernel(query_ref, key_ref, value_ref, result_ref, low_ref, log_ref):
    query = query_ref[0].astype(jnp.float32)
    keys = key_ref[0]
    values = value_ref[0]
    results = []
    logs = []
    for mask in head_mask(HEAD_DIM ** (-0.5)):
        scores = contract((query * mask).astype(jnp.bfloat16), keys, 1, 1)
        row_max = jnp.max(scores, axis=-1, keepdims=True)
        weights = jnp.exp(scores - row_max)
        total = jnp.sum(weights, axis=-1, keepdims=True)
        probabilities = (weights * (1.0 / total)).astype(jnp.bfloat16)
        results.append(contract(probabilities, values, 1, 0))
        logs.append(row_max + jnp.log(total))
    first = lax.broadcasted_iota(jnp.int32, results[0].shape, 1) < HEAD_DIM
    result = jnp.where(first, results[0], results[1])
    result_ref[0] = result
    low_ref[0] = result.astype(jnp.bfloat16)
    log_ref[0] = jnp.where(first, logs[0], logs[1])


def attention_forward(projected):
    seqs, length, width = projected.shape
    pair = width // 3
    rows = min(512, length)
    row_spec = pl.BlockSpec((1, rows, pair), lambda s, q: (s, q, 0))
    return pl.pallas_call(
        forward_kernel,
        grid=(seqs, length // rows),
        in_specs=[
            row_spec,
            pl.BlockSpec((1, length, pair), lambda s, q: (s, 0, 1)),
            pl.BlockSpec((1, length, pair), lambda s, q: (s, 0, 2)),
        ],
        out_specs=[row_spec, row_spec, row_spec],
        out_shape=[
            jax.ShapeDtypeStruct((seqs, length, pair), jnp.float32),
            jax.ShapeDtypeStruct((seqs, length, pair), jnp.bfloat16),
            jax.ShapeDtypeStruct((seqs, length, pair), jnp.float32),
        ],
        compiler_params=pltpu.CompilerParams(vmem_limit_bytes=48 << 20),
        name="attention_forward",
    )(projected, projected, projected)


def backward_kernel(
    query_ref, key_ref, value_ref, grad_ref, result_ref, log_ref,
    query_out, key_out, value_out, query_acc, log_rows, inner_rows,
):
    step = pl.program_id(1)

    @pl.when(step == 0)
    def first_step():
        query_acc[...] = jnp.zeros_like(query_acc)
        logs = jnp.transpose(log_ref[0])
        inner = jnp.transpose(grad_ref[0].astype(jnp.float32) * result_ref[0])
        for h in range(2):
            log_rows[h] = jnp.broadcast_to(
                logs[h * HEAD_DIM : h * HEAD_DIM + 1], log_rows.shape[1:]
            )
            inner_rows[h] = jnp.broadcast_to(
                jnp.sum(inner[h * HEAD_DIM : (h + 1) * HEAD_DIM], axis=0, keepdims=True),
                inner_rows.shape[1:],
            )

    queries = query_ref[0]
    grads = grad_ref[0]
    keys = key_ref[0]
    values = value_ref[0]
    scale = HEAD_DIM ** (-0.5)
    query_parts = []
    key_parts = []
    value_parts = []
    scaled_masks = head_mask(scale)
    masks = head_mask(1.0)
    for h in range(2):
        scores = contract(
            (keys.astype(jnp.float32) * scaled_masks[h]).astype(jnp.bfloat16), queries, 1, 1
        )
        probabilities = jnp.exp(scores - log_rows[h, :1])
        prob_grad = contract(
            (values.astype(jnp.float32) * masks[h]).astype(jnp.bfloat16), grads, 1, 1
        )
        score_grad = (probabilities * (prob_grad - inner_rows[h, :1])).astype(jnp.bfloat16)
        value_parts.append(contract(probabilities.astype(jnp.bfloat16), grads, 1, 0))
        key_parts.append(contract(score_grad, queries, 1, 0))
        query_parts.append(contract(score_grad, keys, 0, 0))
    first = lax.broadcasted_iota(jnp.int32, key_parts[0].shape, 1) < HEAD_DIM
    value_out[0] = jnp.where(first, value_parts[0], value_parts[1]).astype(jnp.bfloat16)
    key_out[0] = (jnp.where(first, key_parts[0], key_parts[1]) * scale).astype(jnp.bfloat16)
    first = lax.broadcasted_iota(jnp.int32, query_parts[0].shape, 1) < HEAD_DIM
    query_acc[...] += jnp.where(first, query_parts[0], query_parts[1])

    @pl.when(step == pl.num_programs(1) - 1)
    def last_step():
        query_out[0] = (query_acc[...] * scale).astype(jnp.bfloat16)


def attention_backward(projected, grads, result, logs):
    seqs, length, width = projected.shape
    pair = width // 3
    rows = min(512, length)
    whole = pl.BlockSpec((1, length, pair), lambda s, k: (s, 0, 0))
    block = pl.BlockSpec((1, rows, pair), lambda s, k: (s, k, 0))
    shape = jax.ShapeDtypeStruct((seqs, length, pair), jnp.bfloat16)
    return pl.pallas_call(
        backward_kernel,
        grid=(seqs, length // rows),
        in_specs=[
            whole,
            pl.BlockSpec((1, rows, pair), lambda s, k: (s, k, 1)),
            pl.BlockSpec((1, rows, pair), lambda s, k: (s, k, 2)),
            whole,
            whole,
            whole,
        ],
        out_specs=[whole, block, block],
        out_shape=[shape, shape, shape],
        scratch_shapes=[
            pltpu.VMEM((length, pair), jnp.float32),
            pltpu.VMEM((2, 8, length), jnp.float32),
            pltpu.VMEM((2, 8, length), jnp.float32),
        ],
        compiler_params=pltpu.CompilerParams(vmem_limit_bytes=48 << 20),
        name="attention_backward",
    )(projected, projected, projected, grads, result, logs)


def ffn_forward_kernel(
    core_ref, left_own, left_other, in_own, in_other, bias_ref, back_own, back_other,
    active_ref, slope_ref, second_ref,
):
    step = pl.program_id(0)
    hidden = contract(left_own[...], in_own[...], 1, 0)
    hidden = hidden + contract(left_other[...], in_other[...], 1, 0) + bias_ref[...]
    below = 0.5 * (1.0 + lax.erf(hidden * 0.7071067811865476))
    slope = below + hidden * (jnp.exp(-0.5 * hidden * hidden) * 0.3989422804014327)
    active = (hidden * below).astype(jnp.bfloat16)
    active_ref[...] = active
    slope_ref[...] = slope.astype(jnp.bfloat16)

    @pl.when(step == 0)
    def first():
        second_ref[...] = contract(active, back_own[...], 1, 0)

    @pl.when((step > 0) & (step < pl.num_programs(0) // 2))
    def own():
        second_ref[...] += contract(active, back_own[...], 1, 0)

    @pl.when(step >= pl.num_programs(0) // 2)
    def other():
        second_ref[...] += contract(active, back_other[...], 1, 0)


def ffn_specs(half, block, width, hidden):
    near = hidden // (2 * block)

    def spot(s, p):
        return jnp.where(s < near, s + p[0] * near, s - p[0] * near)

    weights = [
        pl.BlockSpec((half, block), lambda s, p: (0, spot(s, p))),
        pl.BlockSpec((half, block), lambda s, p: (0, spot(s, p))),
        pl.BlockSpec((block, width), lambda s, p: (jnp.minimum(s, near - 1), 0)),
        pl.BlockSpec((block, width), lambda s, p: (jnp.maximum(s - near, 0), 0)),
    ]
    return spot, weights


def ffn_forward(core, left, in_pair, back_pair, bias):
    tokens, width = left.shape
    half, hidden = in_pair[0].shape
    block = 1024
    spot, weights = ffn_specs(half, block, width, hidden)
    wide = pl.BlockSpec((tokens, block), lambda s, p: (0, spot(s, p)))
    return pl.pallas_call(
        ffn_forward_kernel,
        grid_spec=pltpu.PrefetchScalarGridSpec(
            num_scalar_prefetch=1,
            grid=(hidden // block,),
            in_specs=[
                pl.BlockSpec((tokens, half), lambda s, p: (0, p[0])),
                pl.BlockSpec((tokens, half), lambda s, p: (0, 1 - p[0])),
                weights[0],
                weights[1],
                pl.BlockSpec((1, block), lambda s, p: (0, spot(s, p))),
                weights[2],
                weights[3],
            ],
            out_specs=[wide, wide, pl.BlockSpec((tokens, width), lambda s, p: (0, 0))],
        ),
        out_shape=[
            jax.ShapeDtypeStruct((tokens, hidden), jnp.bfloat16),
            jax.ShapeDtypeStruct((tokens, hidden), jnp.bfloat16),
            jax.ShapeDtypeStruct((tokens, width), jnp.float32),
        ],
        compiler_params=pltpu.CompilerParams(vmem_limit_bytes=40 << 20),
        name="ffn_forward",
    )(core, left, left, *in_pair, bias, *back_pair)


def ffn_backward_kernel(
    core_ref, grad_ref, slope_ref, in_own, in_other, back_own, back_other,
    hidden_ref, total_ref, own_acc, other_acc,
):
    step = pl.program_id(0)
    half = own_acc.shape[1]

    def rest(back_ref):
        active_grad = contract(grad_ref[...], back_ref[...], 1, 1)
        hidden = (active_grad * slope_ref[...].astype(jnp.float32)).astype(jnp.bfloat16)
        hidden_ref[...] = hidden
        own = contract(hidden, in_own[...], 1, 1)
        other = contract(hidden, in_other[...], 1, 1)

        @pl.when(step == 0)
        def first():
            own_acc[...] = own
            other_acc[...] = other

        @pl.when(step > 0)
        def later():
            own_acc[...] += own
            other_acc[...] += other

    @pl.when(step < pl.num_programs(0) // 2)
    def with_own():
        rest(back_own)

    @pl.when(step >= pl.num_programs(0) // 2)
    def with_other():
        rest(back_other)

    @pl.when(step == pl.num_programs(0) - 1)
    def last():
        @pl.when(core_ref[0] == 0)
        def straight():
            total_ref[:, :half] = own_acc[...]
            total_ref[:, half:] = other_acc[...]

        @pl.when(core_ref[0] != 0)
        def crossed():
            total_ref[:, :half] = other_acc[...]
            total_ref[:, half:] = own_acc[...]


def ffn_backward(core, grad, slope, in_pair, back_pair):
    tokens, width = grad.shape
    half, hidden = in_pair[0].shape
    block = 1024
    spot, weights = ffn_specs(half, block, width, hidden)
    wide = pl.BlockSpec((tokens, block), lambda s, p: (0, spot(s, p)))
    whole = pl.BlockSpec((tokens, width), lambda s, p: (0, 0))
    return pl.pallas_call(
        ffn_backward_kernel,
        grid_spec=pltpu.PrefetchScalarGridSpec(
            num_scalar_prefetch=1,
            grid=(hidden // block,),
            in_specs=[whole, wide, *weights],
            out_specs=[wide, whole],
            scratch_shapes=[
                pltpu.VMEM((tokens, half), jnp.float32),
                pltpu.VMEM((tokens, half), jnp.float32),
            ],
        ),
        out_shape=[
            jax.ShapeDtypeStruct((tokens, hidden), jnp.bfloat16),
            jax.ShapeDtypeStruct((tokens, width), jnp.float32),
        ],
        compiler_params=pltpu.CompilerParams(vmem_limit_bytes=40 << 20),
        name="ffn_backward",
    )(core, grad, slope, *in_pair, *back_pair)


def qkv_grad_kernel(core_ref, *refs, pieces):
    token_refs, grad_refs = refs[:pieces], refs[pieces : pieces + 3]
    own_ref, other_ref = refs[pieces + 3 :]
    seqs = token_refs[0].shape[0]
    rows = jnp.concatenate([ref[s] for s in range(seqs) for ref in token_refs], axis=0)
    parts = []
    for ref in grad_refs:
        grads = jnp.concatenate([ref[s] for s in range(seqs)], axis=0)
        parts.append(contract(rows, grads, 0, 0))
    half = pl.num_programs(0) // 2

    @pl.when(pl.program_id(0) < half)
    def outgoing():
        for t in range(3):
            other_ref[t] = parts[t].astype(jnp.bfloat16)

    @pl.when(pl.program_id(0) >= half)
    def kept():
        for t in range(3):
            own_ref[t] = parts[t]


def qkv_grad_parts(core, token_pieces, head_grads):
    seqs, rows, width = token_pieces[0].shape
    pair = head_grads[0].shape[2]
    cols = 256
    steps = width // cols
    half = steps // 2

    def spot(s, p):
        return jnp.where(s < half, s + (1 - p[0]) * half, s - half + p[0] * half)

    grads = pl.BlockSpec(head_grads[0].shape, lambda s, p: (0, 0, 0))
    return pl.pallas_call(
        partial(qkv_grad_kernel, pieces=len(token_pieces)),
        grid_spec=pltpu.PrefetchScalarGridSpec(
            num_scalar_prefetch=1,
            grid=(steps,),
            in_specs=[pl.BlockSpec((seqs, rows, cols), lambda s, p: (0, 0, spot(s, p)))]
            * len(token_pieces)
            + [grads] * 3,
            out_specs=[
                pl.BlockSpec((3, cols, pair), lambda s, p: (0, jnp.maximum(s - half, 0), 0)),
                pl.BlockSpec((3, cols, pair), lambda s, p: (0, jnp.minimum(s, half - 1), 0)),
            ],
        ),
        out_shape=[
            jax.ShapeDtypeStruct((3, width // 2, pair), jnp.float32),
            jax.ShapeDtypeStruct((3, width // 2, pair), jnp.bfloat16),
        ],
        compiler_params=pltpu.CompilerParams(vmem_limit_bytes=40 << 20),
        name="grad_qkv",
    )(core, *token_pieces, *head_grads)


LOW = 2


def grad_kernel(place_ref, left_own, left_other, right_own, right_other, keep_ref, send_ref, *, by_rows):
    step = pl.program_id(0)
    half = pl.num_programs(0) // 2
    total = contract(left_own[...], right_own[...], 0, 0)
    total = total + contract(left_other[...], right_other[...], 0, 0)
    total = total.astype(jnp.bfloat16)
    low = place_ref[0] & ((1 << LOW) - 1)
    _, rows, cols = keep_ref.shape

    def put(out_ref):
        for j in range(1 << LOW):
            if by_rows:
                out_ref[j ^ low] = total[j * rows : (j + 1) * rows]
            else:
                out_ref[j ^ low] = total[:, j * cols : (j + 1) * cols]

    @pl.when(step < half)
    def outgoing():
        put(send_ref)

    @pl.when(step >= half)
    def kept():
        put(keep_ref)


def pair_grad(place, left_pair, right_pair, count, part, parts, by_rows, name):
    tokens, width = left_pair[0].shape
    columns = right_pair[0].shape[1]
    steps = count >> LOW
    half = steps // 2

    def block(step, place_ref):
        return part * steps + (((step + half) % steps) ^ (place_ref[0] >> LOW))

    if by_rows:
        rows, cols = width // (parts * count), columns
        left = pl.BlockSpec((tokens, rows << LOW), lambda s, p: (0, block(s, p)))
        right = pl.BlockSpec((tokens, columns), lambda s, p: (0, 0))
    else:
        rows, cols = width, columns // (parts * count)
        left = pl.BlockSpec((tokens, width), lambda s, p: (0, 0))
        right = pl.BlockSpec((tokens, cols << LOW), lambda s, p: (0, block(s, p)))
    shape = jax.ShapeDtypeStruct((count // 2, rows, cols), jnp.bfloat16)
    out_block = (1 << LOW, rows, cols)
    return pl.pallas_call(
        partial(grad_kernel, by_rows=by_rows),
        grid_spec=pltpu.PrefetchScalarGridSpec(
            num_scalar_prefetch=1,
            grid=(steps,),
            in_specs=[left, left, right, right],
            out_specs=[
                pl.BlockSpec(out_block, lambda s, p: (jnp.maximum(s - half, 0), 0, 0)),
                pl.BlockSpec(out_block, lambda s, p: (jnp.minimum(s, half - 1), 0, 0)),
            ],
        ),
        out_shape=[shape, shape],
        compiler_params=pltpu.CompilerParams(vmem_limit_bytes=48 << 20),
        name=name,
    )(place, left_pair[0], left_pair[1], right_pair[0], right_pair[1])


def place_of(order):
    place = jnp.int32(0)
    for axis, bit in order:
        place = place * 2 + jnp.where((lax.axis_index(axis) & bit) != 0, 1, 0)
    return place.astype(jnp.int32).reshape(1)


def added(first, second):
    return lowered(widened(first) + widened(second))


LINKS = {"x": ("dp", 1), "y": ("ctx", 1), "p": ("ctx", 2), "r": ("ctx", 4)}
ORDERS = {"b0": "pyrx", "b1": "yprx", "i0": "xypr", "i1": "yxpr", "o": "rxpy", "q": "xypr", "v": "xypr", "T": "ypr"}
EVENTS = (
    "b", "A", "i", "q", "o", "b", "i", "q", "v", "o", "v", "b", "i", "v", "o", "q",
    "b", "o", "v", "i", "T", "o", "q", "b", "v", "o", "i", "T", "o", "b", "i", "q",
    "T", "i", "o", "b", "q", "T", "i", "b",
)


def hops(name):
    return [LINKS[letter] for letter in ORDERS[name]]


class Line:
    def __init__(self):
        self.last = None

    def after(self, values):
        if self.last is None:
            return values
        values, self.last.value = lax.optimization_barrier((values, self.last.value))
        return values

    def done(self, holder):
        self.last = holder


class Held:
    def __init__(self, value):
        self.value = value


class Reduction:
    def __init__(self, line, name, keep, send, put):
        self.line, self.order, self.put = line, hops(name), put
        self.value, self.step = keep, 0
        self.arrived = exchange(send, *self.order[0])

    def advance(self):
        last = len(self.order) - 1
        step = self.step
        self.step += 1
        arrived, value = self.line.after((self.arrived, self.value))
        if step < last:
            half = value.shape[0] // 2
            send = added(value[half:], arrived[half:])
            self.value = added(value[:half], arrived[:half])
            self.arrived = exchange(send, *self.order[step + 1])
        elif step == last:
            self.value = added(value, arrived)
            self.arrived = exchange(self.value, *self.order[last])
        elif step <= 2 * last:
            self.value = jnp.concatenate([value, arrived], axis=0)
            self.arrived = exchange(self.value, *self.order[2 * last - step])
            if step == 2 * last:
                self.put(self.value, False)
        else:
            self.value = self.put(arrived, True)
        self.line.done(self)


class Group:
    def __init__(self, line, names, parts, put):
        self.line, self.put, self.step = line, put, 1
        self.orders = [hops(name) for name in names]
        self.value = [keep for keep, send in parts]
        self.arrived = [exchange(send, *o[0]) for (keep, send), o in zip(parts, self.orders)]

    def advance(self):
        arrived, value = self.line.after((self.arrived, self.value))
        tail = self.orders[0][2:]
        step = self.step
        self.step += 1
        if step == 1:
            self.arrived = [
                exchange(added(v[v.shape[0] // 2 :], a[v.shape[0] // 2 :]), *o[1])
                for v, a, o in zip(value, arrived, self.orders)
            ]
            self.value = [
                added(v[: v.shape[0] // 2], a[: v.shape[0] // 2]) for v, a in zip(value, arrived)
            ]
        elif step == 2:
            total = jnp.stack([added(v, a) for v, a in zip(value, arrived)], axis=1)
            self.value = total[:2]
            self.arrived = exchange(total[2:], *tail[0])
        elif step == 3:
            self.value = added(value[:1], arrived[:1])
            self.arrived = exchange(added(value[1:], arrived[1:]), *tail[1])
        elif step == 4:
            self.value = added(value, arrived)
            self.arrived = exchange(self.value, *tail[1])
        elif step == 5:
            self.value = jnp.concatenate([value, arrived], axis=0)
            self.arrived = exchange(self.value, *tail[0])
        elif step == 6:
            total = jnp.concatenate([value, arrived], axis=0)
            self.value = [total[:, 0], total[:, 1]]
            self.arrived = [exchange(v, *o[1]) for v, o in zip(self.value, self.orders)]
        elif step == 7:
            self.value = [jnp.concatenate([v, a], axis=0) for v, a in zip(value, arrived)]
            self.arrived = [exchange(v, *o[0]) for v, o in zip(self.value, self.orders)]
            for part, chunks in enumerate(self.value):
                self.put(chunks, part, False)
        else:
            for part, chunks in enumerate(arrived):
                self.value = self.put(chunks, part, True)
        self.line.done(self)


def place_kernel(place_ref, chunks_ref, *rest, by_rows):
    out_ref = rest[-1]
    low = place_ref[0] & ((1 << LOW) - 1)
    _, rows, cols = chunks_ref.shape
    for j in range(1 << LOW):
        values = chunks_ref[j ^ low].astype(jnp.float32)
        if by_rows:
            out_ref[j * rows : (j + 1) * rows, :] = values
        else:
            out_ref[:, j * cols : (j + 1) * cols] = values


def put_in_place(place, chunks, far, into, part, parts, by_rows, name):
    half, rows, cols = chunks.shape
    steps = half >> LOW
    first = steps if far else 0

    def block(step, place_ref):
        return part * 2 * steps + ((step + first) ^ (place_ref[0] >> LOW))

    if by_rows:
        out_shape = (rows * 2 * half * parts, cols)
        out_spec = pl.BlockSpec((rows << LOW, cols), lambda s, p: (block(s, p), 0))
    else:
        out_shape = (rows, cols * 2 * half * parts)
        out_spec = pl.BlockSpec((rows, cols << LOW), lambda s, p: (0, block(s, p)))
    in_specs = [pl.BlockSpec((1 << LOW, rows, cols), lambda s, p: (s, 0, 0))]
    operands = [place, chunks]
    if into is not None:
        in_specs.append(pl.BlockSpec(memory_space=pl.ANY))
        operands.append(into)
    return pl.pallas_call(
        partial(place_kernel, by_rows=by_rows),
        grid_spec=pltpu.PrefetchScalarGridSpec(
            num_scalar_prefetch=1, grid=(steps,), in_specs=in_specs, out_specs=out_spec
        ),
        out_shape=jax.ShapeDtypeStruct(out_shape, jnp.float32),
        input_output_aliases={} if into is None else {2: 0},
        compiler_params=pltpu.CompilerParams(vmem_limit_bytes=48 << 20),
        name=name,
    )(*operands)


def place_three_kernel(place_ref, chunks_ref, *rest, bits):
    out_ref = rest[-1]
    count, _, _, cols = chunks_ref.shape
    low = place_ref[0] & (count - 1)
    for j in range(count):
        spot = sum(((j // bit) & 1) << (len(bits) - 1 - k) for k, bit in enumerate(bits))
        out_ref[:, j * cols : (j + 1) * cols] = chunks_ref[spot ^ low, 0].astype(jnp.float32)


def put_three_in_place(place, chunks, far, into, bits, dp_count, name):
    total, three, rows, cols = chunks.shape
    ctx_count = 1 << len(bits)
    steps = total // ctx_count
    first = steps if far else 0
    in_specs = [pl.BlockSpec((ctx_count, 1, rows, cols), lambda s, t, p: (s, t, 0, 0))]
    operands = [place, chunks]
    if into is not None:
        in_specs.append(pl.BlockSpec(memory_space=pl.ANY))
        operands.append(into)
    return pl.pallas_call(
        partial(place_three_kernel, bits=bits),
        grid_spec=pltpu.PrefetchScalarGridSpec(
            num_scalar_prefetch=1,
            grid=(steps, three),
            in_specs=in_specs,
            out_specs=pl.BlockSpec(
                (rows, ctx_count * cols),
                lambda s, t, p: ((s + first) ^ (p[0] >> len(bits)), t),
            ),
        ),
        out_shape=jax.ShapeDtypeStruct((rows * dp_count, three * ctx_count * cols), jnp.float32),
        input_output_aliases={} if into is None else {2: 0},
        compiler_params=pltpu.CompilerParams(vmem_limit_bytes=48 << 20),
        name=name,
    )(*operands)


def on_device(
    tokens,
    query_key_value_weight,
    bias_query,
    bias_value,
    attention_out_weight,
    attention_out_bias,
    gain_one,
    shift_one,
    feedforward_in_weight,
    feedforward_in_bias,
    feedforward_out_weight,
    feedforward_out_bias,
    gain_two,
    shift_two,
    d_out,
):
    core = lax.axis_index("fsdp")
    ctx = lax.axis_index("ctx")
    ctx_count = lax.axis_size("ctx")
    seqs, block_rows, width = tokens.shape
    pair = width // ctx_count
    flat = seqs * block_rows

    first_pieces = gather_first(tokens)

    small = (
        bias_query, bias_value, attention_out_bias, gain_one, shift_one,
        feedforward_in_bias, feedforward_out_bias, gain_two, shift_two,
    )
    small, near_piece = lax.optimization_barrier((small, first_pieces[0]))
    first_pieces = (near_piece,) + first_pieces[1:]
    packed = jnp.concatenate(small)
    packed_other = exchange(packed, "fsdp", 1)
    vectors = []
    offset = 0
    for part in small:
        size = part.shape[0]
        vectors.append(widened(pair_join(part, packed_other[offset : offset + size], core)))
        offset += size
    (
        query_bias, value_bias, out_bias, gain_first, shift_first,
        inner_bias, back_bias, gain_second, shift_second,
    ) = vectors
    qkv_full = pair_join(
        query_key_value_weight, exchange(query_key_value_weight, "fsdp", 1), core
    )
    out_full = pair_join(attention_out_weight, exchange(attention_out_weight, "fsdp", 1), core)
    in_pair = (feedforward_in_weight, exchange(feedforward_in_weight, "fsdp", 1))
    back_pair = (feedforward_out_weight, exchange(feedforward_out_weight, "fsdp", 1))
    core_index = core.astype(jnp.int32).reshape(1)

    head_weight = jnp.concatenate(
        [lax.dynamic_slice_in_dim(qkv_full, t * width + ctx * pair, pair, axis=1) for t in range(3)],
        axis=1,
    )
    head_bias = jnp.concatenate(
        [
            lax.dynamic_slice_in_dim(query_bias, ctx * pair, pair),
            jnp.zeros((pair,), jnp.float32),
            lax.dynamic_slice_in_dim(value_bias, ctx * pair, pair),
        ]
    )
    token_pieces, projected_pieces, out_full = gather_rest(
        tokens,
        first_pieces,
        lambda piece: project_block(piece, head_weight, head_bias[None]),
        out_full,
    )
    projected = jnp.concatenate(projected_pieces, axis=1)
    head_result, head_low, head_logs = attention_forward(projected)

    def row_blocks(values):
        return [
            lax.slice_in_dim(values, k * block_rows, (k + 1) * block_rows, axis=1)
            for k in range(ctx_count)
        ]

    attended_pieces = reorder(swap_blocks(row_blocks(head_low)), ctx)
    attended_low = jnp.concatenate(attended_pieces, axis=-1)
    attention_branch = project(attended_low, out_full) + out_bias
    summed_one = widened(tokens) + attention_branch
    first_normalized, pull_one = jax.vjp(norm_apply, summed_one, gain_first, shift_first)
    normed_low = lowered(first_normalized)
    active_flat, slope, second = ffn_forward(
        core_index, normed_low.reshape(flat, width), in_pair, back_pair, inner_bias[None]
    )
    active_low = active_flat.reshape(seqs, block_rows, -1)
    feedforward_branch = second.reshape(tokens.shape) + back_bias

    def second_norm(residual_in, branch_in, gain_vec, shift_vec):
        return norm_apply(residual_in + branch_in, gain_vec, shift_vec)

    result, pull_two = jax.vjp(
        second_norm, first_normalized, feedforward_branch, gain_second, shift_second
    )
    output = lowered(result)
    first_grad_res, second_grad, gain_two_grad, shift_two_grad = pull_two(widened(d_out))
    second_low = lowered(second_grad)

    def left_pair(values):
        rows = values.reshape(flat, values.shape[2])
        return (half_of(rows, core, 1), exchange(half_of(rows, 1 - core, 1), "fsdp", 1))

    def right_pair(values):
        rows = values.reshape(flat, values.shape[2])
        return (rows, exchange(rows, "fsdp", 1))

    places = {name: place_of(hops(name)) for name in ORDERS}
    count = 1 << len(hops("q"))

    active_pair = left_pair(active_low)
    normed_pair = left_pair(normed_low)
    attended_pair = left_pair(attended_low)
    second_pair = right_pair(second_low)
    back_parts = [
        pair_grad(places[n], active_pair, second_pair, count, part, 2, True, "grad_back")
        for part, n in enumerate(("b0", "b1"))
    ]
    back_bias_grad = column_sum(second_low)
    hidden_flat, first_part = ffn_backward(
        core_index, second_low.reshape(flat, width), slope, in_pair, back_pair
    )
    hidden_low = hidden_flat.reshape(seqs, block_rows, -1)
    hidden_low, back_parts = lax.optimization_barrier((hidden_low, back_parts))
    hidden_pair = right_pair(hidden_low)
    in_bias_grad = column_sum(hidden_low)
    first_grad = first_grad_res + first_part.reshape(tokens.shape)
    summed_grad, gain_one_grad, shift_one_grad = pull_one(first_grad)
    branch_low = lowered(summed_grad)
    branch_pair = right_pair(branch_low)
    out_bias_grad = column_sum(branch_low)
    attended_grad = lowered(back_project(branch_low, out_full))
    column_pieces = reorder(
        [attended_grad[..., k * pair : (k + 1) * pair] for k in range(ctx_count)], ctx
    )
    column_pieces, hidden_pair = lax.optimization_barrier((column_pieces, hidden_pair))
    head_grad_pieces = swap_blocks(column_pieces)
    in_parts = [
        pair_grad(places[n], normed_pair, hidden_pair, count, part, 2, False, "grad_in")
        for part, n in enumerate(("i0", "i1"))
    ]
    branch_pair, in_parts = lax.optimization_barrier((branch_pair, in_parts))
    out_parts = pair_grad(
        places["o"], attended_pair, branch_pair, count, 0, 1, True, "grad_out"
    )

    whole = {"back": None, "in": None, "out": None, "qkv": None}

    def placer(target, names, by_rows):
        def put(chunks, part, far):
            whole[target] = put_in_place(
                places[names[part]], chunks, far, whole[target], part, len(names), by_rows,
                "place_" + target,
            )
            return whole[target]

        return put

    put_out = placer("out", ("o",), True)

    class Placed:
        def __init__(self, target):
            self.target = target

        @property
        def value(self):
            return whole[self.target]

        @value.setter
        def value(self, new):
            whole[self.target] = new

    line = Line()
    chains = {
        "b": Group(line, ("b0", "b1"), back_parts, placer("back", ("b0", "b1"), True)),
        "i": Group(line, ("i0", "i1"), in_parts, placer("in", ("i0", "i1"), False)),
        "o": Reduction(line, "o", *out_parts, lambda chunks, far: put_out(chunks, 0, far)),
    }
    targets = {"b": ("back", 9), "i": ("in", 9), "o": ("out", 8)}
    line.done(chains["o"])

    class Attention:
        def advance(self):
            head_grad = jnp.concatenate(line.after(head_grad_pieces), axis=1)
            self.head_grads = attention_backward(projected, head_grad, head_result, head_logs)
            self.value, other = qkv_grad_parts(core_index, token_pieces, self.head_grads)
            self.other = exchange(other, "fsdp", 1)
            chains["v"].begin(self.head_grads)
            line.done(self)

    layer_vectors = (
        in_bias_grad, back_bias_grad, gain_two_grad, shift_two_grad,
        out_bias_grad, gain_one_grad, shift_one_grad,
    )

    class Vectors:
        def begin(self, head_grads):
            spread_out = []
            for part in (head_grads[0], head_grads[2]):
                spread_out.append(
                    lax.dynamic_update_slice_in_dim(
                        jnp.zeros((width,), jnp.float32), column_sum(part), ctx * pair, 0
                    )
                )
            self.value = jnp.concatenate(layer_vectors + tuple(spread_out))
            self.routes = [("fsdp", 1)] + hops("v")
            self.step = 0
            self.arrived = exchange(self.value, *self.routes[0])

        def advance(self):
            arrived, value = line.after((self.arrived, self.value))
            self.value = value + arrived
            self.step += 1
            if self.step < len(self.routes):
                self.arrived = exchange(self.value, *self.routes[self.step])
            line.done(self)

    class QueryKeyValue:
        def __init__(self):
            self.step = 0

        def advance(self):
            step = self.step
            self.step += 1
            order = hops("q")
            if step == 0:
                other, own = line.after((chains["A"].other, chains["A"].value))
                total = own + widened(other)
                half = total.shape[1] // 2
                low, high = total[:, :half], total[:, half:]
                first = lax.axis_index("dp") == 0
                self.value = jnp.where(first, low, high)
                self.arrived = exchange(lowered(jnp.where(first, high, low)), *order[0])
            elif step == 1:
                arrived, value = line.after((self.arrived, self.value))
                self.value = lowered(value + widened(arrived))[None]
                self.arrived = exchange(self.value, *order[-1])
            elif step <= len(order):
                arrived, value = line.after((self.arrived, self.value))
                self.value = jnp.concatenate([value, arrived], axis=0)
                self.arrived = exchange(self.value, *order[len(order) - step])
                if step == len(order):
                    self.put(self.value, False)
            else:
                arrived, value = line.after((self.arrived, self.value))
                self.value = self.put(arrived, True)
                line.done(Placed("qkv"))
                return
            line.done(self)

        def put(self, chunks, far):
            bits = [bit for axis, bit in hops("q")[1:]]
            whole["qkv"] = put_three_in_place(
                places["q"], chunks, far, whole["qkv"], bits, 2, "place_qkv"
            )
            return whole["qkv"]

    class Tokens:
        def __init__(self):
            self.step = 0

        def advance(self):
            order = hops("T")
            if self.step == 0:
                blocks = [row_blocks(part) for part in chains["A"].head_grads]
                pieces = line.after(
                    [jnp.concatenate([m[k] for m in blocks], axis=-1) for k in range(ctx_count)]
                )
                held = {(0, k): piece for k, piece in enumerate(pieces)}
            else:
                bit = order[self.step - 1][1]
                arrived, kept = line.after((self.arrived, self.value))
                held = dict(zip(self.kept, kept))
                for n, (source, target) in enumerate(self.sent):
                    held[source ^ bit, target ^ bit] = arrived[n]
            if self.step < len(order):
                bit = order[self.step][1]
                self.sent = [key for key in sorted(held) if key[1] & bit]
                self.kept = [key for key in sorted(held) if not key[1] & bit]
                self.arrived = exchange(jnp.stack([held[key] for key in self.sent]), *order[self.step])
                self.value = [held[key] for key in self.kept]
            else:
                mixed = reorder([held[k, 0] for k in range(ctx_count)], ctx)
                mixed_grad = jnp.concatenate(
                    [m[..., t * pair : (t + 1) * pair] for t in range(3) for m in mixed], axis=-1
                )
                self.value = summed_grad + back_project(mixed_grad, qkv_full)
            self.step += 1
            line.done(self)

    chains.update(A=Attention(), v=Vectors(), q=QueryKeyValue(), T=Tokens())
    for name in EVENTS:
        chain = chains[name]
        chain.advance()
        if name in targets and chain.step == targets[name][1]:
            line.done(Placed(targets[name][0]))

    reduced = []
    offset = 0
    sizes = [part.shape[0] for part in layer_vectors] + [width, width]
    for size in sizes:
        reduced.append(half_of(chains["v"].value[offset : offset + size], core, 0))
        offset += size
    token_grad = chains["T"].value
    qkv_grad, in_grad, back_grad, out_grad = (
        whole["qkv"], whole["in"], whole["back"], whole["out"]
    )
    bias_grads = reduced[7:]
    return (
        output,
        token_grad,
        qkv_grad,
        bias_grads[0],
        bias_grads[1],
        out_grad,
        reduced[4],
        reduced[5],
        reduced[6],
        in_grad,
        reduced[0],
        back_grad,
        reduced[1],
        reduced[2],
        reduced[3],
    )


def head_parallel(mesh):
    sizes = [mesh.shape["dp"], mesh.shape["ctx"]]
    return sizes == [2, 8] and mesh.shape["fsdp"] == 2 and 2 * sizes[1] == HEADS


def solution(mesh):
    in_specs = (
        P(("dp", "fsdp"), "ctx", None),
        P("fsdp", None),
        P("fsdp"),
        P("fsdp"),
        P("fsdp", None),
        P("fsdp"),
        P("fsdp"),
        P("fsdp"),
        P("fsdp", None),
        P("fsdp"),
        P("fsdp", None),
        P("fsdp"),
        P("fsdp"),
        P("fsdp"),
        P(("dp", "fsdp"), "ctx", None),
    )
    out_specs = (
        P(("dp", "fsdp"), "ctx", None),
        P(("dp", "fsdp"), "ctx", None),
        P("fsdp", None),
        P("fsdp"),
        P("fsdp"),
        P("fsdp", None),
        P("fsdp"),
        P("fsdp"),
        P("fsdp"),
        P("fsdp", None),
        P("fsdp"),
        P("fsdp", None),
        P("fsdp"),
        P("fsdp"),
        P("fsdp"),
    )
    body = on_device if head_parallel(mesh) else ring_on_device
    return jax.shard_map(
        body, mesh=mesh, in_specs=in_specs, out_specs=out_specs, check_vma=False
    )
```

```python
from functools import partial

import jax
import jax.numpy as jnp
from jax import lax
from jax.experimental import pallas as pl
from jax.experimental.pallas import tpu as pltpu
from jax.sharding import PartitionSpec as P

HEADS = 16
HEAD_DIM = 64


EPSILON = 1e-06


def from_behind(block, axis, distance):
    devices = range(lax.axis_size(axis))
    route = [((i - distance) % len(devices), i) for i in devices]
    return lax.ppermute(block, axis, route)


def norm_apply(values, gain_vec, shift_vec):
    centre = jnp.mean(values, axis=-1, keepdims=True)
    centred = values - centre
    variance = jnp.mean(centred * centred, axis=-1, keepdims=True)
    return centred * lax.rsqrt(variance + EPSILON) * gain_vec + shift_vec


def lowered(values):
    return values.astype(jnp.bfloat16)


def widened(values):
    return values.astype(jnp.float32)


def project(left_operand_rows, right_operand_matrix):
    return jnp.einsum(
        "ugj,jn->ugn", left_operand_rows, right_operand_matrix, preferred_element_type=jnp.float32
    )


def weight_grad(left_operand_rows, gradient_row_block):
    return jnp.einsum(
        "xrb,xrw->bw", left_operand_rows, gradient_row_block, preferred_element_type=jnp.float32
    )


def back_project(gradient_row_block, right_operand_matrix):
    return jnp.einsum(
        "wkb,fb->wkf", gradient_row_block, right_operand_matrix, preferred_element_type=jnp.float32
    )


def column_sum(values):
    return jnp.sum(widened(values), axis=(0, 1))


def split_heads(values):
    return values.reshape(values.shape[0], values.shape[1], HEADS, HEAD_DIM)


def merge_heads(values):
    return values.reshape(values.shape[0], values.shape[1], HEADS * HEAD_DIM)


def split_blocks(values, block_rows):
    seq_count = values.shape[0]
    blocks = values.shape[1] // block_rows
    return jnp.moveaxis(values.reshape(seq_count, blocks, block_rows, values.shape[2]), 1, 0)


def block_scores(query_rows, key_rows):
    scores = jnp.einsum(
        "sqhd,skhd->shqk",
        split_heads(query_rows),
        split_heads(key_rows),
        preferred_element_type=jnp.float32,
    )
    return scores * HEAD_DIM ** (-0.5)


def fold_block(state_now, key_block, value_block, query_rows):
    running_max, running_sum, running_acc = state_now
    scores = block_scores(query_rows, key_block)
    new_max = jnp.maximum(running_max, jnp.max(scores, axis=-1))
    rescale = jnp.exp(running_max - new_max)
    weights = jnp.exp(scores - new_max[..., None])
    new_sum = running_sum * rescale + jnp.sum(weights, axis=-1)
    product = jnp.einsum(
        "shqk,skhd->shqd",
        lowered(weights),
        split_heads(value_block),
        preferred_element_type=jnp.float32,
    )
    return (new_max, new_sum, running_acc * rescale[..., None] + product)


def attend_forward(query_rows, key_rows, value_rows):
    seq_count = query_rows.shape[0]
    block_rows = query_rows.shape[1]
    initial = (
        jnp.full((seq_count, HEADS, block_rows), -1e30, jnp.float32),
        jnp.zeros((seq_count, HEADS, block_rows), jnp.float32),
        jnp.zeros((seq_count, HEADS, block_rows, HEAD_DIM), jnp.float32),
    )
    kept = None
    key_part = lax.all_gather(key_rows, "ctx", axis=1, tiled=True)
    value_part = lax.all_gather(value_rows, "ctx", axis=1, tiled=True)

    def one_block(state_in, block_pair):
        return (fold_block(state_in, block_pair[0], block_pair[1], query_rows), None)

    state_out, unused = lax.scan(
        one_block,
        initial,
        (split_blocks(key_part, block_rows), split_blocks(value_part, block_rows)),
    )
    running_max, running_sum, running_acc = state_out
    attention_result = running_acc / running_sum[..., None]
    attention_result = jnp.transpose(attention_result, (0, 2, 1, 3)).reshape(
        seq_count, block_rows, HEADS * HEAD_DIM
    )
    log_total = running_max + jnp.log(running_sum)
    return (attention_result, log_total, kept)


def attend_back(query_rows, gradient_row_block, log_total, row_inner, key_rows, value_rows):
    score_scale = HEAD_DIM ** (-0.5)
    scores = block_scores(query_rows, key_rows)
    probabilities = jnp.exp(scores - log_total[..., None])
    value_grad = jnp.einsum(
        "shqk,sqhd->skhd",
        lowered(probabilities),
        split_heads(gradient_row_block),
        preferred_element_type=jnp.float32,
    )
    prob_grad = jnp.einsum(
        "sqhd,skhd->shqk",
        split_heads(gradient_row_block),
        split_heads(value_rows),
        preferred_element_type=jnp.float32,
    )
    score_grad = lowered(probabilities * (prob_grad - row_inner[..., None]))
    query_grad = (
        jnp.einsum(
            "shqk,skhd->sqhd", score_grad, split_heads(key_rows), preferred_element_type=jnp.float32
        )
        * score_scale
    )
    key_grad = (
        jnp.einsum(
            "shqk,sqhd->skhd",
            score_grad,
            split_heads(query_rows),
            preferred_element_type=jnp.float32,
        )
        * score_scale
    )
    return (merge_heads(query_grad), merge_heads(key_grad), merge_heads(value_grad))


def attend_backward(query_rows, gradient_row_block, log_total, row_inner, key_rows, value_rows):
    zero_rows = jnp.zeros(query_rows.shape, jnp.float32)
    turn_count = lax.axis_size("ctx") // 2

    def turn_keys(turn_index, carried):
        moving_key, moving_value, key_acc, value_acc, query_acc = carried
        for half_step in range(2):
            pieces = attend_back(
                query_rows, gradient_row_block, log_total, row_inner, moving_key, moving_value
            )
            query_acc = query_acc + pieces[0]
            key_acc = key_acc + pieces[1]
            value_acc = value_acc + pieces[2]
            moving_key, moving_value = from_behind((moving_key, moving_value), "ctx", 1)
            key_acc, value_acc = (
                from_behind(key_acc.astype(jnp.bfloat16), "ctx", 1).astype(key_acc.dtype),
                from_behind(value_acc.astype(jnp.bfloat16), "ctx", 1).astype(value_acc.dtype),
            )
        return (moving_key, moving_value, key_acc, value_acc, query_acc)

    finished = lax.fori_loop(
        0, turn_count, turn_keys, (key_rows, value_rows, zero_rows, zero_rows, zero_rows)
    )
    return (finished[4], finished[2], finished[3])


def ring_on_device(
    tokens,
    query_key_value_weight,
    bias_query,
    bias_value,
    attention_out_weight,
    attention_out_bias,
    gain_one,
    shift_one,
    feedforward_in_weight,
    feedforward_in_bias,
    feedforward_out_weight,
    feedforward_out_bias,
    gain_two,
    shift_two,
    d_out,
):
    attn_full = (
        lax.all_gather(query_key_value_weight, "fsdp", axis=0, tiled=True),
        lax.all_gather(attention_out_weight, "fsdp", axis=0, tiled=True),
        lax.all_gather(bias_query, "fsdp", axis=0, tiled=True),
        lax.all_gather(bias_value, "fsdp", axis=0, tiled=True),
        lax.all_gather(attention_out_bias, "fsdp", axis=0, tiled=True),
        lax.all_gather(gain_one, "fsdp", axis=0, tiled=True),
        lax.all_gather(shift_one, "fsdp", axis=0, tiled=True),
    )
    qkv_full, out_full, query_bias, value_bias, out_bias, gain_first, shift_first = attn_full
    model_width = out_full.shape[0]
    projected_rows = project(tokens, qkv_full) + jnp.concatenate(
        [widened(query_bias), jnp.zeros((model_width,), jnp.float32), widened(value_bias)]
    )
    projected_low = lowered(projected_rows)
    query_rows = projected_low[..., :model_width]
    key_rows = projected_low[..., model_width : 2 * model_width]
    value_rows = projected_low[..., 2 * model_width :]
    attention_result, log_total, kept = attend_forward(query_rows, key_rows, value_rows)
    attended_low = lowered(attention_result)
    attention_branch = project(attended_low, out_full) + widened(out_bias)
    summed_one = widened(tokens) + attention_branch
    first_normalized, pull_one = jax.vjp(
        norm_apply, summed_one, widened(gain_first), widened(shift_first)
    )
    normed_low = lowered(first_normalized)
    ffn_full = (
        lax.all_gather(feedforward_in_weight, "fsdp", axis=0, tiled=True),
        lax.all_gather(feedforward_out_weight, "fsdp", axis=0, tiled=True),
        lax.all_gather(feedforward_in_bias, "fsdp", axis=0, tiled=True),
        lax.all_gather(feedforward_out_bias, "fsdp", axis=0, tiled=True),
        lax.all_gather(gain_two, "fsdp", axis=0, tiled=True),
        lax.all_gather(shift_two, "fsdp", axis=0, tiled=True),
    )
    in_full, back_full, inner_bias, back_bias, gain_second, shift_second = ffn_full
    hidden_before_gelu = project(normed_low, in_full) + widened(inner_bias)
    active_low = lowered(jax.nn.gelu(hidden_before_gelu, approximate=False))
    feedforward_branch = project(active_low, back_full) + widened(back_bias)

    def second_norm(residual_in, branch_in, gain_vec, shift_vec):
        return norm_apply(residual_in + branch_in, gain_vec, shift_vec)

    result, pull_two = jax.vjp(
        second_norm,
        first_normalized,
        feedforward_branch,
        widened(gain_second),
        widened(shift_second),
    )
    output = lowered(result)
    first_grad_res, second_grad, gain_two_grad, shift_two_grad = pull_two(widened(d_out))
    in_full, back_full = (
        lax.all_gather(feedforward_in_weight, "fsdp", axis=0, tiled=True),
        lax.all_gather(feedforward_out_weight, "fsdp", axis=0, tiled=True),
    )
    second_low = lowered(second_grad)
    back_grad = weight_grad(active_low, second_low)
    back_bias_grad = column_sum(second_low)
    active_grad = back_project(second_low, back_full)
    gelu_pull = jax.vjp(partial(jax.nn.gelu, approximate=False), hidden_before_gelu)[1]
    hidden_low = lowered(gelu_pull(active_grad)[0])
    in_grad = weight_grad(normed_low, hidden_low)
    in_bias_grad = column_sum(hidden_low)
    first_grad = first_grad_res + back_project(hidden_low, in_full)
    ffn_grads = (
        lax.psum_scatter(
            in_grad.astype(jnp.bfloat16), "fsdp", scatter_dimension=0, tiled=True
        ).astype(jnp.float32),
        lax.psum_scatter(
            in_bias_grad.astype(jnp.bfloat16), "fsdp", scatter_dimension=0, tiled=True
        ).astype(jnp.float32),
        lax.psum_scatter(
            back_grad.astype(jnp.bfloat16), "fsdp", scatter_dimension=0, tiled=True
        ).astype(jnp.float32),
        lax.psum_scatter(
            back_bias_grad.astype(jnp.bfloat16), "fsdp", scatter_dimension=0, tiled=True
        ).astype(jnp.float32),
        lax.psum_scatter(
            gain_two_grad.astype(jnp.bfloat16), "fsdp", scatter_dimension=0, tiled=True
        ).astype(jnp.float32),
        lax.psum_scatter(
            shift_two_grad.astype(jnp.bfloat16), "fsdp", scatter_dimension=0, tiled=True
        ).astype(jnp.float32),
    )
    ffn_grads = lax.psum(
        (ffn_grads[0], ffn_grads[1], ffn_grads[2], ffn_grads[3], ffn_grads[4], ffn_grads[5]),
        ("dp", "ctx"),
    )
    summed_grad, gain_one_grad, shift_one_grad = pull_one(first_grad)
    qkv_full, out_full = (
        lax.all_gather(query_key_value_weight, "fsdp", axis=0, tiled=True),
        lax.all_gather(attention_out_weight, "fsdp", axis=0, tiled=True),
    )
    branch_low = lowered(summed_grad)
    out_grad = weight_grad(attended_low, branch_low)
    out_bias_grad = column_sum(branch_low)
    attended_grad_low = lowered(back_project(branch_low, out_full))
    row_inner = jnp.sum(
        split_heads(widened(attended_grad_low)) * split_heads(attention_result), axis=-1
    )
    row_inner = jnp.transpose(row_inner, (0, 2, 1))
    query_grad, key_grad, value_grad = attend_backward(
        query_rows, attended_grad_low, log_total, row_inner, key_rows, value_rows
    )
    mixed_grad = lowered(jnp.concatenate([query_grad, key_grad, value_grad], axis=-1))
    qkv_grad = weight_grad(tokens, mixed_grad)
    bias_grads = column_sum(mixed_grad)
    query_bias_grad = bias_grads[:model_width]
    value_bias_grad = bias_grads[2 * model_width :]
    token_grad = summed_grad + back_project(mixed_grad, qkv_full)
    attn_grads = (
        lax.psum_scatter(
            qkv_grad.astype(jnp.bfloat16), "fsdp", scatter_dimension=0, tiled=True
        ).astype(jnp.float32),
        lax.psum_scatter(
            query_bias_grad.astype(jnp.bfloat16), "fsdp", scatter_dimension=0, tiled=True
        ).astype(jnp.float32),
        lax.psum_scatter(
            value_bias_grad.astype(jnp.bfloat16), "fsdp", scatter_dimension=0, tiled=True
        ).astype(jnp.float32),
        lax.psum_scatter(
            out_grad.astype(jnp.bfloat16), "fsdp", scatter_dimension=0, tiled=True
        ).astype(jnp.float32),
        lax.psum_scatter(
            out_bias_grad.astype(jnp.bfloat16), "fsdp", scatter_dimension=0, tiled=True
        ).astype(jnp.float32),
        lax.psum_scatter(
            gain_one_grad.astype(jnp.bfloat16), "fsdp", scatter_dimension=0, tiled=True
        ).astype(jnp.float32),
        lax.psum_scatter(
            shift_one_grad.astype(jnp.bfloat16), "fsdp", scatter_dimension=0, tiled=True
        ).astype(jnp.float32),
    )
    attn_grads = lax.psum(
        (
            attn_grads[0],
            attn_grads[1],
            attn_grads[2],
            attn_grads[3],
            attn_grads[4],
            attn_grads[5],
            attn_grads[6],
        ),
        ("dp", "ctx"),
    )
    return (
        output,
        token_grad,
        attn_grads[0],
        attn_grads[1],
        attn_grads[2],
        attn_grads[3],
        attn_grads[4],
        attn_grads[5],
        attn_grads[6],
        ffn_grads[0],
        ffn_grads[1],
        ffn_grads[2],
        ffn_grads[3],
        ffn_grads[4],
        ffn_grads[5],
    )


def exchange(values, axis, bit):
    count = lax.axis_size(axis)
    return lax.ppermute(values, axis, [(i, i ^ bit) for i in range(count)])


def bits_below(count):
    return [1 << k for k in range(count.bit_length() - 1)]


def reorder(pieces, index):
    for bit in bits_below(len(pieces)):
        taken = (index & bit) != 0
        pieces = [jnp.where(taken, pieces[k ^ bit], pieces[k]) for k in range(len(pieces))]
    return pieces


def pair_join(own, other, core, axis=0):
    first = jnp.where(core == 0, own, other)
    second = jnp.where(core == 0, other, own)
    return jnp.concatenate([first, second], axis=axis)


def half_of(values, which, axis):
    size = values.shape[axis] // 2
    low = lax.slice_in_dim(values, 0, size, axis=axis)
    high = lax.slice_in_dim(values, size, 2 * size, axis=axis)
    return jnp.where(which == 0, low, high)


def gather_first(block):
    near, middle, far = (exchange(block, "ctx", bit) for bit in (1, 2, 4))
    return near, middle, far


def gather_rest(block, first, use):
    near, (middle, far) = first[0], lax.optimization_barrier(first[1:])
    third = exchange(middle, "ctx", 1)
    sixth = exchange(far, "ctx", 2)
    fifth = exchange(far, "ctx", 1)
    used = [use(piece) for piece in (block, near, middle, far)]
    third, fifth, sixth, used = lax.optimization_barrier((third, fifth, sixth, used))
    seventh = exchange(sixth, "ctx", 1)
    pieces = [block, near, middle, third, far, fifth, sixth, seventh]
    used = {0: used[0], 1: used[1], 2: used[2], 4: used[3]}
    for k in (3, 5, 6, 7):
        used[k] = use(pieces[k])
    return pieces, [used[k] for k in range(8)]


def swap_blocks(pieces):
    return [pieces[0]] + [exchange(pieces[k], "ctx", k) for k in range(1, len(pieces))]


def head_mask(value):
    lane = lax.broadcasted_iota(jnp.int32, (1, 2 * HEAD_DIM), 1)
    return [
        jnp.where(lane < HEAD_DIM, value, 0.0),
        jnp.where(lane < HEAD_DIM, 0.0, value),
    ]


def contract(left, right, left_dim, right_dim):
    return lax.dot_general(
        left, right, (((left_dim,), (right_dim,)), ((), ())), preferred_element_type=jnp.float32
    )


def project_kernel(block_ref, weight_ref, bias_ref, out_ref):
    for s in range(block_ref.shape[0]):
        out_ref[s] = (contract(block_ref[s], weight_ref[...], 1, 0) + bias_ref[...]).astype(
            jnp.bfloat16
        )


def project_block(block, weight, bias):
    shape = block.shape[:2] + (weight.shape[1],)
    return pl.pallas_call(
        project_kernel,
        out_shape=jax.ShapeDtypeStruct(shape, jnp.bfloat16),
        compiler_params=pltpu.CompilerParams(vmem_limit_bytes=40 << 20),
        name="project_block",
    )(block, weight, bias)


def forward_kernel(query_ref, key_ref, value_ref, result_ref, low_ref, log_ref):
    query = query_ref[0].astype(jnp.float32)
    keys = key_ref[0]
    values = value_ref[0]
    results = []
    logs = []
    for mask in head_mask(HEAD_DIM ** (-0.5)):
        scores = contract((query * mask).astype(jnp.bfloat16), keys, 1, 1)
        row_max = jnp.max(scores, axis=-1, keepdims=True)
        weights = jnp.exp(scores - row_max)
        total = jnp.sum(weights, axis=-1, keepdims=True)
        probabilities = (weights * (1.0 / total)).astype(jnp.bfloat16)
        results.append(contract(probabilities, values, 1, 0))
        logs.append(row_max + jnp.log(total))
    first = lax.broadcasted_iota(jnp.int32, results[0].shape, 1) < HEAD_DIM
    result = jnp.where(first, results[0], results[1])
    result_ref[0] = result
    low_ref[0] = result.astype(jnp.bfloat16)
    log_ref[0] = jnp.where(first, logs[0], logs[1])


def attention_forward(projected):
    seqs, length, width = projected.shape
    pair = width // 3
    rows = min(256, length)
    row_spec = pl.BlockSpec((1, rows, pair), lambda s, q: (s, q, 0))
    return pl.pallas_call(
        forward_kernel,
        grid=(seqs, length // rows),
        in_specs=[
            row_spec,
            pl.BlockSpec((1, length, pair), lambda s, q: (s, 0, 1)),
            pl.BlockSpec((1, length, pair), lambda s, q: (s, 0, 2)),
        ],
        out_specs=[row_spec, row_spec, row_spec],
        out_shape=[
            jax.ShapeDtypeStruct((seqs, length, pair), jnp.float32),
            jax.ShapeDtypeStruct((seqs, length, pair), jnp.bfloat16),
            jax.ShapeDtypeStruct((seqs, length, pair), jnp.float32),
        ],
        compiler_params=pltpu.CompilerParams(vmem_limit_bytes=48 << 20),
        name="attention_forward",
    )(projected, projected, projected)


def backward_kernel(
    query_ref, key_ref, value_ref, grad_ref, result_ref, log_ref,
    query_out, key_out, value_out, query_acc, log_rows, inner_rows,
):
    step = pl.program_id(1)

    @pl.when(step == 0)
    def first_step():
        query_acc[...] = jnp.zeros_like(query_acc)
        logs = jnp.transpose(log_ref[0])
        inner = jnp.transpose(grad_ref[0].astype(jnp.float32) * result_ref[0])
        for h in range(2):
            log_rows[h] = jnp.broadcast_to(
                logs[h * HEAD_DIM : h * HEAD_DIM + 1], log_rows.shape[1:]
            )
            inner_rows[h] = jnp.broadcast_to(
                jnp.sum(inner[h * HEAD_DIM : (h + 1) * HEAD_DIM], axis=0, keepdims=True),
                inner_rows.shape[1:],
            )

    queries = query_ref[0]
    grads = grad_ref[0]
    keys = key_ref[0]
    values = value_ref[0]
    scale = HEAD_DIM ** (-0.5)
    query_parts = []
    key_parts = []
    value_parts = []
    scaled_masks = head_mask(scale)
    masks = head_mask(1.0)
    for h in range(2):
        scores = contract(
            (keys.astype(jnp.float32) * scaled_masks[h]).astype(jnp.bfloat16), queries, 1, 1
        )
        probabilities = jnp.exp(scores - log_rows[h, :1])
        prob_grad = contract(
            (values.astype(jnp.float32) * masks[h]).astype(jnp.bfloat16), grads, 1, 1
        )
        score_grad = (probabilities * (prob_grad - inner_rows[h, :1])).astype(jnp.bfloat16)
        value_parts.append(contract(probabilities.astype(jnp.bfloat16), grads, 1, 0))
        key_parts.append(contract(score_grad, queries, 1, 0))
        query_parts.append(contract(score_grad, keys, 0, 0))
    first = lax.broadcasted_iota(jnp.int32, key_parts[0].shape, 1) < HEAD_DIM
    value_out[0] = jnp.where(first, value_parts[0], value_parts[1]).astype(jnp.bfloat16)
    key_out[0] = (jnp.where(first, key_parts[0], key_parts[1]) * scale).astype(jnp.bfloat16)
    first = lax.broadcasted_iota(jnp.int32, query_parts[0].shape, 1) < HEAD_DIM
    query_acc[...] += jnp.where(first, query_parts[0], query_parts[1])

    @pl.when(step == pl.num_programs(1) - 1)
    def last_step():
        query_out[0] = (query_acc[...] * scale).astype(jnp.bfloat16)


def attention_backward(projected, grads, result, logs):
    seqs, length, width = projected.shape
    pair = width // 3
    rows = min(256, length)
    whole = pl.BlockSpec((1, length, pair), lambda s, k: (s, 0, 0))
    block = pl.BlockSpec((1, rows, pair), lambda s, k: (s, k, 0))
    shape = jax.ShapeDtypeStruct((seqs, length, pair), jnp.bfloat16)
    return pl.pallas_call(
        backward_kernel,
        grid=(seqs, length // rows),
        in_specs=[
            whole,
            pl.BlockSpec((1, rows, pair), lambda s, k: (s, k, 1)),
            pl.BlockSpec((1, rows, pair), lambda s, k: (s, k, 2)),
            whole,
            whole,
            whole,
        ],
        out_specs=[whole, block, block],
        out_shape=[shape, shape, shape],
        scratch_shapes=[
            pltpu.VMEM((length, pair), jnp.float32),
            pltpu.VMEM((2, 8, length), jnp.float32),
            pltpu.VMEM((2, 8, length), jnp.float32),
        ],
        compiler_params=pltpu.CompilerParams(vmem_limit_bytes=48 << 20),
        name="attention_backward",
    )(projected, projected, projected, grads, result, logs)


def ffn_forward_kernel(
    core_ref, left_own, left_other, in_own, in_other, bias_ref, back_own, back_other,
    active_ref, slope_ref, second_ref,
):
    step = pl.program_id(0)
    hidden = contract(left_own[...], in_own[...], 1, 0)
    hidden = hidden + contract(left_other[...], in_other[...], 1, 0) + bias_ref[...]
    below = 0.5 * (1.0 + lax.erf(hidden * 0.7071067811865476))
    slope = below + hidden * (jnp.exp(-0.5 * hidden * hidden) * 0.3989422804014327)
    active = (hidden * below).astype(jnp.bfloat16)
    active_ref[...] = active
    slope_ref[...] = slope.astype(jnp.bfloat16)

    @pl.when(step == 0)
    def first():
        second_ref[...] = contract(active, back_own[...], 1, 0)

    @pl.when((step > 0) & (step < pl.num_programs(0) // 2))
    def own():
        second_ref[...] += contract(active, back_own[...], 1, 0)

    @pl.when(step >= pl.num_programs(0) // 2)
    def other():
        second_ref[...] += contract(active, back_other[...], 1, 0)


def ffn_specs(half, block, width, hidden):
    near = hidden // (2 * block)

    def spot(s, p):
        return jnp.where(s < near, s + p[0] * near, s - p[0] * near)

    weights = [
        pl.BlockSpec((half, block), lambda s, p: (0, spot(s, p))),
        pl.BlockSpec((half, block), lambda s, p: (0, spot(s, p))),
        pl.BlockSpec((block, width), lambda s, p: (jnp.minimum(s, near - 1), 0)),
        pl.BlockSpec((block, width), lambda s, p: (jnp.maximum(s - near, 0), 0)),
    ]
    return spot, weights


def ffn_forward(core, left, in_pair, back_pair, bias):
    tokens, width = left.shape
    half, hidden = in_pair[0].shape
    block = 1024
    spot, weights = ffn_specs(half, block, width, hidden)
    wide = pl.BlockSpec((tokens, block), lambda s, p: (0, spot(s, p)))
    return pl.pallas_call(
        ffn_forward_kernel,
        grid_spec=pltpu.PrefetchScalarGridSpec(
            num_scalar_prefetch=1,
            grid=(hidden // block,),
            in_specs=[
                pl.BlockSpec((tokens, half), lambda s, p: (0, p[0])),
                pl.BlockSpec((tokens, half), lambda s, p: (0, 1 - p[0])),
                weights[0],
                weights[1],
                pl.BlockSpec((1, block), lambda s, p: (0, spot(s, p))),
                weights[2],
                weights[3],
            ],
            out_specs=[wide, wide, pl.BlockSpec((tokens, width), lambda s, p: (0, 0))],
        ),
        out_shape=[
            jax.ShapeDtypeStruct((tokens, hidden), jnp.bfloat16),
            jax.ShapeDtypeStruct((tokens, hidden), jnp.bfloat16),
            jax.ShapeDtypeStruct((tokens, width), jnp.float32),
        ],
        compiler_params=pltpu.CompilerParams(vmem_limit_bytes=40 << 20),
        name="ffn_forward",
    )(core, left, left, *in_pair, bias, *back_pair)


def ffn_backward_kernel(
    core_ref, grad_ref, slope_ref, in_own, in_other, back_own, back_other,
    hidden_ref, total_ref, own_acc, other_acc,
):
    step = pl.program_id(0)
    half = own_acc.shape[1]

    def rest(back_ref):
        active_grad = contract(grad_ref[...], back_ref[...], 1, 1)
        hidden = (active_grad * slope_ref[...].astype(jnp.float32)).astype(jnp.bfloat16)
        hidden_ref[...] = hidden
        own = contract(hidden, in_own[...], 1, 1)
        other = contract(hidden, in_other[...], 1, 1)

        @pl.when(step == 0)
        def first():
            own_acc[...] = own
            other_acc[...] = other

        @pl.when(step > 0)
        def later():
            own_acc[...] += own
            other_acc[...] += other

    @pl.when(step < pl.num_programs(0) // 2)
    def with_own():
        rest(back_own)

    @pl.when(step >= pl.num_programs(0) // 2)
    def with_other():
        rest(back_other)

    @pl.when(step == pl.num_programs(0) - 1)
    def last():
        @pl.when(core_ref[0] == 0)
        def straight():
            total_ref[:, :half] = own_acc[...]
            total_ref[:, half:] = other_acc[...]

        @pl.when(core_ref[0] != 0)
        def crossed():
            total_ref[:, :half] = other_acc[...]
            total_ref[:, half:] = own_acc[...]


def ffn_backward(core, grad, slope, in_pair, back_pair):
    tokens, width = grad.shape
    half, hidden = in_pair[0].shape
    block = 1024
    spot, weights = ffn_specs(half, block, width, hidden)
    wide = pl.BlockSpec((tokens, block), lambda s, p: (0, spot(s, p)))
    whole = pl.BlockSpec((tokens, width), lambda s, p: (0, 0))
    return pl.pallas_call(
        ffn_backward_kernel,
        grid_spec=pltpu.PrefetchScalarGridSpec(
            num_scalar_prefetch=1,
            grid=(hidden // block,),
            in_specs=[whole, wide, *weights],
            out_specs=[wide, whole],
            scratch_shapes=[
                pltpu.VMEM((tokens, half), jnp.float32),
                pltpu.VMEM((tokens, half), jnp.float32),
            ],
        ),
        out_shape=[
            jax.ShapeDtypeStruct((tokens, hidden), jnp.bfloat16),
            jax.ShapeDtypeStruct((tokens, width), jnp.float32),
        ],
        compiler_params=pltpu.CompilerParams(vmem_limit_bytes=40 << 20),
        name="ffn_backward",
    )(core, grad, slope, *in_pair, *back_pair)


def qkv_grad_kernel(core_ref, *refs, pieces):
    token_refs, grad_refs = refs[:pieces], refs[pieces : pieces + 3]
    own_ref, other_ref = refs[pieces + 3 :]
    seqs = token_refs[0].shape[0]
    rows = jnp.concatenate([ref[s] for s in range(seqs) for ref in token_refs], axis=0)
    parts = []
    for ref in grad_refs:
        grads = jnp.concatenate([ref[s] for s in range(seqs)], axis=0)
        parts.append(contract(rows, grads, 0, 0))
    half = pl.num_programs(0) // 2

    @pl.when(pl.program_id(0) < half)
    def outgoing():
        for t in range(3):
            other_ref[t] = parts[t].astype(jnp.bfloat16)

    @pl.when(pl.program_id(0) >= half)
    def kept():
        for t in range(3):
            own_ref[t] = parts[t]


def qkv_grad_parts(core, token_pieces, head_grads):
    seqs, rows, width = token_pieces[0].shape
    pair = head_grads[0].shape[2]
    cols = 256
    steps = width // cols
    half = steps // 2

    def spot(s, p):
        return jnp.where(s < half, s + (1 - p[0]) * half, s - half + p[0] * half)

    grads = pl.BlockSpec(head_grads[0].shape, lambda s, p: (0, 0, 0))
    return pl.pallas_call(
        partial(qkv_grad_kernel, pieces=len(token_pieces)),
        grid_spec=pltpu.PrefetchScalarGridSpec(
            num_scalar_prefetch=1,
            grid=(steps,),
            in_specs=[pl.BlockSpec((seqs, rows, cols), lambda s, p: (0, 0, spot(s, p)))]
            * len(token_pieces)
            + [grads] * 3,
            out_specs=[
                pl.BlockSpec((3, cols, pair), lambda s, p: (0, jnp.maximum(s - half, 0), 0)),
                pl.BlockSpec((3, cols, pair), lambda s, p: (0, jnp.minimum(s, half - 1), 0)),
            ],
        ),
        out_shape=[
            jax.ShapeDtypeStruct((3, width // 2, pair), jnp.float32),
            jax.ShapeDtypeStruct((3, width // 2, pair), jnp.bfloat16),
        ],
        compiler_params=pltpu.CompilerParams(vmem_limit_bytes=40 << 20),
        name="grad_qkv",
    )(core, *token_pieces, *head_grads)


LOW = 2


def grad_kernel(place_ref, left_own, left_other, right_own, right_other, keep_ref, send_ref, *, by_rows):
    step = pl.program_id(0)
    half = pl.num_programs(0) // 2
    total = contract(left_own[...], right_own[...], 0, 0)
    total = total + contract(left_other[...], right_other[...], 0, 0)
    total = total.astype(jnp.bfloat16)
    low = place_ref[0] & ((1 << LOW) - 1)
    _, rows, cols = keep_ref.shape

    def put(out_ref):
        for j in range(1 << LOW):
            if by_rows:
                out_ref[j ^ low] = total[j * rows : (j + 1) * rows]
            else:
                out_ref[j ^ low] = total[:, j * cols : (j + 1) * cols]

    @pl.when(step < half)
    def outgoing():
        put(send_ref)

    @pl.when(step >= half)
    def kept():
        put(keep_ref)


def pair_grad(place, left_pair, right_pair, count, part, parts, by_rows, name):
    tokens, width = left_pair[0].shape
    columns = right_pair[0].shape[1]
    steps = count >> LOW
    half = steps // 2

    def block(step, place_ref):
        return part * steps + (((step + half) % steps) ^ (place_ref[0] >> LOW))

    if by_rows:
        rows, cols = width // (parts * count), columns
        left = pl.BlockSpec((tokens, rows << LOW), lambda s, p: (0, block(s, p)))
        right = pl.BlockSpec((tokens, columns), lambda s, p: (0, 0))
    else:
        rows, cols = width, columns // (parts * count)
        left = pl.BlockSpec((tokens, width), lambda s, p: (0, 0))
        right = pl.BlockSpec((tokens, cols << LOW), lambda s, p: (0, block(s, p)))
    shape = jax.ShapeDtypeStruct((count // 2, rows, cols), jnp.bfloat16)
    out_block = (1 << LOW, rows, cols)
    return pl.pallas_call(
        partial(grad_kernel, by_rows=by_rows),
        grid_spec=pltpu.PrefetchScalarGridSpec(
            num_scalar_prefetch=1,
            grid=(steps,),
            in_specs=[left, left, right, right],
            out_specs=[
                pl.BlockSpec(out_block, lambda s, p: (jnp.maximum(s - half, 0), 0, 0)),
                pl.BlockSpec(out_block, lambda s, p: (jnp.minimum(s, half - 1), 0, 0)),
            ],
        ),
        out_shape=[shape, shape],
        compiler_params=pltpu.CompilerParams(vmem_limit_bytes=48 << 20),
        name=name,
    )(place, left_pair[0], left_pair[1], right_pair[0], right_pair[1])


def place_of(order):
    place = jnp.int32(0)
    for axis, bit in order:
        place = place * 2 + jnp.where((lax.axis_index(axis) & bit) != 0, 1, 0)
    return place.astype(jnp.int32).reshape(1)


def added(first, second):
    return lowered(widened(first) + widened(second))


LINKS = {"x": ("dp", 1), "y": ("ctx", 1), "p": ("ctx", 2), "r": ("ctx", 4)}
ORDERS = {"b0": "yxpr", "b1": "xypr", "i0": "pyxr", "i1": "ypxr", "o": "rypx", "q": "xypr", "v": "xypr", "T": "ypr"}
EVENTS = (
    "b", "A", "b", "o", "q", "i", "o", "q", "v", "b", "v", "i", "o", "v", "q", "i",
    "v", "o", "b", "q", "o", "T", "i", "v", "o", "q", "b", "i", "T", "b", "o", "T",
    "q", "i", "o", "b", "i", "b", "T", "i",
)


def hops(name):
    return [LINKS[letter] for letter in ORDERS[name]]


class Line:
    def __init__(self):
        self.last = None

    def after(self, values):
        if self.last is None:
            return values
        values, self.last.value = lax.optimization_barrier((values, self.last.value))
        return values

    def done(self, holder):
        self.last = holder


class Held:
    def __init__(self, value):
        self.value = value


class Reduction:
    def __init__(self, line, name, keep, send, put):
        self.line, self.order, self.put = line, hops(name), put
        self.value, self.step = keep, 0
        self.arrived = exchange(send, *self.order[0])

    def advance(self):
        last = len(self.order) - 1
        step = self.step
        self.step += 1
        arrived, value = self.line.after((self.arrived, self.value))
        if step < last:
            half = value.shape[0] // 2
            send = added(value[half:], arrived[half:])
            self.value = added(value[:half], arrived[:half])
            self.arrived = exchange(send, *self.order[step + 1])
        elif step == last:
            self.value = added(value, arrived)
            self.arrived = exchange(self.value, *self.order[last])
        elif step <= 2 * last:
            self.value = jnp.concatenate([value, arrived], axis=0)
            self.arrived = exchange(self.value, *self.order[2 * last - step])
            if step == 2 * last:
                self.put(self.value, False)
        else:
            self.value = self.put(arrived, True)
        self.line.done(self)


class Group:
    def __init__(self, line, names, parts, put):
        self.line, self.put, self.step = line, put, 1
        self.orders = [hops(name) for name in names]
        self.value = [keep for keep, send in parts]
        self.arrived = [exchange(send, *o[0]) for (keep, send), o in zip(parts, self.orders)]

    def advance(self):
        arrived, value = self.line.after((self.arrived, self.value))
        tail = self.orders[0][2:]
        step = self.step
        self.step += 1
        if step == 1:
            self.arrived = [
                exchange(added(v[v.shape[0] // 2 :], a[v.shape[0] // 2 :]), *o[1])
                for v, a, o in zip(value, arrived, self.orders)
            ]
            self.value = [
                added(v[: v.shape[0] // 2], a[: v.shape[0] // 2]) for v, a in zip(value, arrived)
            ]
        elif step == 2:
            total = jnp.stack([added(v, a) for v, a in zip(value, arrived)], axis=1)
            self.value = total[:2]
            self.arrived = exchange(total[2:], *tail[0])
        elif step == 3:
            self.value = added(value[:1], arrived[:1])
            self.arrived = exchange(added(value[1:], arrived[1:]), *tail[1])
        elif step == 4:
            self.value = added(value, arrived)
            self.arrived = exchange(self.value, *tail[1])
        elif step == 5:
            self.value = jnp.concatenate([value, arrived], axis=0)
            self.arrived = exchange(self.value, *tail[0])
        elif step == 6:
            total = jnp.concatenate([value, arrived], axis=0)
            self.value = [total[:, 0], total[:, 1]]
            self.arrived = [exchange(v, *o[1]) for v, o in zip(self.value, self.orders)]
        elif step == 7:
            self.value = [jnp.concatenate([v, a], axis=0) for v, a in zip(value, arrived)]
            self.arrived = [exchange(v, *o[0]) for v, o in zip(self.value, self.orders)]
            for part, chunks in enumerate(self.value):
                self.put(chunks, part, False)
        else:
            for part, chunks in enumerate(arrived):
                self.value = self.put(chunks, part, True)
        self.line.done(self)


def place_kernel(place_ref, chunks_ref, *rest, by_rows):
    out_ref = rest[-1]
    low = place_ref[0] & ((1 << LOW) - 1)
    _, rows, cols = chunks_ref.shape
    for j in range(1 << LOW):
        values = chunks_ref[j ^ low].astype(jnp.float32)
        if by_rows:
            out_ref[j * rows : (j + 1) * rows, :] = values
        else:
            out_ref[:, j * cols : (j + 1) * cols] = values


def put_in_place(place, chunks, far, into, part, parts, by_rows, name):
    half, rows, cols = chunks.shape
    steps = half >> LOW
    first = steps if far else 0

    def block(step, place_ref):
        return part * 2 * steps + ((step + first) ^ (place_ref[0] >> LOW))

    if by_rows:
        out_shape = (rows * 2 * half * parts, cols)
        out_spec = pl.BlockSpec((rows << LOW, cols), lambda s, p: (block(s, p), 0))
    else:
        out_shape = (rows, cols * 2 * half * parts)
        out_spec = pl.BlockSpec((rows, cols << LOW), lambda s, p: (0, block(s, p)))
    in_specs = [pl.BlockSpec((1 << LOW, rows, cols), lambda s, p: (s, 0, 0))]
    operands = [place, chunks]
    if into is not None:
        in_specs.append(pl.BlockSpec(memory_space=pl.ANY))
        operands.append(into)
    return pl.pallas_call(
        partial(place_kernel, by_rows=by_rows),
        grid_spec=pltpu.PrefetchScalarGridSpec(
            num_scalar_prefetch=1, grid=(steps,), in_specs=in_specs, out_specs=out_spec
        ),
        out_shape=jax.ShapeDtypeStruct(out_shape, jnp.float32),
        input_output_aliases={} if into is None else {2: 0},
        compiler_params=pltpu.CompilerParams(vmem_limit_bytes=48 << 20),
        name=name,
    )(*operands)


def place_three_kernel(place_ref, chunks_ref, *rest, bits):
    out_ref = rest[-1]
    count, _, _, cols = chunks_ref.shape
    low = place_ref[0] & (count - 1)
    for j in range(count):
        spot = sum(((j // bit) & 1) << (len(bits) - 1 - k) for k, bit in enumerate(bits))
        out_ref[:, j * cols : (j + 1) * cols] = chunks_ref[spot ^ low, 0].astype(jnp.float32)


def put_three_in_place(place, chunks, far, into, bits, dp_count, name):
    total, three, rows, cols = chunks.shape
    ctx_count = 1 << len(bits)
    steps = total // ctx_count
    first = steps if far else 0
    in_specs = [pl.BlockSpec((ctx_count, 1, rows, cols), lambda s, t, p: (s, t, 0, 0))]
    operands = [place, chunks]
    if into is not None:
        in_specs.append(pl.BlockSpec(memory_space=pl.ANY))
        operands.append(into)
    return pl.pallas_call(
        partial(place_three_kernel, bits=bits),
        grid_spec=pltpu.PrefetchScalarGridSpec(
            num_scalar_prefetch=1,
            grid=(steps, three),
            in_specs=in_specs,
            out_specs=pl.BlockSpec(
                (rows, ctx_count * cols),
                lambda s, t, p: ((s + first) ^ (p[0] >> len(bits)), t),
            ),
        ),
        out_shape=jax.ShapeDtypeStruct((rows * dp_count, three * ctx_count * cols), jnp.float32),
        input_output_aliases={} if into is None else {2: 0},
        compiler_params=pltpu.CompilerParams(vmem_limit_bytes=48 << 20),
        name=name,
    )(*operands)


def on_device(
    tokens,
    query_key_value_weight,
    bias_query,
    bias_value,
    attention_out_weight,
    attention_out_bias,
    gain_one,
    shift_one,
    feedforward_in_weight,
    feedforward_in_bias,
    feedforward_out_weight,
    feedforward_out_bias,
    gain_two,
    shift_two,
    d_out,
):
    core = lax.axis_index("fsdp")
    ctx = lax.axis_index("ctx")
    ctx_count = lax.axis_size("ctx")
    seqs, block_rows, width = tokens.shape
    pair = width // ctx_count
    flat = seqs * block_rows

    first_pieces = gather_first(tokens)

    small = (
        bias_query, bias_value, attention_out_bias, gain_one, shift_one,
        feedforward_in_bias, feedforward_out_bias, gain_two, shift_two,
    )
    small, near_piece = lax.optimization_barrier((small, first_pieces[0]))
    first_pieces = (near_piece,) + first_pieces[1:]
    packed = jnp.concatenate(small)
    packed_other = exchange(packed, "fsdp", 1)
    vectors = []
    offset = 0
    for part in small:
        size = part.shape[0]
        vectors.append(widened(pair_join(part, packed_other[offset : offset + size], core)))
        offset += size
    (
        query_bias, value_bias, out_bias, gain_first, shift_first,
        inner_bias, back_bias, gain_second, shift_second,
    ) = vectors
    qkv_full = pair_join(
        query_key_value_weight, exchange(query_key_value_weight, "fsdp", 1), core
    )
    out_full = pair_join(attention_out_weight, exchange(attention_out_weight, "fsdp", 1), core)
    in_pair = (feedforward_in_weight, exchange(feedforward_in_weight, "fsdp", 1))
    back_pair = (feedforward_out_weight, exchange(feedforward_out_weight, "fsdp", 1))
    core_index = core.astype(jnp.int32).reshape(1)

    head_weight = jnp.concatenate(
        [lax.dynamic_slice_in_dim(qkv_full, t * width + ctx * pair, pair, axis=1) for t in range(3)],
        axis=1,
    )
    head_bias = jnp.concatenate(
        [
            lax.dynamic_slice_in_dim(query_bias, ctx * pair, pair),
            jnp.zeros((pair,), jnp.float32),
            lax.dynamic_slice_in_dim(value_bias, ctx * pair, pair),
        ]
    )
    token_pieces, projected_pieces = gather_rest(
        tokens, first_pieces, lambda piece: project_block(piece, head_weight, head_bias[None])
    )
    projected = jnp.concatenate(projected_pieces, axis=1)
    head_result, head_low, head_logs = attention_forward(projected)

    def row_blocks(values):
        return [
            lax.slice_in_dim(values, k * block_rows, (k + 1) * block_rows, axis=1)
            for k in range(ctx_count)
        ]

    attended_pieces = reorder(swap_blocks(row_blocks(head_low)), ctx)
    attended_low = jnp.concatenate(attended_pieces, axis=-1)
    attention_branch = project(attended_low, out_full) + out_bias
    summed_one = widened(tokens) + attention_branch
    first_normalized, pull_one = jax.vjp(norm_apply, summed_one, gain_first, shift_first)
    normed_low = lowered(first_normalized)
    active_flat, slope, second = ffn_forward(
        core_index, normed_low.reshape(flat, width), in_pair, back_pair, inner_bias[None]
    )
    active_low = active_flat.reshape(seqs, block_rows, -1)
    feedforward_branch = second.reshape(tokens.shape) + back_bias

    def second_norm(residual_in, branch_in, gain_vec, shift_vec):
        return norm_apply(residual_in + branch_in, gain_vec, shift_vec)

    result, pull_two = jax.vjp(
        second_norm, first_normalized, feedforward_branch, gain_second, shift_second
    )
    output = lowered(result)
    first_grad_res, second_grad, gain_two_grad, shift_two_grad = pull_two(widened(d_out))
    second_low = lowered(second_grad)

    def left_pair(values):
        rows = values.reshape(flat, values.shape[2])
        return (half_of(rows, core, 1), exchange(half_of(rows, 1 - core, 1), "fsdp", 1))

    def right_pair(values):
        rows = values.reshape(flat, values.shape[2])
        return (rows, exchange(rows, "fsdp", 1))

    places = {name: place_of(hops(name)) for name in ORDERS}
    count = 1 << len(hops("q"))

    active_pair = left_pair(active_low)
    normed_pair = left_pair(normed_low)
    attended_pair = left_pair(attended_low)
    second_pair = right_pair(second_low)
    back_parts = [
        pair_grad(places[n], active_pair, second_pair, count, part, 2, True, "grad_back")
        for part, n in enumerate(("b0", "b1"))
    ]
    back_bias_grad = column_sum(second_low)
    hidden_flat, first_part = ffn_backward(
        core_index, second_low.reshape(flat, width), slope, in_pair, back_pair
    )
    hidden_low = hidden_flat.reshape(seqs, block_rows, -1)
    hidden_low, back_parts = lax.optimization_barrier((hidden_low, back_parts))
    hidden_pair = right_pair(hidden_low)
    in_bias_grad = column_sum(hidden_low)
    first_grad = first_grad_res + first_part.reshape(tokens.shape)
    summed_grad, gain_one_grad, shift_one_grad = pull_one(first_grad)
    branch_low = lowered(summed_grad)
    branch_pair = right_pair(branch_low)
    out_bias_grad = column_sum(branch_low)
    attended_grad = lowered(back_project(branch_low, out_full))
    column_pieces = reorder(
        [attended_grad[..., k * pair : (k + 1) * pair] for k in range(ctx_count)], ctx
    )
    column_pieces, hidden_pair = lax.optimization_barrier((column_pieces, hidden_pair))
    head_grad_pieces = swap_blocks(column_pieces)
    in_parts = [
        pair_grad(places[n], normed_pair, hidden_pair, count, part, 2, False, "grad_in")
        for part, n in enumerate(("i0", "i1"))
    ]
    branch_pair, in_parts = lax.optimization_barrier((branch_pair, in_parts))
    out_parts = pair_grad(
        places["o"], attended_pair, branch_pair, count, 0, 1, True, "grad_out"
    )

    whole = {"back": None, "in": None, "out": None, "qkv": None}

    def placer(target, names, by_rows):
        def put(chunks, part, far):
            whole[target] = put_in_place(
                places[names[part]], chunks, far, whole[target], part, len(names), by_rows,
                "place_" + target,
            )
            return whole[target]

        return put

    put_out = placer("out", ("o",), True)

    class Placed:
        def __init__(self, target):
            self.target = target

        @property
        def value(self):
            return whole[self.target]

        @value.setter
        def value(self, new):
            whole[self.target] = new

    line = Line()
    chains = {
        "b": Group(line, ("b0", "b1"), back_parts, placer("back", ("b0", "b1"), True)),
        "i": Group(line, ("i0", "i1"), in_parts, placer("in", ("i0", "i1"), False)),
        "o": Reduction(line, "o", *out_parts, lambda chunks, far: put_out(chunks, 0, far)),
    }
    targets = {"b": ("back", 9), "i": ("in", 9), "o": ("out", 8)}
    line.done(chains["o"])

    class Attention:
        def advance(self):
            head_grad = jnp.concatenate(line.after(head_grad_pieces), axis=1)
            self.head_grads = attention_backward(projected, head_grad, head_result, head_logs)
            self.value, other = qkv_grad_parts(core_index, token_pieces, self.head_grads)
            self.other = exchange(other, "fsdp", 1)
            chains["v"].begin(self.head_grads)
            line.done(self)

    layer_vectors = (
        in_bias_grad, back_bias_grad, gain_two_grad, shift_two_grad,
        out_bias_grad, gain_one_grad, shift_one_grad,
    )

    class Vectors:
        def begin(self, head_grads):
            spread_out = []
            for part in (head_grads[0], head_grads[2]):
                spread_out.append(
                    lax.dynamic_update_slice_in_dim(
                        jnp.zeros((width,), jnp.float32), column_sum(part), ctx * pair, 0
                    )
                )
            self.value = jnp.concatenate(layer_vectors + tuple(spread_out))
            self.routes = [("fsdp", 1)] + hops("v")
            self.step = 0
            self.arrived = exchange(self.value, *self.routes[0])

        def advance(self):
            arrived, value = line.after((self.arrived, self.value))
            self.value = value + arrived
            self.step += 1
            if self.step < len(self.routes):
                self.arrived = exchange(self.value, *self.routes[self.step])
            line.done(self)

    class QueryKeyValue:
        def __init__(self):
            self.step = 0

        def advance(self):
            step = self.step
            self.step += 1
            order = hops("q")
            if step == 0:
                other, own = line.after((chains["A"].other, chains["A"].value))
                total = own + widened(other)
                half = total.shape[1] // 2
                low, high = total[:, :half], total[:, half:]
                first = lax.axis_index("dp") == 0
                self.value = jnp.where(first, low, high)
                self.arrived = exchange(lowered(jnp.where(first, high, low)), *order[0])
            elif step == 1:
                arrived, value = line.after((self.arrived, self.value))
                self.value = lowered(value + widened(arrived))[None]
                self.arrived = exchange(self.value, *order[-1])
            elif step <= len(order):
                arrived, value = line.after((self.arrived, self.value))
                self.value = jnp.concatenate([value, arrived], axis=0)
                self.arrived = exchange(self.value, *order[len(order) - step])
                if step == len(order):
                    self.put(self.value, False)
            else:
                arrived, value = line.after((self.arrived, self.value))
                self.value = self.put(arrived, True)
                line.done(Placed("qkv"))
                return
            line.done(self)

        def put(self, chunks, far):
            bits = [bit for axis, bit in hops("q")[1:]]
            whole["qkv"] = put_three_in_place(
                places["q"], chunks, far, whole["qkv"], bits, 2, "place_qkv"
            )
            return whole["qkv"]

    class Tokens:
        def __init__(self):
            self.step = 0

        def advance(self):
            order = hops("T")
            if self.step == 0:
                blocks = [row_blocks(part) for part in chains["A"].head_grads]
                pieces = line.after(
                    [jnp.concatenate([m[k] for m in blocks], axis=-1) for k in range(ctx_count)]
                )
                held = {(0, k): piece for k, piece in enumerate(pieces)}
            else:
                bit = order[self.step - 1][1]
                arrived, kept = line.after((self.arrived, self.value))
                held = dict(zip(self.kept, kept))
                for n, (source, target) in enumerate(self.sent):
                    held[source ^ bit, target ^ bit] = arrived[n]
            if self.step < len(order):
                bit = order[self.step][1]
                self.sent = [key for key in sorted(held) if key[1] & bit]
                self.kept = [key for key in sorted(held) if not key[1] & bit]
                self.arrived = exchange(jnp.stack([held[key] for key in self.sent]), *order[self.step])
                self.value = [held[key] for key in self.kept]
            else:
                mixed = reorder([held[k, 0] for k in range(ctx_count)], ctx)
                mixed_grad = jnp.concatenate(
                    [m[..., t * pair : (t + 1) * pair] for t in range(3) for m in mixed], axis=-1
                )
                self.value = summed_grad + back_project(mixed_grad, qkv_full)
            self.step += 1
            line.done(self)

    chains.update(A=Attention(), v=Vectors(), q=QueryKeyValue(), T=Tokens())
    for name in EVENTS:
        chain = chains[name]
        chain.advance()
        if name in targets and chain.step == targets[name][1]:
            line.done(Placed(targets[name][0]))

    reduced = []
    offset = 0
    sizes = [part.shape[0] for part in layer_vectors] + [width, width]
    for size in sizes:
        reduced.append(half_of(chains["v"].value[offset : offset + size], core, 0))
        offset += size
    token_grad = chains["T"].value
    qkv_grad, in_grad, back_grad, out_grad = (
        whole["qkv"], whole["in"], whole["back"], whole["out"]
    )
    bias_grads = reduced[7:]
    return (
        output,
        token_grad,
        qkv_grad,
        bias_grads[0],
        bias_grads[1],
        out_grad,
        reduced[4],
        reduced[5],
        reduced[6],
        in_grad,
        reduced[0],
        back_grad,
        reduced[1],
        reduced[2],
        reduced[3],
    )


def head_parallel(mesh):
    sizes = [mesh.shape["dp"], mesh.shape["ctx"]]
    return sizes == [2, 8] and mesh.shape["fsdp"] == 2 and 2 * sizes[1] == HEADS


def solution(mesh):
    in_specs = (
        P(("dp", "fsdp"), "ctx", None),
        P("fsdp", None),
        P("fsdp"),
        P("fsdp"),
        P("fsdp", None),
        P("fsdp"),
        P("fsdp"),
        P("fsdp"),
        P("fsdp", None),
        P("fsdp"),
        P("fsdp", None),
        P("fsdp"),
        P("fsdp"),
        P("fsdp"),
        P(("dp", "fsdp"), "ctx", None),
    )
    out_specs = (
        P(("dp", "fsdp"), "ctx", None),
        P(("dp", "fsdp"), "ctx", None),
        P("fsdp", None),
        P("fsdp"),
        P("fsdp"),
        P("fsdp", None),
        P("fsdp"),
        P("fsdp"),
        P("fsdp"),
        P("fsdp", None),
        P("fsdp"),
        P("fsdp", None),
        P("fsdp"),
        P("fsdp"),
        P("fsdp"),
    )
    body = on_device if head_parallel(mesh) else ring_on_device
    return jax.shard_map(
        body, mesh=mesh, in_specs=in_specs, out_specs=out_specs, check_vma=False
    )
```
